32 devices in a mesh: head: 2 (over x), blk: 16 (over z, y, core).
Axes of the slice: x: 2, y: 2, z: 4, core: 2. Of those that a mesh axis runs over, the one named last changes fastest.
Arguments:
- tokens: bfloat16 [2, 2048, 1024], P(None, ('head', 'blk')), may hold values from -6 to 6
- cotangent: bfloat16 [2, 2048, 1024], P(None, ('head', 'blk')), may hold values from -6 to 6
- ln1_gain: bfloat16 [1024], P(('head', 'blk')), may hold values from 0.5 to 1.5
- ln1_bias: bfloat16 [1024], P(('head', 'blk')), may hold values from -3 to 3
- w_query: bfloat16 [1024, 1024], P(('head', 'blk')), may hold values from -0.3125 to 0.3125
- w_key: bfloat16 [1024, 1024], P(('head', 'blk')), may hold values from -0.3125 to 0.3125
- w_value: bfloat16 [1024, 1024], P(('head', 'blk')), may hold values from -0.1875 to 0.1875
- w_out: bfloat16 [1024, 1024], P(('head', 'blk')), may hold values from -0.5 to 0.5
- ln2_gain: bfloat16 [1024], P(('head', 'blk')), may hold values from 0.5 to 1.5
- ln2_bias: bfloat16 [1024], P(('head', 'blk')), may hold values from -3 to 3
- w_inner: bfloat16 [1024, 4096], P(('head', 'blk')), may hold values from -0.1875 to 0.1875
- w_outer: bfloat16 [4096, 1024], P(('head', 'blk')), may hold values from -0.125 to 0.125
Outputs:
- result: bfloat16 [2, 2048, 1024], P(None, ('head', 'blk'))
- grad_tokens: float32 [2, 2048, 1024], P(None, ('head', 'blk'))
- grad_ln1_gain: float32 [1024], P(('head', 'blk'))
- grad_ln1_bias: float32 [1024], P(('head', 'blk'))
- grad_w_query: float32 [1024, 1024], P(('head', 'blk'))
- grad_w_key: float32 [1024, 1024], P(('head', 'blk'))
- grad_w_value: float32 [1024, 1024], P(('head', 'blk'))
- grad_w_out: float32 [1024, 1024], P(('head', 'blk'))
- grad_ln2_gain: float32 [1024], P(('head', 'blk'))
- grad_ln2_bias: float32 [1024], P(('head', 'blk'))
- grad_w_inner: float32 [1024, 4096], P(('head', 'blk'))
- grad_w_outer: float32 [4096, 1024], P(('head', 'blk'))
The draws below stay inside these ranges and needn't reach their ends.
All inputs are finite; a program needn't handle non-finite values.
Results may differ from the reference program's by a relative error of at most 0.015.
The reference program's roundings to bfloat16 on the way count: a program that leaves them out, or rounds other values in their place, can miss the bound.
Values may be sent and summed in bfloat16 or wider, within the bound.
No kernel may reach another device: no remote copies, remote signals or barrier semaphores. Data moves between devices by JAX's collectives and lax.ppermute only.
A program may use at most 320 MiB of HBM per device.

```python
import math
import jax
import jax.numpy as jnp
from jax import lax

D = 1024
HEADS = 8
HD = 128
FF = 4096
SEQS = 2
LEN = 2048


def shard_levels(own_key, extent, shards, least, largest):
    level = 1.0
    for axis_at, shards_of in shards:
        steps = jax.random.uniform(jax.random.fold_in(jax.random.fold_in(own_key, 6), axis_at), (shards_of,), jnp.float32, least / len(shards), largest / len(shards))
        level = level * jnp.repeat(jnp.exp(steps), extent[axis_at] // shards_of).reshape((-1,) + (1,) * (len(extent) - 1 - axis_at))
    return level


def normal_values(key, dims, spread, most, shards=(), kind=jnp.bfloat16):
    factor_of = shard_levels(key, dims, shards, -0.22, 0.18) if shards else 1.0
    entries = jax.random.normal(key, dims, jnp.float32) * spread * factor_of
    return jnp.minimum(jnp.maximum(entries, -most), most).astype(kind)


def setup_inputs(seed: int = 0) -> dict:
    splits = jax.random.split(jax.random.key(seed), 13)
    return {
        "tokens": normal_values(splits[0], (SEQS, LEN, D), 1.0, 6.0, ((1, 32),)),
        "cotangent": normal_values(splits[1], (SEQS, LEN, D), 1.0, 6.0, ((1, 32),)),
        "ln1_gain": jnp.clip(1.0 + 0.1 * jax.random.normal(splits[2], (D,), jnp.float32), 0.5, 1.5).astype(jnp.bfloat16),
        "ln1_bias": normal_values(splits[3], (D,), 0.3, 3.0, ((0, 32),)),
        "w_query": normal_values(splits[4], (D, D), (2 * D // 5) ** -0.5, 0.3125, ((0, 32),)),
        "w_key": normal_values(splits[5], (D, D), (2 * D // 5) ** -0.5, 0.3125, ((0, 32),)),
        "w_value": normal_values(splits[6], (D, D), D ** -0.5, 0.1875, ((0, 32),)),
        "w_out": normal_values(splits[7], (D, D), (D // 8) ** -0.5, 0.5, ((0, 32),)),
        "ln2_gain": jnp.clip(1.0 + 0.1 * jax.random.normal(splits[8], (D,), jnp.float32), 0.5, 1.5).astype(jnp.bfloat16),
        "ln2_bias": normal_values(splits[9], (D,), 0.3, 3.0, ((0, 32),)),
        "w_inner": normal_values(splits[10], (D, FF), D ** -0.5, 0.1875, ((0, 32),)),
        "w_outer": normal_values(splits[11], (FF, D), (FF // 2) ** -0.5, 0.125, ((0, 32),)),
    }


@jax.custom_vjp
def low(v):
    return lax.optimization_barrier(v.astype(jnp.bfloat16)).astype(jnp.float32)

@jax.custom_vjp
def low_back(v):
    return v

def low_keep(v):
    return (low(v), None)

def low_pass(kept, grad):
    return (grad,)

def back_keep(v):
    return (v, None)

def back_low(kept, grad):
    return (low(grad),)
low.defvjp(low_keep, low_pass)
low_back.defvjp(back_keep, back_low)
highest = lax.Precision.HIGHEST
eps_norm = 1e-05
gelu_coef = math.sqrt(2.0 / math.pi)

def gelu_tanh(values):
    return 0.5 * values * (1.0 + jnp.tanh(gelu_coef * (values + 0.044715 * values * values * values)))

def project(former, latter):
    return jnp.dot(former, latter, precision=highest, preferred_element_type=jnp.float32)

def norm_layer(values, norm_gain, norm_bias):
    centered = values - lax.optimization_barrier(jnp.mean(values, -1, keepdims=True))
    inverse = lax.rsqrt(lax.optimization_barrier(jnp.mean(centered * centered, -1, keepdims=True)) + eps_norm)
    return centered * inverse * norm_gain + norm_bias

def attend(query, keys, values):
    length = query.shape[0]
    block_rows = min(512, length)
    key_pos = jnp.arange(length, dtype=jnp.int32)
    query_blocks = query.reshape(length // block_rows, block_rows, HEADS, HD)

    def one_block(inputs):
        query_block, block_index = inputs
        scores = jnp.einsum('qhd,khd->hqk', query_block, keys, precision=highest) * HD ** (-0.5)
        scores = low_back(scores)
        query_pos = block_index * block_rows + jnp.arange(block_rows, dtype=jnp.int32)
        allowed = key_pos[None, None, :] <= query_pos[None, :, None]
        scores = jnp.where(allowed, scores, -1e+30)
        weights = low(jax.nn.softmax(scores, axis=-1))
        return jnp.einsum('hqk,khd->qhd', weights, values, precision=highest)
    outputs = lax.map(jax.checkpoint(one_block), (query_blocks, jnp.arange(length // block_rows, dtype=jnp.int32)))
    return outputs.reshape(length, HEADS * HD)

def block_layer(tokens_f, ln1_gain, ln1_bias, w_query, w_key, w_value, w_out, ln2_gain, ln2_bias, w_inner, w_outer):
    length = tokens_f.shape[0]
    normed_one = low(norm_layer(tokens_f, ln1_gain, ln1_bias))
    query = low(low_back(project(normed_one, w_query)))
    keys = low(low_back(project(normed_one, w_key)))
    values = low(low_back(project(normed_one, w_value)))
    attn_out = attend(query.reshape(length, HEADS, HD), keys.reshape(length, HEADS, HD), values.reshape(length, HEADS, HD))
    mixed_out = low(low_back(attn_out))
    middle = tokens_f + low_back(project(mixed_out, w_out))
    normed_two = low(norm_layer(middle, ln2_gain, ln2_bias))
    hidden = low(gelu_tanh(low_back(project(normed_two, w_inner))))
    return middle + project(hidden, w_outer)

def reference(tokens, cotangent, ln1_gain, ln1_bias, w_query, w_key, w_value, w_out, ln2_gain, ln2_bias, w_inner, w_outer):
    params = (ln1_gain.astype(jnp.float32), ln1_bias.astype(jnp.float32), w_query.astype(jnp.float32), w_key.astype(jnp.float32), w_value.astype(jnp.float32), w_out.astype(jnp.float32), ln2_gain.astype(jnp.float32), ln2_bias.astype(jnp.float32), w_inner.astype(jnp.float32), w_outer.astype(jnp.float32))

    def per_sequence(totals, inputs):
        seq_tokens, seq_grad = inputs
        output_f, pullback = jax.vjp(block_layer, seq_tokens.astype(jnp.float32), *params)
        grads = pullback(seq_grad.astype(jnp.float32))
        totals = tuple((total_one + grad_one for total_one, grad_one in zip(totals, grads[1:])))
        return (totals, (output_f.astype(jnp.bfloat16), grads[0]))
    zeros = tuple((jnp.zeros_like(param_one) for param_one in params))
    totals, (outputs, grad_in) = lax.scan(per_sequence, zeros, (tokens, cotangent))
    return (outputs, grad_in, totals[0], totals[1], totals[2], totals[3], totals[4], totals[5], totals[6], totals[7], totals[8], totals[9])
```

```python
import functools
import math

import jax
import jax.numpy as jnp
from jax import lax
from jax.experimental import pallas as pl
from jax.experimental.pallas import tpu as pltpu
from jax.sharding import Mesh
from jax.sharding import PartitionSpec as P

HD = 128
TILE = 256
SCALE = HD ** (-0.5)
MASKED = -1e30
eps_norm = 1e-05
gelu_coef = math.sqrt(2.0 / math.pi)
BF = jnp.bfloat16
F32 = jnp.float32


def mm(a, b):
    return jnp.dot(a, b, preferred_element_type=F32)


def mm_nt(a, b):
    return lax.dot_general(a, b, (((1,), (1,)), ((), ())), preferred_element_type=F32)


def mm_tn(a, b):
    return lax.dot_general(a, b, (((0,), (0,)), ((), ())), preferred_element_type=F32)


def norm_stats(values):
    centered = values - jnp.mean(values, -1, keepdims=True)
    inverse = lax.rsqrt(jnp.mean(centered * centered, -1, keepdims=True) + eps_norm)
    return centered * inverse, inverse


def norm_back(grad_normed, scaled, inverse, gain):
    g = grad_normed * gain
    return inverse * (
        g - jnp.mean(g, -1, keepdims=True) - scaled * jnp.mean(g * scaled, -1, keepdims=True)
    )


def swap(v, axis):
    return lax.ppermute(v, axis, [(0, 1), (1, 0)])


def pick(v, index, axis=0):
    return lax.dynamic_index_in_dim(v, index, axis, keepdims=False)


def pair_gather(v, axis):
    other = swap(v, axis)
    first = lax.axis_index(axis) == 0
    return jnp.stack([jnp.where(first, v, other), jnp.where(first, other, v)])


def pair_scatter(v, axis, dim):
    me = lax.axis_index(axis)
    return pick(v, me, dim) + swap(pick(v, 1 - me, dim).astype(BF), axis).astype(F32)


def z_shift(v, k):
    return lax.ppermute(v, "za", [(s, (s + k) % 4) for s in range(4)])


def t_gather(v):
    if lax.axis_size("za") * lax.axis_size("zb") != 4:
        return lax.all_gather(v, ("za", "zb"), axis=0, tiled=False)
    z = lax.axis_index("za")
    out = jnp.zeros((4,) + v.shape, v.dtype)
    for k in range(4):
        part = v if k == 0 else z_shift(v, k)
        out = lax.dynamic_update_index_in_dim(out, part, (z - k) % 4, 0)
    return out


def t_scatter(v):
    if lax.axis_size("za") * lax.axis_size("zb") != 4:
        return lax.psum_scatter(v, ("za", "zb"), scatter_dimension=0, tiled=False)
    z = lax.axis_index("za")
    total = pick(v, z)
    for k in range(1, 4):
        total = total + z_shift(pick(v, (z + k) % 4).astype(BF), k).astype(F32)
    return total


def plane_gather(v):
    half = v.shape[0] // 2
    a, b = v[:half], v[half:]
    a = jnp.stack([a, swap(a, "x")])
    b = jnp.stack([b, swap(b, "y")])
    a = jnp.stack([a, swap(a, "y")])
    b = jnp.stack([b, swap(b, "x")])
    both = jnp.stack([a, b])
    return jnp.stack([both, swap(both, "c")]).reshape(8 * v.shape[0], v.shape[1])


def plane_scatter(v):
    rows, width = v.shape
    v = v.reshape(2, 2, 2, 2, rows // 16, width)

    def fold(u, axis):
        return u[0] + swap(u[1].astype(BF), axis).astype(F32)

    v = fold(v, "c")
    a, b = v[0], v[1]
    a = fold(a, "y")
    b = fold(b, "x")
    a = fold(a, "x")
    b = fold(b, "y")
    return jnp.concatenate([a, b], 0)


def shares(count, body):
    if count <= 2:
        for k in range(count):
            body(k)
    else:
        lax.fori_loop(0, count, lambda k, c: (body(k), c)[1], 0)


def mask_of(count, q_tile, k_tile, q_share, k_share):
    rows = lax.broadcasted_iota(jnp.int32, (TILE, TILE), 0) + q_tile * TILE
    cols = lax.broadcasted_iota(jnp.int32, (TILE, TILE), 1) + k_tile * TILE
    q_pos = (lax.shift_right_logical(rows, 6) * count + q_share) * 64 + (rows & 63)
    k_pos = (lax.shift_right_logical(cols, 6) * count + k_share) * 64 + (cols & 63)
    return k_pos <= q_pos


def forward_kernel(count, meta, q_ref, k_ref, v_ref, o_ref, of_ref, lse_ref, qa, ka, va, s_ref):
    blocks = q_ref.shape[0]
    for j in range(blocks):
        slot = meta[j]
        rows = pl.ds(j * 64, 64)
        qa[rows, :] = q_ref[slot]

        def place(k, rows=rows, slot=slot):
            ka[k, rows, :] = k_ref[k, slot]
            va[k, rows, :] = v_ref[k, slot]

        shares(count, place)
    mine = meta[blocks]
    tiles = blocks * 64 // TILE
    for t in range(tiles):
        q = qa[pl.ds(t * TILE, TILE), :]
        top = jnp.full((TILE, 1), MASKED, F32)
        for u in range(t + 1):
            cols = pl.ds(u * TILE, TILE)

            def score(k, top, u=u, cols=cols):
                s = mm_nt(q, ka[k, cols, :]) * SCALE
                if u == t:
                    s = jnp.where(mask_of(count, t, u, mine, meta[blocks + 1 + k]), s, MASKED)
                s_ref[k * tiles + u] = s
                return jnp.maximum(top, jnp.max(s, -1, keepdims=True))

            if count <= 2:
                for k in range(count):
                    top = score(k, top)
            else:
                top = lax.fori_loop(0, count, score, top)
        total = jnp.zeros((TILE, 1), F32)
        for u in range(t + 1):

            def expo(k, total, u=u):
                p = jnp.exp(s_ref[k * tiles + u] - top)
                s_ref[k * tiles + u] = p
                return total + jnp.sum(p, -1, keepdims=True)

            if count <= 2:
                for k in range(count):
                    total = expo(k, total)
            else:
                total = lax.fori_loop(0, count, expo, total)
        inverse = 1.0 / total
        out = jnp.zeros((TILE, HD), F32)
        for u in range(t + 1):
            cols = pl.ds(u * TILE, TILE)

            def weigh(k, out, u=u, cols=cols):
                p = (s_ref[k * tiles + u] * inverse).astype(BF)
                return out + mm(p, va[k, cols, :])

            if count <= 2:
                for k in range(count):
                    out = weigh(k, out)
            else:
                out = lax.fori_loop(0, count, weigh, out)
        rows = pl.ds(t * TILE, TILE)
        of_ref[rows, :] = out
        o_ref[rows, :] = out.astype(BF)
        lse_ref[rows, :] = jnp.broadcast_to(top + jnp.log(total), (TILE, HD))


def attention_forward(count, meta, q, k, v):
    blocks = q.shape[0]
    rows = blocks * 64
    tiles = rows // TILE
    vm = pl.BlockSpec(memory_space=pltpu.VMEM)
    pairs = tiles * (tiles + 1) // 2 * count
    return pl.pallas_call(
        functools.partial(forward_kernel, count),
        in_specs=[pl.BlockSpec(memory_space=pltpu.SMEM), vm, vm, vm],
        out_specs=[vm] * 6,
        out_shape=[
            jax.ShapeDtypeStruct((rows, HD), BF),
            jax.ShapeDtypeStruct((rows, HD), F32),
            jax.ShapeDtypeStruct((rows, HD), F32),
            jax.ShapeDtypeStruct((rows, HD), BF),
            jax.ShapeDtypeStruct((count, rows, HD), BF),
            jax.ShapeDtypeStruct((count, rows, HD), BF),
        ],
        scratch_shapes=[pltpu.VMEM((count * tiles, TILE, TILE), F32)],
        cost_estimate=pl.CostEstimate(
            flops=pairs * TILE * TILE * HD * 4,
            bytes_accessed=rows * HD * 2 * (2 + 4 * count) + rows * HD * 8,
            transcendentals=pairs * TILE * TILE,
        ),
        compiler_params=pltpu.CompilerParams(vmem_limit_bytes=(16 if count <= 2 else 52) << 20),
        name="attention_forward",
    )(meta, q, k, v)


def backward_kernel(count, meta, q_ref, k_ref, v_ref, go_ref, of_ref, lse_ref, gq_ref, gk, gv):
    rows_all = q_ref.shape[0]
    blocks = rows_all // 64
    mine = meta[blocks]
    tiles = rows_all // TILE

    def zero(k):
        gk[k] = jnp.zeros((rows_all, HD), F32)
        gv[k] = jnp.zeros((rows_all, HD), F32)

    shares(count, zero)
    for t in range(tiles):
        rows = pl.ds(t * TILE, TILE)
        q = q_ref[rows, :]
        go = go_ref[rows, :]
        delta = jnp.sum(go.astype(F32) * of_ref[rows, :], -1, keepdims=True)
        lse = lse_ref[rows, :][:, :1]
        gq = jnp.zeros((TILE, HD), F32)
        for u in range(t + 1):
            cols = pl.ds(u * TILE, TILE)

            def one(k, gq, u=u, cols=cols):
                kk = k_ref[k, cols, :]
                p = jnp.exp(mm_nt(q, kk) * SCALE - lse)
                if u == t:
                    p = jnp.where(mask_of(count, t, u, mine, meta[blocks + 1 + k]), p, 0.0)
                gv[k, cols, :] += mm_tn(p.astype(BF), go)
                ds = (p * (mm_nt(go, v_ref[k, cols, :]) - delta)).astype(BF)
                gk[k, cols, :] += mm_tn(ds, q)
                return gq + mm(ds, kk)

            if count <= 2:
                for k in range(count):
                    gq = one(k, gq)
            else:
                gq = lax.fori_loop(0, count, one, gq)
        gq_ref[rows, :] = (gq * SCALE).astype(BF)

    def scale(k):
        gk[k] = gk[k] * SCALE

    shares(count, scale)


def attention_backward(count, meta, q, k, v, go, of, lse):
    rows = q.shape[0]
    tiles = rows // TILE
    vm = pl.BlockSpec(memory_space=pltpu.VMEM)
    pairs = tiles * (tiles + 1) // 2 * count
    return pl.pallas_call(
        functools.partial(backward_kernel, count),
        in_specs=[pl.BlockSpec(memory_space=pltpu.SMEM)] + [vm] * 6,
        out_specs=[vm] * 3,
        out_shape=[
            jax.ShapeDtypeStruct((rows, HD), BF),
            jax.ShapeDtypeStruct((count, rows, HD), F32),
            jax.ShapeDtypeStruct((count, rows, HD), F32),
        ],
        cost_estimate=pl.CostEstimate(
            flops=pairs * TILE * TILE * HD * 10,
            bytes_accessed=rows * HD * (16 + 12 * count),
            transcendentals=pairs * TILE * TILE,
        ),
        compiler_params=pltpu.CompilerParams(vmem_limit_bytes=(16 if count <= 2 else 52) << 20),
        name="attention_backward",
    )(meta, q, k, v, go, of, lse)


def reorder_kernel(meta, g_ref, out_ref):
    for j in range(g_ref.shape[0]):
        out_ref[meta[j]] = g_ref[j]


def reorder(meta, g):
    vm = pl.BlockSpec(memory_space=pltpu.VMEM)
    return pl.pallas_call(
        reorder_kernel,
        in_specs=[pl.BlockSpec(memory_space=pltpu.SMEM), vm],
        out_specs=vm,
        out_shape=jax.ShapeDtypeStruct(g.shape, g.dtype),
        cost_estimate=pl.CostEstimate(flops=0, bytes_accessed=4 * g.size, transcendentals=0),
        compiler_params=pltpu.CompilerParams(vmem_limit_bytes=8 << 20),
        name="reorder",
    )(meta, g)


def on_device(
    hd_axes,
    sh_axes,
    tokens,
    cotangent,
    ln1_gain,
    ln1_bias,
    w_query,
    w_key,
    w_value,
    w_out,
    ln2_gain,
    ln2_bias,
    w_inner,
    w_outer,
):
    small = hd_axes == ("za", "y")
    everything = ("x", "za", "zb", "y", "c")
    planes = lax.axis_size("za") * lax.axis_size("zb")
    count = math.prod(lax.axis_size(a) for a in sh_axes)
    devices = 8 * planes
    seqs, tok, width = tokens.shape
    rows = seqs * tok
    x, z, y, c = (lax.axis_index(a) for a in ("x", "za", "y", "c"))
    share = lax.axis_index(sh_axes)

    gains = jnp.stack([ln1_gain, ln1_bias, ln2_gain, ln2_bias]).reshape(1, -1)
    gains = lax.all_to_all(
        jnp.broadcast_to(gains, (devices, gains.shape[1])), everything, 0, 0, tiled=True
    )
    gains = gains.reshape(devices, 4, -1).transpose(1, 0, 2).reshape(4, width).astype(F32)
    gain_one, bias_one, gain_two, bias_two = gains[0], gains[1], gains[2], gains[3]

    block = jnp.stack([pick(tokens, x), swap(pick(tokens, 1 - x), "x")])
    if small:
        parts = []
        for k in range(4):
            part = block if k == 0 else z_shift(block, k)
            parts += [part, swap(part, "y")]
        seen = jnp.stack(parts)
    else:
        seen = lax.all_gather(block, hd_axes, axis=0, tiled=False)
    at = jnp.arange(16, dtype=jnp.int32)
    at_x, at_hd = at // 8, at % 8
    if small:
        slots = (((z - at_hd // 2) % 4) * 2 + (y ^ (at_hd % 2))) * 2 + (at_x ^ x)
    else:
        slots = at_hd * 2 + (at_x ^ x)

    head_w = jnp.stack([w_query, w_key, w_value], 1).reshape(-1, 3, 8, HD).transpose(2, 0, 1, 3)
    head_w = lax.all_to_all(head_w.reshape(8, -1, 3 * HD), hd_axes, 0, 0, tiled=True)
    head_w = pair_gather(head_w, "x")
    for axis in reversed(sh_axes):
        if lax.axis_size(axis) == 2:
            head_w = pair_gather(head_w, axis)
        else:
            head_w = lax.all_gather(head_w, axis, axis=0, tiled=False)
    head_w = jnp.moveaxis(
        head_w.reshape(count, 2, 8, -1, 3 * HD), 0, 2
    ).reshape(width, 3 * HD)

    unit = w_outer.shape[0]
    inner_w = w_inner.reshape(-1, 2, planes, 4, unit).transpose(1, 3, 0, 2, 4)
    inner_w = lax.all_to_all(
        inner_w.reshape(8, -1, planes * unit), ("x", "y", "c"), 0, 0, tiled=True
    )
    inner_w = t_gather(inner_w)
    inner_w = (
        inner_w.reshape(planes, 2, -1, planes * unit).transpose(1, 0, 2, 3).reshape(width, -1)
    )
    outer_w = t_gather(w_outer).reshape(-1, width)
    grad_plane = plane_gather(cotangent.reshape(rows, width))

    out_w = lax.all_gather(w_out, everything, axis=0, tiled=True)
    qkv_w = lax.all_gather(
        jnp.concatenate([w_query, w_key, w_value], 1), everything, axis=0, tiled=True
    )

    normed, _ = norm_stats(seen.reshape(-1, width).astype(F32))
    h1 = (normed * gain_one + bias_one).astype(BF)
    qkv = mm(h1, head_w).astype(BF)
    query = qkv[:, :HD].reshape(16, tok, HD)
    kv = qkv[:, HD:]
    if count == 2:
        kv = jnp.stack([kv, swap(kv, "c")])
        order = jnp.stack([share, 1 - share])
    else:
        kv = lax.all_gather(kv, sh_axes, axis=0, tiled=False)
        order = jnp.arange(count)
    kv = kv.reshape(count, 16, tok, 2 * HD)
    meta = jnp.concatenate([slots, share.reshape(1), order]).astype(jnp.int32)
    out, out_f, lse, q_at, k_at, v_at = attention_forward(
        count, meta, query, kv[..., :HD], kv[..., HD:]
    )

    mixed = lax.all_to_all(out.reshape(16, tok, HD), ("x",) + hd_axes, 0, 0, tiled=True)
    mixed = mixed.reshape(2, 8, tok, HD).transpose(0, 2, 1, 3).reshape(rows, width)
    flat_in = tokens.reshape(rows, width).astype(F32)
    middle = flat_in + mm(mixed, out_w)
    scaled_two, inverse_two = norm_stats(middle)
    h2 = plane_gather((scaled_two * gain_two + bias_two).astype(BF))

    inner = mm(h2, inner_w)
    bent = jnp.tanh(gelu_coef * (inner + 0.044715 * inner * inner * inner))
    hidden = (0.5 * inner * (1.0 + bent)).astype(BF)
    slope = 0.5 * (1.0 + bent) + 0.5 * inner * (1.0 - bent * bent) * gelu_coef * (
        1.0 + 3.0 * 0.044715 * inner * inner
    )
    grad_inner = (mm_nt(grad_plane, outer_w) * slope).astype(BF)
    grad_h2 = plane_scatter(mm_nt(grad_inner, inner_w))
    result = (middle + plane_scatter(mm(hidden, outer_w))).astype(BF)
    grad_outer = mm_tn(hidden, grad_plane).reshape(planes, -1, width)
    grad_outer = t_scatter(grad_outer)
    grad_in = mm_tn(h2, grad_inner).reshape(2, planes, -1, planes * unit).transpose(1, 0, 2, 3)
    grad_in = t_scatter(grad_in).astype(BF).reshape(8, -1, planes * unit)
    grad_in = lax.all_to_all(grad_in, ("x", "y", "c"), 0, 0, tiled=True)
    grad_in = grad_in.reshape(2, 4, -1, planes, unit).transpose(2, 0, 3, 1, 4)
    grad_in = grad_in.reshape(-1, devices * unit).astype(F32)

    grad_out = cotangent.reshape(rows, width).astype(F32)
    grad_middle = grad_out + norm_back(grad_h2, scaled_two, inverse_two, gain_two)
    branch = grad_middle.astype(BF)
    go = mm_nt(branch, out_w).astype(BF)
    go = go.reshape(2, tok, 8, HD).transpose(0, 2, 1, 3).reshape(16, tok, HD)
    go = lax.all_to_all(go, ("x",) + hd_axes, 0, 0, tiled=True).reshape(16 * tok, HD)
    grad_out_w = mm_tn(mixed, branch).reshape(2, planes, 2, 2, -1, width)
    grad_out_w = pair_scatter(grad_out_w, "c", 3)
    grad_out_w = pair_scatter(grad_out_w, "y", 2)
    grad_out_w = pair_scatter(grad_out_w, "x", 0)
    grad_out_w = t_scatter(grad_out_w)

    gq, gk, gv = attention_backward(count, meta, q_at, k_at, v_at, go, out_f, lse)
    gkv = jnp.concatenate([gk, gv], -1)
    if count == 2:
        gkv = gkv[0] + swap(gkv[1].astype(BF), "c").astype(F32)
    else:
        gkv = lax.psum_scatter(gkv, sh_axes, scatter_dimension=0, tiled=False)
    grads = jnp.concatenate([gq, gkv.astype(BF)], -1).reshape(16, tok, 3 * HD)
    back = lax.all_to_all(grads, ("x",) + hd_axes, 0, 0, tiled=True)
    back = back.reshape(2, 8, tok, 3, HD).transpose(0, 2, 3, 1, 4).reshape(rows, 3 * width)

    head_g = mm_tn(h1, reorder(meta, grads).reshape(16 * tok, 3 * HD))
    head_g = head_g.reshape((2, 8) + tuple(lax.axis_size(a) for a in sh_axes) + (-1, 3 * HD))
    for axis in sh_axes:
        if lax.axis_size(axis) == 2:
            head_g = pair_scatter(head_g, axis, 2)
        else:
            head_g = lax.psum_scatter(head_g, axis, scatter_dimension=2, tiled=False)
    head_g = pair_scatter(head_g, "x", 0).astype(BF)
    head_g = lax.all_to_all(head_g, hd_axes, 0, 0, tiled=True)
    head_g = head_g.reshape(8, -1, 3, HD).transpose(2, 1, 0, 3).reshape(3, -1, width).astype(F32)

    scaled_one, inverse_one = norm_stats(flat_in)
    grad_h1 = mm_nt(back, qkv_w)
    grad_input = grad_middle + norm_back(grad_h1, scaled_one, inverse_one, gain_one)

    sums = jnp.stack(
        [
            jnp.sum(grad_h1 * scaled_one, 0),
            jnp.sum(grad_h1, 0),
            jnp.sum(grad_h2 * scaled_two, 0),
            jnp.sum(grad_h2, 0),
        ]
    )
    sums = sums.reshape(4, devices, -1).transpose(1, 0, 2).reshape(devices, -1)
    sums = lax.all_to_all(sums, everything, 0, 0, tiled=True)
    sums = jnp.sum(sums, 0).reshape(4, -1)
    return (
        result.reshape(seqs, tok, width),
        grad_input.reshape(seqs, tok, width),
        sums[0],
        sums[1],
        head_g[0],
        head_g[1],
        head_g[2],
        grad_out_w,
        sums[2],
        sums[3],
        grad_in,
        grad_outer,
    )


def solution(mesh):
    blocks = mesh.shape["blk"]
    if blocks == 16:
        sizes, hd_axes, sh_axes = (2, 4, 1, 2, 2), ("za", "y"), ("c",)
    else:
        sizes, hd_axes, sh_axes = (2, 8, blocks // 32, 2, 2), ("za",), ("zb", "y", "c")
    fine = Mesh(mesh.devices.reshape(sizes), ("x", "za", "zb", "y", "c"))
    whole = ("x", "za", "zb", "y", "c")
    tok, row, vec = P(None, whole, None), P(whole, None), P(whole)
    in_specs = (tok, tok, vec, vec, row, row, row, row, vec, vec, row, row)
    out_specs = (tok, tok, vec, vec, row, row, row, row, vec, vec, row, row)
    return jax.shard_map(
        functools.partial(on_device, hd_axes, sh_axes),
        mesh=fine,
        in_specs=in_specs,
        out_specs=out_specs,
        check_vma=False,
    )
```

```python
import functools
import math

import jax
import jax.numpy as jnp
from jax import lax
from jax.experimental import pallas as pl
from jax.experimental.pallas import tpu as pltpu
from jax.sharding import Mesh
from jax.sharding import PartitionSpec as P

HD = 128
TILE = 256
SCALE = HD ** (-0.5)
MASKED = -1e30
eps_norm = 1e-05
gelu_coef = math.sqrt(2.0 / math.pi)
BF = jnp.bfloat16
F32 = jnp.float32
AXES = ("x", "za", "zb", "zl", "y", "c")
T_AXES = ("x", "za", "zb")
W_AXES = ("zl", "y", "c")


def mm(a, b):
    return jnp.dot(a, b, preferred_element_type=F32)


def mm_nt(a, b):
    return lax.dot_general(a, b, (((1,), (1,)), ((), ())), preferred_element_type=F32)


def mm_tn(a, b):
    return lax.dot_general(a, b, (((0,), (0,)), ((), ())), preferred_element_type=F32)


def norm_stats(values):
    centered = values - jnp.mean(values, -1, keepdims=True)
    inverse = lax.rsqrt(jnp.mean(centered * centered, -1, keepdims=True) + eps_norm)
    return centered * inverse, inverse


def norm_back(grad_normed, scaled, inverse, gain):
    g = grad_normed * gain
    return inverse * (
        g - jnp.mean(g, -1, keepdims=True) - scaled * jnp.mean(g * scaled, -1, keepdims=True)
    )


def swap(v, axis):
    return lax.ppermute(v, axis, [(0, 1), (1, 0)])


def pick(v, index, axis=0):
    return lax.dynamic_index_in_dim(v, index, axis, keepdims=False)


def pair_gather(v, axis):
    other = swap(v, axis)
    first = lax.axis_index(axis) == 0
    return jnp.stack([jnp.where(first, v, other), jnp.where(first, other, v)])


def pair_scatter(v, axis, dim):
    me = lax.axis_index(axis)
    return pick(v, me, dim) + swap(pick(v, 1 - me, dim).astype(BF), axis).astype(F32)


def after(v, *others):
    return lax.optimization_barrier((v,) + others)[0]


def t_gather(v):
    if lax.axis_size("za") * lax.axis_size("zb") != 2:
        return lax.all_gather(v, T_AXES, axis=0, tiled=False)
    x, z = lax.axis_index("x"), lax.axis_index("za")
    over_x, over_z = swap(v, "x"), swap(v, "za")
    out = jnp.zeros((4,) + v.shape, v.dtype)
    for part, at in (
        (v, 2 * x + z),
        (over_x, 2 * (1 - x) + z),
        (over_z, 2 * x + 1 - z),
        (swap(over_z, "x"), 2 * (1 - x) + 1 - z),
    ):
        out = lax.dynamic_update_index_in_dim(out, part, at, 0)
    return out


def t_scatter(v):
    if lax.axis_size("za") * lax.axis_size("zb") != 2:
        return lax.psum_scatter(v, T_AXES, scatter_dimension=0, tiled=False)
    v = pair_scatter(v.reshape((2, 2) + v.shape[1:]), "x", 0)
    return pair_scatter(v, "za", 0)


def plane_gather(v):
    half = v.shape[0] // 2
    a, b = v[:half], v[half:]
    a = jnp.stack([a, swap(a, "zl")])
    b = jnp.stack([b, swap(b, "y")])
    a = jnp.stack([a, swap(a, "y")])
    b = jnp.stack([b, swap(b, "zl")])
    both = jnp.stack([a, b])
    return jnp.stack([both, swap(both, "c")]).reshape(8 * v.shape[0], v.shape[1])


def plane_scatter(v):
    rows, width = v.shape
    v = v.reshape(2, 2, 2, 2, rows // 16, width)

    def fold(u, axis):
        return u[0] + swap(u[1].astype(BF), axis).astype(F32)

    v = fold(v, "c")
    a, b = v[0], v[1]
    a = fold(a, "y")
    b = fold(b, "zl")
    a = fold(a, "zl")
    b = fold(b, "y")
    return jnp.concatenate([a, b], 0)


def shares(count, body):
    if count <= 2:
        for k in range(count):
            body(k)
    else:
        lax.fori_loop(0, count, lambda k, c: (body(k), c)[1], 0)


def mask_of(count, q_tile, k_tile, q_share, k_share):
    rows = lax.broadcasted_iota(jnp.int32, (TILE, TILE), 0) + q_tile * TILE
    cols = lax.broadcasted_iota(jnp.int32, (TILE, TILE), 1) + k_tile * TILE
    q_pos = (lax.shift_right_logical(rows, 6) * count + q_share) * 64 + (rows & 63)
    k_pos = (lax.shift_right_logical(cols, 6) * count + k_share) * 64 + (cols & 63)
    return k_pos <= q_pos


def forward_kernel(count, meta, q_ref, k_ref, v_ref, o_ref, of_ref, lse_ref, qa, ka, va, s_ref):
    blocks = q_ref.shape[0]
    for j in range(blocks):
        slot = meta[j]
        rows = pl.ds(j * 64, 64)
        qa[rows, :] = q_ref[slot]

        def place(k, rows=rows, slot=slot):
            ka[k, rows, :] = k_ref[k, slot]
            va[k, rows, :] = v_ref[k, slot]

        shares(count, place)
    mine = meta[blocks]
    tiles = blocks * 64 // TILE
    for t in range(tiles):
        q = qa[pl.ds(t * TILE, TILE), :]
        top = jnp.full((TILE, 1), MASKED, F32)
        for u in range(t + 1):
            cols = pl.ds(u * TILE, TILE)

            def score(k, top, u=u, cols=cols):
                s = mm_nt(q, ka[k, cols, :]) * SCALE
                if u == t:
                    s = jnp.where(mask_of(count, t, u, mine, meta[blocks + 1 + k]), s, MASKED)
                s_ref[k * tiles + u] = s
                return jnp.maximum(top, jnp.max(s, -1, keepdims=True))

            if count <= 2:
                for k in range(count):
                    top = score(k, top)
            else:
                top = lax.fori_loop(0, count, score, top)
        total = jnp.zeros((TILE, 1), F32)
        for u in range(t + 1):

            def expo(k, total, u=u):
                p = jnp.exp(s_ref[k * tiles + u] - top)
                s_ref[k * tiles + u] = p
                return total + jnp.sum(p, -1, keepdims=True)

            if count <= 2:
                for k in range(count):
                    total = expo(k, total)
            else:
                total = lax.fori_loop(0, count, expo, total)
        inverse = 1.0 / total
        out = jnp.zeros((TILE, HD), F32)
        for u in range(t + 1):
            cols = pl.ds(u * TILE, TILE)

            def weigh(k, out, u=u, cols=cols):
                p = (s_ref[k * tiles + u] * inverse).astype(BF)
                return out + mm(p, va[k, cols, :])

            if count <= 2:
                for k in range(count):
                    out = weigh(k, out)
            else:
                out = lax.fori_loop(0, count, weigh, out)
        rows = pl.ds(t * TILE, TILE)
        of_ref[rows, :] = out
        o_ref[rows, :] = out.astype(BF)
        lse_ref[rows, :] = jnp.broadcast_to(top + jnp.log(total), (TILE, HD))


def attention_forward(count, meta, q, k, v):
    blocks = q.shape[0]
    rows = blocks * 64
    tiles = rows // TILE
    vm = pl.BlockSpec(memory_space=pltpu.VMEM)
    pairs = tiles * (tiles + 1) // 2 * count
    return pl.pallas_call(
        functools.partial(forward_kernel, count),
        in_specs=[pl.BlockSpec(memory_space=pltpu.SMEM), vm, vm, vm],
        out_specs=[vm] * 6,
        out_shape=[
            jax.ShapeDtypeStruct((rows, HD), BF),
            jax.ShapeDtypeStruct((rows, HD), F32),
            jax.ShapeDtypeStruct((rows, HD), F32),
            jax.ShapeDtypeStruct((rows, HD), BF),
            jax.ShapeDtypeStruct((count, rows, HD), BF),
            jax.ShapeDtypeStruct((count, rows, HD), BF),
        ],
        scratch_shapes=[pltpu.VMEM((count * tiles, TILE, TILE), F32)],
        cost_estimate=pl.CostEstimate(
            flops=pairs * TILE * TILE * HD * 4,
            bytes_accessed=rows * HD * 2 * (2 + 4 * count) + rows * HD * 8,
            transcendentals=pairs * TILE * TILE,
        ),
        compiler_params=pltpu.CompilerParams(vmem_limit_bytes=(16 if count <= 2 else 52) << 20),
        name="attention_forward",
    )(meta, q, k, v)


def backward_kernel(count, meta, q_ref, k_ref, v_ref, go_ref, of_ref, lse_ref, gq_ref, gk, gv):
    rows_all = q_ref.shape[0]
    blocks = rows_all // 64
    mine = meta[blocks]
    tiles = rows_all // TILE

    def zero(k):
        gk[k] = jnp.zeros((rows_all, HD), F32)
        gv[k] = jnp.zeros((rows_all, HD), F32)

    shares(count, zero)
    for t in range(tiles):
        rows = pl.ds(t * TILE, TILE)
        q = q_ref[rows, :]
        go = go_ref[rows, :]
        delta = jnp.sum(go.astype(F32) * of_ref[rows, :], -1, keepdims=True)
        lse = lse_ref[rows, :][:, :1]
        gq = jnp.zeros((TILE, HD), F32)
        for u in range(t + 1):
            cols = pl.ds(u * TILE, TILE)

            def one(k, gq, u=u, cols=cols):
                kk = k_ref[k, cols, :]
                p = jnp.exp(mm_nt(q, kk) * SCALE - lse)
                if u == t:
                    p = jnp.where(mask_of(count, t, u, mine, meta[blocks + 1 + k]), p, 0.0)
                gv[k, cols, :] += mm_tn(p.astype(BF), go)
                ds = (p * (mm_nt(go, v_ref[k, cols, :]) - delta)).astype(BF)
                gk[k, cols, :] += mm_tn(ds, q)
                return gq + mm(ds, kk)

            if count <= 2:
                for k in range(count):
                    gq = one(k, gq)
            else:
                gq = lax.fori_loop(0, count, one, gq)
        gq_ref[rows, :] = (gq * SCALE).astype(BF)

    def scale(k):
        gk[k] = gk[k] * SCALE

    shares(count, scale)


def attention_backward(count, meta, q, k, v, go, of, lse):
    rows = q.shape[0]
    tiles = rows // TILE
    vm = pl.BlockSpec(memory_space=pltpu.VMEM)
    pairs = tiles * (tiles + 1) // 2 * count
    return pl.pallas_call(
        functools.partial(backward_kernel, count),
        in_specs=[pl.BlockSpec(memory_space=pltpu.SMEM)] + [vm] * 6,
        out_specs=[vm] * 3,
        out_shape=[
            jax.ShapeDtypeStruct((rows, HD), BF),
            jax.ShapeDtypeStruct((count, rows, HD), F32),
            jax.ShapeDtypeStruct((count, rows, HD), F32),
        ],
        cost_estimate=pl.CostEstimate(
            flops=pairs * TILE * TILE * HD * 10,
            bytes_accessed=rows * HD * (16 + 12 * count),
            transcendentals=pairs * TILE * TILE,
        ),
        compiler_params=pltpu.CompilerParams(vmem_limit_bytes=(16 if count <= 2 else 52) << 20),
        name="attention_backward",
    )(meta, q, k, v, go, of, lse)


def reorder_kernel(meta, g_ref, out_ref):
    for j in range(g_ref.shape[0]):
        out_ref[meta[j]] = g_ref[j]


def reorder(meta, g):
    vm = pl.BlockSpec(memory_space=pltpu.VMEM)
    return pl.pallas_call(
        reorder_kernel,
        in_specs=[pl.BlockSpec(memory_space=pltpu.SMEM), vm],
        out_specs=vm,
        out_shape=jax.ShapeDtypeStruct(g.shape, g.dtype),
        cost_estimate=pl.CostEstimate(flops=0, bytes_accessed=4 * g.size, transcendentals=0),
        compiler_params=pltpu.CompilerParams(vmem_limit_bytes=8 << 20),
        name="reorder",
    )(meta, g)


def on_device(
    roles,
    tokens,
    cotangent,
    ln1_gain,
    ln1_bias,
    w_query,
    w_key,
    w_value,
    w_out,
    ln2_gain,
    ln2_bias,
    w_inner,
    w_outer,
):
    small, seq_axis, hd_axes, sh_axes, own_axes = roles
    planes = math.prod(lax.axis_size(a) for a in T_AXES)
    count = math.prod(lax.axis_size(a) for a in sh_axes)
    devices = 8 * planes
    seqs, tok, width = tokens.shape
    rows = seqs * tok
    per = w_query.shape[0]
    unit = w_outer.shape[0]
    seq = lax.axis_index(seq_axis)
    share = lax.axis_index(sh_axes)

    block = jnp.stack([pick(tokens, seq), swap(pick(tokens, 1 - seq), seq_axis)])
    if small:
        on_x, on_z, on_y = (swap(block, a) for a in hd_axes)
        on_xz, on_xy, on_zy = swap(on_x, "zl"), swap(on_y, "x"), swap(on_z, "y")
        on_xyz = swap(on_xz, "y")
        seen = jnp.stack([block, on_y, on_z, on_zy, on_x, on_xy, on_xz, on_xyz])
    else:
        seen = lax.all_gather(block, hd_axes, axis=0, tiled=False)
    at = jnp.arange(16, dtype=jnp.int32)
    if small:
        at_x, at_za, at_zl, at_y = at // 8, at // 4 % 2, at // 2 % 2, at % 2
        x, zl, y = (lax.axis_index(a) for a in hd_axes)
        slots = ((at_x ^ x) * 4 + (at_zl ^ zl) * 2 + (at_y ^ y)) * 2 + (at_za ^ seq)
    else:
        slots = at % 8 * 2 + (at // 8 ^ seq)

    gains = jnp.concatenate([ln1_gain, ln1_bias, ln2_gain, ln2_bias])
    gains = jnp.broadcast_to(jnp.pad(gains, (0, HD - gains.shape[0])), (8, 1, HD))
    head_w = jnp.stack([w_query, w_key, w_value]).reshape(3, per, 8, HD).transpose(2, 0, 1, 3)
    head_w = jnp.concatenate([head_w.reshape(8, 3 * per, HD), gains], 1)
    head_w = lax.all_to_all(head_w, hd_axes, 0, 0, tiled=True)
    head_w = pair_gather(head_w, seq_axis)
    for axis in reversed(sh_axes):
        if lax.axis_size(axis) == 2:
            head_w = pair_gather(head_w, axis)
        else:
            head_w = lax.all_gather(head_w, axis, axis=0, tiled=False)
    if small:
        head_w = head_w.reshape(2, 2, 2, 4, 3 * per + 1, HD).transpose(2, 1, 3, 0, 4, 5)
    else:
        head_w = head_w.reshape(count, 16, 3 * per + 1, HD).transpose(1, 0, 2, 3)
    head_w = head_w.reshape(devices, 3 * per + 1, HD)
    gains = head_w[:, -1, : 4 * per].reshape(devices, 4, per).transpose(1, 0, 2)
    gains = gains.reshape(4, width).astype(F32)
    gain_one, bias_one, gain_two, bias_two = gains[0], gains[1], gains[2], gains[3]
    head_w = head_w[:, :-1].reshape(devices, 3, per, HD).transpose(0, 2, 1, 3)
    head_w = head_w.reshape(width, 3 * HD)

    inner_w = w_inner.reshape(per, planes, 8, unit).transpose(2, 0, 1, 3)
    inner_w = lax.all_to_all(inner_w.reshape(8, per, planes * unit), W_AXES, 0, 0, tiled=True)
    inner_w = t_gather(after(inner_w, seen)).reshape(width, planes * unit)
    outer_w = t_gather(w_outer).reshape(planes * unit, width)
    grad_plane = plane_gather(after(cotangent, seen).reshape(rows, width))

    out_w = lax.all_gather(w_out, AXES, axis=0, tiled=True)
    qkv_w = jnp.concatenate([w_query, w_key, w_value], 1)
    qkv_w = lax.all_gather(after(qkv_w, seen), AXES, axis=0, tiled=True)

    normed, _ = norm_stats(seen.reshape(-1, width).astype(F32))
    h1 = (normed * gain_one + bias_one).astype(BF)
    qkv = mm(h1, head_w).astype(BF)
    query = qkv[:, :HD].reshape(16, tok, HD)
    kv = qkv[:, HD:]
    if count == 2:
        kv = jnp.stack([kv, swap(kv, "c")])
        order = jnp.stack([share, 1 - share])
    else:
        kv = lax.all_gather(kv, sh_axes, axis=0, tiled=False)
        order = jnp.arange(count)
    kv = kv.reshape(count, 16, tok, 2 * HD)
    meta = jnp.concatenate([slots, share.reshape(1), order]).astype(jnp.int32)
    out, out_f, lse, q_at, k_at, v_at = attention_forward(
        count, meta, query, kv[..., :HD], kv[..., HD:]
    )

    def to_tokens(v):
        v = lax.all_to_all(v, own_axes, 0, 0, tiled=True)
        n = v.shape[-1] // HD
        if small:
            v = v.reshape(2, 2, 4, tok, n, HD).transpose(1, 3, 4, 0, 2, 5)
        else:
            v = v.reshape(2, 8, tok, n, HD).transpose(0, 2, 3, 1, 4)
        return v.reshape(2, tok, n, 8 * HD)

    mixed = to_tokens(out.reshape(16, tok, HD)).reshape(rows, width)
    flat_in = tokens.reshape(rows, width).astype(F32)
    middle = flat_in + mm(mixed, out_w)
    scaled_two, inverse_two = norm_stats(middle)
    h2 = plane_gather((scaled_two * gain_two + bias_two).astype(BF))

    inner = mm(h2, inner_w)
    bent = jnp.tanh(gelu_coef * (inner + 0.044715 * inner * inner * inner))
    hidden = (0.5 * inner * (1.0 + bent)).astype(BF)
    slope = 0.5 * (1.0 + bent) + 0.5 * inner * (1.0 - bent * bent) * gelu_coef * (
        1.0 + 3.0 * 0.044715 * inner * inner
    )
    grad_inner = (mm_nt(grad_plane, outer_w) * slope).astype(BF)
    grad_h2 = plane_scatter(mm_nt(grad_inner, inner_w))
    grad_outer = mm_tn(hidden, grad_plane).reshape(planes, unit, width)
    grad_outer = t_scatter(grad_outer)
    grad_in = mm_tn(h2, grad_inner).reshape(planes, 8 * per, planes * unit)
    grad_in = t_scatter(grad_in).astype(BF).reshape(8, per, planes * unit)
    result = plane_scatter(mm(hidden, outer_w))

    grad_out = cotangent.reshape(rows, width).astype(F32)
    grad_middle = grad_out + norm_back(grad_h2, scaled_two, inverse_two, gain_two)
    branch = grad_middle.astype(BF)
    go = mm_nt(branch, out_w).astype(BF)
    if small:
        go = go.reshape(2, tok, 2, 4, HD).transpose(2, 0, 3, 1, 4)
    else:
        go = go.reshape(2, tok, 8, HD).transpose(0, 2, 1, 3)
    go = lax.all_to_all(go.reshape(16, tok, HD), own_axes, 0, 0, tiled=True)
    go = go.reshape(16 * tok, HD)

    gq, gk, gv = attention_backward(count, meta, q_at, k_at, v_at, go, out_f, lse)
    gkv = jnp.concatenate([gk, gv], -1)
    if count == 2:
        gkv = gkv[0] + swap(gkv[1].astype(BF), "c").astype(F32)
    else:
        gkv = lax.psum_scatter(gkv, sh_axes, scatter_dimension=0, tiled=False)
    grads = jnp.concatenate([gq, gkv.astype(BF)], -1).reshape(16, tok, 3 * HD)
    grads, result, grad_in, grad_outer = lax.optimization_barrier(
        (grads, result, grad_in, grad_outer)
    )
    back = to_tokens(grads).reshape(rows, 3 * width)
    result = (middle + result).astype(BF)
    grad_in = lax.all_to_all(after(grad_in, back), W_AXES, 0, 0, tiled=True)
    grad_in = grad_in.reshape(8, per, planes, unit).transpose(1, 2, 0, 3)
    grad_in = grad_in.reshape(per, devices * unit).astype(F32)

    head_g = mm_tn(h1, reorder(meta, grads).reshape(16 * tok, 3 * HD))
    head_g = head_g.reshape(tuple(lax.axis_size(a) for a in AXES) + (per, 3 * HD))
    dims = list(AXES)
    for axis in sh_axes[::-1] + (seq_axis,):
        dim = dims.index(axis)
        dims.remove(axis)
        if lax.axis_size(axis) == 2:
            head_g = pair_scatter(head_g, axis, dim)
        else:
            head_g = lax.psum_scatter(head_g, axis, scatter_dimension=dim, tiled=False)
    head_g = head_g.astype(BF).reshape(8, per, 3 * HD)
    head_g = lax.all_to_all(head_g, hd_axes, 0, 0, tiled=True)
    head_g = head_g.reshape(8, per, 3, HD).transpose(2, 1, 0, 3).reshape(3, per, width)
    head_g = head_g.astype(F32)

    grad_out_w = mm_tn(mixed, branch).reshape(planes, 2, 2, 2, per, width)
    grad_out_w = pair_scatter(grad_out_w, "c", 3)
    grad_out_w = pair_scatter(grad_out_w, "y", 2)
    grad_out_w = pair_scatter(grad_out_w, "zl", 1)
    grad_out_w = t_scatter(grad_out_w)

    scaled_one, inverse_one = norm_stats(flat_in)
    grad_h1 = mm_nt(back, qkv_w)
    grad_input = grad_middle + norm_back(grad_h1, scaled_one, inverse_one, gain_one)

    sums = jnp.stack(
        [
            jnp.sum(grad_h1 * scaled_one, 0),
            jnp.sum(grad_h1, 0),
            jnp.sum(grad_h2 * scaled_two, 0),
            jnp.sum(grad_h2, 0),
        ]
    )
    sums = sums.reshape(4, devices, per).transpose(1, 0, 2).reshape(devices, 4 * per)
    sums = lax.all_to_all(sums, AXES, 0, 0, tiled=True)
    sums = jnp.sum(sums, 0).reshape(4, per)
    return (
        result.reshape(seqs, tok, width),
        grad_input.reshape(seqs, tok, width),
        sums[0],
        sums[1],
        head_g[0],
        head_g[1],
        head_g[2],
        grad_out_w,
        sums[2],
        sums[3],
        grad_in,
        grad_outer,
    )


MIB = {}


def call(kernel, outs, ins, coords=None, far=(), raw=(), save=(), scratch=(), name=None):
    vm = pl.BlockSpec(memory_space=pltpu.VMEM)
    hbm = pl.BlockSpec(memory_space=pltpu.HBM)
    outs = [tuple(o) + ("near",) * (3 - len(o)) for o in outs]
    specs = [hbm if i in far or i in raw else vm for i in range(len(ins))]
    lead = 0 if coords is None else 1
    late = [i for i, o in enumerate(outs) if o[2] == "far"]
    extra = [pltpu.VMEM(ins[i].shape, ins[i].dtype) for i in far]
    extra += [pltpu.VMEM(outs[i][0], outs[i][1]) for i in late]
    moves = len(far) + len(late) + len(save)
    if moves:
        extra.append(pltpu.SemaphoreType.DMA((moves,)))
    count_in, count_out = len(ins), len(outs) + len(save)

    def body(*refs):
        front, refs = refs[:lead], refs[lead:]
        got, put = list(refs[:count_in]), list(refs[count_in : count_in + count_out])
        work = refs[count_in + count_out :]
        own, work = work[: len(scratch)], work[len(scratch) :]
        copies = []

        def move(source, target):
            copies.append(pltpu.make_async_copy(source, target, work[-1].at[len(copies)]))
            copies[-1].start()

        for n, i in enumerate(far):
            move(got[i], work[n])
            got[i] = work[n]
        for copy in copies:
            copy.wait()
        for n, i in enumerate(save):
            move(got[i], put[len(outs) + n])
        inside = put[: len(outs)]
        for n, i in enumerate(late):
            inside[i] = work[len(far) + n]
        kernel(*front, *got, *inside, *own)
        for n, i in enumerate(late):
            move(inside[i], put[i])
        for copy in copies[len(far) :]:
            copy.wait()

    if coords is not None:
        specs = [pl.BlockSpec(memory_space=pltpu.SMEM)] + specs
    saved = [jax.ShapeDtypeStruct(ins[i].shape, ins[i].dtype) for i in save]
    return pl.pallas_call(
        body,
        in_specs=specs,
        out_specs=[vm if o[2] == "near" else hbm for o in outs] + [hbm] * len(save),
        out_shape=[jax.ShapeDtypeStruct(o[0], o[1]) for o in outs] + saved,
        scratch_shapes=list(scratch) + extra,
        cost_estimate=pl.CostEstimate(flops=0, bytes_accessed=0, transcendentals=0),
        compiler_params=pltpu.CompilerParams(vmem_limit_bytes=MIB.get(name, 58) << 20),
        name=name,
    )(*([] if coords is None else [coords]), *ins)


def aligned(index, size):
    if isinstance(index, int):
        return pl.ds(index * size, size)
    return pl.ds(pl.multiple_of(index * size, size), size)


def pack_kernel(wq, wk, wv, g1, b1, g2, b2, w_inner, head, inner):
    per = wq.shape[0]
    gains = jnp.concatenate([g1[...], b1[...], g2[...], b2[...]], 1)
    for d in range(16):
        cols = pl.ds(((d >> 3) * 4 + (d & 3)) * HD, HD)
        for n, w in enumerate((wq, wk, wv)):
            head[d, pl.ds(n * per, per), :] = w[:, cols]
        head[d, pl.ds(3 * per, 16), :] = jnp.broadcast_to(gains, (16, HD))
    for h in range(8):
        for t in range(4):
            inner[h, :, pl.ds(t * HD, HD)] = w_inner[:, pl.ds((t * 8 + h) * HD, HD)]


def norm_of(values):
    centered = values - jnp.mean(values, -1, keepdims=True)
    inverse = lax.rsqrt(jnp.mean(centered * centered, -1, keepdims=True) + eps_norm)
    return centered * inverse, inverse


def qkv_kernel(at, *refs):
    blocks, pieces = refs[:8], refs[8:10]
    h1, query, kv, gains, weights = refs[10:]
    x, za, zl, y, c = (at[i] for i in range(5))
    width = h1.shape[1]
    per = width // 32
    for n, piece in enumerate(pieces):
        for d in range(16):
            for i in range(3):
                weights[aligned(2 * d + (c ^ n), per), pl.ds(i * HD, HD)] = piece[
                    d, pl.ds(i * per, per), :
                ]
    got = jnp.concatenate([p[d, 3 * per : 3 * per + 1, :] for p in pieces for d in range(16)], 0)
    line = lax.broadcasted_iota(jnp.int32, (32, width), 0)
    lane = lax.broadcasted_iota(jnp.int32, (32, width), 1)
    owner = (line & 15) * 2 + (c ^ (line >> 4))
    mine = lax.shift_right_logical(lane, 5) == owner
    source = lax.broadcasted_iota(jnp.int32, (HD, width), 0)
    target = lax.broadcasted_iota(jnp.int32, (HD, width), 1)
    for k in range(4):
        spread = jnp.where(source == k * per + (target & (per - 1)), 1.0, 0.0).astype(BF)
        gains[k : k + 1, :] = jnp.sum(jnp.where(mine, mm(got, spread), 0.0), 0, keepdims=True)
    gain, bias = gains[0:1, :], gains[1:2, :]
    for n, block in enumerate(blocks):
        xx, zz, yy = x ^ (n >> 2), zl ^ (n >> 1 & 1), y ^ (n & 1)
        for s in range(2):
            j = xx * 8 + (za ^ s) * 4 + zz * 2 + yy
            normed, _ = norm_of(block[s].astype(F32))
            h1[aligned(j, 64), :] = (normed * gain + bias).astype(BF)
    for t in range(h1.shape[0] // TILE):
        rows = pl.ds(t * TILE, TILE)
        out = mm(h1[rows, :], weights[...]).astype(BF)
        query[rows, :] = out[:, :HD]
        kv[rows, :] = out[:, HD:]


def causal(q_share, k_share):
    rows = lax.broadcasted_iota(jnp.int32, (TILE, TILE), 0)
    cols = lax.broadcasted_iota(jnp.int32, (TILE, TILE), 1)
    q_pos = (lax.shift_right_logical(rows, 6) * 2 + q_share) * 64 + (rows & 63)
    k_pos = (lax.shift_right_logical(cols, 6) * 2 + k_share) * 64 + (cols & 63)
    return k_pos <= q_pos


def fine_forward_kernel(at, query, own, other, out, out_f, lse, s_ref):
    tiles = query.shape[0] // TILE
    c = at[4]
    both = (own, other)

    def tile(t, carry):
        rows = aligned(t, TILE)
        q = query[rows, :]

        def score(u, top, masked):
            for n in range(2):
                s = mm_nt(q, both[n][aligned(u, TILE), pl.ds(0, HD)]) * SCALE
                if masked:
                    s = jnp.where(causal(c, c if n == 0 else 1 - c), s, MASKED)
                s_ref[u * 2 + n] = s
                top = jnp.maximum(top, jnp.max(s, -1, keepdims=True))
            return top

        top = jnp.full((TILE, 1), MASKED, F32)
        for u in range(t + 1):
            top = score(u, top, u == t)

        def expo(u, total):
            for n in range(2):
                p = jnp.exp(s_ref[u * 2 + n] - top)
                s_ref[u * 2 + n] = p
                total = total + jnp.sum(p, -1, keepdims=True)
            return total

        total = jnp.zeros((TILE, 1), F32)
        for u in range(t + 1):
            total = expo(u, total)
        inverse = 1.0 / total

        def weigh(u, acc):
            for n in range(2):
                p = (s_ref[u * 2 + n] * inverse).astype(BF)
                acc = acc + mm(p, both[n][aligned(u, TILE), pl.ds(HD, HD)])
            return acc

        acc = jnp.zeros((TILE, HD), F32)
        for u in range(t + 1):
            acc = weigh(u, acc)
        out_f[rows, :] = acc
        out[pl.ds(t * (TILE // 64), TILE // 64)] = acc.astype(BF).reshape(TILE // 64, 64, HD)
        lse[rows, :] = jnp.broadcast_to(top + jnp.log(total), (TILE, HD))
        return carry

    for t in range(tiles):
        tile(t, 0)


def place_w_out(at, pieces, out_w, sems):
    x, za, zl, y, c = (at[i] for i in range(5))
    copies = []
    for n, piece in enumerate(pieces):
        side = (zl ^ (n & 1)) * 4 + (y ^ (n >> 1 & 1)) * 2 + (c ^ (n >> 2))
        for i in range(4):
            p = (x ^ (i >> 1)) * 16 + (za ^ (i & 1)) * 8 + side
            copies.append(
                pltpu.make_async_copy(
                    piece.at[i], out_w.at[aligned(p, piece.shape[1]), :], sems.at[len(copies)]
                )
            )
            copies[-1].start()
    return copies


def middle_kernel(at, got, tokens, gains, *refs):
    pieces, (mixed, middle, scaled, inverse, h2, out_w, sems) = refs[:8], refs[8:]
    copies = place_w_out(at, pieces, out_w, sems)
    rows, width = middle.shape
    tok = rows // 2
    for s in range(16):
        head = (s >> 3) * 4 + (s & 3)
        mixed[pl.ds((s >> 2 & 1) * tok, tok), pl.ds(head * HD, HD)] = got[s]
    for s in range(2):
        middle[pl.ds(s * tok, tok), :] = tokens[s].astype(F32)
    for copy in copies:
        copy.wait()
    middle[...] += mm(mixed[...], out_w[...])
    normed, inv = norm_of(middle[...])
    scaled[...] = normed
    inverse[...] = jnp.broadcast_to(inv, (rows, HD))
    h2[...] = (normed * gains[2:3, :] + gains[3:4, :]).astype(BF)


def inner_kernel(at, *refs):
    h2_parts, cot_parts, in_parts, out_parts = refs[:10], refs[10:20], refs[20:24], refs[24:28]
    h2_out, cot_out, outer_out, hidden, grad_inner, keep, send = refs[28:35]
    h2, cot, w_in, w_outer, sems = refs[35:]
    x, za = at[0], at[1]
    copies = []

    def move(source, target):
        copy = pltpu.make_async_copy(source, target, sems.at[len(copies)])
        copy.start()
        copies.append(copy)

    for n in range(4):
        t = (x ^ (n & 1)) * 2 + (za ^ (n >> 1))
        move(in_parts[n], w_in.at[aligned(t, in_parts[n].shape[0]), :])
    for n in range(4):
        t = (x ^ (n & 1)) * 2 + (za ^ (n >> 1))
        move(out_parts[n], w_outer.at[aligned(t, out_parts[n].shape[0]), :])
    row = 0
    for part in cot_parts:
        move(part, cot.at[pl.ds(row, part.shape[0]), :])
        row += part.shape[0]
    row = 0
    for part in h2_parts:
        h2[pl.ds(row, part.shape[0]), :] = part[...]
        row += part.shape[0]
    move(h2, h2_out)
    for copy in copies[:4]:
        copy.wait()
    first = mm(h2[pl.ds(0, TILE), :], w_in[...])
    for copy in copies[4:18]:
        copy.wait()
    arrived = 18
    move(cot, cot_out)
    move(w_outer, outer_out)
    half = h2.shape[0] // 2

    def tile(t, carry):
        rows = aligned(t, TILE)
        u = first if t == 0 else mm(h2[rows, :], w_in[...])
        squared = u * u
        bent = jnp.tanh(gelu_coef * (u + 0.044715 * squared * u))
        hidden[rows, :] = (0.5 * u * (1.0 + bent)).astype(BF)
        slope = 0.5 * (1.0 + bent) + 0.5 * u * (1.0 - bent * bent) * gelu_coef * (
            1.0 + 3.0 * 0.044715 * squared
        )
        grad = (mm_nt(cot[rows, :], w_outer[...]) * slope).astype(BF)
        grad_inner[rows, :] = grad
        return mm_nt(grad, w_in[...]), carry

    for t in range(2):
        keep[pl.ds(t * TILE, TILE), :] = tile(t, 0)[0]
    for t in range(2):
        send[pl.ds(t * TILE, TILE), :] = tile(half // TILE + t, 0)[0].astype(BF)
    for copy in copies[arrived:]:
        copy.wait()


def half_grad(x, left, right, keep, send):
    n = keep.shape[0]
    for s in range(2):
        part = mm_tn(left[:, pl.ds(s * n, n)], right[...])

        @pl.when(x == s)
        def _():
            keep[...] = part

        @pl.when(x != s)
        def _():
            send[...] = part.astype(BF)


def inner_grad_kernel(at, h2, grad_inner, keep, send):
    half_grad(at[0], h2, grad_inner, keep, send)


def outer_grad_kernel(at, hidden, cot, w_outer, out_keep, out_send, keep, send):
    half = keep.shape[0]
    send[...] = mm(hidden[pl.ds(half, half), :], w_outer[...]).astype(BF)
    keep[...] = mm(hidden[pl.ds(0, half), :], w_outer[...])
    half_grad(at[0], hidden, cot, out_keep, out_send)


def payload_kernel(at, head_keep, head_got, own, other, payload):
    x = at[0]
    m = head_keep.shape[1] // 4
    n = own.shape[1]
    wide = head_keep.shape[2]
    for d in range(8):
        rows = pl.ds((d & 3) * m, m)
        payload[d, pl.ds(0, m), pl.ds(0, wide)] = (
            head_keep[d >> 2, rows, :] + head_got[d >> 2, rows, :].astype(F32)
        ).astype(BF)
        payload[d, pl.ds(0, m), pl.ds(wide, HD)] = jnp.zeros((m, HD), BF)
        for s, part in enumerate((own, other)):
            here = pl.ds(m + s * n, n)

            @pl.when(x == d >> 2)
            def _():
                payload[d, here, :] = part[d & 3]

            @pl.when(x != d >> 2)
            def _():
                payload[d, here, :] = jnp.zeros(part.shape[1:], BF)


def last_kernel(at, got, query, key, value, sums, inner_g):
    x, c = at[0], at[4]
    per = query.shape[0]
    m = per + 16
    lanes = got.shape[2]
    total = got[0, pl.ds(per, 16), pl.ds(0, HD)].astype(F32)
    for h in range(8):
        for n, out in enumerate((query, key, value)):
            out[:, pl.ds(h * HD, HD)] = got[h, pl.ds(0, per), pl.ds(n * HD, HD)].astype(F32)
        if h:
            total = total + got[h, pl.ds(per, 16), pl.ds(0, HD)].astype(F32)
    sums[...] = total[:8]
    for w in range(4):
        for s in range(2):
            part = got[4 * x + w, pl.ds(m + s * per, per), :].astype(F32)
            side = 2 * w + (c if s == 0 else 1 - c)
            for t in range(lanes // HD):
                inner_g[:, aligned(t * 8 + side, HD)] = part[:, t * HD : (t + 1) * HD]


def branch_kernel(at, parts, scaled, inverse, gains, cot, *refs):
    pieces, (grad_middle, branch, go, sums, out_w, sems) = refs[:8], refs[8:]
    copies = place_w_out(at, pieces, out_w, sems)
    rows, width = scaled.shape
    tok = rows // 2
    grad = parts[0].astype(F32)
    for n in range(1, 4):
        grad = grad + parts[n].astype(F32)
    n2 = scaled[...]
    sums[0:1, :] = jnp.sum(grad * n2, 0, keepdims=True)
    sums[1:2, :] = jnp.sum(grad, 0, keepdims=True)
    a = grad * gains[2:3, :]
    grad = inverse[:, 0:1] * (
        a - jnp.mean(a, -1, keepdims=True) - n2 * jnp.mean(a * n2, -1, keepdims=True)
    )
    for s in range(2):
        part = pl.ds(s * tok, tok)
        grad_middle[part, :] = cot[s].astype(F32) + grad[s * tok : (s + 1) * tok]
    branch[...] = grad_middle[...].astype(BF)
    for copy in copies:
        copy.wait()
    out = mm_nt(branch[...], out_w[...]).astype(BF)
    for s in range(16):
        head = (s >> 3) * 4 + (s & 3)
        seq = s >> 2 & 1
        go[s] = out[seq * tok : (seq + 1) * tok, head * HD : (head + 1) * HD]


def fine_backward_kernel(at, query, own, other, go_ref, out_f, lse_ref, gq_ref, keep, send, acc):
    rows_all = query.shape[0]
    tiles = rows_all // TILE
    c = at[4]
    both = (own, other)
    keep[...] = jnp.zeros_like(keep)
    acc[...] = jnp.zeros_like(acc)
    totals = (keep, acc)

    def tile(t, carry):
        rows = aligned(t, TILE)
        q = query[rows, :]
        go = go_ref[pl.ds(t * (TILE // 64), TILE // 64)].reshape(TILE, HD)
        delta = jnp.sum(go.astype(F32) * out_f[rows, :], -1, keepdims=True)
        lse = lse_ref[rows, 0:1]

        def one(u, gq, masked):
            cols = aligned(u, TILE)
            for n in range(2):
                kk = both[n][cols, pl.ds(0, HD)]
                p = jnp.exp(mm_nt(q, kk) * SCALE - lse)
                if masked:
                    p = jnp.where(causal(c, c if n == 0 else 1 - c), p, 0.0)
                totals[n][cols, pl.ds(HD, HD)] += mm_tn(p.astype(BF), go)
                ds = (p * (mm_nt(go, both[n][cols, pl.ds(HD, HD)]) - delta)).astype(BF)
                totals[n][cols, pl.ds(0, HD)] += mm_tn(ds, q)
                gq = gq + mm(ds, kk)
            return gq

        gq = jnp.zeros((TILE, HD), F32)
        for u in range(t + 1):
            gq = one(u, gq, u == t)
        gq_ref[rows, :] = (gq * SCALE).astype(BF)
        return carry

    for t in range(tiles):
        tile(t, 0)
    keep[:, :HD] = keep[:, :HD] * SCALE
    send[:, :HD] = (acc[:, :HD] * SCALE).astype(BF)
    send[:, HD:] = acc[:, HD:].astype(BF)


def partial_kernel(at, *refs):
    blocks, (gq, keep, got, weights) = refs[:8], refs[8:12]
    grads, parts, sums, tokens, sems = refs[12:]
    x, za, zl, y = (at[i] for i in range(4))
    copies = []
    for n in range(8):
        for s in range(2):
            j = (x ^ (n >> 2)) * 8 + (za ^ s) * 4 + (zl ^ (n >> 1 & 1)) * 2 + (y ^ (n & 1))
            copies.append(
                pltpu.make_async_copy(
                    blocks[n].at[s], tokens.at[aligned(j, 64), :], sems.at[len(copies)]
                )
            )
            copies[-1].start()
    for copy in copies:
        copy.wait()
    tiles = gq.shape[0] // TILE
    for t in range(tiles):
        rows = pl.ds(t * TILE, TILE)
        grads[rows, pl.ds(0, HD)] = gq[rows, :]
        grads[rows, pl.ds(HD, 2 * HD)] = (keep[rows, :] + got[rows, :].astype(F32)).astype(BF)
        part = mm_nt(grads[rows, :], weights[...])
        normed, _ = norm_of(tokens[rows, :].astype(F32))
        one = jnp.sum(part * normed, 0, keepdims=True)
        two = jnp.sum(part, 0, keepdims=True)
        if t == 0:
            sums[0:1, :] = one
            sums[1:2, :] = two
        else:
            sums[0:1, :] += one
            sums[1:2, :] += two
        for i in range(4):
            parts[(t >> 1) * 4 + i, za ^ (t & 1)] = part[i * 64 : (i + 1) * 64].astype(BF)


def total_kernel(parts, keep, send):
    total = parts[0, 0].astype(F32)
    other = parts[0, 1].astype(F32)
    for n in range(1, 8):
        total = total + parts[n, 0].astype(F32)
        other = other + parts[n, 1].astype(F32)
    keep[...] = total
    send[...] = other.astype(BF)


def head_grad_kernel(at, left, right, sums, keep, send, big):
    c = at[4]
    per = left.shape[1] // 32
    big[...] = mm_tn(left[...], right[...])
    spare = keep.shape[2] - sums.shape[1]
    for q in range(16):
        keep[q, pl.ds(0, per), :] = big[aligned(2 * q + c, per), :]
        send[q, pl.ds(0, per), :] = big[aligned(2 * q + 1 - c, per), :].astype(BF)
    pad = jnp.zeros((16, spare), F32)
    for q in range(16):
        pair = jnp.concatenate([sums[2 * q : 2 * q + 2, :], pad[:2]], 1)
        mine = jnp.where(c == 0, pair[0:1], pair[1:2])
        other = jnp.where(c == 0, pair[1:2], pair[0:1])
        keep[q, pl.ds(per, 16), :] = jnp.broadcast_to(mine, (16, keep.shape[2]))
        send[q, pl.ds(per, 16), :] = jnp.broadcast_to(other, (16, keep.shape[2])).astype(BF)


def core_grad_kernel(at, left, right, keep, send, big):
    c = at[4]
    per = left.shape[1] // 32
    big[...] = mm_tn(left[...], right[...])
    for q in range(16):
        rows = pl.ds(q * per, per)
        keep[rows, :] = big[aligned(2 * q + c, per), :]
        send[rows, :] = big[aligned(2 * q + 1 - c, per), :].astype(BF)


def input_kernel(at, keep, got, tokens, grad_middle, gains, grad_tokens):
    za = at[1]
    tok = tokens.shape[1]
    for n in range(2):
        seq = za if n == 0 else 1 - za
        part = keep[...] if n == 0 else got[...].astype(F32)
        n1, inv = norm_of(tokens[seq].astype(F32))
        a = part * gains[0:1, :]
        grad_tokens[seq] = grad_middle[aligned(seq, tok), :] + inv * (
            a - jnp.mean(a, -1, keepdims=True) - n1 * jnp.mean(a * n1, -1, keepdims=True)
        )


def far_kernel(keep, got, own, on_z, on_y, far_a, far_b):
    n = own.shape[0]
    for i, out in enumerate((own, on_z, on_y)):
        rows = pl.ds(i * n, n)
        out[...] = keep[rows, :] + got[rows, :].astype(F32)
    for i, out in enumerate((far_a, far_b)):
        rows = pl.ds(3 * n + i * (n // 2), n // 2)
        out[...] = (keep[rows, :] + got[rows, :].astype(F32)).astype(BF)


def near_kernel(on_z, on_y, got_a, got_b, send_z, send_y):
    n = got_a.shape[0]
    first, second = pl.ds(0, n), pl.ds(n, n)
    send_z[first, :] = (on_z[first, :] + got_a[...].astype(F32)).astype(BF)
    send_z[second, :] = on_z[second, :].astype(BF)
    send_y[first, :] = on_y[first, :].astype(BF)
    send_y[second, :] = (on_y[second, :] + got_b[...].astype(F32)).astype(BF)


def result_sum_kernel(middle, own, got_z, got_y, out):
    out[...] = (
        middle[...] + own[...] + got_z[...].astype(F32) + got_y[...].astype(F32)
    ).astype(BF)


def fold_kernel(at, keep, got, parts):
    zl, y = at[2], at[3]
    rows = parts.shape[1]
    for n in range(4):
        here = pl.ds(n * rows, rows)
        z = zl ^ (1 if n in (1, 3) else 0)
        w = y ^ (1 if n in (2, 3) else 0)
        parts[z * 2 + w] = (keep[here, :] + got[here, :].astype(F32)).astype(BF)


def stage(*values):
    return lax.optimization_barrier(values)


def grow(v, axis):
    return jnp.concatenate([v, swap(v, axis)], 0)


def half_swap(v, axis):
    return swap(pick(v, 1 - lax.axis_index(axis)), axis)


def fine_layer(
    tokens,
    cotangent,
    ln1_gain,
    ln1_bias,
    w_query,
    w_key,
    w_value,
    w_out,
    ln2_gain,
    ln2_bias,
    w_inner,
    w_outer,
):
    seqs, tok, width = tokens.shape
    rows = seqs * tok
    half = rows // 2
    per = w_query.shape[0]
    unit = w_outer.shape[0]
    hidden_units = 4 * unit
    all_rows = 8 * rows
    coords = jnp.stack([lax.axis_index(a) for a in ("x", "za", "zl", "y", "c")]).astype(jnp.int32)
    x, za = lax.axis_index("x"), lax.axis_index("za")
    cube, owners = ("x", "zl", "y"), ("x", "za", "zl", "y")
    cot = cotangent.reshape(rows, width)

    def split(axis, keep, got, shape):
        keep, got = keep.reshape(shape), got.reshape(shape)
        i = lax.axis_index(axis)
        mine = pick(keep, i, 1) + pick(got, i, 1).astype(F32)
        return mine, (pick(keep, 1 - i, 1) + pick(got, 1 - i, 1).astype(F32)).astype(BF)

    head_w, inner_w = call(
        pack_kernel,
        [((16, 3 * per + 16, HD), BF, "far"), ((8, per, hidden_units), BF, "far")],
        [w_query, w_key, w_value]
        + [g.reshape(1, per) for g in (ln1_gain, ln1_bias, ln2_gain, ln2_bias)]
        + [w_inner],
        far=range(8),
        name="pack",
    )
    moved, head_w, inner_w, w_out, w_outer = stage(
        swap(pick(tokens, 1 - za), "za"), head_w, inner_w, w_out, w_outer
    )
    block = jnp.stack([pick(tokens, za), moved])
    on_x, on_z, on_y, head_w = stage(
        swap(block, "x"), swap(block, "zl"), swap(block, "y"), head_w
    )
    on_xz, on_xy, on_zy, on_xyz, head_w, out_w = stage(
        swap(on_x, "zl"),
        swap(on_y, "x"),
        swap(on_z, "y"),
        lax.ppermute(block, cube, [(i, 7 - i) for i in range(8)]),
        lax.all_to_all(head_w, owners, 0, 0, tiled=True),
        grow(after(w_out, on_x)[None], "za"),
    )
    head_c, w_outer, inner_w = stage(swap(head_w, "c"), w_outer, inner_w)
    blocks = [block, on_y, on_z, on_zy, on_x, on_xy, on_xz, on_xyz]
    outer_z, outer_x = swap(w_outer, "za"), swap(w_outer, "x")
    h1, query, kv, gains, head_w = call(
        qkv_kernel,
        [
            ((16 * tok, width), BF, "far"),
            ((16 * tok, HD), BF),
            ((16 * tok, 2 * HD), BF),
            ((8, width), F32, "far"),
            ((width, 3 * HD), BF, "far"),
        ],
        blocks + [head_w, head_c],
        coords,
        far=range(10),
        name="qkv",
    )
    kv, query, out_w, outer_z, outer_x = stage(kv, query, grow(out_w, "x"), outer_z, outer_x)
    kv_other, out_w, outer_z = stage(swap(kv, "c"), out_w, outer_z)
    out, out_f, lse, query, kv, kv_other = call(
        fine_forward_kernel,
        [((16, tok, HD), BF, "far"), ((16 * tok, HD), F32, "far"), ((16 * tok, HD), F32, "far")],
        [query, kv, kv_other],
        coords,
        save=(0, 1, 2),
        scratch=[pltpu.VMEM((2 * 16 * tok // TILE, TILE, TILE), F32)],
        name="attention_forward",
    )
    out, out_z, out_y, outer_zx, inner_w, cot = stage(
        out,
        swap(out_w, "zl"),
        swap(out_w, "y"),
        swap(outer_z, "x"),
        lax.all_to_all(after(inner_w, kv_other), W_AXES, 0, 0, tiled=True),
        cot,
    )
    mixed, cot_z, cot_y, cot_c, out_zy, inner_z, inner_x, *out_c = stage(
        lax.all_to_all(out, owners, 0, 0, tiled=True),
        swap(cot, "zl"),
        swap(cot, "y"),
        swap(cot, "c"),
        swap(out_z, "y"),
        swap(inner_w, "za"),
        swap(inner_w, "x"),
        swap(out_w, "c"),
        swap(out_z, "c"),
        swap(out_y, "c"),
    )
    (out_zyc,) = stage(swap(out_zy, "c"))
    pieces = [out_w, out_z, out_y, out_zy] + out_c + [out_zyc]
    mixed, middle, scaled, inverse, h2 = call(
        middle_kernel,
        [
            ((rows, width), BF, "far"),
            ((rows, width), F32, "far"),
            ((rows, width), F32, "far"),
            ((rows, HD), F32, "far"),
            ((rows, width), BF),
        ],
        [mixed, tokens, gains] + pieces,
        coords,
        far=(1, 2),
        raw=range(3, 11),
        scratch=[pltpu.VMEM((width, width), BF), pltpu.SemaphoreType.DMA((32,))],
        name="middle",
    )
    h2_z, h2_y, h2_c, cot_a, cot_b, cot_zc, cot_yc, inner_zx = stage(
        swap(h2, "zl"),
        swap(h2, "y"),
        swap(h2, "c"),
        swap(cot_z[:half], "y"),
        swap(cot_y[half:], "zl"),
        swap(cot_z, "c"),
        swap(cot_y, "c"),
        swap(inner_z, "x"),
    )
    h2_a, h2_b, h2_zc, h2_yc, cot_ac, cot_bc = stage(
        swap(h2_z[:half], "y"),
        swap(h2_y[half:], "zl"),
        swap(h2_z, "c"),
        swap(h2_y, "c"),
        swap(cot_a, "c"),
        swap(cot_b, "c"),
    )
    h2_ac, h2_bc = stage(swap(h2_a, "c"), swap(h2_b, "c"))
    h2_all, cot_all, outer_w, hidden, grad_inner, keep, send = call(
        inner_kernel,
        [
            ((all_rows, width), BF, "raw"),
            ((all_rows, width), BF, "raw"),
            ((hidden_units, width), BF, "raw"),
            ((all_rows, hidden_units), BF, "far"),
            ((all_rows, hidden_units), BF, "far"),
            ((all_rows // 2, width), F32),
            ((all_rows // 2, width), BF),
        ],
        [h2, h2_z, h2_y, h2_a, h2_b, h2_c, h2_zc, h2_yc, h2_ac, h2_bc]
        + [cot, cot_z, cot_y, cot_a, cot_b, cot_c, cot_zc, cot_yc, cot_ac, cot_bc]
        + [p.reshape(8 * per, hidden_units) for p in (inner_w, inner_x, inner_z, inner_zx)]
        + [w_outer, outer_x, outer_z, outer_zx],
        coords,
        raw=range(10, 28),
        scratch=[
            pltpu.VMEM((all_rows, width), BF),
            pltpu.VMEM((all_rows, width), BF),
            pltpu.VMEM((width, hidden_units), BF),
            pltpu.VMEM((hidden_units, width), BF),
            pltpu.SemaphoreType.DMA((21,)),
        ],
        name="inner",
    )

    (got,) = stage(swap(send, "c"))
    (parts,) = call(
        fold_kernel, [((4, rows, width), BF, "far")], [keep, got], coords, name="fold"
    )
    in_keep, in_send = call(
        inner_grad_kernel,
        [((width // 2, hidden_units), F32, "far"), ((width // 2, hidden_units), BF)],
        [h2_all, grad_inner],
        coords,
        far=(0, 1),
        name="inner_grad",
    )
    parts, in_keep, in_send = stage(parts, in_keep, in_send)
    outer_keep, outer_send, res_keep, res_send = call(
        outer_grad_kernel,
        [
            ((hidden_units // 2, width), F32, "far"),
            ((hidden_units // 2, width), BF),
            ((all_rows // 2, width), F32, "far"),
            ((all_rows // 2, width), BF),
        ],
        [after(hidden, in_send), cot_all, outer_w],
        coords,
        far=range(3),
        name="outer_grad",
    )
    parts, in_got, outer_keep, outer_send, res_keep, res_send = stage(
        lax.all_to_all(parts, ("zl", "y"), 0, 0, tiled=True),
        swap(in_send, "x"),
        outer_keep,
        outer_send,
        res_keep,
        res_send,
    )
    grad_middle, branch, go, sums_two = call(
        branch_kernel,
        [
            ((rows, width), F32, "far"),
            ((rows, width), BF, "far"),
            ((16, tok, HD), BF, "far"),
            ((2, width), F32, "far"),
        ],
        [parts, scaled, inverse, gains, cotangent] + pieces,
        coords,
        far=range(1, 5),
        raw=range(5, 13),
        scratch=[pltpu.VMEM((width, width), BF), pltpu.SemaphoreType.DMA((32,))],
        name="branch",
    )
    in_keep, in_send = split("za", in_keep, in_got, (1, 2, 8 * per, hidden_units))
    go, branch, res_got, in_keep, in_send = stage(
        go, branch, swap(res_send, "c"), in_keep, in_send
    )
    res = (res_keep + res_got.astype(F32)).reshape(4, rows, width)
    far_a, far_b = res[3, :half].astype(BF), res[3, half:].astype(BF)
    out_keep, out_send = call(
        core_grad_kernel,
        [((width // 2, width), F32, "far"), ((width // 2, width), BF)],
        [mixed, branch],
        coords,
        far=(0, 1),
        scratch=[pltpu.VMEM((width, width), F32)],
        name="out_grad",
    )
    go, in_got, outer_got, out_keep, out_send, res, far_a, far_b = stage(
        lax.all_to_all(go, owners, 0, 0, tiled=True),
        swap(in_send, "za"),
        swap(outer_send, "x"),
        out_keep,
        out_send,
        res,
        far_a,
        far_b,
    )
    gq, keep, send = call(
        fine_backward_kernel,
        [((16 * tok, HD), BF, "far"), ((16 * tok, 2 * HD), F32, "far"), ((16 * tok, 2 * HD), BF)],
        [query, kv, kv_other, go, out_f, lse],
        coords,
        far=(0, 1, 2, 4, 5),
        scratch=[pltpu.VMEM((16 * tok, 2 * HD), F32)],
        name="attention_backward",
    )
    outer_keep, outer_send = split("za", outer_keep, outer_got, (1, 2, unit, width))
    inner_g = (in_keep + in_got.astype(F32)).astype(BF).reshape(8, per, hidden_units)
    gq, keep, send, got_a, got_b, out_got, outer_keep, outer_send, inner_g = stage(
        gq,
        keep,
        send,
        swap(far_a, "y"),
        swap(far_b, "zl"),
        swap(out_send, "c"),
        outer_keep,
        outer_send,
        inner_g,
    )
    out_keep, out_send = split("x", out_keep, out_got, (1, 2, 8 * per, width))
    got, out_keep, out_send = stage(swap(send, "c"), out_keep, out_send)
    grads, parts, sums = call(
        partial_kernel,
        [
            ((16 * tok, 3 * HD), BF, "far"),
            ((8, 2, tok, width), BF, "far"),
            ((2, width), F32, "far"),
        ],
        blocks + [gq, keep, got, head_w],
        coords,
        far=(8, 9, 11),
        raw=range(8),
        scratch=[pltpu.VMEM((16 * tok, width), BF), pltpu.SemaphoreType.DMA((16,))],
        name="partial",
    )
    grads, parts, sums, outer_got, out_keep, out_got = stage(
        grads, parts, sums, swap(outer_send, "za"), out_keep, swap(out_send, "x")
    )
    parts = lax.all_to_all(parts, cube, 0, 0, tiled=True)
    sums = jnp.concatenate([sums, sums_two], 0)
    sums = sums.reshape(4, 32, per).transpose(1, 0, 2).reshape(32, 4 * per)
    head_keep, head_send = call(
        head_grad_kernel,
        [((16, per + 16, 3 * HD), F32, "far"), ((16, per + 16, 3 * HD), BF)],
        [h1, grads, sums],
        coords,
        far=(0, 1),
        scratch=[pltpu.VMEM((width, 3 * HD), F32)],
        name="head_grad",
    )
    head_keep, head_send = stage(head_keep, head_send)
    out_keep, out_send = split(
        "za", out_keep, after(out_got, head_send), (1, 2, 4 * per, width)
    )
    res_z = jnp.concatenate([res[1, :half] + got_a.astype(F32), res[1, half:]], 0).astype(BF)
    res_y = jnp.concatenate([res[2, :half], res[2, half:] + got_b.astype(F32)], 0).astype(BF)
    inner_g = inner_g.reshape(4, 2, per, hidden_units)
    inner_own = pick(inner_g, lax.axis_index("c"), 1)
    inner_send = pick(inner_g, 1 - lax.axis_index("c"), 1)
    head_keep, head_got, out_keep, out_send, res_z, res_y, inner_own, inner_send = stage(
        head_keep,
        swap(head_send, "c"),
        out_keep,
        out_send,
        res_z,
        res_y,
        inner_own,
        inner_send,
    )
    head_keep, head_send = split("za", head_keep, head_got, (2, 2, 4 * (per + 16), 3 * HD))
    head_keep, head_send = stage(head_keep, head_send)
    outer_g = outer_keep[0] + after(outer_got, head_send)[0].astype(F32)
    head_keep, head_got, out_keep, out_got, inner_got, got_z, got_y, outer_g = stage(
        head_keep,
        swap(head_send, "za"),
        out_keep,
        swap(out_send, "za"),
        swap(inner_send, "c"),
        swap(res_z, "zl"),
        swap(res_y, "y"),
        outer_g,
    )
    (payload,) = call(
        payload_kernel,
        [((8, 3 * per + 16, hidden_units), BF, "far")],
        [head_keep, head_got, inner_own, inner_got],
        coords,
        far=range(4),
        name="payload",
    )
    out_keep, out_send = split("zl", out_keep, out_got, (1, 2, 2 * per, width))
    parts, payload, out_keep, out_send = stage(parts, payload, out_keep, out_send)
    total, send = call(
        total_kernel, [((tok, width), F32, "far"), ((tok, width), BF)], [parts], name="total"
    )
    total, send, payload = stage(total, send, payload)
    result = (middle + res[0] + after(got_z, send).astype(F32) + got_y.astype(F32)).astype(BF)
    got, payload, out_got, result = stage(
        swap(send, "za"),
        lax.all_to_all(payload, cube, 0, 0, tiled=True),
        swap(out_send, "zl"),
        result,
    )
    out_keep, out_send = split("y", out_keep, out_got, (1, 2, per, width))
    out_keep, out_send = stage(out_keep, out_send)
    (grad_tokens,) = call(
        input_kernel,
        [((seqs, tok, width), F32, "far")],
        [total, got, tokens, grad_middle, gains],
        coords,
        far=(0, 2, 3, 4),
        name="input",
    )
    query_g, key_g, value_g, sums, inner_g = call(
        last_kernel,
        [((per, width), F32, "far")] * 3
        + [((8, HD), F32, "far"), ((per, 8 * hidden_units), F32, "far")],
        [payload],
        coords,
        name="last",
    )
    grad_tokens, query_g, key_g, value_g, sums, inner_g, out_got = stage(
        grad_tokens, query_g, key_g, value_g, sums, inner_g, swap(out_send, "y")
    )
    sums = sums[0].reshape(4, per)
    return (
        result.reshape(seqs, tok, width),
        grad_tokens,
        sums[0],
        sums[1],
        query_g,
        key_g,
        value_g,
        out_keep[0] + out_got[0].astype(F32),
        sums[2],
        sums[3],
        inner_g,
        outer_g,
    )


def solution(mesh):
    blocks = mesh.shape["blk"]
    if blocks == 16:
        sizes = (2, 2, 1, 2, 2, 2)
        roles = (True, "za", ("x", "zl", "y"), ("c",), ("x", "za", "zl", "y"))
    else:
        sizes = (2, 8, blocks // 64, 2, 2, 2)
        roles = (False, "x", ("za",), ("zb", "zl", "y", "c"), ("x", "za"))
    fine = Mesh(mesh.devices.reshape(sizes), AXES)
    tok, row, vec = P(None, AXES, None), P(AXES, None), P(AXES)
    in_specs = (tok, tok, vec, vec, row, row, row, row, vec, vec, row, row)
    out_specs = (tok, tok, vec, vec, row, row, row, row, vec, vec, row, row)
    return jax.shard_map(
        fine_layer if blocks == 16 else functools.partial(on_device, roles),
        mesh=fine,
        in_specs=in_specs,
        out_specs=out_specs,
        check_vma=False,
    )
```

```python
import functools
import math

import jax
import jax.numpy as jnp
from jax import lax
from jax.experimental import pallas as pl
from jax.experimental.pallas import tpu as pltpu
from jax.sharding import Mesh
from jax.sharding import PartitionSpec as P

HD = 128
TILE = 256
SCALE = HD ** (-0.5)
MASKED = -1e30
eps_norm = 1e-05
gelu_coef = math.sqrt(2.0 / math.pi)
BF = jnp.bfloat16
F32 = jnp.float32
AXES = ("x", "za", "zb", "zl", "y", "c")
T_AXES = ("x", "za", "zb")
W_AXES = ("zl", "y", "c")


def mm(a, b):
    return jnp.dot(a, b, preferred_element_type=F32)


def mm_nt(a, b):
    return lax.dot_general(a, b, (((1,), (1,)), ((), ())), preferred_element_type=F32)


def mm_tn(a, b):
    return lax.dot_general(a, b, (((0,), (0,)), ((), ())), preferred_element_type=F32)


def norm_stats(values):
    centered = values - jnp.mean(values, -1, keepdims=True)
    inverse = lax.rsqrt(jnp.mean(centered * centered, -1, keepdims=True) + eps_norm)
    return centered * inverse, inverse


def norm_back(grad_normed, scaled, inverse, gain):
    g = grad_normed * gain
    return inverse * (
        g - jnp.mean(g, -1, keepdims=True) - scaled * jnp.mean(g * scaled, -1, keepdims=True)
    )


def swap(v, axis):
    return lax.ppermute(v, axis, [(0, 1), (1, 0)])


def pick(v, index, axis=0):
    return lax.dynamic_index_in_dim(v, index, axis, keepdims=False)


def pair_gather(v, axis):
    other = swap(v, axis)
    first = lax.axis_index(axis) == 0
    return jnp.stack([jnp.where(first, v, other), jnp.where(first, other, v)])


def pair_scatter(v, axis, dim):
    me = lax.axis_index(axis)
    return pick(v, me, dim) + swap(pick(v, 1 - me, dim).astype(BF), axis).astype(F32)


def after(v, *others):
    return lax.optimization_barrier((v,) + others)[0]


def t_gather(v):
    if lax.axis_size("za") * lax.axis_size("zb") != 2:
        return lax.all_gather(v, T_AXES, axis=0, tiled=False)
    x, z = lax.axis_index("x"), lax.axis_index("za")
    over_x, over_z = swap(v, "x"), swap(v, "za")
    out = jnp.zeros((4,) + v.shape, v.dtype)
    for part, at in (
        (v, 2 * x + z),
        (over_x, 2 * (1 - x) + z),
        (over_z, 2 * x + 1 - z),
        (swap(over_z, "x"), 2 * (1 - x) + 1 - z),
    ):
        out = lax.dynamic_update_index_in_dim(out, part, at, 0)
    return out


def t_scatter(v):
    if lax.axis_size("za") * lax.axis_size("zb") != 2:
        return lax.psum_scatter(v, T_AXES, scatter_dimension=0, tiled=False)
    v = pair_scatter(v.reshape((2, 2) + v.shape[1:]), "x", 0)
    return pair_scatter(v, "za", 0)


def plane_gather(v):
    half = v.shape[0] // 2
    a, b = v[:half], v[half:]
    a = jnp.stack([a, swap(a, "zl")])
    b = jnp.stack([b, swap(b, "y")])
    a = jnp.stack([a, swap(a, "y")])
    b = jnp.stack([b, swap(b, "zl")])
    both = jnp.stack([a, b])
    return jnp.stack([both, swap(both, "c")]).reshape(8 * v.shape[0], v.shape[1])


def plane_scatter(v):
    rows, width = v.shape
    v = v.reshape(2, 2, 2, 2, rows // 16, width)

    def fold(u, axis):
        return u[0] + swap(u[1].astype(BF), axis).astype(F32)

    v = fold(v, "c")
    a, b = v[0], v[1]
    a = fold(a, "y")
    b = fold(b, "zl")
    a = fold(a, "zl")
    b = fold(b, "y")
    return jnp.concatenate([a, b], 0)


def shares(count, body):
    if count <= 2:
        for k in range(count):
            body(k)
    else:
        lax.fori_loop(0, count, lambda k, c: (body(k), c)[1], 0)


def mask_of(count, q_tile, k_tile, q_share, k_share):
    rows = lax.broadcasted_iota(jnp.int32, (TILE, TILE), 0) + q_tile * TILE
    cols = lax.broadcasted_iota(jnp.int32, (TILE, TILE), 1) + k_tile * TILE
    q_pos = (lax.shift_right_logical(rows, 6) * count + q_share) * 64 + (rows & 63)
    k_pos = (lax.shift_right_logical(cols, 6) * count + k_share) * 64 + (cols & 63)
    return k_pos <= q_pos


def forward_kernel(count, meta, q_ref, k_ref, v_ref, o_ref, of_ref, lse_ref, qa, ka, va, s_ref):
    blocks = q_ref.shape[0]
    for j in range(blocks):
        slot = meta[j]
        rows = pl.ds(j * 64, 64)
        qa[rows, :] = q_ref[slot]

        def place(k, rows=rows, slot=slot):
            ka[k, rows, :] = k_ref[k, slot]
            va[k, rows, :] = v_ref[k, slot]

        shares(count, place)
    mine = meta[blocks]
    tiles = blocks * 64 // TILE
    for t in range(tiles):
        q = qa[pl.ds(t * TILE, TILE), :]
        top = jnp.full((TILE, 1), MASKED, F32)
        for u in range(t + 1):
            cols = pl.ds(u * TILE, TILE)

            def score(k, top, u=u, cols=cols):
                s = mm_nt(q, ka[k, cols, :]) * SCALE
                if u == t:
                    s = jnp.where(mask_of(count, t, u, mine, meta[blocks + 1 + k]), s, MASKED)
                s_ref[k * tiles + u] = s
                return jnp.maximum(top, jnp.max(s, -1, keepdims=True))

            if count <= 2:
                for k in range(count):
                    top = score(k, top)
            else:
                top = lax.fori_loop(0, count, score, top)
        total = jnp.zeros((TILE, 1), F32)
        for u in range(t + 1):

            def expo(k, total, u=u):
                p = jnp.exp(s_ref[k * tiles + u] - top)
                s_ref[k * tiles + u] = p
                return total + jnp.sum(p, -1, keepdims=True)

            if count <= 2:
                for k in range(count):
                    total = expo(k, total)
            else:
                total = lax.fori_loop(0, count, expo, total)
        inverse = 1.0 / total
        out = jnp.zeros((TILE, HD), F32)
        for u in range(t + 1):
            cols = pl.ds(u * TILE, TILE)

            def weigh(k, out, u=u, cols=cols):
                p = (s_ref[k * tiles + u] * inverse).astype(BF)
                return out + mm(p, va[k, cols, :])

            if count <= 2:
                for k in range(count):
                    out = weigh(k, out)
            else:
                out = lax.fori_loop(0, count, weigh, out)
        rows = pl.ds(t * TILE, TILE)
        of_ref[rows, :] = out
        o_ref[rows, :] = out.astype(BF)
        lse_ref[rows, :] = jnp.broadcast_to(top + jnp.log(total), (TILE, HD))


def attention_forward(count, meta, q, k, v):
    blocks = q.shape[0]
    rows = blocks * 64
    tiles = rows // TILE
    vm = pl.BlockSpec(memory_space=pltpu.VMEM)
    pairs = tiles * (tiles + 1) // 2 * count
    return pl.pallas_call(
        functools.partial(forward_kernel, count),
        in_specs=[pl.BlockSpec(memory_space=pltpu.SMEM), vm, vm, vm],
        out_specs=[vm] * 6,
        out_shape=[
            jax.ShapeDtypeStruct((rows, HD), BF),
            jax.ShapeDtypeStruct((rows, HD), F32),
            jax.ShapeDtypeStruct((rows, HD), F32),
            jax.ShapeDtypeStruct((rows, HD), BF),
            jax.ShapeDtypeStruct((count, rows, HD), BF),
            jax.ShapeDtypeStruct((count, rows, HD), BF),
        ],
        scratch_shapes=[pltpu.VMEM((count * tiles, TILE, TILE), F32)],
        cost_estimate=pl.CostEstimate(
            flops=pairs * TILE * TILE * HD * 4,
            bytes_accessed=rows * HD * 2 * (2 + 4 * count) + rows * HD * 8,
            transcendentals=pairs * TILE * TILE,
        ),
        compiler_params=pltpu.CompilerParams(vmem_limit_bytes=(16 if count <= 2 else 52) << 20),
        name="attention_forward",
    )(meta, q, k, v)


def backward_kernel(count, meta, q_ref, k_ref, v_ref, go_ref, of_ref, lse_ref, gq_ref, gk, gv):
    rows_all = q_ref.shape[0]
    blocks = rows_all // 64
    mine = meta[blocks]
    tiles = rows_all // TILE

    def zero(k):
        gk[k] = jnp.zeros((rows_all, HD), F32)
        gv[k] = jnp.zeros((rows_all, HD), F32)

    shares(count, zero)
    for t in range(tiles):
        rows = pl.ds(t * TILE, TILE)
        q = q_ref[rows, :]
        go = go_ref[rows, :]
        delta = jnp.sum(go.astype(F32) * of_ref[rows, :], -1, keepdims=True)
        lse = lse_ref[rows, :][:, :1]
        gq = jnp.zeros((TILE, HD), F32)
        for u in range(t + 1):
            cols = pl.ds(u * TILE, TILE)

            def one(k, gq, u=u, cols=cols):
                kk = k_ref[k, cols, :]
                p = jnp.exp(mm_nt(q, kk) * SCALE - lse)
                if u == t:
                    p = jnp.where(mask_of(count, t, u, mine, meta[blocks + 1 + k]), p, 0.0)
                gv[k, cols, :] += mm_tn(p.astype(BF), go)
                ds = (p * (mm_nt(go, v_ref[k, cols, :]) - delta)).astype(BF)
                gk[k, cols, :] += mm_tn(ds, q)
                return gq + mm(ds, kk)

            if count <= 2:
                for k in range(count):
                    gq = one(k, gq)
            else:
                gq = lax.fori_loop(0, count, one, gq)
        gq_ref[rows, :] = (gq * SCALE).astype(BF)

    def scale(k):
        gk[k] = gk[k] * SCALE

    shares(count, scale)


def attention_backward(count, meta, q, k, v, go, of, lse):
    rows = q.shape[0]
    tiles = rows // TILE
    vm = pl.BlockSpec(memory_space=pltpu.VMEM)
    pairs = tiles * (tiles + 1) // 2 * count
    return pl.pallas_call(
        functools.partial(backward_kernel, count),
        in_specs=[pl.BlockSpec(memory_space=pltpu.SMEM)] + [vm] * 6,
        out_specs=[vm] * 3,
        out_shape=[
            jax.ShapeDtypeStruct((rows, HD), BF),
            jax.ShapeDtypeStruct((count, rows, HD), F32),
            jax.ShapeDtypeStruct((count, rows, HD), F32),
        ],
        cost_estimate=pl.CostEstimate(
            flops=pairs * TILE * TILE * HD * 10,
            bytes_accessed=rows * HD * (16 + 12 * count),
            transcendentals=pairs * TILE * TILE,
        ),
        compiler_params=pltpu.CompilerParams(vmem_limit_bytes=(16 if count <= 2 else 52) << 20),
        name="attention_backward",
    )(meta, q, k, v, go, of, lse)


def reorder_kernel(meta, g_ref, out_ref):
    for j in range(g_ref.shape[0]):
        out_ref[meta[j]] = g_ref[j]


def reorder(meta, g):
    vm = pl.BlockSpec(memory_space=pltpu.VMEM)
    return pl.pallas_call(
        reorder_kernel,
        in_specs=[pl.BlockSpec(memory_space=pltpu.SMEM), vm],
        out_specs=vm,
        out_shape=jax.ShapeDtypeStruct(g.shape, g.dtype),
        cost_estimate=pl.CostEstimate(flops=0, bytes_accessed=4 * g.size, transcendentals=0),
        compiler_params=pltpu.CompilerParams(vmem_limit_bytes=8 << 20),
        name="reorder",
    )(meta, g)


def on_device(
    roles,
    tokens,
    cotangent,
    ln1_gain,
    ln1_bias,
    w_query,
    w_key,
    w_value,
    w_out,
    ln2_gain,
    ln2_bias,
    w_inner,
    w_outer,
):
    small, seq_axis, hd_axes, sh_axes, own_axes = roles
    planes = math.prod(lax.axis_size(a) for a in T_AXES)
    count = math.prod(lax.axis_size(a) for a in sh_axes)
    devices = 8 * planes
    seqs, tok, width = tokens.shape
    rows = seqs * tok
    per = w_query.shape[0]
    unit = w_outer.shape[0]
    seq = lax.axis_index(seq_axis)
    share = lax.axis_index(sh_axes)

    block = jnp.stack([pick(tokens, seq), swap(pick(tokens, 1 - seq), seq_axis)])
    if small:
        on_x, on_z, on_y = (swap(block, a) for a in hd_axes)
        on_xz, on_xy, on_zy = swap(on_x, "zl"), swap(on_y, "x"), swap(on_z, "y")
        on_xyz = swap(on_xz, "y")
        seen = jnp.stack([block, on_y, on_z, on_zy, on_x, on_xy, on_xz, on_xyz])
    else:
        seen = lax.all_gather(block, hd_axes, axis=0, tiled=False)
    at = jnp.arange(16, dtype=jnp.int32)
    if small:
        at_x, at_za, at_zl, at_y = at // 8, at // 4 % 2, at // 2 % 2, at % 2
        x, zl, y = (lax.axis_index(a) for a in hd_axes)
        slots = ((at_x ^ x) * 4 + (at_zl ^ zl) * 2 + (at_y ^ y)) * 2 + (at_za ^ seq)
    else:
        slots = at % 8 * 2 + (at // 8 ^ seq)

    gains = jnp.concatenate([ln1_gain, ln1_bias, ln2_gain, ln2_bias])
    gains = jnp.broadcast_to(jnp.pad(gains, (0, HD - gains.shape[0])), (8, 1, HD))
    head_w = jnp.stack([w_query, w_key, w_value]).reshape(3, per, 8, HD).transpose(2, 0, 1, 3)
    head_w = jnp.concatenate([head_w.reshape(8, 3 * per, HD), gains], 1)
    head_w = lax.all_to_all(head_w, hd_axes, 0, 0, tiled=True)
    head_w = pair_gather(head_w, seq_axis)
    for axis in reversed(sh_axes):
        if lax.axis_size(axis) == 2:
            head_w = pair_gather(head_w, axis)
        else:
            head_w = lax.all_gather(head_w, axis, axis=0, tiled=False)
    if small:
        head_w = head_w.reshape(2, 2, 2, 4, 3 * per + 1, HD).transpose(2, 1, 3, 0, 4, 5)
    else:
        head_w = head_w.reshape(count, 16, 3 * per + 1, HD).transpose(1, 0, 2, 3)
    head_w = head_w.reshape(devices, 3 * per + 1, HD)
    gains = head_w[:, -1, : 4 * per].reshape(devices, 4, per).transpose(1, 0, 2)
    gains = gains.reshape(4, width).astype(F32)
    gain_one, bias_one, gain_two, bias_two = gains[0], gains[1], gains[2], gains[3]
    head_w = head_w[:, :-1].reshape(devices, 3, per, HD).transpose(0, 2, 1, 3)
    head_w = head_w.reshape(width, 3 * HD)

    inner_w = w_inner.reshape(per, planes, 8, unit).transpose(2, 0, 1, 3)
    inner_w = lax.all_to_all(inner_w.reshape(8, per, planes * unit), W_AXES, 0, 0, tiled=True)
    inner_w = t_gather(after(inner_w, seen)).reshape(width, planes * unit)
    outer_w = t_gather(w_outer).reshape(planes * unit, width)
    grad_plane = plane_gather(after(cotangent, seen).reshape(rows, width))

    out_w = lax.all_gather(w_out, AXES, axis=0, tiled=True)
    qkv_w = jnp.concatenate([w_query, w_key, w_value], 1)
    qkv_w = lax.all_gather(after(qkv_w, seen), AXES, axis=0, tiled=True)

    normed, _ = norm_stats(seen.reshape(-1, width).astype(F32))
    h1 = (normed * gain_one + bias_one).astype(BF)
    qkv = mm(h1, head_w).astype(BF)
    query = qkv[:, :HD].reshape(16, tok, HD)
    kv = qkv[:, HD:]
    if count == 2:
        kv = jnp.stack([kv, swap(kv, "c")])
        order = jnp.stack([share, 1 - share])
    else:
        kv = lax.all_gather(kv, sh_axes, axis=0, tiled=False)
        order = jnp.arange(count)
    kv = kv.reshape(count, 16, tok, 2 * HD)
    meta = jnp.concatenate([slots, share.reshape(1), order]).astype(jnp.int32)
    out, out_f, lse, q_at, k_at, v_at = attention_forward(
        count, meta, query, kv[..., :HD], kv[..., HD:]
    )

    def to_tokens(v):
        v = lax.all_to_all(v, own_axes, 0, 0, tiled=True)
        n = v.shape[-1] // HD
        if small:
            v = v.reshape(2, 2, 4, tok, n, HD).transpose(1, 3, 4, 0, 2, 5)
        else:
            v = v.reshape(2, 8, tok, n, HD).transpose(0, 2, 3, 1, 4)
        return v.reshape(2, tok, n, 8 * HD)

    mixed = to_tokens(out.reshape(16, tok, HD)).reshape(rows, width)
    flat_in = tokens.reshape(rows, width).astype(F32)
    middle = flat_in + mm(mixed, out_w)
    scaled_two, inverse_two = norm_stats(middle)
    h2 = plane_gather((scaled_two * gain_two + bias_two).astype(BF))

    inner = mm(h2, inner_w)
    bent = jnp.tanh(gelu_coef * (inner + 0.044715 * inner * inner * inner))
    hidden = (0.5 * inner * (1.0 + bent)).astype(BF)
    slope = 0.5 * (1.0 + bent) + 0.5 * inner * (1.0 - bent * bent) * gelu_coef * (
        1.0 + 3.0 * 0.044715 * inner * inner
    )
    grad_inner = (mm_nt(grad_plane, outer_w) * slope).astype(BF)
    grad_h2 = plane_scatter(mm_nt(grad_inner, inner_w))
    grad_outer = mm_tn(hidden, grad_plane).reshape(planes, unit, width)
    grad_outer = t_scatter(grad_outer)
    grad_in = mm_tn(h2, grad_inner).reshape(planes, 8 * per, planes * unit)
    grad_in = t_scatter(grad_in).astype(BF).reshape(8, per, planes * unit)
    result = plane_scatter(mm(hidden, outer_w))

    grad_out = cotangent.reshape(rows, width).astype(F32)
    grad_middle = grad_out + norm_back(grad_h2, scaled_two, inverse_two, gain_two)
    branch = grad_middle.astype(BF)
    go = mm_nt(branch, out_w).astype(BF)
    if small:
        go = go.reshape(2, tok, 2, 4, HD).transpose(2, 0, 3, 1, 4)
    else:
        go = go.reshape(2, tok, 8, HD).transpose(0, 2, 1, 3)
    go = lax.all_to_all(go.reshape(16, tok, HD), own_axes, 0, 0, tiled=True)
    go = go.reshape(16 * tok, HD)

    gq, gk, gv = attention_backward(count, meta, q_at, k_at, v_at, go, out_f, lse)
    gkv = jnp.concatenate([gk, gv], -1)
    if count == 2:
        gkv = gkv[0] + swap(gkv[1].astype(BF), "c").astype(F32)
    else:
        gkv = lax.psum_scatter(gkv, sh_axes, scatter_dimension=0, tiled=False)
    grads = jnp.concatenate([gq, gkv.astype(BF)], -1).reshape(16, tok, 3 * HD)
    grads, result, grad_in, grad_outer = lax.optimization_barrier(
        (grads, result, grad_in, grad_outer)
    )
    back = to_tokens(grads).reshape(rows, 3 * width)
    result = (middle + result).astype(BF)
    grad_in = lax.all_to_all(after(grad_in, back), W_AXES, 0, 0, tiled=True)
    grad_in = grad_in.reshape(8, per, planes, unit).transpose(1, 2, 0, 3)
    grad_in = grad_in.reshape(per, devices * unit).astype(F32)

    head_g = mm_tn(h1, reorder(meta, grads).reshape(16 * tok, 3 * HD))
    head_g = head_g.reshape(tuple(lax.axis_size(a) for a in AXES) + (per, 3 * HD))
    dims = list(AXES)
    for axis in sh_axes[::-1] + (seq_axis,):
        dim = dims.index(axis)
        dims.remove(axis)
        if lax.axis_size(axis) == 2:
            head_g = pair_scatter(head_g, axis, dim)
        else:
            head_g = lax.psum_scatter(head_g, axis, scatter_dimension=dim, tiled=False)
    head_g = head_g.astype(BF).reshape(8, per, 3 * HD)
    head_g = lax.all_to_all(head_g, hd_axes, 0, 0, tiled=True)
    head_g = head_g.reshape(8, per, 3, HD).transpose(2, 1, 0, 3).reshape(3, per, width)
    head_g = head_g.astype(F32)

    grad_out_w = mm_tn(mixed, branch).reshape(planes, 2, 2, 2, per, width)
    grad_out_w = pair_scatter(grad_out_w, "c", 3)
    grad_out_w = pair_scatter(grad_out_w, "y", 2)
    grad_out_w = pair_scatter(grad_out_w, "zl", 1)
    grad_out_w = t_scatter(grad_out_w)

    scaled_one, inverse_one = norm_stats(flat_in)
    grad_h1 = mm_nt(back, qkv_w)
    grad_input = grad_middle + norm_back(grad_h1, scaled_one, inverse_one, gain_one)

    sums = jnp.stack(
        [
            jnp.sum(grad_h1 * scaled_one, 0),
            jnp.sum(grad_h1, 0),
            jnp.sum(grad_h2 * scaled_two, 0),
            jnp.sum(grad_h2, 0),
        ]
    )
    sums = sums.reshape(4, devices, per).transpose(1, 0, 2).reshape(devices, 4 * per)
    sums = lax.all_to_all(sums, AXES, 0, 0, tiled=True)
    sums = jnp.sum(sums, 0).reshape(4, per)
    return (
        result.reshape(seqs, tok, width),
        grad_input.reshape(seqs, tok, width),
        sums[0],
        sums[1],
        head_g[0],
        head_g[1],
        head_g[2],
        grad_out_w,
        sums[2],
        sums[3],
        grad_in,
        grad_outer,
    )


MIB = {}


def call(kernel, outs, ins, coords=None, near=(), raw=(), save=(), scratch=(), name=None):
    vm = pl.BlockSpec(memory_space=pltpu.VMEM)
    hbm = pl.BlockSpec(memory_space=pltpu.HBM)
    outs = [tuple(o) + ("far",) * (3 - len(o)) for o in outs]
    far = [i for i in range(len(ins)) if i not in raw and i not in near]
    specs = [hbm if i in far or i in raw else vm for i in range(len(ins))]
    lead = 0 if coords is None else 1
    late = [i for i, o in enumerate(outs) if o[2] == "far"]
    extra = [pltpu.VMEM(ins[i].shape, ins[i].dtype) for i in far]
    extra += [pltpu.VMEM(outs[i][0], outs[i][1]) for i in late]
    moves = len(far) + len(late) + len(save)
    if moves:
        extra.append(pltpu.SemaphoreType.DMA((moves,)))
    count_in, count_out = len(ins), len(outs) + len(save)

    def body(*refs):
        front, refs = refs[:lead], refs[lead:]
        got, put = list(refs[:count_in]), list(refs[count_in : count_in + count_out])
        work = refs[count_in + count_out :]
        own, work = work[: len(scratch)], work[len(scratch) :]
        copies = []

        def move(source, target):
            copies.append(pltpu.make_async_copy(source, target, work[-1].at[len(copies)]))
            copies[-1].start()

        for n, i in enumerate(far):
            move(got[i], work[n])
            got[i] = work[n]
        for copy in copies:
            copy.wait()
        for n, i in enumerate(save):
            move(got[i], put[len(outs) + n])
        inside = put[: len(outs)]
        for n, i in enumerate(late):
            inside[i] = work[len(far) + n]
        kernel(*front, *got, *inside, *own)
        for n, i in enumerate(late):
            move(inside[i], put[i])
        for copy in copies[len(far) :]:
            copy.wait()

    if coords is not None:
        specs = [pl.BlockSpec(memory_space=pltpu.SMEM)] + specs
    saved = [jax.ShapeDtypeStruct(ins[i].shape, ins[i].dtype) for i in save]
    return pl.pallas_call(
        body,
        in_specs=specs,
        out_specs=[vm if o[2] == "near" else hbm for o in outs] + [hbm] * len(save),
        out_shape=[jax.ShapeDtypeStruct(o[0], o[1]) for o in outs] + saved,
        scratch_shapes=list(scratch) + extra,
        cost_estimate=pl.CostEstimate(flops=0, bytes_accessed=0, transcendentals=0),
        compiler_params=pltpu.CompilerParams(vmem_limit_bytes=MIB.get(name, 58) << 20),
        name=name,
    )(*([] if coords is None else [coords]), *ins)


def aligned(index, size):
    if isinstance(index, int):
        return pl.ds(index * size, size)
    return pl.ds(pl.multiple_of(index * size, size), size)


def pack_kernel(wq, wk, wv, g1, b1, g2, b2, w_inner, head, inner):
    per = wq.shape[0]
    gains = jnp.concatenate([g1[...], b1[...], g2[...], b2[...]], 1)
    for d in range(16):
        cols = pl.ds(((d >> 3) * 4 + (d & 3)) * HD, HD)
        for n, w in enumerate((wq, wk, wv)):
            head[d, pl.ds(n * per, per), :] = w[:, cols]
        head[d, pl.ds(3 * per, 16), :] = jnp.broadcast_to(gains, (16, HD))
    for h in range(8):
        for t in range(4):
            inner[h, :, pl.ds(t * HD, HD)] = w_inner[:, pl.ds((t * 8 + h) * HD, HD)]


def norm_of(values):
    centered = values - jnp.mean(values, -1, keepdims=True)
    inverse = lax.rsqrt(jnp.mean(centered * centered, -1, keepdims=True) + eps_norm)
    return centered * inverse, inverse


def qkv_kernel(at, *refs):
    blocks, pieces = refs[:8], refs[8:10]
    h1, query, kv, gains, weights = refs[10:]
    x, za, zl, y, c = (at[i] for i in range(5))
    width = h1.shape[1]
    per = width // 32
    for n, piece in enumerate(pieces):
        for d in range(16):
            for i in range(3):
                weights[aligned(2 * d + (c ^ n), per), pl.ds(i * HD, HD)] = piece[
                    d, pl.ds(i * per, per), :
                ]
    got = jnp.concatenate([p[d, 3 * per : 3 * per + 1, :] for p in pieces for d in range(16)], 0)
    line = lax.broadcasted_iota(jnp.int32, (32, width), 0)
    lane = lax.broadcasted_iota(jnp.int32, (32, width), 1)
    owner = (line & 15) * 2 + (c ^ (line >> 4))
    mine = lax.shift_right_logical(lane, 5) == owner
    source = lax.broadcasted_iota(jnp.int32, (HD, width), 0)
    target = lax.broadcasted_iota(jnp.int32, (HD, width), 1)
    for k in range(4):
        spread = jnp.where(source == k * per + (target & (per - 1)), 1.0, 0.0).astype(BF)
        gains[k : k + 1, :] = jnp.sum(jnp.where(mine, mm(got, spread), 0.0), 0, keepdims=True)
    gain, bias = gains[0:1, :], gains[1:2, :]
    for n, block in enumerate(blocks):
        xx, zz, yy = x ^ (n >> 2), zl ^ (n >> 1 & 1), y ^ (n & 1)
        for s in range(2):
            j = xx * 8 + (za ^ s) * 4 + zz * 2 + yy
            normed, _ = norm_of(block[s].astype(F32))
            h1[aligned(j, 64), :] = (normed * gain + bias).astype(BF)
    for t in range(h1.shape[0] // TILE):
        rows = pl.ds(t * TILE, TILE)
        out = mm(h1[rows, :], weights[...]).astype(BF)
        query[rows, :] = out[:, :HD]
        kv[rows, :] = out[:, HD:]


def causal(q_share, k_share):
    rows = lax.broadcasted_iota(jnp.int32, (TILE, TILE), 0)
    cols = lax.broadcasted_iota(jnp.int32, (TILE, TILE), 1)
    q_pos = (lax.shift_right_logical(rows, 6) * 2 + q_share) * 64 + (rows & 63)
    k_pos = (lax.shift_right_logical(cols, 6) * 2 + k_share) * 64 + (cols & 63)
    return k_pos <= q_pos


def fine_forward_kernel(at, query, own, other, out, out_f, lse, s_ref):
    tiles = query.shape[0] // TILE
    c = at[4]
    both = (own, other)

    def tile(t, carry):
        rows = aligned(t, TILE)
        q = query[rows, :]

        def score(u, top, masked):
            for n in range(2):
                s = mm_nt(q, both[n][aligned(u, TILE), pl.ds(0, HD)]) * SCALE
                if masked:
                    s = jnp.where(causal(c, c if n == 0 else 1 - c), s, MASKED)
                s_ref[u * 2 + n] = s
                top = jnp.maximum(top, jnp.max(s, -1, keepdims=True))
            return top

        top = jnp.full((TILE, 1), MASKED, F32)
        for u in range(t + 1):
            top = score(u, top, u == t)

        def expo(u, total):
            for n in range(2):
                p = jnp.exp(s_ref[u * 2 + n] - top)
                s_ref[u * 2 + n] = p
                total = total + jnp.sum(p, -1, keepdims=True)
            return total

        total = jnp.zeros((TILE, 1), F32)
        for u in range(t + 1):
            total = expo(u, total)
        inverse = 1.0 / total

        def weigh(u, acc):
            for n in range(2):
                p = (s_ref[u * 2 + n] * inverse).astype(BF)
                acc = acc + mm(p, both[n][aligned(u, TILE), pl.ds(HD, HD)])
            return acc

        acc = jnp.zeros((TILE, HD), F32)
        for u in range(t + 1):
            acc = weigh(u, acc)
        out_f[rows, :] = acc
        out[pl.ds(t * (TILE // 64), TILE // 64)] = acc.astype(BF).reshape(TILE // 64, 64, HD)
        lse[rows, :] = jnp.broadcast_to(top + jnp.log(total), (TILE, HD))
        return carry

    for t in range(tiles):
        tile(t, 0)


def place_w_out(at, pieces, out_w, sems):
    x, za, zl, y, c = (at[i] for i in range(5))
    copies = []
    for n, piece in enumerate(pieces):
        side = (zl ^ (n & 1)) * 4 + (y ^ (n >> 1 & 1)) * 2 + (c ^ (n >> 2))
        for i in range(4):
            p = (x ^ (i >> 1)) * 16 + (za ^ (i & 1)) * 8 + side
            copies.append(
                pltpu.make_async_copy(
                    piece.at[i], out_w.at[aligned(p, piece.shape[1]), :], sems.at[len(copies)]
                )
            )
            copies[-1].start()
    return copies


def middle_kernel(at, got, tokens, gains, *refs):
    pieces, (mixed, middle, scaled, inverse, h2, out_w, sems) = refs[:8], refs[8:]
    copies = place_w_out(at, pieces, out_w, sems)
    rows, width = middle.shape
    tok = rows // 2
    for s in range(16):
        head = (s >> 3) * 4 + (s & 3)
        mixed[pl.ds((s >> 2 & 1) * tok, tok), pl.ds(head * HD, HD)] = got[s]
    for s in range(2):
        middle[pl.ds(s * tok, tok), :] = tokens[s].astype(F32)
    for copy in copies:
        copy.wait()
    middle[...] += mm(mixed[...], out_w[...])
    normed, inv = norm_of(middle[...])
    scaled[...] = normed
    inverse[...] = jnp.broadcast_to(inv, (rows, HD))
    h2[...] = (normed * gains[2:3, :] + gains[3:4, :]).astype(BF)


def inner_kernel(at, *refs):
    h2_parts, cot_parts, in_parts, out_parts = refs[:10], refs[10:20], refs[20:24], refs[24:28]
    h2_out, cot_out, outer_out, hidden, grad_inner, keep, send = refs[28:35]
    h2, cot, w_in, w_outer, sems = refs[35:]
    x, za = at[0], at[1]
    copies = []

    def move(source, target):
        copy = pltpu.make_async_copy(source, target, sems.at[len(copies)])
        copy.start()
        copies.append(copy)

    for n in range(4):
        t = (x ^ (n & 1)) * 2 + (za ^ (n >> 1))
        move(in_parts[n], w_in.at[aligned(t, in_parts[n].shape[0]), :])
    for n in range(4):
        t = (x ^ (n & 1)) * 2 + (za ^ (n >> 1))
        move(out_parts[n], w_outer.at[aligned(t, out_parts[n].shape[0]), :])
    row = 0
    for part in cot_parts:
        move(part, cot.at[pl.ds(row, part.shape[0]), :])
        row += part.shape[0]
    row = 0
    for part in h2_parts:
        h2[pl.ds(row, part.shape[0]), :] = part[...]
        row += part.shape[0]
    move(h2, h2_out)
    for copy in copies[:4]:
        copy.wait()
    first = mm(h2[pl.ds(0, TILE), :], w_in[...])
    for copy in copies[4:18]:
        copy.wait()
    arrived = 18
    move(cot, cot_out)
    move(w_outer, outer_out)
    half = h2.shape[0] // 2

    def tile(t, carry):
        rows = aligned(t, TILE)
        u = first if t == 0 else mm(h2[rows, :], w_in[...])
        squared = u * u
        bent = jnp.tanh(gelu_coef * (u + 0.044715 * squared * u))
        hidden[rows, :] = (0.5 * u * (1.0 + bent)).astype(BF)
        slope = 0.5 * (1.0 + bent) + 0.5 * u * (1.0 - bent * bent) * gelu_coef * (
            1.0 + 3.0 * 0.044715 * squared
        )
        grad = (mm_nt(cot[rows, :], w_outer[...]) * slope).astype(BF)
        grad_inner[rows, :] = grad
        return mm_nt(grad, w_in[...]), carry

    for t in range(2):
        keep[pl.ds(t * TILE, TILE), :] = tile(t, 0)[0].astype(BF)
    for t in range(2):
        send[pl.ds(t * TILE, TILE), :] = tile(half // TILE + t, 0)[0].astype(BF)
    for copy in copies[arrived:]:
        copy.wait()


def four_parts(at, big, own, to_x, to_z, to_xz):
    x, za = at[0], at[1]
    n = own.shape[0]
    own[...] = big[aligned(2 * x + za, n), :]
    to_x[...] = big[aligned(2 * (1 - x) + za, n), :].astype(BF)
    to_z[...] = big[aligned(2 * x + 1 - za, n), :].astype(BF)
    to_xz[...] = big[aligned(2 * (1 - x) + 1 - za, n), :].astype(BF)


def inner_grad_kernel(at, h2, grad_inner, own, to_x, to_z, to_xz, big):
    big[...] = mm_tn(h2[...], grad_inner[...])
    four_parts(at, big, own, to_x, to_z, to_xz)


def outer_grad_kernel(
    at, hidden, cot, w_outer, own, to_x, to_z, to_xz, keep, send, big
):
    half = keep.shape[0]
    send[...] = mm(hidden[pl.ds(half, half), :], w_outer[...]).astype(BF)
    keep[...] = mm(hidden[pl.ds(0, half), :], w_outer[...])
    big[...] = mm_tn(hidden[...], cot[...])
    four_parts(at, big, own, to_x, to_z, to_xz)


def payload_kernel(at, head_keep, head_got, own, other, payload):
    x = at[0]
    m = head_keep.shape[1] // 4
    n = own.shape[1]
    wide = head_keep.shape[2]
    for d in range(8):
        rows = pl.ds((d & 3) * m, m)
        payload[d, pl.ds(0, m), pl.ds(0, wide)] = (
            head_keep[d >> 2, rows, :] + head_got[d >> 2, rows, :].astype(F32)
        ).astype(BF)
        payload[d, pl.ds(0, m), pl.ds(wide, HD)] = jnp.zeros((m, HD), BF)
        for s, part in enumerate((own, other)):
            here = pl.ds(m + s * n, n)

            @pl.when(x == d >> 2)
            def _():
                payload[d, here, :] = part[d & 3]

            @pl.when(x != d >> 2)
            def _():
                payload[d, here, :] = jnp.zeros(part.shape[1:], BF)


def last_kernel(at, got, query, key, value, sum_a, sum_b, sum_c, sum_d, inner_g):
    x, c = at[0], at[4]
    per = query.shape[0]
    m = per + 16
    lanes = got.shape[2]
    total = got[0, pl.ds(per, 16), pl.ds(0, HD)].astype(F32)
    for h in range(8):
        for n, out in enumerate((query, key, value)):
            out[:, pl.ds(h * HD, HD)] = got[h, pl.ds(0, per), pl.ds(n * HD, HD)].astype(F32)
        if h:
            total = total + got[h, pl.ds(per, 16), pl.ds(0, HD)].astype(F32)
    for n, out in enumerate((sum_a, sum_b, sum_c, sum_d)):
        out[...] = total[0:1, n * per : (n + 1) * per]
    for w in range(4):
        for s in range(2):
            part = got[4 * x + w, pl.ds(m + s * per, per), :].astype(F32)
            side = 2 * w + (c if s == 0 else 1 - c)
            for t in range(lanes // HD):
                inner_g[:, aligned(t * 8 + side, HD)] = part[:, t * HD : (t + 1) * HD]


def branch_kernel(at, parts, scaled, inverse, gains, cot, *refs):
    pieces, (grad_middle, branch, go, sums, out_w, sems) = refs[:8], refs[8:]
    copies = place_w_out(at, pieces, out_w, sems)
    rows, width = scaled.shape
    tok = rows // 2
    grad = parts[0].astype(F32)
    for n in range(1, 4):
        grad = grad + parts[n].astype(F32)
    n2 = scaled[...]
    sums[0:1, :] = jnp.sum(grad * n2, 0, keepdims=True)
    sums[1:2, :] = jnp.sum(grad, 0, keepdims=True)
    a = grad * gains[2:3, :]
    grad = inverse[:, 0:1] * (
        a - jnp.mean(a, -1, keepdims=True) - n2 * jnp.mean(a * n2, -1, keepdims=True)
    )
    for s in range(2):
        part = pl.ds(s * tok, tok)
        grad_middle[part, :] = cot[s].astype(F32) + grad[s * tok : (s + 1) * tok]
    branch[...] = grad_middle[...].astype(BF)
    for copy in copies:
        copy.wait()
    out = mm_nt(branch[...], out_w[...]).astype(BF)
    for s in range(16):
        head = (s >> 3) * 4 + (s & 3)
        seq = s >> 2 & 1
        go[s] = out[seq * tok : (seq + 1) * tok, head * HD : (head + 1) * HD]


def fine_backward_kernel(at, query, own, other, go_ref, out_f, lse_ref, gq_ref, keep, send, acc):
    rows_all = query.shape[0]
    tiles = rows_all // TILE
    c = at[4]
    both = (own, other)
    keep[...] = jnp.zeros_like(keep)
    acc[...] = jnp.zeros_like(acc)
    totals = (keep, acc)

    def tile(t, carry):
        rows = aligned(t, TILE)
        q = query[rows, :]
        go = go_ref[pl.ds(t * (TILE // 64), TILE // 64)].reshape(TILE, HD)
        delta = jnp.sum(go.astype(F32) * out_f[rows, :], -1, keepdims=True)
        lse = lse_ref[rows, 0:1]

        def one(u, gq, masked):
            cols = aligned(u, TILE)
            for n in range(2):
                kk = both[n][cols, pl.ds(0, HD)]
                p = jnp.exp(mm_nt(q, kk) * SCALE - lse)
                if masked:
                    p = jnp.where(causal(c, c if n == 0 else 1 - c), p, 0.0)
                totals[n][cols, pl.ds(HD, HD)] += mm_tn(p.astype(BF), go)
                ds = (p * (mm_nt(go, both[n][cols, pl.ds(HD, HD)]) - delta)).astype(BF)
                totals[n][cols, pl.ds(0, HD)] += mm_tn(ds, q)
                gq = gq + mm(ds, kk)
            return gq

        gq = jnp.zeros((TILE, HD), F32)
        for u in range(t + 1):
            gq = one(u, gq, u == t)
        gq_ref[rows, :] = (gq * SCALE).astype(BF)
        return carry

    for t in range(tiles):
        tile(t, 0)
    keep[:, :HD] = keep[:, :HD] * SCALE
    send[:, :HD] = (acc[:, :HD] * SCALE).astype(BF)
    send[:, HD:] = acc[:, HD:].astype(BF)


def partial_kernel(at, *refs):
    blocks, (gq, keep, got, weights) = refs[:8], refs[8:12]
    grads, parts, sums, tokens, sems = refs[12:]
    x, za, zl, y = (at[i] for i in range(4))
    copies = []
    for n in range(8):
        for s in range(2):
            j = (x ^ (n >> 2)) * 8 + (za ^ s) * 4 + (zl ^ (n >> 1 & 1)) * 2 + (y ^ (n & 1))
            copies.append(
                pltpu.make_async_copy(
                    blocks[n].at[s], tokens.at[aligned(j, 64), :], sems.at[len(copies)]
                )
            )
            copies[-1].start()
    for copy in copies:
        copy.wait()
    tiles = gq.shape[0] // TILE
    for t in range(tiles):
        rows = pl.ds(t * TILE, TILE)
        grads[rows, pl.ds(0, HD)] = gq[rows, :]
        grads[rows, pl.ds(HD, 2 * HD)] = (keep[rows, :] + got[rows, :].astype(F32)).astype(BF)
        part = mm_nt(grads[rows, :], weights[...])
        normed, _ = norm_of(tokens[rows, :].astype(F32))
        one = jnp.sum(part * normed, 0, keepdims=True)
        two = jnp.sum(part, 0, keepdims=True)
        if t == 0:
            sums[0:1, :] = one
            sums[1:2, :] = two
        else:
            sums[0:1, :] += one
            sums[1:2, :] += two
        for i in range(4):
            parts[(t >> 1) * 4 + i, za ^ (t & 1)] = part[i * 64 : (i + 1) * 64].astype(BF)


def total_kernel(parts, keep, send):
    total = parts[0, 0].astype(F32)
    other = parts[0, 1].astype(F32)
    for n in range(1, 8):
        total = total + parts[n, 0].astype(F32)
        other = other + parts[n, 1].astype(F32)
    keep[...] = total
    send[...] = other.astype(BF)


def head_grad_kernel(at, left, right, sums, keep, send, big):
    c = at[4]
    per = left.shape[1] // 32
    big[...] = mm_tn(left[...], right[...])
    spare = keep.shape[2] - sums.shape[1]
    for q in range(16):
        keep[q, pl.ds(0, per), :] = big[aligned(2 * q + c, per), :]
        send[q, pl.ds(0, per), :] = big[aligned(2 * q + 1 - c, per), :].astype(BF)
    pad = jnp.zeros((16, spare), F32)
    for q in range(16):
        pair = jnp.concatenate([sums[2 * q : 2 * q + 2, :], pad[:2]], 1)
        mine = jnp.where(c == 0, pair[0:1], pair[1:2])
        other = jnp.where(c == 0, pair[1:2], pair[0:1])
        keep[q, pl.ds(per, 16), :] = jnp.broadcast_to(mine, (16, keep.shape[2]))
        send[q, pl.ds(per, 16), :] = jnp.broadcast_to(other, (16, keep.shape[2])).astype(BF)


def core_grad_kernel(at, left, right, keep, send, big):
    c = at[4]
    per = left.shape[1] // 32
    big[...] = mm_tn(left[...], right[...])
    for q in range(16):
        rows = pl.ds(q * per, per)
        keep[rows, :] = big[aligned(2 * q + c, per), :]
        send[rows, :] = big[aligned(2 * q + 1 - c, per), :].astype(BF)


def input_kernel(at, keep, got, tokens, grad_middle, gains, grad_tokens):
    za = at[1]
    tok = tokens.shape[1]
    for n in range(2):
        seq = za if n == 0 else 1 - za
        part = keep[...] if n == 0 else got[...].astype(F32)
        n1, inv = norm_of(tokens[seq].astype(F32))
        a = part * gains[0:1, :]
        grad_tokens[seq] = grad_middle[aligned(seq, tok), :] + inv * (
            a - jnp.mean(a, -1, keepdims=True) - n1 * jnp.mean(a * n1, -1, keepdims=True)
        )


def far_kernel(keep, got, own, on_z, on_y, far_a, far_b):
    n = own.shape[0]
    for i, out in enumerate((own, on_z, on_y)):
        rows = pl.ds(i * n, n)
        out[...] = keep[rows, :] + got[rows, :].astype(F32)
    for i, out in enumerate((far_a, far_b)):
        rows = pl.ds(3 * n + i * (n // 2), n // 2)
        out[...] = (keep[rows, :] + got[rows, :].astype(F32)).astype(BF)


def near_kernel(on_z, on_y, got_a, got_b, send_z, send_y):
    n = got_a.shape[0]
    first, second = pl.ds(0, n), pl.ds(n, n)
    send_z[first, :] = (on_z[first, :] + got_a[...].astype(F32)).astype(BF)
    send_z[second, :] = on_z[second, :].astype(BF)
    send_y[first, :] = on_y[first, :].astype(BF)
    send_y[second, :] = (on_y[second, :] + got_b[...].astype(F32)).astype(BF)


def result_sum_kernel(middle, own, got_z, got_y, out):
    out[...] = (
        middle[...] + own[...] + got_z[...].astype(F32) + got_y[...].astype(F32)
    ).astype(BF)


def fold_kernel(at, keep, got, parts):
    zl, y = at[2], at[3]
    rows = parts.shape[1]
    for n in range(4):
        here = pl.ds(n * rows, rows)
        z = zl ^ (1 if n in (1, 3) else 0)
        w = y ^ (1 if n in (2, 3) else 0)
        parts[z * 2 + w] = (keep[here, :].astype(F32) + got[here, :].astype(F32)).astype(BF)


def stage(*values):
    return lax.optimization_barrier(values)


def grow(v, axis):
    return jnp.concatenate([v, swap(v, axis)], 0)


def half_swap(v, axis):
    return swap(pick(v, 1 - lax.axis_index(axis)), axis)


def fine_layer(
    tokens,
    cotangent,
    ln1_gain,
    ln1_bias,
    w_query,
    w_key,
    w_value,
    w_out,
    ln2_gain,
    ln2_bias,
    w_inner,
    w_outer,
):
    seqs, tok, width = tokens.shape
    rows = seqs * tok
    half = rows // 2
    per = w_query.shape[0]
    unit = w_outer.shape[0]
    hidden_units = 4 * unit
    all_rows = 8 * rows
    coords = jnp.stack([lax.axis_index(a) for a in ("x", "za", "zl", "y", "c")]).astype(jnp.int32)
    x, za = lax.axis_index("x"), lax.axis_index("za")
    cube, owners = ("x", "zl", "y"), ("x", "za", "zl", "y")
    cot = cotangent.reshape(rows, width)

    def split(axis, keep, got, shape):
        keep, got = keep.reshape(shape), got.reshape(shape)
        i = lax.axis_index(axis)
        mine = pick(keep, i, 1) + pick(got, i, 1).astype(F32)
        return mine, (pick(keep, 1 - i, 1) + pick(got, 1 - i, 1).astype(F32)).astype(BF)

    head_w, inner_w = call(
        pack_kernel,
        [((16, 3 * per + 16, HD), BF), ((8, per, hidden_units), BF)],
        [w_query, w_key, w_value]
        + [g.reshape(1, per) for g in (ln1_gain, ln1_bias, ln2_gain, ln2_bias)]
        + [w_inner],
        name="pack",
    )
    moved, head_w, inner_w, w_out, w_outer = stage(
        swap(pick(tokens, 1 - za), "za"), head_w, inner_w, w_out, w_outer
    )
    block = jnp.stack([pick(tokens, za), moved])
    on_x, on_z, on_y, head_w = stage(
        swap(block, "x"), swap(block, "zl"), swap(block, "y"), head_w
    )
    on_xz, on_xy, on_zy, on_xyz, head_w, w_out_z = stage(
        swap(on_x, "zl"),
        swap(on_y, "x"),
        swap(on_z, "y"),
        lax.ppermute(block, cube, [(i, 7 - i) for i in range(8)]),
        lax.all_to_all(head_w, owners, 0, 0, tiled=True),
        swap(after(w_out, on_x), "za"),
    )
    head_c, w_outer, inner_w, w_out_z = stage(swap(head_w, "c"), w_outer, inner_w, w_out_z)
    blocks = [block, on_y, on_z, on_zy, on_x, on_xy, on_xz, on_xyz]
    out_w = jnp.stack([w_out, w_out_z])
    h1, query, kv, gains, head_w = call(
        qkv_kernel,
        [
            ((16 * tok, width), BF),
            ((16 * tok, HD), BF),
            ((16 * tok, 2 * HD), BF),
            ((8, width), F32),
            ((width, 3 * HD), BF),
        ],
        blocks + [head_w, head_c],
        coords,
        name="qkv",
    )
    kv, query, out_x, outer_z, outer_x, inner_w = stage(
        kv,
        query,
        swap(out_w, "x"),
        swap(w_outer, "za"),
        swap(w_outer, "x"),
        lax.all_to_all(inner_w, W_AXES, 0, 0, tiled=True),
    )
    out_w = jnp.concatenate([out_w, out_x], 0)
    kv_other, out_w, inner_w = stage(swap(kv, "c"), out_w, inner_w)
    out, out_f, lse, query, kv, kv_other = call(
        fine_forward_kernel,
        [((16, tok, HD), BF), ((16 * tok, HD), F32), ((16 * tok, HD), F32)],
        [query, kv, kv_other],
        coords,
        save=(0, 1, 2),
        scratch=[pltpu.VMEM((2 * 16 * tok // TILE, TILE, TILE), F32)],
        name="attention_forward",
    )
    out, out_z, out_y, inner_z, inner_x, cot = stage(
        out,
        swap(out_w, "zl"),
        swap(out_w, "y"),
        swap(inner_w, "za"),
        swap(inner_w, "x"),
        cot,
    )
    mixed, cot_z, cot_y, cot_c, out_zy, outer_zx, inner_zx, *out_c = stage(
        lax.all_to_all(out, owners, 0, 0, tiled=True),
        swap(cot, "zl"),
        swap(cot, "y"),
        swap(cot, "c"),
        swap(out_z, "y"),
        swap(outer_z, "x"),
        swap(inner_z, "x"),
        swap(out_w, "c"),
        swap(out_z, "c"),
        swap(out_y, "c"),
    )
    (out_zyc,) = stage(swap(out_zy, "c"))
    pieces = [out_w, out_z, out_y, out_zy] + out_c + [out_zyc]
    mixed, middle, scaled, inverse, h2 = call(
        middle_kernel,
        [
            ((rows, width), BF),
            ((rows, width), F32),
            ((rows, width), F32),
            ((rows, HD), F32),
            ((rows, width), BF),
        ],
        [mixed, tokens, gains] + pieces,
        coords,
        raw=range(3, 11),
        scratch=[pltpu.VMEM((width, width), BF), pltpu.SemaphoreType.DMA((32,))],
        name="middle",
    )
    cot_z, cot_y = after(cot_z, h2), after(cot_y, h2)
    h2_z, h2_y, h2_c, cot_a, cot_b, cot_zc, cot_yc = stage(
        swap(h2, "zl"),
        swap(h2, "y"),
        swap(h2, "c"),
        swap(cot_z[:half], "y"),
        swap(cot_y[half:], "zl"),
        swap(cot_z, "c"),
        swap(cot_y, "c"),
    )
    h2_a, h2_b, h2_zc, h2_yc, cot_ac, cot_bc = stage(
        swap(h2_z[:half], "y"),
        swap(h2_y[half:], "zl"),
        swap(h2_z, "c"),
        swap(h2_y, "c"),
        swap(cot_a, "c"),
        swap(cot_b, "c"),
    )
    h2_ac, h2_bc = stage(swap(h2_a, "c"), swap(h2_b, "c"))
    h2_all, cot_all, outer_w, hidden, grad_inner, keep, send = call(
        inner_kernel,
        [
            ((all_rows, width), BF, "raw"),
            ((all_rows, width), BF, "raw"),
            ((hidden_units, width), BF, "raw"),
            ((all_rows, hidden_units), BF),
            ((all_rows, hidden_units), BF),
            ((all_rows // 2, width), BF),
            ((all_rows // 2, width), BF),
        ],
        [h2, h2_z, h2_y, h2_a, h2_b, h2_c, h2_zc, h2_yc, h2_ac, h2_bc]
        + [cot, cot_z, cot_y, cot_a, cot_b, cot_c, cot_zc, cot_yc, cot_ac, cot_bc]
        + [p.reshape(8 * per, hidden_units) for p in (inner_w, inner_x, inner_z, inner_zx)]
        + [w_outer, outer_x, outer_z, outer_zx],
        coords,
        raw=range(10, 28),
        scratch=[
            pltpu.VMEM((all_rows, width), BF),
            pltpu.VMEM((all_rows, width), BF),
            pltpu.VMEM((width, hidden_units), BF),
            pltpu.VMEM((hidden_units, width), BF),
            pltpu.SemaphoreType.DMA((21,)),
        ],
        name="inner",
    )

    (got,) = stage(swap(send, "c"))
    (parts,) = call(
        fold_kernel, [((4, rows, width), BF)], [keep, got], coords, name="fold"
    )
    n_in, n_out = 8 * per, unit
    inner_g, in_x, in_z, in_xz = call(
        inner_grad_kernel,
        [((n_in, hidden_units), F32)] + [((n_in, hidden_units), BF)] * 3,
        [h2_all, grad_inner],
        coords,
        scratch=[pltpu.VMEM((width, hidden_units), F32)],
        name="inner_grad",
    )
    parts, inner_g, in_x, in_z, in_xz = stage(parts, inner_g, in_x, in_z, in_xz)
    outer_g, outer_x, outer_z, outer_xz, res_keep, res_send = call(
        outer_grad_kernel,
        [((n_out, width), F32)]
        + [((n_out, width), BF)] * 3
        + [((all_rows // 2, width), F32), ((all_rows // 2, width), BF)],
        [after(hidden, in_x), cot_all, outer_w],
        coords,
        scratch=[pltpu.VMEM((hidden_units, width), F32)],
        name="outer_grad",
    )
    parts, in_x, in_z, outer_g, outer_x, outer_z, outer_xz, res_keep, res_send, in_xz = stage(
        lax.all_to_all(parts, ("zl", "y"), 0, 0, tiled=True),
        swap(in_x, "x"),
        swap(in_z, "za"),
        outer_g,
        outer_x,
        outer_z,
        outer_xz,
        res_keep,
        res_send,
        in_xz,
    )
    grad_middle, branch, go, sums_two = call(
        branch_kernel,
        [
            ((rows, width), F32),
            ((rows, width), BF),
            ((16, tok, HD), BF),
            ((2, width), F32),
        ],
        [parts, scaled, inverse, gains, cotangent] + pieces,
        coords,
        raw=range(5, 13),
        scratch=[pltpu.VMEM((width, width), BF), pltpu.SemaphoreType.DMA((32,))],
        name="branch",
    )
    go, branch, res_got, outer_x, outer_z = stage(
        go, branch, swap(res_send, "c"), outer_x, outer_z
    )
    res = (res_keep + res_got.astype(F32)).reshape(4, rows, width)
    far_a, far_b = res[3, :half].astype(BF), res[3, half:].astype(BF)
    out_keep, out_send = call(
        core_grad_kernel,
        [((width // 2, width), F32), ((width // 2, width), BF)],
        [mixed, branch],
        coords,
        scratch=[pltpu.VMEM((width, width), F32)],
        name="out_grad",
    )
    diagonal = [(i, 3 - i) for i in range(4)]
    go, outer_x, outer_z, in_xz, outer_xz, out_keep, out_send, res, far_a, far_b = stage(
        lax.all_to_all(go, owners, 0, 0, tiled=True),
        swap(outer_x, "x"),
        swap(outer_z, "za"),
        in_xz,
        outer_xz,
        out_keep,
        out_send,
        res,
        far_a,
        far_b,
    )
    gq, keep, send = call(
        fine_backward_kernel,
        [((16 * tok, HD), BF), ((16 * tok, 2 * HD), F32), ((16 * tok, 2 * HD), BF)],
        [query, kv, kv_other, go, out_f, lse],
        coords,
        scratch=[pltpu.VMEM((16 * tok, 2 * HD), F32)],
        name="attention_backward",
    )
    gq, keep, send, got_a, got_b, out_got, in_xz = stage(
        gq,
        keep,
        send,
        swap(far_a, "y"),
        swap(far_b, "zl"),
        swap(out_send, "c"),
        lax.ppermute(in_xz, ("x", "za"), diagonal),
    )
    out_keep, out_send = split("x", out_keep, out_got, (1, 2, 8 * per, width))
    res_z = jnp.concatenate([res[1, :half] + got_a.astype(F32), res[1, half:]], 0).astype(BF)
    res_y = jnp.concatenate([res[2, :half], res[2, half:] + got_b.astype(F32)], 0).astype(BF)
    got, out_keep, out_send, res_z, res_y, outer_xz = stage(
        swap(send, "c"), out_keep, out_send, res_z, res_y, outer_xz
    )
    grads, parts, sums = call(
        partial_kernel,
        [
            ((16 * tok, 3 * HD), BF),
            ((8, 2, tok, width), BF),
            ((2, width), F32),
        ],
        blocks + [gq, keep, got, head_w],
        coords,
        raw=range(8),
        scratch=[pltpu.VMEM((16 * tok, width), BF), pltpu.SemaphoreType.DMA((16,))],
        name="partial",
    )
    grads, parts, sums, got_z, got_y, out_keep, out_got, outer_xz = stage(
        grads,
        parts,
        sums,
        swap(res_z, "zl"),
        swap(res_y, "y"),
        out_keep,
        swap(out_send, "x"),
        lax.ppermute(outer_xz, ("x", "za"), diagonal),
    )
    parts = lax.all_to_all(parts, cube, 0, 0, tiled=True)
    sums = jnp.concatenate([sums, sums_two], 0)
    sums = sums.reshape(4, 32, per).transpose(1, 0, 2).reshape(32, 4 * per)
    head_keep, head_send = call(
        head_grad_kernel,
        [((16, per + 16, 3 * HD), F32), ((16, per + 16, 3 * HD), BF)],
        [h1, grads, sums],
        coords,
        scratch=[pltpu.VMEM((width, 3 * HD), F32)],
        name="head_grad",
    )
    head_keep, head_send = stage(head_keep, head_send)
    out_keep, out_send = split(
        "y", out_keep, after(out_got, head_send), (4, 2, per, width)
    )
    inner_g = inner_g + after(in_x, head_send).astype(F32) + in_z.astype(F32) + in_xz.astype(F32)
    inner_g = inner_g.astype(BF).reshape(4, 2, per, hidden_units)
    inner_own = pick(inner_g, lax.axis_index("c"), 1)
    inner_send = pick(inner_g, 1 - lax.axis_index("c"), 1)
    head_keep, head_got, out_keep, out_send, inner_own, inner_send = stage(
        head_keep, swap(head_send, "c"), out_keep, out_send, inner_own, inner_send
    )
    head_keep, head_send = split("za", head_keep, head_got, (2, 2, 4 * (per + 16), 3 * HD))
    head_keep, head_send, out_send = stage(head_keep, head_send, out_send)
    result = (
        middle + res[0] + after(got_z, head_send).astype(F32) + got_y.astype(F32)
    ).astype(BF)
    outer_g = (
        outer_g
        + after(outer_x, head_send).astype(F32)
        + outer_z.astype(F32)
        + outer_xz.astype(F32)
    )
    head_keep, head_got, out_keep, out_got, inner_got, result, outer_g = stage(
        head_keep,
        swap(head_send, "za"),
        out_keep,
        swap(out_send, "y"),
        swap(inner_send, "c"),
        result,
        outer_g,
    )
    out_keep, out_send = split("za", out_keep, out_got, (1, 2, 2 * per, width))
    (payload,) = call(
        payload_kernel,
        [((8, 3 * per + 16, hidden_units), BF)],
        [head_keep, head_got, inner_own, inner_got],
        coords,
        name="payload",
    )
    parts, payload, out_keep, out_send = stage(parts, payload, out_keep, out_send)
    total, send = call(
        total_kernel, [((tok, width), F32), ((tok, width), BF)], [parts], name="total"
    )
    total, send, payload, out_send = stage(total, send, payload, out_send)
    got, payload, out_send = stage(swap(send, "za"), payload, out_send)
    (grad_tokens,) = call(
        input_kernel,
        [((seqs, tok, width), F32)],
        [total, got, tokens, grad_middle, gains],
        coords,
        name="input",
    )
    payload, out_got, grad_tokens = stage(
        lax.all_to_all(payload, cube, 0, 0, tiled=True), swap(out_send, "za"), grad_tokens
    )
    out_keep, out_send = split("zl", out_keep, out_got, (1, 2, per, width))
    out_keep, out_send = stage(out_keep, out_send)
    query_g, key_g, value_g, *sums, inner_g = call(
        last_kernel,
        [((per, width), F32)] * 3
        + [((1, per), F32)] * 4
        + [((per, 8 * hidden_units), F32)],
        [payload],
        coords,
        name="last",
    )
    query_g, key_g, value_g, inner_g, out_got, *sums = stage(
        query_g, key_g, value_g, inner_g, swap(out_send, "zl"), *sums
    )
    sums = [v.reshape(per) for v in sums]
    return (
        result.reshape(seqs, tok, width),
        grad_tokens,
        sums[0],
        sums[1],
        query_g,
        key_g,
        value_g,
        out_keep[0] + out_got[0].astype(F32),
        sums[2],
        sums[3],
        inner_g,
        outer_g,
    )


def solution(mesh):
    blocks = mesh.shape["blk"]
    if blocks == 16:
        sizes = (2, 2, 1, 2, 2, 2)
        roles = (True, "za", ("x", "zl", "y"), ("c",), ("x", "za", "zl", "y"))
    else:
        sizes = (2, 8, blocks // 64, 2, 2, 2)
        roles = (False, "x", ("za",), ("zb", "zl", "y", "c"), ("x", "za"))
    fine = Mesh(mesh.devices.reshape(sizes), AXES)
    tok, row, vec = P(None, AXES, None), P(AXES, None), P(AXES)
    in_specs = (tok, tok, vec, vec, row, row, row, row, vec, vec, row, row)
    out_specs = (tok, tok, vec, vec, row, row, row, row, vec, vec, row, row)
    return jax.shard_map(
        fine_layer if blocks == 16 else functools.partial(on_device, roles),
        mesh=fine,
        in_specs=in_specs,
        out_specs=out_specs,
        check_vma=False,
    )
```

```python
import functools
import math

import jax
import jax.numpy as jnp
from jax import lax
from jax.experimental import pallas as pl
from jax.experimental.pallas import tpu as pltpu
from jax.sharding import Mesh
from jax.sharding import PartitionSpec as P

HD = 128
TILE = 256
SCALE = HD ** (-0.5)
MASKED = -1e30
eps_norm = 1e-05
gelu_coef = math.sqrt(2.0 / math.pi)
BF = jnp.bfloat16
F32 = jnp.float32
AXES = ("x", "za", "zb", "zl", "y", "c")
T_AXES = ("x", "za", "zb")
W_AXES = ("zl", "y", "c")


def mm(a, b):
    return jnp.dot(a, b, preferred_element_type=F32)


def mm_nt(a, b):
    return lax.dot_general(a, b, (((1,), (1,)), ((), ())), preferred_element_type=F32)


def mm_tn(a, b):
    return lax.dot_general(a, b, (((0,), (0,)), ((), ())), preferred_element_type=F32)


def norm_stats(values):
    centered = values - jnp.mean(values, -1, keepdims=True)
    inverse = lax.rsqrt(jnp.mean(centered * centered, -1, keepdims=True) + eps_norm)
    return centered * inverse, inverse


def norm_back(grad_normed, scaled, inverse, gain):
    g = grad_normed * gain
    return inverse * (
        g - jnp.mean(g, -1, keepdims=True) - scaled * jnp.mean(g * scaled, -1, keepdims=True)
    )


def swap(v, axis):
    return lax.ppermute(v, axis, [(0, 1), (1, 0)])


def pick(v, index, axis=0):
    return lax.dynamic_index_in_dim(v, index, axis, keepdims=False)


def pair_gather(v, axis):
    other = swap(v, axis)
    first = lax.axis_index(axis) == 0
    return jnp.stack([jnp.where(first, v, other), jnp.where(first, other, v)])


def pair_scatter(v, axis, dim):
    me = lax.axis_index(axis)
    return pick(v, me, dim) + swap(pick(v, 1 - me, dim).astype(BF), axis).astype(F32)


def after(v, *others):
    return lax.optimization_barrier((v,) + others)[0]


def t_gather(v):
    if lax.axis_size("za") * lax.axis_size("zb") != 2:
        return lax.all_gather(v, T_AXES, axis=0, tiled=False)
    x, z = lax.axis_index("x"), lax.axis_index("za")
    over_x, over_z = swap(v, "x"), swap(v, "za")
    out = jnp.zeros((4,) + v.shape, v.dtype)
    for part, at in (
        (v, 2 * x + z),
        (over_x, 2 * (1 - x) + z),
        (over_z, 2 * x + 1 - z),
        (swap(over_z, "x"), 2 * (1 - x) + 1 - z),
    ):
        out = lax.dynamic_update_index_in_dim(out, part, at, 0)
    return out


def t_scatter(v):
    if lax.axis_size("za") * lax.axis_size("zb") != 2:
        return lax.psum_scatter(v, T_AXES, scatter_dimension=0, tiled=False)
    v = pair_scatter(v.reshape((2, 2) + v.shape[1:]), "x", 0)
    return pair_scatter(v, "za", 0)


def plane_gather(v):
    half = v.shape[0] // 2
    a, b = v[:half], v[half:]
    a = jnp.stack([a, swap(a, "zl")])
    b = jnp.stack([b, swap(b, "y")])
    a = jnp.stack([a, swap(a, "y")])
    b = jnp.stack([b, swap(b, "zl")])
    both = jnp.stack([a, b])
    return jnp.stack([both, swap(both, "c")]).reshape(8 * v.shape[0], v.shape[1])


def plane_scatter(v):
    rows, width = v.shape
    v = v.reshape(2, 2, 2, 2, rows // 16, width)

    def fold(u, axis):
        return u[0] + swap(u[1].astype(BF), axis).astype(F32)

    v = fold(v, "c")
    a, b = v[0], v[1]
    a = fold(a, "y")
    b = fold(b, "zl")
    a = fold(a, "zl")
    b = fold(b, "y")
    return jnp.concatenate([a, b], 0)


def shares(count, body):
    if count <= 2:
        for k in range(count):
            body(k)
    else:
        lax.fori_loop(0, count, lambda k, c: (body(k), c)[1], 0)


def mask_of(count, q_tile, k_tile, q_share, k_share):
    rows = lax.broadcasted_iota(jnp.int32, (TILE, TILE), 0) + q_tile * TILE
    cols = lax.broadcasted_iota(jnp.int32, (TILE, TILE), 1) + k_tile * TILE
    q_pos = (lax.shift_right_logical(rows, 6) * count + q_share) * 64 + (rows & 63)
    k_pos = (lax.shift_right_logical(cols, 6) * count + k_share) * 64 + (cols & 63)
    return k_pos <= q_pos


def forward_kernel(count, meta, q_ref, k_ref, v_ref, o_ref, of_ref, lse_ref, qa, ka, va, s_ref):
    blocks = q_ref.shape[0]
    for j in range(blocks):
        slot = meta[j]
        rows = pl.ds(j * 64, 64)
        qa[rows, :] = q_ref[slot]

        def place(k, rows=rows, slot=slot):
            ka[k, rows, :] = k_ref[k, slot]
            va[k, rows, :] = v_ref[k, slot]

        shares(count, place)
    mine = meta[blocks]
    tiles = blocks * 64 // TILE
    for t in range(tiles):
        q = qa[pl.ds(t * TILE, TILE), :]
        top = jnp.full((TILE, 1), MASKED, F32)
        for u in range(t + 1):
            cols = pl.ds(u * TILE, TILE)

            def score(k, top, u=u, cols=cols):
                s = mm_nt(q, ka[k, cols, :]) * SCALE
                if u == t:
                    s = jnp.where(mask_of(count, t, u, mine, meta[blocks + 1 + k]), s, MASKED)
                s_ref[k * tiles + u] = s
                return jnp.maximum(top, jnp.max(s, -1, keepdims=True))

            if count <= 2:
                for k in range(count):
                    top = score(k, top)
            else:
                top = lax.fori_loop(0, count, score, top)
        total = jnp.zeros((TILE, 1), F32)
        for u in range(t + 1):

            def expo(k, total, u=u):
                p = jnp.exp(s_ref[k * tiles + u] - top)
                s_ref[k * tiles + u] = p
                return total + jnp.sum(p, -1, keepdims=True)

            if count <= 2:
                for k in range(count):
                    total = expo(k, total)
            else:
                total = lax.fori_loop(0, count, expo, total)
        inverse = 1.0 / total
        out = jnp.zeros((TILE, HD), F32)
        for u in range(t + 1):
            cols = pl.ds(u * TILE, TILE)

            def weigh(k, out, u=u, cols=cols):
                p = (s_ref[k * tiles + u] * inverse).astype(BF)
                return out + mm(p, va[k, cols, :])

            if count <= 2:
                for k in range(count):
                    out = weigh(k, out)
            else:
                out = lax.fori_loop(0, count, weigh, out)
        rows = pl.ds(t * TILE, TILE)
        of_ref[rows, :] = out
        o_ref[rows, :] = out.astype(BF)
        lse_ref[rows, :] = jnp.broadcast_to(top + jnp.log(total), (TILE, HD))


def attention_forward(count, meta, q, k, v):
    blocks = q.shape[0]
    rows = blocks * 64
    tiles = rows // TILE
    vm = pl.BlockSpec(memory_space=pltpu.VMEM)
    pairs = tiles * (tiles + 1) // 2 * count
    return pl.pallas_call(
        functools.partial(forward_kernel, count),
        in_specs=[pl.BlockSpec(memory_space=pltpu.SMEM), vm, vm, vm],
        out_specs=[vm] * 6,
        out_shape=[
            jax.ShapeDtypeStruct((rows, HD), BF),
            jax.ShapeDtypeStruct((rows, HD), F32),
            jax.ShapeDtypeStruct((rows, HD), F32),
            jax.ShapeDtypeStruct((rows, HD), BF),
            jax.ShapeDtypeStruct((count, rows, HD), BF),
            jax.ShapeDtypeStruct((count, rows, HD), BF),
        ],
        scratch_shapes=[pltpu.VMEM((count * tiles, TILE, TILE), F32)],
        cost_estimate=pl.CostEstimate(
            flops=pairs * TILE * TILE * HD * 4,
            bytes_accessed=rows * HD * 2 * (2 + 4 * count) + rows * HD * 8,
            transcendentals=pairs * TILE * TILE,
        ),
        compiler_params=pltpu.CompilerParams(vmem_limit_bytes=(16 if count <= 2 else 52) << 20),
        name="attention_forward",
    )(meta, q, k, v)


def backward_kernel(count, meta, q_ref, k_ref, v_ref, go_ref, of_ref, lse_ref, gq_ref, gk, gv):
    rows_all = q_ref.shape[0]
    blocks = rows_all // 64
    mine = meta[blocks]
    tiles = rows_all // TILE

    def zero(k):
        gk[k] = jnp.zeros((rows_all, HD), F32)
        gv[k] = jnp.zeros((rows_all, HD), F32)

    shares(count, zero)
    for t in range(tiles):
        rows = pl.ds(t * TILE, TILE)
        q = q_ref[rows, :]
        go = go_ref[rows, :]
        delta = jnp.sum(go.astype(F32) * of_ref[rows, :], -1, keepdims=True)
        lse = lse_ref[rows, :][:, :1]
        gq = jnp.zeros((TILE, HD), F32)
        for u in range(t + 1):
            cols = pl.ds(u * TILE, TILE)

            def one(k, gq, u=u, cols=cols):
                kk = k_ref[k, cols, :]
                p = jnp.exp(mm_nt(q, kk) * SCALE - lse)
                if u == t:
                    p = jnp.where(mask_of(count, t, u, mine, meta[blocks + 1 + k]), p, 0.0)
                gv[k, cols, :] += mm_tn(p.astype(BF), go)
                ds = (p * (mm_nt(go, v_ref[k, cols, :]) - delta)).astype(BF)
                gk[k, cols, :] += mm_tn(ds, q)
                return gq + mm(ds, kk)

            if count <= 2:
                for k in range(count):
                    gq = one(k, gq)
            else:
                gq = lax.fori_loop(0, count, one, gq)
        gq_ref[rows, :] = (gq * SCALE).astype(BF)

    def scale(k):
        gk[k] = gk[k] * SCALE

    shares(count, scale)


def attention_backward(count, meta, q, k, v, go, of, lse):
    rows = q.shape[0]
    tiles = rows // TILE
    vm = pl.BlockSpec(memory_space=pltpu.VMEM)
    pairs = tiles * (tiles + 1) // 2 * count
    return pl.pallas_call(
        functools.partial(backward_kernel, count),
        in_specs=[pl.BlockSpec(memory_space=pltpu.SMEM)] + [vm] * 6,
        out_specs=[vm] * 3,
        out_shape=[
            jax.ShapeDtypeStruct((rows, HD), BF),
            jax.ShapeDtypeStruct((count, rows, HD), F32),
            jax.ShapeDtypeStruct((count, rows, HD), F32),
        ],
        cost_estimate=pl.CostEstimate(
            flops=pairs * TILE * TILE * HD * 10,
            bytes_accessed=rows * HD * (16 + 12 * count),
            transcendentals=pairs * TILE * TILE,
        ),
        compiler_params=pltpu.CompilerParams(vmem_limit_bytes=(16 if count <= 2 else 52) << 20),
        name="attention_backward",
    )(meta, q, k, v, go, of, lse)


def reorder_kernel(meta, g_ref, out_ref):
    for j in range(g_ref.shape[0]):
        out_ref[meta[j]] = g_ref[j]


def reorder(meta, g):
    vm = pl.BlockSpec(memory_space=pltpu.VMEM)
    return pl.pallas_call(
        reorder_kernel,
        in_specs=[pl.BlockSpec(memory_space=pltpu.SMEM), vm],
        out_specs=vm,
        out_shape=jax.ShapeDtypeStruct(g.shape, g.dtype),
        cost_estimate=pl.CostEstimate(flops=0, bytes_accessed=4 * g.size, transcendentals=0),
        compiler_params=pltpu.CompilerParams(vmem_limit_bytes=8 << 20),
        name="reorder",
    )(meta, g)


def on_device(
    roles,
    tokens,
    cotangent,
    ln1_gain,
    ln1_bias,
    w_query,
    w_key,
    w_value,
    w_out,
    ln2_gain,
    ln2_bias,
    w_inner,
    w_outer,
):
    small, seq_axis, hd_axes, sh_axes, own_axes = roles
    planes = math.prod(lax.axis_size(a) for a in T_AXES)
    count = math.prod(lax.axis_size(a) for a in sh_axes)
    devices = 8 * planes
    seqs, tok, width = tokens.shape
    rows = seqs * tok
    per = w_query.shape[0]
    unit = w_outer.shape[0]
    seq = lax.axis_index(seq_axis)
    share = lax.axis_index(sh_axes)

    block = jnp.stack([pick(tokens, seq), swap(pick(tokens, 1 - seq), seq_axis)])
    if small:
        on_x, on_z, on_y = (swap(block, a) for a in hd_axes)
        on_xz, on_xy, on_zy = swap(on_x, "zl"), swap(on_y, "x"), swap(on_z, "y")
        on_xyz = swap(on_xz, "y")
        seen = jnp.stack([block, on_y, on_z, on_zy, on_x, on_xy, on_xz, on_xyz])
    else:
        seen = lax.all_gather(block, hd_axes, axis=0, tiled=False)
    at = jnp.arange(16, dtype=jnp.int32)
    if small:
        at_x, at_za, at_zl, at_y = at // 8, at // 4 % 2, at // 2 % 2, at % 2
        x, zl, y = (lax.axis_index(a) for a in hd_axes)
        slots = ((at_x ^ x) * 4 + (at_zl ^ zl) * 2 + (at_y ^ y)) * 2 + (at_za ^ seq)
    else:
        slots = at % 8 * 2 + (at // 8 ^ seq)

    gains = jnp.concatenate([ln1_gain, ln1_bias, ln2_gain, ln2_bias])
    gains = jnp.broadcast_to(jnp.pad(gains, (0, HD - gains.shape[0])), (8, 1, HD))
    head_w = jnp.stack([w_query, w_key, w_value]).reshape(3, per, 8, HD).transpose(2, 0, 1, 3)
    head_w = jnp.concatenate([head_w.reshape(8, 3 * per, HD), gains], 1)
    head_w = lax.all_to_all(head_w, hd_axes, 0, 0, tiled=True)
    head_w = pair_gather(head_w, seq_axis)
    for axis in reversed(sh_axes):
        if lax.axis_size(axis) == 2:
            head_w = pair_gather(head_w, axis)
        else:
            head_w = lax.all_gather(head_w, axis, axis=0, tiled=False)
    if small:
        head_w = head_w.reshape(2, 2, 2, 4, 3 * per + 1, HD).transpose(2, 1, 3, 0, 4, 5)
    else:
        head_w = head_w.reshape(count, 16, 3 * per + 1, HD).transpose(1, 0, 2, 3)
    head_w = head_w.reshape(devices, 3 * per + 1, HD)
    gains = head_w[:, -1, : 4 * per].reshape(devices, 4, per).transpose(1, 0, 2)
    gains = gains.reshape(4, width).astype(F32)
    gain_one, bias_one, gain_two, bias_two = gains[0], gains[1], gains[2], gains[3]
    head_w = head_w[:, :-1].reshape(devices, 3, per, HD).transpose(0, 2, 1, 3)
    head_w = head_w.reshape(width, 3 * HD)

    inner_w = w_inner.reshape(per, planes, 8, unit).transpose(2, 0, 1, 3)
    inner_w = lax.all_to_all(inner_w.reshape(8, per, planes * unit), W_AXES, 0, 0, tiled=True)
    inner_w = t_gather(after(inner_w, seen)).reshape(width, planes * unit)
    outer_w = t_gather(w_outer).reshape(planes * unit, width)
    grad_plane = plane_gather(after(cotangent, seen).reshape(rows, width))

    out_w = lax.all_gather(w_out, AXES, axis=0, tiled=True)
    qkv_w = jnp.concatenate([w_query, w_key, w_value], 1)
    qkv_w = lax.all_gather(after(qkv_w, seen), AXES, axis=0, tiled=True)

    normed, _ = norm_stats(seen.reshape(-1, width).astype(F32))
    h1 = (normed * gain_one + bias_one).astype(BF)
    qkv = mm(h1, head_w).astype(BF)
    query = qkv[:, :HD].reshape(16, tok, HD)
    kv = qkv[:, HD:]
    if count == 2:
        kv = jnp.stack([kv, swap(kv, "c")])
        order = jnp.stack([share, 1 - share])
    else:
        kv = lax.all_gather(kv, sh_axes, axis=0, tiled=False)
        order = jnp.arange(count)
    kv = kv.reshape(count, 16, tok, 2 * HD)
    meta = jnp.concatenate([slots, share.reshape(1), order]).astype(jnp.int32)
    out, out_f, lse, q_at, k_at, v_at = attention_forward(
        count, meta, query, kv[..., :HD], kv[..., HD:]
    )

    def to_tokens(v):
        v = lax.all_to_all(v, own_axes, 0, 0, tiled=True)
        n = v.shape[-1] // HD
        if small:
            v = v.reshape(2, 2, 4, tok, n, HD).transpose(1, 3, 4, 0, 2, 5)
        else:
            v = v.reshape(2, 8, tok, n, HD).transpose(0, 2, 3, 1, 4)
        return v.reshape(2, tok, n, 8 * HD)

    mixed = to_tokens(out.reshape(16, tok, HD)).reshape(rows, width)
    flat_in = tokens.reshape(rows, width).astype(F32)
    middle = flat_in + mm(mixed, out_w)
    scaled_two, inverse_two = norm_stats(middle)
    h2 = plane_gather((scaled_two * gain_two + bias_two).astype(BF))

    inner = mm(h2, inner_w)
    bent = jnp.tanh(gelu_coef * (inner + 0.044715 * inner * inner * inner))
    hidden = (0.5 * inner * (1.0 + bent)).astype(BF)
    slope = 0.5 * (1.0 + bent) + 0.5 * inner * (1.0 - bent * bent) * gelu_coef * (
        1.0 + 3.0 * 0.044715 * inner * inner
    )
    grad_inner = (mm_nt(grad_plane, outer_w) * slope).astype(BF)
    grad_h2 = plane_scatter(mm_nt(grad_inner, inner_w))
    grad_outer = mm_tn(hidden, grad_plane).reshape(planes, unit, width)
    grad_outer = t_scatter(grad_outer)
    grad_in = mm_tn(h2, grad_inner).reshape(planes, 8 * per, planes * unit)
    grad_in = t_scatter(grad_in).astype(BF).reshape(8, per, planes * unit)
    result = plane_scatter(mm(hidden, outer_w))

    grad_out = cotangent.reshape(rows, width).astype(F32)
    grad_middle = grad_out + norm_back(grad_h2, scaled_two, inverse_two, gain_two)
    branch = grad_middle.astype(BF)
    go = mm_nt(branch, out_w).astype(BF)
    if small:
        go = go.reshape(2, tok, 2, 4, HD).transpose(2, 0, 3, 1, 4)
    else:
        go = go.reshape(2, tok, 8, HD).transpose(0, 2, 1, 3)
    go = lax.all_to_all(go.reshape(16, tok, HD), own_axes, 0, 0, tiled=True)
    go = go.reshape(16 * tok, HD)

    gq, gk, gv = attention_backward(count, meta, q_at, k_at, v_at, go, out_f, lse)
    gkv = jnp.concatenate([gk, gv], -1)
    if count == 2:
        gkv = gkv[0] + swap(gkv[1].astype(BF), "c").astype(F32)
    else:
        gkv = lax.psum_scatter(gkv, sh_axes, scatter_dimension=0, tiled=False)
    grads = jnp.concatenate([gq, gkv.astype(BF)], -1).reshape(16, tok, 3 * HD)
    grads, result, grad_in, grad_outer = lax.optimization_barrier(
        (grads, result, grad_in, grad_outer)
    )
    back = to_tokens(grads).reshape(rows, 3 * width)
    result = (middle + result).astype(BF)
    grad_in = lax.all_to_all(after(grad_in, back), W_AXES, 0, 0, tiled=True)
    grad_in = grad_in.reshape(8, per, planes, unit).transpose(1, 2, 0, 3)
    grad_in = grad_in.reshape(per, devices * unit).astype(F32)

    head_g = mm_tn(h1, reorder(meta, grads).reshape(16 * tok, 3 * HD))
    head_g = head_g.reshape(tuple(lax.axis_size(a) for a in AXES) + (per, 3 * HD))
    dims = list(AXES)
    for axis in sh_axes[::-1] + (seq_axis,):
        dim = dims.index(axis)
        dims.remove(axis)
        if lax.axis_size(axis) == 2:
            head_g = pair_scatter(head_g, axis, dim)
        else:
            head_g = lax.psum_scatter(head_g, axis, scatter_dimension=dim, tiled=False)
    head_g = head_g.astype(BF).reshape(8, per, 3 * HD)
    head_g = lax.all_to_all(head_g, hd_axes, 0, 0, tiled=True)
    head_g = head_g.reshape(8, per, 3, HD).transpose(2, 1, 0, 3).reshape(3, per, width)
    head_g = head_g.astype(F32)

    grad_out_w = mm_tn(mixed, branch).reshape(planes, 2, 2, 2, per, width)
    grad_out_w = pair_scatter(grad_out_w, "c", 3)
    grad_out_w = pair_scatter(grad_out_w, "y", 2)
    grad_out_w = pair_scatter(grad_out_w, "zl", 1)
    grad_out_w = t_scatter(grad_out_w)

    scaled_one, inverse_one = norm_stats(flat_in)
    grad_h1 = mm_nt(back, qkv_w)
    grad_input = grad_middle + norm_back(grad_h1, scaled_one, inverse_one, gain_one)

    sums = jnp.stack(
        [
            jnp.sum(grad_h1 * scaled_one, 0),
            jnp.sum(grad_h1, 0),
            jnp.sum(grad_h2 * scaled_two, 0),
            jnp.sum(grad_h2, 0),
        ]
    )
    sums = sums.reshape(4, devices, per).transpose(1, 0, 2).reshape(devices, 4 * per)
    sums = lax.all_to_all(sums, AXES, 0, 0, tiled=True)
    sums = jnp.sum(sums, 0).reshape(4, per)
    return (
        result.reshape(seqs, tok, width),
        grad_input.reshape(seqs, tok, width),
        sums[0],
        sums[1],
        head_g[0],
        head_g[1],
        head_g[2],
        grad_out_w,
        sums[2],
        sums[3],
        grad_in,
        grad_outer,
    )


class Arriving:
    def __init__(self, ref, copy):
        self.ref, self.copy = ref, copy
        self.shape, self.dtype = ref.shape, ref.dtype

    def __getitem__(self, index):
        if self.copy is not None:
            self.copy.wait()
            self.copy = None
        return self.ref[index]


class Leaving:
    def __init__(self, ref, target, move):
        self.ref, self.target, self.move, self.pushed = ref, target, move, False
        self.shape, self.dtype = ref.shape, ref.dtype

    def __getitem__(self, index):
        return self.ref[index]

    def __setitem__(self, index, value):
        self.ref[index] = value

    def push(self, rows=None):
        self.pushed = True
        if rows is None:
            self.move(self.ref, self.target)
        else:
            self.move(self.ref.at[rows], self.target.at[rows])


def call(kernel, outs, ins, coords=None, raw=(), save=(), scratch=(), eager=False, name=None):
    hbm = pl.BlockSpec(memory_space=pltpu.HBM)
    outs = [tuple(o) + ("far",) * (3 - len(o)) for o in outs]
    far = [i for i in range(len(ins)) if i not in raw]
    lead = 0 if coords is None else 1
    late = [i for i, o in enumerate(outs) if o[2] == "far"]
    extra = [pltpu.VMEM(ins[i].shape, ins[i].dtype) for i in far]
    extra += [pltpu.VMEM(outs[i][0], outs[i][1]) for i in late]
    extra.append(pltpu.SemaphoreType.DMA((len(far) + 4 * len(late) + len(save),)))
    count_in, count_out = len(ins), len(outs) + len(save)

    def body(*refs):
        front, refs = refs[:lead], refs[lead:]
        got, put = list(refs[:count_in]), list(refs[count_in : count_in + count_out])
        work = refs[count_in + count_out :]
        own, work = work[: len(scratch)], work[len(scratch) :]
        started = []

        def move(source, target):
            copy = pltpu.make_async_copy(source, target, work[-1].at[len(started)])
            copy.start()
            started.append(copy)
            return copy

        for n, i in enumerate(far):
            got[i] = Arriving(work[n], move(got[i], work[n]))
        leaving = []
        for n, i in enumerate(save):
            got[i].copy.wait()
            got[i].copy = None
            leaving.append(move(got[i].ref, put[len(outs) + n]))
        if eager:
            for i in far:
                got[i].copy.wait()
                got[i].copy = None
        inside = put[: len(outs)]
        for n, i in enumerate(late):
            inside[i] = Leaving(
                work[len(far) + n], put[i], lambda a, b: leaving.append(move(a, b))
            )
        kernel(*front, *got, *inside, *own)
        for i in late:
            if not inside[i].pushed:
                inside[i].push()
        for i in far:
            if got[i].copy is not None:
                got[i].copy.wait()
        for copy in leaving:
            copy.wait()

    specs = [hbm] * len(ins)
    if coords is not None:
        specs = [pl.BlockSpec(memory_space=pltpu.SMEM)] + specs
    saved = [jax.ShapeDtypeStruct(ins[i].shape, ins[i].dtype) for i in save]
    return pl.pallas_call(
        body,
        in_specs=specs,
        out_specs=[hbm] * count_out,
        out_shape=[jax.ShapeDtypeStruct(o[0], o[1]) for o in outs] + saved,
        scratch_shapes=list(scratch) + extra,
        cost_estimate=pl.CostEstimate(flops=0, bytes_accessed=0, transcendentals=0),
        compiler_params=pltpu.CompilerParams(vmem_limit_bytes=58 << 20),
        name=name,
    )(*([] if coords is None else [coords]), *ins)


def aligned(index, size):
    if isinstance(index, int):
        return pl.ds(index * size, size)
    return pl.ds(pl.multiple_of(index * size, size), size)


def pack_kernel(wq, wk, wv, g1, b1, g2, b2, w_inner, head, inner):
    per = wq.shape[0]
    gains = jnp.concatenate([g1[...], b1[...], g2[...], b2[...]], 1)
    for d in range(16):
        cols = pl.ds(((d >> 3) * 4 + (d & 3)) * HD, HD)
        for n, w in enumerate((wq, wk, wv)):
            head[d, pl.ds(n * per, per), :] = w[:, cols]
        head[d, pl.ds(3 * per, 16), :] = jnp.broadcast_to(gains, (16, HD))
    for w in range(8):
        for t in range(4):
            p = (w >> 2) * 16 + t * 4 + (w & 3)
            inner[w, :, pl.ds(t * HD, HD)] = w_inner[:, pl.ds(p * HD, HD)]


def norm_of(values):
    centered = values - jnp.mean(values, -1, keepdims=True)
    inverse = lax.rsqrt(jnp.mean(centered * centered, -1, keepdims=True) + eps_norm)
    return centered * inverse, inverse


def qkv_kernel(at, *refs):
    blocks, pieces = refs[:8], refs[8:10]
    h1, query, kv, gains, weights = refs[10:]
    x, za, zl, y, c = (at[i] for i in range(5))
    width = h1.shape[1]
    per = width // 32
    got = jnp.concatenate([p[d, 3 * per : 3 * per + 1, :] for p in pieces for d in range(16)], 0)
    line = lax.broadcasted_iota(jnp.int32, (32, width), 0)
    lane = lax.broadcasted_iota(jnp.int32, (32, width), 1)
    owner = (line & 15) * 2 + (c ^ (line >> 4))
    mine = lax.shift_right_logical(lane, 5) == owner
    source = lax.broadcasted_iota(jnp.int32, (HD, width), 0)
    target = lax.broadcasted_iota(jnp.int32, (HD, width), 1)
    for k in range(4):
        spread = jnp.where(source == k * per + (target & (per - 1)), 1.0, 0.0).astype(BF)
        gains[k : k + 1, :] = jnp.sum(jnp.where(mine, mm(got, spread), 0.0), 0, keepdims=True)
    gain, bias = gains[0:1, :], gains[1:2, :]
    for n, block in enumerate(blocks):
        xx, zz, yy = x ^ (n >> 2), zl ^ (n >> 1 & 1), y ^ (n & 1)
        for s in range(2):
            j = xx * 8 + (za ^ s) * 4 + zz * 2 + yy
            normed, _ = norm_of(block[s].astype(F32))
            h1[aligned(j, 64), :] = (normed * gain + bias).astype(BF)
    h1.push()
    for n, piece in enumerate(pieces):
        for d in range(16):
            for i in range(3):
                weights[aligned(2 * d + (c ^ n), per), pl.ds(i * HD, HD)] = piece[
                    d, pl.ds(i * per, per), :
                ]
    weights.push()
    for t in range(h1.shape[0] // TILE):
        rows = pl.ds(t * TILE, TILE)
        out = mm(h1[rows, :], weights[...]).astype(BF)
        query[rows, :] = out[:, :HD]
        kv[rows, :] = out[:, HD:]
        query.push(rows)
        kv.push(rows)


def causal(q_share, k_share):
    rows = lax.broadcasted_iota(jnp.int32, (TILE, TILE), 0)
    cols = lax.broadcasted_iota(jnp.int32, (TILE, TILE), 1)
    q_pos = (lax.shift_right_logical(rows, 6) * 2 + q_share) * 64 + (rows & 63)
    k_pos = (lax.shift_right_logical(cols, 6) * 2 + k_share) * 64 + (cols & 63)
    return k_pos <= q_pos


def fine_forward_kernel(at, query, own, other, out, out_f, lse, s_ref):
    tiles = query.shape[0] // TILE
    c = at[4]
    both = (own, other)

    def tile(t, carry):
        rows = aligned(t, TILE)
        q = query[rows, :]

        def score(u, top, masked):
            for n in range(2):
                s = mm_nt(q, both[n][aligned(u, TILE), pl.ds(0, HD)]) * SCALE
                if masked:
                    s = jnp.where(causal(c, c if n == 0 else 1 - c), s, MASKED)
                s_ref[u * 2 + n] = s
                top = jnp.maximum(top, jnp.max(s, -1, keepdims=True))
            return top

        top = jnp.full((TILE, 1), MASKED, F32)
        for u in range(t + 1):
            top = score(u, top, u == t)

        def expo(u, total):
            for n in range(2):
                p = jnp.exp(s_ref[u * 2 + n] - top)
                s_ref[u * 2 + n] = p
                total = total + jnp.sum(p, -1, keepdims=True)
            return total

        total = jnp.zeros((TILE, 1), F32)
        for u in range(t + 1):
            total = expo(u, total)
        inverse = 1.0 / total

        def weigh(u, acc):
            for n in range(2):
                p = (s_ref[u * 2 + n] * inverse).astype(BF)
                acc = acc + mm(p, both[n][aligned(u, TILE), pl.ds(HD, HD)])
            return acc

        acc = jnp.zeros((TILE, HD), F32)
        for u in range(t + 1):
            acc = weigh(u, acc)
        out_f[rows, :] = acc
        out[pl.ds(t * (TILE // 64), TILE // 64)] = acc.astype(BF).reshape(TILE // 64, 64, HD)
        lse[rows, :] = jnp.broadcast_to(top + jnp.log(total), (TILE, HD))
        out.push(pl.ds(t * (TILE // 64), TILE // 64))
        out_f.push(rows)
        lse.push(rows)
        return carry

    for t in range(tiles):
        tile(t, 0)


def place_w_out(at, pieces, out_w, sems):
    x, za, zl, y, c = (at[i] for i in range(5))
    copies = []
    for n, piece in enumerate(pieces):
        side = (zl ^ (n & 1)) * 4 + (y ^ (n >> 1 & 1)) * 2 + (c ^ (n >> 2))
        for i in range(4):
            p = (x ^ (i >> 1)) * 16 + (za ^ (i & 1)) * 8 + side
            copies.append(
                pltpu.make_async_copy(
                    piece.at[i], out_w.at[aligned(p, piece.shape[1]), :], sems.at[len(copies)]
                )
            )
            copies[-1].start()
    return copies


def middle_kernel(at, got, tokens, gains, *refs):
    pieces, (mixed, middle, scaled, inverse, h2, out_w, sems) = refs[:8], refs[8:]
    copies = place_w_out(at, pieces, out_w, sems)
    rows, width = middle.shape
    tok = rows // 2
    for s in range(16):
        head = (s >> 3) * 4 + (s & 3)
        mixed[pl.ds((s >> 2 & 1) * tok, tok), pl.ds(head * HD, HD)] = got[s]
    for s in range(2):
        middle[pl.ds(s * tok, tok), :] = tokens[s].astype(F32)
    for copy in copies:
        copy.wait()
    mixed.push()
    middle[...] += mm(mixed[...], out_w[...])
    middle.push()
    normed, inv = norm_of(middle[...])
    scaled[...] = normed
    inverse[...] = jnp.broadcast_to(inv, (rows, HD))
    h2[...] = (normed * gains[2:3, :] + gains[3:4, :]).astype(BF)


def inner_kernel(at, *refs):
    h2_parts, cot_parts, in_parts, out_parts = refs[:10], refs[10:20], refs[20:24], refs[24:28]
    h2_out, cot_out, outer_out, hidden, grad_inner, keep, send = refs[28:35]
    h2, cot, w_in, w_outer, sems = refs[35:]
    za, zl = at[1], at[2]
    copies = []

    def move(source, target):
        copy = pltpu.make_async_copy(source, target, sems.at[len(copies)])
        copy.start()
        copies.append(copy)

    for n in range(4):
        t = (za ^ (n >> 1)) * 2 + (zl ^ (n & 1))
        for i in range(2):
            rows = in_parts[n].shape[1]
            move(in_parts[n].at[i], w_in.at[aligned(i * 4 + t, rows), :])
    for n in range(4):
        t = (za ^ (n >> 1)) * 2 + (zl ^ (n & 1))
        move(out_parts[n], w_outer.at[aligned(t, out_parts[n].shape[0]), :])
    row = 0
    for part in cot_parts:
        move(part, cot.at[pl.ds(row, part.shape[0]), :])
        row += part.shape[0]
    row = 0
    for part in h2_parts:
        h2[pl.ds(row, part.shape[0]), :] = part[...]
        row += part.shape[0]
    for copy in copies[:8]:
        copy.wait()
    first = mm(h2[pl.ds(0, TILE), :], w_in[...])
    for copy in copies[8:22]:
        copy.wait()
    arrived = 22
    move(h2, h2_out)
    move(cot, cot_out)
    move(w_outer, outer_out)
    half = h2.shape[0] // 2

    def tile(t, carry):
        rows = aligned(t, TILE)
        u = first if t == 0 else mm(h2[rows, :], w_in[...])
        squared = u * u
        bent = jnp.tanh(gelu_coef * (u + 0.044715 * squared * u))
        hidden[rows, :] = (0.5 * u * (1.0 + bent)).astype(BF)
        slope = 0.5 * (1.0 + bent) + 0.5 * u * (1.0 - bent * bent) * gelu_coef * (
            1.0 + 3.0 * 0.044715 * squared
        )
        grad = (mm_nt(cot[rows, :], w_outer[...]) * slope).astype(BF)
        grad_inner[rows, :] = grad
        hidden.push(rows)
        grad_inner.push(rows)
        return mm_nt(grad, w_in[...]), carry

    for out, first_tile in ((keep, 0), (send, half // TILE)):
        for t in range(2):
            rows = pl.ds(t * TILE, TILE)
            out[rows, :] = tile(first_tile + t, 0)[0].astype(BF)
            out.push(rows)
    for copy in copies[arrived:]:
        copy.wait()


def others_of(at):
    za, zl = at[1], at[2]
    return za * 2 + zl, za * 2 + 1 - zl, 2 - 2 * za + zl, 3 - 2 * za - zl


def inner_grad_kernel(at, h2, grad_inner, own, to_l, to_a, to_la, big):
    big[...] = mm_tn(h2[...], grad_inner[...])
    n = own.shape[0] // 2
    for t, out in zip(others_of(at), (own, to_l, to_a, to_la)):
        for i in range(2):
            out[pl.ds(i * n, n), :] = big[aligned(i * 4 + t, n), :].astype(out.dtype)


def outer_grad_kernel(at, hidden, cot, w_outer, own, to_l, to_a, to_la, keep, send, big):
    half = keep.shape[0]
    send[...] = mm(hidden[pl.ds(half, half), :], w_outer[...]).astype(BF)
    keep[...] = mm(hidden[pl.ds(0, half), :], w_outer[...])
    big[...] = mm_tn(hidden[...], cot[...])
    n = own.shape[0]
    for t, out in zip(others_of(at), (own, to_l, to_a, to_la)):
        out[...] = big[aligned(t, n), :].astype(out.dtype)


def payload_kernel(at, head_keep, head_got, own, other, payload):
    zl = at[2]
    m = head_keep.shape[1] // 4
    n = own.shape[1]
    wide = head_keep.shape[2]
    for d in range(8):
        rows = pl.ds((d & 3) * m, m)
        payload[d, pl.ds(0, m), pl.ds(0, wide)] = (
            head_keep[d >> 2, rows, :] + head_got[d >> 2, rows, :].astype(F32)
        ).astype(BF)
        payload[d, pl.ds(0, m), pl.ds(wide, HD)] = jnp.zeros((m, HD), BF)
        for s, part in enumerate((own, other)):
            here = pl.ds(m + s * n, n)

            @pl.when(zl == (d >> 1 & 1))
            def _():
                payload[d, here, :] = part[(d >> 2) * 2 + (d & 1)]

            @pl.when(zl != (d >> 1 & 1))
            def _():
                payload[d, here, :] = jnp.zeros(part.shape[1:], BF)


def last_kernel(at, got, query, key, value, sum_a, sum_b, sum_c, sum_d, inner_g):
    zl, c = at[2], at[4]
    per = query.shape[0]
    m = per + 16
    lanes = got.shape[2]
    total = got[0, pl.ds(per, 16), pl.ds(0, HD)].astype(F32)
    for h in range(8):
        for n, out in enumerate((query, key, value)):
            out[:, pl.ds(h * HD, HD)] = got[h, pl.ds(0, per), pl.ds(n * HD, HD)].astype(F32)
        if h:
            total = total + got[h, pl.ds(per, 16), pl.ds(0, HD)].astype(F32)
    for n, out in enumerate((sum_a, sum_b, sum_c, sum_d)):
        out[...] = total[0:1, n * per : (n + 1) * per]
    for w in range(4):
        for s in range(2):
            source = (w >> 1) * 4 + zl * 2 + (w & 1)
            part = got[source, pl.ds(m + s * per, per), :].astype(F32)
            side = (w >> 1) * 16 + (w & 1) * 2 + (c if s == 0 else 1 - c)
            for t in range(lanes // HD):
                inner_g[:, aligned(t * 4 + side, HD)] = part[:, t * HD : (t + 1) * HD]


def branch_kernel(at, parts, scaled, inverse, gains, cot, *refs):
    pieces, (grad_middle, branch, go, sums, out_w, sems) = refs[:8], refs[8:]
    copies = place_w_out(at, pieces, out_w, sems)
    rows, width = scaled.shape
    tok = rows // 2
    grad = parts[0].astype(F32)
    for n in range(1, 4):
        grad = grad + parts[n].astype(F32)
    n2 = scaled[...]
    sums[0:1, :] = jnp.sum(grad * n2, 0, keepdims=True)
    sums[1:2, :] = jnp.sum(grad, 0, keepdims=True)
    a = grad * gains[2:3, :]
    grad = inverse[:, 0:1] * (
        a - jnp.mean(a, -1, keepdims=True) - n2 * jnp.mean(a * n2, -1, keepdims=True)
    )
    for s in range(2):
        part = pl.ds(s * tok, tok)
        grad_middle[part, :] = cot[s].astype(F32) + grad[s * tok : (s + 1) * tok]
    grad_middle.push()
    branch[...] = grad_middle[...].astype(BF)
    branch.push()
    for copy in copies:
        copy.wait()
    out = mm_nt(branch[...], out_w[...]).astype(BF)
    for s in range(16):
        head = (s >> 3) * 4 + (s & 3)
        seq = s >> 2 & 1
        go[s] = out[seq * tok : (seq + 1) * tok, head * HD : (head + 1) * HD]


def fine_backward_kernel(at, query, own, other, go_ref, out_f, lse_ref, gq_ref, keep, send, acc):
    rows_all = query.shape[0]
    tiles = rows_all // TILE
    c = at[4]
    both = (own, other)
    keep[...] = jnp.zeros(keep.shape, keep.dtype)
    acc[...] = jnp.zeros_like(acc)
    totals = (keep, acc)

    def tile(t, carry):
        rows = aligned(t, TILE)
        q = query[rows, :]
        go = go_ref[pl.ds(t * (TILE // 64), TILE // 64)].reshape(TILE, HD)
        delta = jnp.sum(go.astype(F32) * out_f[rows, :], -1, keepdims=True)
        lse = lse_ref[rows, 0:1]

        def one(u, gq, masked):
            cols = aligned(u, TILE)
            for n in range(2):
                kk = both[n][cols, pl.ds(0, HD)]
                p = jnp.exp(mm_nt(q, kk) * SCALE - lse)
                if masked:
                    p = jnp.where(causal(c, c if n == 0 else 1 - c), p, 0.0)
                totals[n][cols, pl.ds(HD, HD)] += mm_tn(p.astype(BF), go)
                ds = (p * (mm_nt(go, both[n][cols, pl.ds(HD, HD)]) - delta)).astype(BF)
                totals[n][cols, pl.ds(0, HD)] += mm_tn(ds, q)
                gq = gq + mm(ds, kk)
            return gq

        gq = jnp.zeros((TILE, HD), F32)
        for u in range(t + 1):
            gq = one(u, gq, u == t)
        gq_ref[rows, :] = (gq * SCALE).astype(BF)
        gq_ref.push(rows)
        return carry

    for t in range(tiles):
        tile(t, 0)
    send[:, :HD] = (acc[:, :HD] * SCALE).astype(BF)
    send[:, HD:] = acc[:, HD:].astype(BF)
    send.push()
    keep[:, :HD] = keep[:, :HD] * SCALE


def partial_kernel(at, *refs):
    blocks, (gq, keep, got, weights) = refs[:8], refs[8:12]
    grads, parts, sums, tokens, sems = refs[12:]
    x, za, zl, y = (at[i] for i in range(4))
    copies = []
    for n in range(8):
        for s in range(2):
            j = (x ^ (n >> 2)) * 8 + (za ^ s) * 4 + (zl ^ (n >> 1 & 1)) * 2 + (y ^ (n & 1))
            copies.append(
                pltpu.make_async_copy(
                    blocks[n].at[s], tokens.at[aligned(j, 64), :], sems.at[len(copies)]
                )
            )
            copies[-1].start()
    for copy in copies:
        copy.wait()
    tiles = gq.shape[0] // TILE
    for t in range(tiles):
        rows = pl.ds(t * TILE, TILE)
        grads[rows, pl.ds(0, HD)] = gq[rows, :]
        grads[rows, pl.ds(HD, 2 * HD)] = (keep[rows, :] + got[rows, :].astype(F32)).astype(BF)
        part = mm_nt(grads[rows, :], weights[...])
        normed, _ = norm_of(tokens[rows, :].astype(F32))
        one = jnp.sum(part * normed, 0, keepdims=True)
        two = jnp.sum(part, 0, keepdims=True)
        if t == 0:
            sums[0:1, :] = one
            sums[1:2, :] = two
        else:
            sums[0:1, :] += one
            sums[1:2, :] += two
        for i in range(4):
            parts[(t >> 1) * 4 + i, za ^ (t & 1)] = part[i * 64 : (i + 1) * 64].astype(BF)
        grads.push(rows)
        if t & 1:
            parts.push(pl.ds((t >> 1) * 4, 4))


def total_kernel(parts, keep, send):
    total = parts[0, 0].astype(F32)
    other = parts[0, 1].astype(F32)
    for n in range(1, 8):
        total = total + parts[n, 0].astype(F32)
        other = other + parts[n, 1].astype(F32)
    keep[...] = total
    send[...] = other.astype(BF)


def head_grad_kernel(at, left, right, sums, keep, send, big):
    c = at[4]
    per = left.shape[1] // 32
    big[...] = mm_tn(left[...], right[...])
    spare = keep.shape[2] - sums.shape[1]
    for q in range(16):
        keep[q, pl.ds(0, per), :] = big[aligned(2 * q + c, per), :]
        send[q, pl.ds(0, per), :] = big[aligned(2 * q + 1 - c, per), :].astype(BF)
    pad = jnp.zeros((16, spare), F32)
    for q in range(16):
        pair = jnp.concatenate([sums[2 * q : 2 * q + 2, :], pad[:2]], 1)
        mine = jnp.where(c == 0, pair[0:1], pair[1:2])
        other = jnp.where(c == 0, pair[1:2], pair[0:1])
        keep[q, pl.ds(per, 16), :] = jnp.broadcast_to(mine, (16, keep.shape[2]))
        send[q, pl.ds(per, 16), :] = jnp.broadcast_to(other, (16, keep.shape[2])).astype(BF)


def core_grad_kernel(at, left, right, keep, send, big):
    c = at[4]
    per = left.shape[1] // 32
    big[...] = mm_tn(left[...], right[...])
    for q in range(16):
        rows = pl.ds(q * per, per)
        keep[rows, :] = big[aligned(2 * q + c, per), :]
        send[rows, :] = big[aligned(2 * q + 1 - c, per), :].astype(BF)


def input_kernel(at, keep, got, tokens, grad_middle, gains, grad_tokens):
    za = at[1]
    tok = tokens.shape[1]
    for n in range(2):
        seq = za if n == 0 else 1 - za
        part = keep[...] if n == 0 else got[...].astype(F32)
        n1, inv = norm_of(tokens[seq].astype(F32))
        a = part * gains[0:1, :]
        grad_tokens[seq] = grad_middle[aligned(seq, tok), :] + inv * (
            a - jnp.mean(a, -1, keepdims=True) - n1 * jnp.mean(a * n1, -1, keepdims=True)
        )


def far_kernel(keep, got, own, on_z, on_y, far_a, far_b):
    n = own.shape[0]
    for i, out in enumerate((own, on_z, on_y)):
        rows = pl.ds(i * n, n)
        out[...] = keep[rows, :] + got[rows, :].astype(F32)
    for i, out in enumerate((far_a, far_b)):
        rows = pl.ds(3 * n + i * (n // 2), n // 2)
        out[...] = (keep[rows, :] + got[rows, :].astype(F32)).astype(BF)


def near_kernel(on_z, on_y, got_a, got_b, send_z, send_y):
    n = got_a.shape[0]
    first, second = pl.ds(0, n), pl.ds(n, n)
    send_z[first, :] = (on_z[first, :] + got_a[...].astype(F32)).astype(BF)
    send_z[second, :] = on_z[second, :].astype(BF)
    send_y[first, :] = on_y[first, :].astype(BF)
    send_y[second, :] = (on_y[second, :] + got_b[...].astype(F32)).astype(BF)


def result_sum_kernel(middle, own, got_z, got_y, out):
    out[...] = (
        middle[...] + own[...] + got_z[...].astype(F32) + got_y[...].astype(F32)
    ).astype(BF)


def fold_kernel(at, keep, got, parts):
    x, y = at[0], at[3]
    rows = parts.shape[1]
    for n in range(4):
        here = pl.ds(n * rows, rows)
        z = x ^ (1 if n in (1, 3) else 0)
        w = y ^ (1 if n in (2, 3) else 0)
        parts[z * 2 + w] = (keep[here, :].astype(F32) + got[here, :].astype(F32)).astype(BF)


def stage(*values):
    return lax.optimization_barrier(values)


def grow(v, axis):
    return jnp.concatenate([v, swap(v, axis)], 0)


def half_swap(v, axis):
    return swap(pick(v, 1 - lax.axis_index(axis)), axis)


def fine_layer(
    tokens,
    cotangent,
    ln1_gain,
    ln1_bias,
    w_query,
    w_key,
    w_value,
    w_out,
    ln2_gain,
    ln2_bias,
    w_inner,
    w_outer,
):
    seqs, tok, width = tokens.shape
    rows = seqs * tok
    half = rows // 2
    per = w_query.shape[0]
    unit = w_outer.shape[0]
    hidden_units = 4 * unit
    all_rows = 8 * rows
    coords = jnp.stack([lax.axis_index(a) for a in ("x", "za", "zl", "y", "c")]).astype(jnp.int32)
    x, za = lax.axis_index("x"), lax.axis_index("za")
    cube, owners = ("x", "zl", "y"), ("x", "za", "zl", "y")
    cot = cotangent.reshape(rows, width)

    def split(axis, keep, got, shape):
        keep, got = keep.reshape(shape), got.reshape(shape)
        i = lax.axis_index(axis)
        mine = pick(keep, i, 1) + pick(got, i, 1).astype(F32)
        return mine, (pick(keep, 1 - i, 1) + pick(got, 1 - i, 1).astype(F32)).astype(BF)

    head_w, inner_w = call(
        pack_kernel,
        [((16, 3 * per + 16, HD), BF), ((8, per, hidden_units), BF)],
        [w_query, w_key, w_value]
        + [g.reshape(1, per) for g in (ln1_gain, ln1_bias, ln2_gain, ln2_bias)]
        + [w_inner],
        name="pack",
    )
    moved, head_w, inner_w, w_out, w_outer = stage(
        swap(pick(tokens, 1 - za), "za"), head_w, inner_w, w_out, w_outer
    )
    block = jnp.stack([pick(tokens, za), moved])
    on_x, on_z, on_y, head_w = stage(
        swap(block, "x"), swap(block, "zl"), swap(block, "y"), head_w
    )
    on_xz, on_xy, on_zy, on_xyz, head_w, w_out_z = stage(
        swap(on_x, "zl"),
        swap(on_y, "x"),
        swap(on_z, "y"),
        lax.ppermute(block, cube, [(i, 7 - i) for i in range(8)]),
        lax.all_to_all(head_w, owners, 0, 0, tiled=True),
        swap(after(w_out, on_x), "za"),
    )
    head_c, w_outer, inner_w, w_out_z = stage(swap(head_w, "c"), w_outer, inner_w, w_out_z)
    blocks = [block, on_y, on_z, on_zy, on_x, on_xy, on_xz, on_xyz]
    out_w = jnp.stack([w_out, w_out_z])
    h1, query, kv, gains, head_w = call(
        qkv_kernel,
        [
            ((16 * tok, width), BF),
            ((16 * tok, HD), BF),
            ((16 * tok, 2 * HD), BF),
            ((8, width), F32),
            ((width, 3 * HD), BF),
        ],
        blocks + [head_w, head_c],
        coords,
        name="qkv",
    )
    kv, query, out_x, outer_a, outer_l, inner_w = stage(
        kv,
        query,
        swap(out_w, "x"),
        swap(w_outer, "za"),
        swap(w_outer, "zl"),
        lax.all_to_all(inner_w, ("x", "y", "c"), 0, 0, tiled=True),
    )
    out_w = jnp.concatenate([out_w, out_x], 0)
    kv_other, out_w, inner_w = stage(swap(kv, "c"), out_w, inner_w)
    out, out_f, lse, query, kv, kv_other = call(
        fine_forward_kernel,
        [((16, tok, HD), BF), ((16 * tok, HD), F32), ((16 * tok, HD), F32)],
        [query, kv, kv_other],
        coords,
        save=(0, 1, 2),
        scratch=[pltpu.VMEM((2 * 16 * tok // TILE, TILE, TILE), F32)],
        name="attention_forward",
    )
    out, out_z, out_y, inner_a, inner_l, cot = stage(
        out,
        swap(out_w, "zl"),
        swap(out_w, "y"),
        swap(inner_w, "za"),
        swap(inner_w, "zl"),
        cot,
    )
    mixed, cot_z, cot_y, cot_c, out_zy, outer_la, inner_la, *out_c = stage(
        lax.all_to_all(out, owners, 0, 0, tiled=True),
        swap(cot, "x"),
        swap(cot, "y"),
        swap(cot, "c"),
        swap(out_z, "y"),
        swap(outer_a, "zl"),
        swap(inner_a, "zl"),
        swap(out_w, "c"),
        swap(out_z, "c"),
        swap(out_y, "c"),
    )
    (out_zyc,) = stage(swap(out_zy, "c"))
    pieces = [out_w, out_z, out_y, out_zy] + out_c + [out_zyc]
    mixed, middle, scaled, inverse, h2 = call(
        middle_kernel,
        [
            ((rows, width), BF),
            ((rows, width), F32),
            ((rows, width), F32),
            ((rows, HD), F32),
            ((rows, width), BF),
        ],
        [mixed, tokens, gains] + pieces,
        coords,
        raw=range(3, 11),
        scratch=[pltpu.VMEM((width, width), BF), pltpu.SemaphoreType.DMA((32,))],
        name="middle",
    )
    cot_z, cot_y = after(cot_z, h2), after(cot_y, h2)
    h2_z, h2_y, h2_c, cot_a, cot_b, cot_zc, cot_yc = stage(
        swap(h2, "x"),
        swap(h2, "y"),
        swap(h2, "c"),
        swap(cot_z[:half], "y"),
        swap(cot_y[half:], "x"),
        swap(cot_z, "c"),
        swap(cot_y, "c"),
    )
    h2_a, h2_b, h2_zc, h2_yc, cot_ac, cot_bc = stage(
        swap(h2_z[:half], "y"),
        swap(h2_y[half:], "x"),
        swap(h2_z, "c"),
        swap(h2_y, "c"),
        swap(cot_a, "c"),
        swap(cot_b, "c"),
    )
    h2_ac, h2_bc = stage(swap(h2_a, "c"), swap(h2_b, "c"))
    h2_all, cot_all, outer_w, hidden, grad_inner, keep, send = call(
        inner_kernel,
        [
            ((all_rows, width), BF, "raw"),
            ((all_rows, width), BF, "raw"),
            ((hidden_units, width), BF, "raw"),
            ((all_rows, hidden_units), BF),
            ((all_rows, hidden_units), BF),
            ((all_rows // 2, width), BF),
            ((all_rows // 2, width), BF),
        ],
        [h2, h2_z, h2_y, h2_a, h2_b, h2_c, h2_zc, h2_yc, h2_ac, h2_bc]
        + [cot, cot_z, cot_y, cot_a, cot_b, cot_c, cot_zc, cot_yc, cot_ac, cot_bc]
        + [p.reshape(2, 4 * per, hidden_units) for p in (inner_w, inner_l, inner_a, inner_la)]
        + [w_outer, outer_l, outer_a, outer_la],
        coords,
        raw=range(10, 28),
        scratch=[
            pltpu.VMEM((all_rows, width), BF),
            pltpu.VMEM((all_rows, width), BF),
            pltpu.VMEM((width, hidden_units), BF),
            pltpu.VMEM((hidden_units, width), BF),
            pltpu.SemaphoreType.DMA((25,)),
        ],
        name="inner",
    )

    (got,) = stage(swap(send, "c"))
    (parts,) = call(
        fold_kernel, [((4, rows, width), BF)], [keep, got], coords, name="fold"
    )
    n_in, n_out = 8 * per, unit
    inner_g, in_l, in_a, in_la = call(
        inner_grad_kernel,
        [((n_in, hidden_units), F32)] + [((n_in, hidden_units), BF)] * 3,
        [h2_all, grad_inner],
        coords,
        scratch=[pltpu.VMEM((width, hidden_units), F32)],
        name="inner_grad",
    )
    parts, inner_g, in_l, in_a, in_la = stage(parts, inner_g, in_l, in_a, in_la)
    outer_g, outer_l, outer_a, outer_la, res_keep, res_send = call(
        outer_grad_kernel,
        [((n_out, width), F32)]
        + [((n_out, width), BF)] * 3
        + [((all_rows // 2, width), F32), ((all_rows // 2, width), BF)],
        [after(hidden, in_l), cot_all, outer_w],
        coords,
        scratch=[pltpu.VMEM((hidden_units, width), F32)],
        name="outer_grad",
    )
    parts, in_l, in_a, outer_g, outer_l, outer_a, outer_la, res_keep, res_send, in_la = stage(
        lax.all_to_all(parts, ("x", "y"), 0, 0, tiled=True),
        swap(in_l, "zl"),
        swap(in_a, "za"),
        outer_g,
        outer_l,
        outer_a,
        outer_la,
        res_keep,
        res_send,
        in_la,
    )
    grad_middle, branch, go, sums_two = call(
        branch_kernel,
        [
            ((rows, width), F32),
            ((rows, width), BF),
            ((16, tok, HD), BF),
            ((2, width), F32),
        ],
        [parts, scaled, inverse, gains, cotangent] + pieces,
        coords,
        raw=range(5, 13),
        scratch=[pltpu.VMEM((width, width), BF), pltpu.SemaphoreType.DMA((32,))],
        name="branch",
    )
    go, branch, res_got, outer_l, outer_a = stage(
        go, branch, swap(res_send, "c"), outer_l, outer_a
    )
    res = (res_keep + res_got.astype(F32)).reshape(4, rows, width)
    far_a, far_b = res[3, :half].astype(BF), res[3, half:].astype(BF)
    out_keep, out_send = call(
        core_grad_kernel,
        [((width // 2, width), F32), ((width // 2, width), BF)],
        [mixed, branch],
        coords,
        scratch=[pltpu.VMEM((width, width), F32)],
        name="out_grad",
    )
    diagonal = [(i, 3 - i) for i in range(4)]
    go, outer_l, outer_a, in_la, outer_la, out_keep, out_send, res, far_a, far_b = stage(
        lax.all_to_all(go, owners, 0, 0, tiled=True),
        swap(outer_l, "zl"),
        swap(outer_a, "za"),
        in_la,
        outer_la,
        out_keep,
        out_send,
        res,
        far_a,
        far_b,
    )
    gq, keep, send = call(
        fine_backward_kernel,
        [((16 * tok, HD), BF), ((16 * tok, 2 * HD), F32), ((16 * tok, 2 * HD), BF)],
        [query, kv, kv_other, go, out_f, lse],
        coords,
        scratch=[pltpu.VMEM((16 * tok, 2 * HD), F32)],
        name="attention_backward",
    )
    gq, keep, send, got_a, got_b, out_got, in_la = stage(
        gq,
        keep,
        send,
        swap(far_a, "y"),
        swap(far_b, "x"),
        swap(out_send, "c"),
        lax.ppermute(in_la, ("za", "zl"), diagonal),
    )
    out_keep, out_send = split("x", out_keep, out_got, (1, 2, 8 * per, width))
    got, out_keep, out_send, outer_la = stage(swap(send, "c"), out_keep, out_send, outer_la)
    grads, parts, sums = call(
        partial_kernel,
        [
            ((16 * tok, 3 * HD), BF),
            ((8, 2, tok, width), BF),
            ((2, width), F32),
        ],
        blocks + [gq, keep, got, head_w],
        coords,
        raw=range(8),
        scratch=[pltpu.VMEM((16 * tok, width), BF), pltpu.SemaphoreType.DMA((16,))],
        name="partial",
    )
    grads, parts, sums, out_keep, out_got, outer_la = stage(
        grads,
        parts,
        sums,
        out_keep,
        swap(out_send, "x"),
        lax.ppermute(outer_la, ("za", "zl"), diagonal),
    )
    parts = lax.all_to_all(parts, cube, 0, 0, tiled=True)
    sums = jnp.concatenate([sums, sums_two], 0)
    sums = sums.reshape(4, 32, per).transpose(1, 0, 2).reshape(32, 4 * per)
    head_keep, head_send = call(
        head_grad_kernel,
        [((16, per + 16, 3 * HD), F32), ((16, per + 16, 3 * HD), BF)],
        [h1, grads, sums],
        coords,
        scratch=[pltpu.VMEM((width, 3 * HD), F32)],
        name="head_grad",
    )
    head_keep, head_send = stage(head_keep, head_send)
    out_keep, out_send = split(
        "y", out_keep, after(out_got, head_send), (4, 2, per, width)
    )
    inner_g = inner_g + after(in_l, head_send).astype(F32) + in_a.astype(F32) + in_la.astype(F32)
    inner_g = inner_g.astype(BF).reshape(4, 2, per, hidden_units)
    got_a = after(got_a, head_send)
    res_z = jnp.concatenate([res[1, :half] + got_a.astype(F32), res[1, half:]], 0).astype(BF)
    res_y = jnp.concatenate([res[2, :half], res[2, half:] + got_b.astype(F32)], 0).astype(BF)
    inner_own = pick(inner_g, lax.axis_index("c"), 1)
    inner_send = pick(inner_g, 1 - lax.axis_index("c"), 1)
    head_keep, head_got, out_keep, out_send, inner_own, inner_send, res_z, res_y = stage(
        head_keep, swap(head_send, "c"), out_keep, out_send, inner_own, inner_send, res_z, res_y
    )
    head_keep, head_send = split("za", head_keep, head_got, (2, 2, 4 * (per + 16), 3 * HD))
    head_keep, head_send, out_send = stage(head_keep, head_send, out_send)
    outer_g = (
        outer_g
        + after(outer_l, head_send).astype(F32)
        + outer_a.astype(F32)
        + outer_la.astype(F32)
    )
    head_keep, head_got, out_keep, out_got, inner_got, got_z, res_y, outer_g = stage(
        head_keep,
        swap(head_send, "za"),
        out_keep,
        swap(out_send, "y"),
        swap(inner_send, "c"),
        swap(res_z, "x"),
        res_y,
        outer_g,
    )
    parts, head_keep, head_got, inner_own, inner_got = stage(
        parts, head_keep, head_got, inner_own, inner_got
    )
    total, send = call(
        total_kernel, [((tok, width), F32), ((tok, width), BF)], [parts], name="total"
    )
    total, send, head_keep, head_got, inner_own, inner_got, out_got, res_y = stage(
        total, send, head_keep, head_got, inner_own, inner_got, out_got, res_y
    )
    (payload,) = call(
        payload_kernel,
        [((8, 3 * per + 16, hidden_units), BF)],
        [head_keep, head_got, inner_own, inner_got],
        coords,
        eager=True,
        name="payload",
    )
    out_keep, out_send = split("za", out_keep, out_got, (1, 2, 2 * per, width))
    got, payload, out_keep, out_send, got_y = stage(
        swap(send, "za"), payload, out_keep, out_send, swap(res_y, "y")
    )
    (grad_tokens,) = call(
        input_kernel,
        [((seqs, tok, width), F32)],
        [total, got, tokens, grad_middle, gains],
        coords,
        name="input",
    )
    result = (
        middle + res[0] + after(got_z, got).astype(F32) + got_y.astype(F32)
    ).astype(BF)
    payload, out_got, grad_tokens, result = stage(
        lax.all_to_all(payload, cube, 0, 0, tiled=True),
        swap(out_send, "za"),
        grad_tokens,
        result,
    )
    out_keep, out_send = split("zl", out_keep, out_got, (1, 2, per, width))
    out_keep, out_send = stage(out_keep, out_send)
    query_g, key_g, value_g, *sums, inner_g = call(
        last_kernel,
        [((per, width), F32)] * 3
        + [((1, per), F32)] * 4
        + [((per, 8 * hidden_units), F32)],
        [payload],
        coords,
        name="last",
    )
    query_g, key_g, value_g, inner_g, out_got, result, *sums = stage(
        query_g, key_g, value_g, inner_g, swap(out_send, "zl"), result, *sums
    )
    sums = [v.reshape(per) for v in sums]
    return (
        result.reshape(seqs, tok, width),
        grad_tokens,
        sums[0],
        sums[1],
        query_g,
        key_g,
        value_g,
        out_keep[0] + out_got[0].astype(F32),
        sums[2],
        sums[3],
        inner_g,
        outer_g,
    )


def solution(mesh):
    blocks = mesh.shape["blk"]
    if blocks == 16:
        sizes = (2, 2, 1, 2, 2, 2)
        roles = (True, "za", ("x", "zl", "y"), ("c",), ("x", "za", "zl", "y"))
    else:
        sizes = (2, 8, blocks // 64, 2, 2, 2)
        roles = (False, "x", ("za",), ("zb", "zl", "y", "c"), ("x", "za"))
    fine = Mesh(mesh.devices.reshape(sizes), AXES)
    tok, row, vec = P(None, AXES, None), P(AXES, None), P(AXES)
    in_specs = (tok, tok, vec, vec, row, row, row, row, vec, vec, row, row)
    out_specs = (tok, tok, vec, vec, row, row, row, row, vec, vec, row, row)
    return jax.shard_map(
        fine_layer if blocks == 16 else functools.partial(on_device, roles),
        mesh=fine,
        in_specs=in_specs,
        out_specs=out_specs,
        check_vma=False,
    )
```

```python
import functools
import math

import jax
import jax.numpy as jnp
from jax import lax
from jax.experimental import pallas as pl
from jax.experimental.pallas import tpu as pltpu
from jax.sharding import Mesh
from jax.sharding import PartitionSpec as P

HD = 128
TILE = 256
SCALE = HD ** (-0.5)
MASKED = -1e30
eps_norm = 1e-05
gelu_coef = math.sqrt(2.0 / math.pi)
BF = jnp.bfloat16
F32 = jnp.float32
AXES = ("x", "za", "zb", "zl", "y", "c")
T_AXES = ("x", "za", "zb")
W_AXES = ("zl", "y", "c")


def mm(a, b):
    return jnp.dot(a, b, preferred_element_type=F32)


def mm_nt(a, b):
    return lax.dot_general(a, b, (((1,), (1,)), ((), ())), preferred_element_type=F32)


def mm_tn(a, b):
    return lax.dot_general(a, b, (((0,), (0,)), ((), ())), preferred_element_type=F32)


def norm_stats(values):
    centered = values - jnp.mean(values, -1, keepdims=True)
    inverse = lax.rsqrt(jnp.mean(centered * centered, -1, keepdims=True) + eps_norm)
    return centered * inverse, inverse


def norm_back(grad_normed, scaled, inverse, gain):
    g = grad_normed * gain
    return inverse * (
        g - jnp.mean(g, -1, keepdims=True) - scaled * jnp.mean(g * scaled, -1, keepdims=True)
    )


def swap(v, axis):
    return lax.ppermute(v, axis, [(0, 1), (1, 0)])


def pick(v, index, axis=0):
    return lax.dynamic_index_in_dim(v, index, axis, keepdims=False)


def pair_gather(v, axis):
    other = swap(v, axis)
    first = lax.axis_index(axis) == 0
    return jnp.stack([jnp.where(first, v, other), jnp.where(first, other, v)])


def pair_scatter(v, axis, dim):
    me = lax.axis_index(axis)
    return pick(v, me, dim) + swap(pick(v, 1 - me, dim).astype(BF), axis).astype(F32)


def after(v, *others):
    return lax.optimization_barrier((v,) + others)[0]


def t_gather(v):
    if lax.axis_size("za") * lax.axis_size("zb") != 2:
        return lax.all_gather(v, T_AXES, axis=0, tiled=False)
    x, z = lax.axis_index("x"), lax.axis_index("za")
    over_x, over_z = swap(v, "x"), swap(v, "za")
    out = jnp.zeros((4,) + v.shape, v.dtype)
    for part, at in (
        (v, 2 * x + z),
        (over_x, 2 * (1 - x) + z),
        (over_z, 2 * x + 1 - z),
        (swap(over_z, "x"), 2 * (1 - x) + 1 - z),
    ):
        out = lax.dynamic_update_index_in_dim(out, part, at, 0)
    return out


def t_scatter(v):
    if lax.axis_size("za") * lax.axis_size("zb") != 2:
        return lax.psum_scatter(v, T_AXES, scatter_dimension=0, tiled=False)
    v = pair_scatter(v.reshape((2, 2) + v.shape[1:]), "x", 0)
    return pair_scatter(v, "za", 0)


def plane_gather(v):
    half = v.shape[0] // 2
    a, b = v[:half], v[half:]
    a = jnp.stack([a, swap(a, "zl")])
    b = jnp.stack([b, swap(b, "y")])
    a = jnp.stack([a, swap(a, "y")])
    b = jnp.stack([b, swap(b, "zl")])
    both = jnp.stack([a, b])
    return jnp.stack([both, swap(both, "c")]).reshape(8 * v.shape[0], v.shape[1])


def plane_scatter(v):
    rows, width = v.shape
    v = v.reshape(2, 2, 2, 2, rows // 16, width)

    def fold(u, axis):
        return u[0] + swap(u[1].astype(BF), axis).astype(F32)

    v = fold(v, "c")
    a, b = v[0], v[1]
    a = fold(a, "y")
    b = fold(b, "zl")
    a = fold(a, "zl")
    b = fold(b, "y")
    return jnp.concatenate([a, b], 0)


def shares(count, body):
    if count <= 2:
        for k in range(count):
            body(k)
    else:
        lax.fori_loop(0, count, lambda k, c: (body(k), c)[1], 0)


def mask_of(count, q_tile, k_tile, q_share, k_share):
    rows = lax.broadcasted_iota(jnp.int32, (TILE, TILE), 0) + q_tile * TILE
    cols = lax.broadcasted_iota(jnp.int32, (TILE, TILE), 1) + k_tile * TILE
    q_pos = (lax.shift_right_logical(rows, 6) * count + q_share) * 64 + (rows & 63)
    k_pos = (lax.shift_right_logical(cols, 6) * count + k_share) * 64 + (cols & 63)
    return k_pos <= q_pos


def forward_kernel(count, meta, q_ref, k_ref, v_ref, o_ref, of_ref, lse_ref, qa, ka, va, s_ref):
    blocks = q_ref.shape[0]
    for j in range(blocks):
        slot = meta[j]
        rows = pl.ds(j * 64, 64)
        qa[rows, :] = q_ref[slot]

        def place(k, rows=rows, slot=slot):
            ka[k, rows, :] = k_ref[k, slot]
            va[k, rows, :] = v_ref[k, slot]

        shares(count, place)
    mine = meta[blocks]
    tiles = blocks * 64 // TILE
    for t in range(tiles):
        q = qa[pl.ds(t * TILE, TILE), :]
        top = jnp.full((TILE, 1), MASKED, F32)
        for u in range(t + 1):
            cols = pl.ds(u * TILE, TILE)

            def score(k, top, u=u, cols=cols):
                s = mm_nt(q, ka[k, cols, :]) * SCALE
                if u == t:
                    s = jnp.where(mask_of(count, t, u, mine, meta[blocks + 1 + k]), s, MASKED)
                s_ref[k * tiles + u] = s
                return jnp.maximum(top, jnp.max(s, -1, keepdims=True))

            if count <= 2:
                for k in range(count):
                    top = score(k, top)
            else:
                top = lax.fori_loop(0, count, score, top)
        total = jnp.zeros((TILE, 1), F32)
        for u in range(t + 1):

            def expo(k, total, u=u):
                p = jnp.exp(s_ref[k * tiles + u] - top)
                s_ref[k * tiles + u] = p
                return total + jnp.sum(p, -1, keepdims=True)

            if count <= 2:
                for k in range(count):
                    total = expo(k, total)
            else:
                total = lax.fori_loop(0, count, expo, total)
        inverse = 1.0 / total
        out = jnp.zeros((TILE, HD), F32)
        for u in range(t + 1):
            cols = pl.ds(u * TILE, TILE)

            def weigh(k, out, u=u, cols=cols):
                p = (s_ref[k * tiles + u] * inverse).astype(BF)
                return out + mm(p, va[k, cols, :])

            if count <= 2:
                for k in range(count):
                    out = weigh(k, out)
            else:
                out = lax.fori_loop(0, count, weigh, out)
        rows = pl.ds(t * TILE, TILE)
        of_ref[rows, :] = out
        o_ref[rows, :] = out.astype(BF)
        lse_ref[rows, :] = jnp.broadcast_to(top + jnp.log(total), (TILE, HD))


def attention_forward(count, meta, q, k, v):
    blocks = q.shape[0]
    rows = blocks * 64
    tiles = rows // TILE
    vm = pl.BlockSpec(memory_space=pltpu.VMEM)
    pairs = tiles * (tiles + 1) // 2 * count
    return pl.pallas_call(
        functools.partial(forward_kernel, count),
        in_specs=[pl.BlockSpec(memory_space=pltpu.SMEM), vm, vm, vm],
        out_specs=[vm] * 6,
        out_shape=[
            jax.ShapeDtypeStruct((rows, HD), BF),
            jax.ShapeDtypeStruct((rows, HD), F32),
            jax.ShapeDtypeStruct((rows, HD), F32),
            jax.ShapeDtypeStruct((rows, HD), BF),
            jax.ShapeDtypeStruct((count, rows, HD), BF),
            jax.ShapeDtypeStruct((count, rows, HD), BF),
        ],
        scratch_shapes=[pltpu.VMEM((count * tiles, TILE, TILE), F32)],
        cost_estimate=pl.CostEstimate(
            flops=pairs * TILE * TILE * HD * 4,
            bytes_accessed=rows * HD * 2 * (2 + 4 * count) + rows * HD * 8,
            transcendentals=pairs * TILE * TILE,
        ),
        compiler_params=pltpu.CompilerParams(vmem_limit_bytes=(16 if count <= 2 else 52) << 20),
        name="attention_forward",
    )(meta, q, k, v)


def backward_kernel(count, meta, q_ref, k_ref, v_ref, go_ref, of_ref, lse_ref, gq_ref, gk, gv):
    rows_all = q_ref.shape[0]
    blocks = rows_all // 64
    mine = meta[blocks]
    tiles = rows_all // TILE

    def zero(k):
        gk[k] = jnp.zeros((rows_all, HD), F32)
        gv[k] = jnp.zeros((rows_all, HD), F32)

    shares(count, zero)
    for t in range(tiles):
        rows = pl.ds(t * TILE, TILE)
        q = q_ref[rows, :]
        go = go_ref[rows, :]
        delta = jnp.sum(go.astype(F32) * of_ref[rows, :], -1, keepdims=True)
        lse = lse_ref[rows, :][:, :1]
        gq = jnp.zeros((TILE, HD), F32)
        for u in range(t + 1):
            cols = pl.ds(u * TILE, TILE)

            def one(k, gq, u=u, cols=cols):
                kk = k_ref[k, cols, :]
                p = jnp.exp(mm_nt(q, kk) * SCALE - lse)
                if u == t:
                    p = jnp.where(mask_of(count, t, u, mine, meta[blocks + 1 + k]), p, 0.0)
                gv[k, cols, :] += mm_tn(p.astype(BF), go)
                ds = (p * (mm_nt(go, v_ref[k, cols, :]) - delta)).astype(BF)
                gk[k, cols, :] += mm_tn(ds, q)
                return gq + mm(ds, kk)

            if count <= 2:
                for k in range(count):
                    gq = one(k, gq)
            else:
                gq = lax.fori_loop(0, count, one, gq)
        gq_ref[rows, :] = (gq * SCALE).astype(BF)

    def scale(k):
        gk[k] = gk[k] * SCALE

    shares(count, scale)


def attention_backward(count, meta, q, k, v, go, of, lse):
    rows = q.shape[0]
    tiles = rows // TILE
    vm = pl.BlockSpec(memory_space=pltpu.VMEM)
    pairs = tiles * (tiles + 1) // 2 * count
    return pl.pallas_call(
        functools.partial(backward_kernel, count),
        in_specs=[pl.BlockSpec(memory_space=pltpu.SMEM)] + [vm] * 6,
        out_specs=[vm] * 3,
        out_shape=[
            jax.ShapeDtypeStruct((rows, HD), BF),
            jax.ShapeDtypeStruct((count, rows, HD), F32),
            jax.ShapeDtypeStruct((count, rows, HD), F32),
        ],
        cost_estimate=pl.CostEstimate(
            flops=pairs * TILE * TILE * HD * 10,
            bytes_accessed=rows * HD * (16 + 12 * count),
            transcendentals=pairs * TILE * TILE,
        ),
        compiler_params=pltpu.CompilerParams(vmem_limit_bytes=(16 if count <= 2 else 52) << 20),
        name="attention_backward",
    )(meta, q, k, v, go, of, lse)


def reorder_kernel(meta, g_ref, out_ref):
    for j in range(g_ref.shape[0]):
        out_ref[meta[j]] = g_ref[j]


def reorder(meta, g):
    vm = pl.BlockSpec(memory_space=pltpu.VMEM)
    return pl.pallas_call(
        reorder_kernel,
        in_specs=[pl.BlockSpec(memory_space=pltpu.SMEM), vm],
        out_specs=vm,
        out_shape=jax.ShapeDtypeStruct(g.shape, g.dtype),
        cost_estimate=pl.CostEstimate(flops=0, bytes_accessed=4 * g.size, transcendentals=0),
        compiler_params=pltpu.CompilerParams(vmem_limit_bytes=8 << 20),
        name="reorder",
    )(meta, g)


def on_device(
    roles,
    tokens,
    cotangent,
    ln1_gain,
    ln1_bias,
    w_query,
    w_key,
    w_value,
    w_out,
    ln2_gain,
    ln2_bias,
    w_inner,
    w_outer,
):
    small, seq_axis, hd_axes, sh_axes, own_axes = roles
    planes = math.prod(lax.axis_size(a) for a in T_AXES)
    count = math.prod(lax.axis_size(a) for a in sh_axes)
    devices = 8 * planes
    seqs, tok, width = tokens.shape
    rows = seqs * tok
    per = w_query.shape[0]
    unit = w_outer.shape[0]
    seq = lax.axis_index(seq_axis)
    share = lax.axis_index(sh_axes)

    block = jnp.stack([pick(tokens, seq), swap(pick(tokens, 1 - seq), seq_axis)])
    if small:
        on_x, on_z, on_y = (swap(block, a) for a in hd_axes)
        on_xz, on_xy, on_zy = swap(on_x, "zl"), swap(on_y, "x"), swap(on_z, "y")
        on_xyz = swap(on_xz, "y")
        seen = jnp.stack([block, on_y, on_z, on_zy, on_x, on_xy, on_xz, on_xyz])
    else:
        seen = lax.all_gather(block, hd_axes, axis=0, tiled=False)
    at = jnp.arange(16, dtype=jnp.int32)
    if small:
        at_x, at_za, at_zl, at_y = at // 8, at // 4 % 2, at // 2 % 2, at % 2
        x, zl, y = (lax.axis_index(a) for a in hd_axes)
        slots = ((at_x ^ x) * 4 + (at_zl ^ zl) * 2 + (at_y ^ y)) * 2 + (at_za ^ seq)
    else:
        slots = at % 8 * 2 + (at // 8 ^ seq)

    gains = jnp.concatenate([ln1_gain, ln1_bias, ln2_gain, ln2_bias])
    gains = jnp.broadcast_to(jnp.pad(gains, (0, HD - gains.shape[0])), (8, 1, HD))
    head_w = jnp.stack([w_query, w_key, w_value]).reshape(3, per, 8, HD).transpose(2, 0, 1, 3)
    head_w = jnp.concatenate([head_w.reshape(8, 3 * per, HD), gains], 1)
    head_w = lax.all_to_all(head_w, hd_axes, 0, 0, tiled=True)
    head_w = pair_gather(head_w, seq_axis)
    for axis in reversed(sh_axes):
        if lax.axis_size(axis) == 2:
            head_w = pair_gather(head_w, axis)
        else:
            head_w = lax.all_gather(head_w, axis, axis=0, tiled=False)
    if small:
        head_w = head_w.reshape(2, 2, 2, 4, 3 * per + 1, HD).transpose(2, 1, 3, 0, 4, 5)
    else:
        head_w = head_w.reshape(count, 16, 3 * per + 1, HD).transpose(1, 0, 2, 3)
    head_w = head_w.reshape(devices, 3 * per + 1, HD)
    gains = head_w[:, -1, : 4 * per].reshape(devices, 4, per).transpose(1, 0, 2)
    gains = gains.reshape(4, width).astype(F32)
    gain_one, bias_one, gain_two, bias_two = gains[0], gains[1], gains[2], gains[3]
    head_w = head_w[:, :-1].reshape(devices, 3, per, HD).transpose(0, 2, 1, 3)
    head_w = head_w.reshape(width, 3 * HD)

    inner_w = w_inner.reshape(per, planes, 8, unit).transpose(2, 0, 1, 3)
    inner_w = lax.all_to_all(inner_w.reshape(8, per, planes * unit), W_AXES, 0, 0, tiled=True)
    inner_w = t_gather(after(inner_w, seen)).reshape(width, planes * unit)
    outer_w = t_gather(w_outer).reshape(planes * unit, width)
    grad_plane = plane_gather(after(cotangent, seen).reshape(rows, width))

    out_w = lax.all_gather(w_out, AXES, axis=0, tiled=True)
    qkv_w = jnp.concatenate([w_query, w_key, w_value], 1)
    qkv_w = lax.all_gather(after(qkv_w, seen), AXES, axis=0, tiled=True)

    normed, _ = norm_stats(seen.reshape(-1, width).astype(F32))
    h1 = (normed * gain_one + bias_one).astype(BF)
    qkv = mm(h1, head_w).astype(BF)
    query = qkv[:, :HD].reshape(16, tok, HD)
    kv = qkv[:, HD:]
    if count == 2:
        kv = jnp.stack([kv, swap(kv, "c")])
        order = jnp.stack([share, 1 - share])
    else:
        kv = lax.all_gather(kv, sh_axes, axis=0, tiled=False)
        order = jnp.arange(count)
    kv = kv.reshape(count, 16, tok, 2 * HD)
    meta = jnp.concatenate([slots, share.reshape(1), order]).astype(jnp.int32)
    out, out_f, lse, q_at, k_at, v_at = attention_forward(
        count, meta, query, kv[..., :HD], kv[..., HD:]
    )

    def to_tokens(v):
        v = lax.all_to_all(v, own_axes, 0, 0, tiled=True)
        n = v.shape[-1] // HD
        if small:
            v = v.reshape(2, 2, 4, tok, n, HD).transpose(1, 3, 4, 0, 2, 5)
        else:
            v = v.reshape(2, 8, tok, n, HD).transpose(0, 2, 3, 1, 4)
        return v.reshape(2, tok, n, 8 * HD)

    mixed = to_tokens(out.reshape(16, tok, HD)).reshape(rows, width)
    flat_in = tokens.reshape(rows, width).astype(F32)
    middle = flat_in + mm(mixed, out_w)
    scaled_two, inverse_two = norm_stats(middle)
    h2 = plane_gather((scaled_two * gain_two + bias_two).astype(BF))

    inner = mm(h2, inner_w)
    bent = jnp.tanh(gelu_coef * (inner + 0.044715 * inner * inner * inner))
    hidden = (0.5 * inner * (1.0 + bent)).astype(BF)
    slope = 0.5 * (1.0 + bent) + 0.5 * inner * (1.0 - bent * bent) * gelu_coef * (
        1.0 + 3.0 * 0.044715 * inner * inner
    )
    grad_inner = (mm_nt(grad_plane, outer_w) * slope).astype(BF)
    grad_h2 = plane_scatter(mm_nt(grad_inner, inner_w))
    grad_outer = mm_tn(hidden, grad_plane).reshape(planes, unit, width)
    grad_outer = t_scatter(grad_outer)
    grad_in = mm_tn(h2, grad_inner).reshape(planes, 8 * per, planes * unit)
    grad_in = t_scatter(grad_in).astype(BF).reshape(8, per, planes * unit)
    result = plane_scatter(mm(hidden, outer_w))

    grad_out = cotangent.reshape(rows, width).astype(F32)
    grad_middle = grad_out + norm_back(grad_h2, scaled_two, inverse_two, gain_two)
    branch = grad_middle.astype(BF)
    go = mm_nt(branch, out_w).astype(BF)
    if small:
        go = go.reshape(2, tok, 2, 4, HD).transpose(2, 0, 3, 1, 4)
    else:
        go = go.reshape(2, tok, 8, HD).transpose(0, 2, 1, 3)
    go = lax.all_to_all(go.reshape(16, tok, HD), own_axes, 0, 0, tiled=True)
    go = go.reshape(16 * tok, HD)

    gq, gk, gv = attention_backward(count, meta, q_at, k_at, v_at, go, out_f, lse)
    gkv = jnp.concatenate([gk, gv], -1)
    if count == 2:
        gkv = gkv[0] + swap(gkv[1].astype(BF), "c").astype(F32)
    else:
        gkv = lax.psum_scatter(gkv, sh_axes, scatter_dimension=0, tiled=False)
    grads = jnp.concatenate([gq, gkv.astype(BF)], -1).reshape(16, tok, 3 * HD)
    grads, result, grad_in, grad_outer = lax.optimization_barrier(
        (grads, result, grad_in, grad_outer)
    )
    back = to_tokens(grads).reshape(rows, 3 * width)
    result = (middle + result).astype(BF)
    grad_in = lax.all_to_all(after(grad_in, back), W_AXES, 0, 0, tiled=True)
    grad_in = grad_in.reshape(8, per, planes, unit).transpose(1, 2, 0, 3)
    grad_in = grad_in.reshape(per, devices * unit).astype(F32)

    head_g = mm_tn(h1, reorder(meta, grads).reshape(16 * tok, 3 * HD))
    head_g = head_g.reshape(tuple(lax.axis_size(a) for a in AXES) + (per, 3 * HD))
    dims = list(AXES)
    for axis in sh_axes[::-1] + (seq_axis,):
        dim = dims.index(axis)
        dims.remove(axis)
        if lax.axis_size(axis) == 2:
            head_g = pair_scatter(head_g, axis, dim)
        else:
            head_g = lax.psum_scatter(head_g, axis, scatter_dimension=dim, tiled=False)
    head_g = head_g.astype(BF).reshape(8, per, 3 * HD)
    head_g = lax.all_to_all(head_g, hd_axes, 0, 0, tiled=True)
    head_g = head_g.reshape(8, per, 3, HD).transpose(2, 1, 0, 3).reshape(3, per, width)
    head_g = head_g.astype(F32)

    grad_out_w = mm_tn(mixed, branch).reshape(planes, 2, 2, 2, per, width)
    grad_out_w = pair_scatter(grad_out_w, "c", 3)
    grad_out_w = pair_scatter(grad_out_w, "y", 2)
    grad_out_w = pair_scatter(grad_out_w, "zl", 1)
    grad_out_w = t_scatter(grad_out_w)

    scaled_one, inverse_one = norm_stats(flat_in)
    grad_h1 = mm_nt(back, qkv_w)
    grad_input = grad_middle + norm_back(grad_h1, scaled_one, inverse_one, gain_one)

    sums = jnp.stack(
        [
            jnp.sum(grad_h1 * scaled_one, 0),
            jnp.sum(grad_h1, 0),
            jnp.sum(grad_h2 * scaled_two, 0),
            jnp.sum(grad_h2, 0),
        ]
    )
    sums = sums.reshape(4, devices, per).transpose(1, 0, 2).reshape(devices, 4 * per)
    sums = lax.all_to_all(sums, AXES, 0, 0, tiled=True)
    sums = jnp.sum(sums, 0).reshape(4, per)
    return (
        result.reshape(seqs, tok, width),
        grad_input.reshape(seqs, tok, width),
        sums[0],
        sums[1],
        head_g[0],
        head_g[1],
        head_g[2],
        grad_out_w,
        sums[2],
        sums[3],
        grad_in,
        grad_outer,
    )


class Arriving:
    def __init__(self, ref, copy):
        self.ref, self.copy = ref, copy
        self.shape, self.dtype = ref.shape, ref.dtype

    def __getitem__(self, index):
        if self.copy is not None:
            self.copy.wait()
            self.copy = None
        return self.ref[index]


class Leaving:
    def __init__(self, ref, target, move):
        self.ref, self.target, self.move, self.pushed = ref, target, move, False
        self.shape, self.dtype = ref.shape, ref.dtype

    def __getitem__(self, index):
        return self.ref[index]

    def __setitem__(self, index, value):
        self.ref[index] = value

    def push(self, rows=None):
        self.pushed = True
        if rows is None:
            self.move(self.ref, self.target)
        else:
            self.move(self.ref.at[rows], self.target.at[rows])


def call(kernel, outs, ins, coords=None, raw=(), save=(), scratch=(), eager=False, name=None):
    hbm = pl.BlockSpec(memory_space=pltpu.HBM)
    outs = [tuple(o) + ("far",) * (3 - len(o)) for o in outs]
    far = [i for i in range(len(ins)) if i not in raw]
    lead = 0 if coords is None else 1
    late = [i for i, o in enumerate(outs) if o[2] == "far"]
    extra = [pltpu.VMEM(ins[i].shape, ins[i].dtype) for i in far]
    extra += [pltpu.VMEM(outs[i][0], outs[i][1]) for i in late]
    extra.append(pltpu.SemaphoreType.DMA((len(far) + 4 * len(late) + len(save),)))
    count_in, count_out = len(ins), len(outs) + len(save)

    def body(*refs):
        front, refs = refs[:lead], refs[lead:]
        got, put = list(refs[:count_in]), list(refs[count_in : count_in + count_out])
        work = refs[count_in + count_out :]
        own, work = work[: len(scratch)], work[len(scratch) :]
        started = []

        def move(source, target):
            copy = pltpu.make_async_copy(source, target, work[-1].at[len(started)])
            copy.start()
            started.append(copy)
            return copy

        for n, i in enumerate(far):
            got[i] = Arriving(work[n], move(got[i], work[n]))
        leaving = []
        for n, i in enumerate(save):
            got[i].copy.wait()
            got[i].copy = None
            leaving.append(move(got[i].ref, put[len(outs) + n]))
        if eager:
            for i in far:
                got[i].copy.wait()
                got[i].copy = None
        inside = put[: len(outs)]
        for n, i in enumerate(late):
            inside[i] = Leaving(
                work[len(far) + n], put[i], lambda a, b: leaving.append(move(a, b))
            )
        kernel(*front, *got, *inside, *own)
        for i in late:
            if not inside[i].pushed:
                inside[i].push()
        for i in far:
            if got[i].copy is not None:
                got[i].copy.wait()
        for copy in leaving:
            copy.wait()

    specs = [hbm] * len(ins)
    if coords is not None:
        specs = [pl.BlockSpec(memory_space=pltpu.SMEM)] + specs
    saved = [jax.ShapeDtypeStruct(ins[i].shape, ins[i].dtype) for i in save]
    return pl.pallas_call(
        body,
        in_specs=specs,
        out_specs=[hbm] * count_out,
        out_shape=[jax.ShapeDtypeStruct(o[0], o[1]) for o in outs] + saved,
        scratch_shapes=list(scratch) + extra,
        cost_estimate=pl.CostEstimate(flops=0, bytes_accessed=0, transcendentals=0),
        compiler_params=pltpu.CompilerParams(vmem_limit_bytes=58 << 20),
        name=name,
    )(*([] if coords is None else [coords]), *ins)


def aligned(index, size):
    if isinstance(index, int):
        return pl.ds(index * size, size)
    return pl.ds(pl.multiple_of(index * size, size), size)


def pack_kernel(wq, wk, wv, g1, b1, g2, b2, w_inner, head, inner):
    per = wq.shape[0]
    gains = jnp.concatenate([g1[...], b1[...], g2[...], b2[...]], 1)
    for d in range(16):
        cols = pl.ds(((d >> 3) * 4 + (d & 3)) * HD, HD)
        for n, w in enumerate((wq, wk, wv)):
            head[d, pl.ds(n * per, per), :] = w[:, cols]
        head[d, pl.ds(3 * per, 16), :] = jnp.broadcast_to(gains, (16, HD))
    for w in range(8):
        for t in range(4):
            p = (w >> 2) * 16 + t * 4 + (w & 3)
            inner[w, :, pl.ds(t * HD, HD)] = w_inner[:, pl.ds(p * HD, HD)]


def norm_of(values):
    centered = values - jnp.mean(values, -1, keepdims=True)
    inverse = lax.rsqrt(jnp.mean(centered * centered, -1, keepdims=True) + eps_norm)
    return centered * inverse, inverse


def qkv_kernel(at, *refs):
    blocks, pieces = refs[:8], refs[8:10]
    h1, query, kv, gains, weights = refs[10:]
    x, za, zl, y, c = (at[i] for i in range(5))
    width = h1.shape[1]
    per = width // 32
    got = jnp.concatenate([p[d, 3 * per : 3 * per + 1, :] for p in pieces for d in range(16)], 0)
    line = lax.broadcasted_iota(jnp.int32, (32, width), 0)
    lane = lax.broadcasted_iota(jnp.int32, (32, width), 1)
    owner = (line & 15) * 2 + (c ^ (line >> 4))
    mine = lax.shift_right_logical(lane, 5) == owner
    source = lax.broadcasted_iota(jnp.int32, (HD, width), 0)
    target = lax.broadcasted_iota(jnp.int32, (HD, width), 1)
    for k in range(4):
        spread = jnp.where(source == k * per + (target & (per - 1)), 1.0, 0.0).astype(BF)
        gains[k : k + 1, :] = jnp.sum(jnp.where(mine, mm(got, spread), 0.0), 0, keepdims=True)
    gain, bias = gains[0:1, :], gains[1:2, :]
    for n, block in enumerate(blocks):
        xx, zz, yy = x ^ (n >> 2), zl ^ (n >> 1 & 1), y ^ (n & 1)
        for s in range(2):
            j = xx * 8 + (za ^ s) * 4 + zz * 2 + yy
            normed, _ = norm_of(block[s].astype(F32))
            h1[aligned(j, 64), :] = (normed * gain + bias).astype(BF)
    h1.push()
    for n, piece in enumerate(pieces):
        for d in range(16):
            for i in range(3):
                weights[aligned(2 * d + (c ^ n), per), pl.ds(i * HD, HD)] = piece[
                    d, pl.ds(i * per, per), :
                ]
    weights.push()
    for t in range(h1.shape[0] // TILE):
        rows = pl.ds(t * TILE, TILE)
        out = mm(h1[rows, :], weights[...]).astype(BF)
        query[rows, :] = out[:, :HD]
        kv[rows, :] = out[:, HD:]
        query.push(rows)
        kv.push(rows)


def causal(q_share, k_share):
    rows = lax.broadcasted_iota(jnp.int32, (TILE, TILE), 0)
    cols = lax.broadcasted_iota(jnp.int32, (TILE, TILE), 1)
    q_pos = (lax.shift_right_logical(rows, 6) * 2 + q_share) * 64 + (rows & 63)
    k_pos = (lax.shift_right_logical(cols, 6) * 2 + k_share) * 64 + (cols & 63)
    return k_pos <= q_pos


def fine_forward_kernel(at, query, own, other, out, out_f, lse, s_ref):
    tiles = query.shape[0] // TILE
    c = at[4]
    both = (own, other)

    def tile(t, carry):
        rows = aligned(t, TILE)
        q = query[rows, :]

        def score(u, top, masked):
            for n in range(2):
                s = mm_nt(q, both[n][aligned(u, TILE), pl.ds(0, HD)]) * SCALE
                if masked:
                    s = jnp.where(causal(c, c if n == 0 else 1 - c), s, MASKED)
                s_ref[u * 2 + n] = s
                top = jnp.maximum(top, jnp.max(s, -1, keepdims=True))
            return top

        top = jnp.full((TILE, 1), MASKED, F32)
        for u in range(t + 1):
            top = score(u, top, u == t)

        def expo(u, total):
            for n in range(2):
                p = jnp.exp(s_ref[u * 2 + n] - top)
                s_ref[u * 2 + n] = p
                total = total + jnp.sum(p, -1, keepdims=True)
            return total

        total = jnp.zeros((TILE, 1), F32)
        for u in range(t + 1):
            total = expo(u, total)
        inverse = 1.0 / total

        def weigh(u, acc):
            for n in range(2):
                p = (s_ref[u * 2 + n] * inverse).astype(BF)
                acc = acc + mm(p, both[n][aligned(u, TILE), pl.ds(HD, HD)])
            return acc

        acc = jnp.zeros((TILE, HD), F32)
        for u in range(t + 1):
            acc = weigh(u, acc)
        out_f[rows, :] = acc
        out[pl.ds(t * (TILE // 64), TILE // 64)] = acc.astype(BF).reshape(TILE // 64, 64, HD)
        lse[rows, :] = jnp.broadcast_to(top + jnp.log(total), (TILE, HD))
        out.push(pl.ds(t * (TILE // 64), TILE // 64))
        out_f.push(rows)
        lse.push(rows)
        return carry

    for t in range(tiles):
        tile(t, 0)


def place_w_out(at, pieces, out_w, sems):
    x, za, zl, y, c = (at[i] for i in range(5))
    copies = []
    for n, piece in enumerate(pieces):
        side = (zl ^ (n & 1)) * 4 + (y ^ (n >> 1 & 1)) * 2 + (c ^ (n >> 2))
        for i in range(4):
            p = (x ^ (i >> 1)) * 16 + (za ^ (i & 1)) * 8 + side
            copies.append(
                pltpu.make_async_copy(
                    piece.at[i], out_w.at[aligned(p, piece.shape[1]), :], sems.at[len(copies)]
                )
            )
            copies[-1].start()
    return copies


def middle_kernel(at, got, tokens, gains, *refs):
    pieces, (mixed, middle, scaled, inverse, h2, out_w, sems) = refs[:8], refs[8:]
    copies = place_w_out(at, pieces, out_w, sems)
    rows, width = middle.shape
    tok = rows // 2
    for s in range(16):
        head = (s >> 3) * 4 + (s & 3)
        mixed[pl.ds((s >> 2 & 1) * tok, tok), pl.ds(head * HD, HD)] = got[s]
    for s in range(2):
        middle[pl.ds(s * tok, tok), :] = tokens[s].astype(F32)
    for copy in copies:
        copy.wait()
    mixed.push()
    middle[...] += mm(mixed[...], out_w[...])
    middle.push()
    normed, inv = norm_of(middle[...])
    scaled[...] = normed
    inverse[...] = jnp.broadcast_to(inv, (rows, HD))
    h2[...] = (normed * gains[2:3, :] + gains[3:4, :]).astype(BF)


def inner_kernel(at, *refs):
    h2_parts, cot_parts, in_parts, out_parts = refs[:10], refs[10:20], refs[20:24], refs[24:28]
    h2_out, cot_out, outer_out, hidden, grad_inner, keep, send = refs[28:35]
    h2, cot, w_in, w_outer, sems = refs[35:]
    za, zl = at[1], at[2]
    copies = []

    def move(source, target):
        copy = pltpu.make_async_copy(source, target, sems.at[len(copies)])
        copy.start()
        copies.append(copy)

    for n in range(4):
        t = (za ^ (n >> 1)) * 2 + (zl ^ (n & 1))
        for i in range(2):
            rows = in_parts[n].shape[1]
            move(in_parts[n].at[i], w_in.at[aligned(i * 4 + t, rows), :])
    for n in range(4):
        t = (za ^ (n >> 1)) * 2 + (zl ^ (n & 1))
        move(out_parts[n], w_outer.at[aligned(t, out_parts[n].shape[0]), :])
    row = 0
    for part in cot_parts:
        move(part, cot.at[pl.ds(row, part.shape[0]), :])
        row += part.shape[0]
    row = 0
    for part in h2_parts:
        h2[pl.ds(row, part.shape[0]), :] = part[...]
        row += part.shape[0]
    for copy in copies[:8]:
        copy.wait()
    first = mm(h2[pl.ds(0, TILE), :], w_in[...])
    for copy in copies[8:22]:
        copy.wait()
    arrived = 22
    move(h2, h2_out)
    move(cot, cot_out)
    move(w_outer, outer_out)
    half = h2.shape[0] // 2

    def tile(t, carry):
        rows = aligned(t, TILE)
        u = first if t == 0 else mm(h2[rows, :], w_in[...])
        squared = u * u
        bent = jnp.tanh(gelu_coef * (u + 0.044715 * squared * u))
        hidden[rows, :] = (0.5 * u * (1.0 + bent)).astype(BF)
        slope = 0.5 * (1.0 + bent) + 0.5 * u * (1.0 - bent * bent) * gelu_coef * (
            1.0 + 3.0 * 0.044715 * squared
        )
        grad = (mm_nt(cot[rows, :], w_outer[...]) * slope).astype(BF)
        grad_inner[rows, :] = grad
        hidden.push(rows)
        grad_inner.push(rows)
        return mm_nt(grad, w_in[...]), carry

    for out, first_tile in ((keep, 0), (send, half // TILE)):
        for t in range(2):
            rows = pl.ds(t * TILE, TILE)
            out[rows, :] = tile(first_tile + t, 0)[0].astype(BF)
            out.push(rows)
    for copy in copies[arrived:]:
        copy.wait()


def transposed_product(big, left, right, tile=TILE):
    left[0:8, :], right[0:8, :]

    def one(i, carry):
        cols = pl.ds(pl.multiple_of(i * tile, tile), tile)
        big[cols, :] = mm_tn(left[:, cols], right[...])
        return carry

    lax.fori_loop(0, left.shape[1] // tile, one, 0)


def others_of(at):
    za, zl = at[1], at[2]
    return za * 2 + zl, za * 2 + 1 - zl, 2 - 2 * za + zl, 3 - 2 * za - zl


def inner_grad_kernel(at, h2, grad_inner, own, to_l, to_a, to_la, big):
    transposed_product(big, h2, grad_inner)
    n = own.shape[0] // 2
    for t, out in zip(others_of(at), (own, to_l, to_a, to_la)):
        for i in range(2):
            out[pl.ds(i * n, n), :] = big[aligned(i * 4 + t, n), :].astype(out.dtype)


def outer_grad_kernel(at, hidden, cot, w_outer, own, to_l, to_a, to_la, keep, send, big):
    half = keep.shape[0]
    send[...] = mm(hidden[pl.ds(half, half), :], w_outer[...]).astype(BF)
    keep[...] = mm(hidden[pl.ds(0, half), :], w_outer[...])
    transposed_product(big, hidden, cot)
    n = own.shape[0]
    for t, out in zip(others_of(at), (own, to_l, to_a, to_la)):
        out[...] = big[aligned(t, n), :].astype(out.dtype)


def payload_kernel(head_keep, head_got, payload):
    m = head_keep.shape[1] // 4
    for d in range(8):
        rows = pl.ds((d & 3) * m, m)
        payload[d] = (head_keep[d >> 2, rows, :] + head_got[d >> 2, rows, :].astype(F32)).astype(BF)


def last_kernel(
    at, got, near_x, far_x, far_y, query, key, value, sum_a, sum_b, sum_c, sum_d, inner_g
):
    x, y, c = at[0], at[3], at[4]
    per = query.shape[0]
    for w in range(4):
        part = ((near_x, far_x)[w >> 1])[...] if w & 1 == 0 else far_y[w >> 1]
        for s in range(2):
            side = (x ^ (w >> 1)) * 16 + (y ^ (w & 1)) * 2 + (c ^ s)
            for t in range(part.shape[2] // HD):
                inner_g[:, aligned(t * 4 + side, HD)] = part[s, :, t * HD : (t + 1) * HD].astype(F32)
    inner_g.push()
    total = got[0, pl.ds(per, 16), pl.ds(0, HD)].astype(F32)
    for h in range(8):
        for n, out in enumerate((query, key, value)):
            out[:, pl.ds(h * HD, HD)] = got[h, pl.ds(0, per), pl.ds(n * HD, HD)].astype(F32)
        if h:
            total = total + got[h, pl.ds(per, 16), pl.ds(0, HD)].astype(F32)
    for n, out in enumerate((sum_a, sum_b, sum_c, sum_d)):
        out[...] = total[0:1, n * per : (n + 1) * per]


def branch_kernel(at, parts, scaled, inverse, gains, cot, *refs):
    pieces, (grad_middle, branch, go, sums, out_w, sems) = refs[:8], refs[8:]
    copies = place_w_out(at, pieces, out_w, sems)
    rows, width = scaled.shape
    tok = rows // 2
    grad = parts[0].astype(F32)
    for n in range(1, 4):
        grad = grad + parts[n].astype(F32)
    n2 = scaled[...]
    sums[0:1, :] = jnp.sum(grad * n2, 0, keepdims=True)
    sums[1:2, :] = jnp.sum(grad, 0, keepdims=True)
    a = grad * gains[2:3, :]
    grad = inverse[:, 0:1] * (
        a - jnp.mean(a, -1, keepdims=True) - n2 * jnp.mean(a * n2, -1, keepdims=True)
    )
    for s in range(2):
        part = pl.ds(s * tok, tok)
        grad_middle[part, :] = cot[s].astype(F32) + grad[s * tok : (s + 1) * tok]
    grad_middle.push()
    branch[...] = grad_middle[...].astype(BF)
    branch.push()
    for copy in copies:
        copy.wait()
    out = mm_nt(branch[...], out_w[...]).astype(BF)
    for s in range(16):
        head = (s >> 3) * 4 + (s & 3)
        seq = s >> 2 & 1
        go[s] = out[seq * tok : (seq + 1) * tok, head * HD : (head + 1) * HD]


def fine_backward_kernel(at, query, own, other, go_ref, out_f, lse_ref, gq_ref, keep, send, acc):
    rows_all = query.shape[0]
    tiles = rows_all // TILE
    c = at[4]
    both = (own, other)
    keep[...] = jnp.zeros(keep.shape, keep.dtype)
    acc[...] = jnp.zeros_like(acc)
    totals = (keep, acc)

    def tile(t, carry):
        rows = aligned(t, TILE)
        q = query[rows, :]
        go = go_ref[pl.ds(t * (TILE // 64), TILE // 64)].reshape(TILE, HD)
        delta = jnp.sum(go.astype(F32) * out_f[rows, :], -1, keepdims=True)
        lse = lse_ref[rows, 0:1]

        def one(u, gq, masked):
            cols = aligned(u, TILE)
            for n in range(2):
                kk = both[n][cols, pl.ds(0, HD)]
                p = jnp.exp(mm_nt(q, kk) * SCALE - lse)
                if masked:
                    p = jnp.where(causal(c, c if n == 0 else 1 - c), p, 0.0)
                totals[n][cols, pl.ds(HD, HD)] += mm_tn(p.astype(BF), go)
                ds = (p * (mm_nt(go, both[n][cols, pl.ds(HD, HD)]) - delta)).astype(BF)
                totals[n][cols, pl.ds(0, HD)] += mm_tn(ds, q)
                gq = gq + mm(ds, kk)
            return gq

        gq = jnp.zeros((TILE, HD), F32)
        for u in range(t + 1):
            gq = one(u, gq, u == t)
        gq_ref[rows, :] = (gq * SCALE).astype(BF)
        gq_ref.push(rows)
        return carry

    for t in range(tiles):
        tile(t, 0)
    send[:, :HD] = (acc[:, :HD] * SCALE).astype(BF)
    send[:, HD:] = acc[:, HD:].astype(BF)
    send.push()
    keep[:, :HD] = keep[:, :HD] * SCALE


def partial_kernel(at, *refs):
    blocks, (gq, keep, got, weights) = refs[:8], refs[8:12]
    grads, parts, sums, tokens, sems = refs[12:]
    x, za, zl, y = (at[i] for i in range(4))
    copies = []
    for n in range(8):
        for s in range(2):
            j = (x ^ (n >> 2)) * 8 + (za ^ s) * 4 + (zl ^ (n >> 1 & 1)) * 2 + (y ^ (n & 1))
            copies.append(
                pltpu.make_async_copy(
                    blocks[n].at[s], tokens.at[aligned(j, 64), :], sems.at[len(copies)]
                )
            )
            copies[-1].start()
    for copy in copies:
        copy.wait()
    tiles = gq.shape[0] // TILE
    for t in range(tiles):
        rows = pl.ds(t * TILE, TILE)
        grads[rows, pl.ds(0, HD)] = gq[rows, :]
        grads[rows, pl.ds(HD, 2 * HD)] = (keep[rows, :] + got[rows, :].astype(F32)).astype(BF)
        part = mm_nt(grads[rows, :], weights[...])
        normed, _ = norm_of(tokens[rows, :].astype(F32))
        one = jnp.sum(part * normed, 0, keepdims=True)
        two = jnp.sum(part, 0, keepdims=True)
        if t == 0:
            sums[0:1, :] = one
            sums[1:2, :] = two
        else:
            sums[0:1, :] += one
            sums[1:2, :] += two
        for i in range(4):
            parts[(t >> 1) * 4 + i, za ^ (t & 1)] = part[i * 64 : (i + 1) * 64].astype(BF)
        grads.push(rows)
        if t & 1:
            parts.push(pl.ds((t >> 1) * 4, 4))


def total_kernel(parts, keep, send):
    total = parts[0, 0].astype(F32)
    other = parts[0, 1].astype(F32)
    for n in range(1, 8):
        total = total + parts[n, 0].astype(F32)
        other = other + parts[n, 1].astype(F32)
    keep[...] = total
    send[...] = other.astype(BF)


def head_grad_kernel(at, left, right, sums, keep, send, big):
    c = at[4]
    per = left.shape[1] // 32
    transposed_product(big, left, right)
    spare = keep.shape[2] - sums.shape[1]
    for q in range(16):
        keep[q, pl.ds(0, per), :] = big[aligned(2 * q + c, per), :]
        send[q, pl.ds(0, per), :] = big[aligned(2 * q + 1 - c, per), :].astype(BF)
    pad = jnp.zeros((16, spare), F32)
    for q in range(16):
        pair = jnp.concatenate([sums[2 * q : 2 * q + 2, :], pad[:2]], 1)
        mine = jnp.where(c == 0, pair[0:1], pair[1:2])
        other = jnp.where(c == 0, pair[1:2], pair[0:1])
        keep[q, pl.ds(per, 16), :] = jnp.broadcast_to(mine, (16, keep.shape[2]))
        send[q, pl.ds(per, 16), :] = jnp.broadcast_to(other, (16, keep.shape[2])).astype(BF)


def core_grad_kernel(at, left, right, keep, send, big):
    c = at[4]
    per = left.shape[1] // 32
    transposed_product(big, left, right)
    for q in range(16):
        rows = pl.ds(q * per, per)
        keep[rows, :] = big[aligned(2 * q + c, per), :]
        send[rows, :] = big[aligned(2 * q + 1 - c, per), :].astype(BF)


def input_kernel(at, keep, got, tokens, grad_middle, gains, grad_tokens):
    za = at[1]
    tok = tokens.shape[1]
    for n in range(2):
        seq = za if n == 0 else 1 - za
        part = keep[...] if n == 0 else got[...].astype(F32)
        n1, inv = norm_of(tokens[seq].astype(F32))
        a = part * gains[0:1, :]
        grad_tokens[seq] = grad_middle[aligned(seq, tok), :] + inv * (
            a - jnp.mean(a, -1, keepdims=True) - n1 * jnp.mean(a * n1, -1, keepdims=True)
        )


def far_kernel(keep, got, own, on_z, on_y, far_a, far_b):
    n = own.shape[0]
    for i, out in enumerate((own, on_z, on_y)):
        rows = pl.ds(i * n, n)
        out[...] = keep[rows, :] + got[rows, :].astype(F32)
    for i, out in enumerate((far_a, far_b)):
        rows = pl.ds(3 * n + i * (n // 2), n // 2)
        out[...] = (keep[rows, :] + got[rows, :].astype(F32)).astype(BF)


def near_kernel(on_z, on_y, got_a, got_b, send_z, send_y):
    n = got_a.shape[0]
    first, second = pl.ds(0, n), pl.ds(n, n)
    send_z[first, :] = (on_z[first, :] + got_a[...].astype(F32)).astype(BF)
    send_z[second, :] = on_z[second, :].astype(BF)
    send_y[first, :] = on_y[first, :].astype(BF)
    send_y[second, :] = (on_y[second, :] + got_b[...].astype(F32)).astype(BF)


def result_sum_kernel(middle, own, got_z, got_y, out):
    out[...] = (
        middle[...] + own[...] + got_z[...].astype(F32) + got_y[...].astype(F32)
    ).astype(BF)


def fold_kernel(at, keep, got, parts):
    x, y = at[0], at[3]
    rows = parts.shape[1]
    for n in range(4):
        here = pl.ds(n * rows, rows)
        z = x ^ (1 if n in (1, 3) else 0)
        w = y ^ (1 if n in (2, 3) else 0)
        parts[z * 2 + w] = (keep[here, :].astype(F32) + got[here, :].astype(F32)).astype(BF)


def stage(*values):
    return lax.optimization_barrier(values)


def grow(v, axis):
    return jnp.concatenate([v, swap(v, axis)], 0)


def half_swap(v, axis):
    return swap(pick(v, 1 - lax.axis_index(axis)), axis)


def fine_layer(
    tokens,
    cotangent,
    ln1_gain,
    ln1_bias,
    w_query,
    w_key,
    w_value,
    w_out,
    ln2_gain,
    ln2_bias,
    w_inner,
    w_outer,
):
    seqs, tok, width = tokens.shape
    rows = seqs * tok
    half = rows // 2
    per = w_query.shape[0]
    unit = w_outer.shape[0]
    hidden_units = 4 * unit
    all_rows = 8 * rows
    coords = jnp.stack([lax.axis_index(a) for a in ("x", "za", "zl", "y", "c")]).astype(jnp.int32)
    x, za = lax.axis_index("x"), lax.axis_index("za")
    cube, owners = ("x", "zl", "y"), ("x", "za", "zl", "y")
    cot = cotangent.reshape(rows, width)

    def split(axis, keep, got, shape):
        keep, got = keep.reshape(shape), got.reshape(shape)
        i = lax.axis_index(axis)
        mine = pick(keep, i, 1) + pick(got, i, 1).astype(F32)
        return mine, (pick(keep, 1 - i, 1) + pick(got, 1 - i, 1).astype(F32)).astype(BF)

    head_w, inner_w = call(
        pack_kernel,
        [((16, 3 * per + 16, HD), BF), ((8, per, hidden_units), BF)],
        [w_query, w_key, w_value]
        + [g.reshape(1, per) for g in (ln1_gain, ln1_bias, ln2_gain, ln2_bias)]
        + [w_inner],
        name="pack",
    )
    moved, head_w, inner_w, w_out, w_outer = stage(
        swap(pick(tokens, 1 - za), "za"), head_w, inner_w, w_out, w_outer
    )
    block = jnp.stack([pick(tokens, za), moved])
    on_x, on_z, on_y, head_w = stage(
        swap(block, "x"), swap(block, "zl"), swap(block, "y"), head_w
    )
    on_xz, on_xy, on_zy, on_xyz, head_w, w_out_z = stage(
        swap(on_x, "zl"),
        swap(on_y, "x"),
        swap(on_z, "y"),
        lax.ppermute(block, cube, [(i, 7 - i) for i in range(8)]),
        lax.all_to_all(head_w, owners, 0, 0, tiled=True),
        swap(after(w_out, on_x), "za"),
    )
    head_c, w_outer, inner_w, w_out_z = stage(swap(head_w, "c"), w_outer, inner_w, w_out_z)
    blocks = [block, on_y, on_z, on_zy, on_x, on_xy, on_xz, on_xyz]
    out_w = jnp.stack([w_out, w_out_z])
    h1, query, kv, gains, head_w = call(
        qkv_kernel,
        [
            ((16 * tok, width), BF),
            ((16 * tok, HD), BF),
            ((16 * tok, 2 * HD), BF),
            ((8, width), F32),
            ((width, 3 * HD), BF),
        ],
        blocks + [head_w, head_c],
        coords,
        name="qkv",
    )
    kv, query, out_x, outer_a, outer_l, inner_w = stage(
        kv,
        query,
        swap(out_w, "x"),
        swap(w_outer, "za"),
        swap(w_outer, "zl"),
        lax.all_to_all(inner_w, ("x", "y", "c"), 0, 0, tiled=True),
    )
    out_w = jnp.concatenate([out_w, out_x], 0)
    kv_other, out_w, inner_w = stage(swap(kv, "c"), out_w, inner_w)
    out, out_f, lse, query, kv, kv_other = call(
        fine_forward_kernel,
        [((16, tok, HD), BF), ((16 * tok, HD), F32), ((16 * tok, HD), F32)],
        [query, kv, kv_other],
        coords,
        save=(0, 1, 2),
        scratch=[pltpu.VMEM((2 * 16 * tok // TILE, TILE, TILE), F32)],
        name="attention_forward",
    )
    out, out_z, out_y, inner_a, inner_l, cot = stage(
        out,
        swap(out_w, "zl"),
        swap(out_w, "y"),
        swap(inner_w, "za"),
        swap(inner_w, "zl"),
        cot,
    )
    mixed, cot_z, cot_y, cot_c, out_zy, outer_la, inner_la, *out_c = stage(
        lax.all_to_all(out, owners, 0, 0, tiled=True),
        swap(cot, "x"),
        swap(cot, "y"),
        swap(cot, "c"),
        swap(out_z, "y"),
        swap(outer_a, "zl"),
        swap(inner_a, "zl"),
        swap(out_w, "c"),
        swap(out_z, "c"),
        swap(out_y, "c"),
    )
    (out_zyc,) = stage(swap(out_zy, "c"))
    pieces = [out_w, out_z, out_y, out_zy] + out_c + [out_zyc]
    mixed, middle, scaled, inverse, h2 = call(
        middle_kernel,
        [
            ((rows, width), BF),
            ((rows, width), F32),
            ((rows, width), F32),
            ((rows, HD), F32),
            ((rows, width), BF),
        ],
        [mixed, tokens, gains] + pieces,
        coords,
        raw=range(3, 11),
        scratch=[pltpu.VMEM((width, width), BF), pltpu.SemaphoreType.DMA((32,))],
        name="middle",
    )
    cot_z, cot_y = after(cot_z, h2), after(cot_y, h2)
    h2_z, h2_y, h2_c, cot_a, cot_b, cot_zc, cot_yc = stage(
        swap(h2, "x"),
        swap(h2, "y"),
        swap(h2, "c"),
        swap(cot_z[:half], "y"),
        swap(cot_y[half:], "x"),
        swap(cot_z, "c"),
        swap(cot_y, "c"),
    )
    h2_a, h2_b, h2_zc, h2_yc, cot_ac, cot_bc = stage(
        swap(h2_z[:half], "y"),
        swap(h2_y[half:], "x"),
        swap(h2_z, "c"),
        swap(h2_y, "c"),
        swap(cot_a, "c"),
        swap(cot_b, "c"),
    )
    h2_ac, h2_bc = stage(swap(h2_a, "c"), swap(h2_b, "c"))
    h2_all, cot_all, outer_w, hidden, grad_inner, keep, send = call(
        inner_kernel,
        [
            ((all_rows, width), BF, "raw"),
            ((all_rows, width), BF, "raw"),
            ((hidden_units, width), BF, "raw"),
            ((all_rows, hidden_units), BF),
            ((all_rows, hidden_units), BF),
            ((all_rows // 2, width), BF),
            ((all_rows // 2, width), BF),
        ],
        [h2, h2_z, h2_y, h2_a, h2_b, h2_c, h2_zc, h2_yc, h2_ac, h2_bc]
        + [cot, cot_z, cot_y, cot_a, cot_b, cot_c, cot_zc, cot_yc, cot_ac, cot_bc]
        + [p.reshape(2, 4 * per, hidden_units) for p in (inner_w, inner_l, inner_a, inner_la)]
        + [w_outer, outer_l, outer_a, outer_la],
        coords,
        raw=range(10, 28),
        scratch=[
            pltpu.VMEM((all_rows, width), BF),
            pltpu.VMEM((all_rows, width), BF),
            pltpu.VMEM((width, hidden_units), BF),
            pltpu.VMEM((hidden_units, width), BF),
            pltpu.SemaphoreType.DMA((25,)),
        ],
        name="inner",
    )

    (got,) = stage(swap(send, "c"))
    (parts,) = call(
        fold_kernel, [((4, rows, width), BF)], [keep, got], coords, name="fold"
    )
    n_in, n_out = 8 * per, unit
    inner_g, in_l, in_a, in_la = call(
        inner_grad_kernel,
        [((n_in, hidden_units), F32)] + [((n_in, hidden_units), BF)] * 3,
        [h2_all, grad_inner],
        coords,
        scratch=[pltpu.VMEM((width, hidden_units), F32)],
        name="inner_grad",
    )
    parts, inner_g, in_l, in_a, in_la = stage(parts, inner_g, in_l, in_a, in_la)
    outer_g, outer_l, outer_a, outer_la, res_keep, res_send = call(
        outer_grad_kernel,
        [((n_out, width), F32)]
        + [((n_out, width), BF)] * 3
        + [((all_rows // 2, width), F32), ((all_rows // 2, width), BF)],
        [after(hidden, in_l), cot_all, outer_w],
        coords,
        scratch=[pltpu.VMEM((hidden_units, width), F32)],
        name="outer_grad",
    )
    parts, in_l, in_a, outer_g, outer_l, outer_a, outer_la, res_keep, res_send, in_la = stage(
        lax.all_to_all(parts, ("x", "y"), 0, 0, tiled=True),
        swap(in_l, "zl"),
        swap(in_a, "za"),
        outer_g,
        outer_l,
        outer_a,
        outer_la,
        res_keep,
        res_send,
        in_la,
    )
    grad_middle, branch, go, sums_two = call(
        branch_kernel,
        [
            ((rows, width), F32),
            ((rows, width), BF),
            ((16, tok, HD), BF),
            ((2, width), F32),
        ],
        [parts, scaled, inverse, gains, cotangent] + pieces,
        coords,
        raw=range(5, 13),
        scratch=[pltpu.VMEM((width, width), BF), pltpu.SemaphoreType.DMA((32,))],
        name="branch",
    )
    go, branch, res_got, outer_l, outer_a = stage(
        go, branch, swap(res_send, "c"), outer_l, outer_a
    )
    res = (res_keep + res_got.astype(F32)).reshape(4, rows, width)
    far_a, far_b = res[3, :half].astype(BF), res[3, half:].astype(BF)
    out_keep, out_send = call(
        core_grad_kernel,
        [((width // 2, width), F32), ((width // 2, width), BF)],
        [mixed, branch],
        coords,
        scratch=[pltpu.VMEM((width, width), F32)],
        name="out_grad",
    )
    diagonal = [(i, 3 - i) for i in range(4)]
    go, outer_l, outer_a, in_la, outer_la, out_keep, out_send, res, far_a, far_b = stage(
        lax.all_to_all(go, owners, 0, 0, tiled=True),
        swap(outer_l, "zl"),
        swap(outer_a, "za"),
        in_la,
        outer_la,
        out_keep,
        out_send,
        res,
        far_a,
        far_b,
    )
    gq, keep, send = call(
        fine_backward_kernel,
        [((16 * tok, HD), BF), ((16 * tok, 2 * HD), F32), ((16 * tok, 2 * HD), BF)],
        [query, kv, kv_other, go, out_f, lse],
        coords,
        scratch=[pltpu.VMEM((16 * tok, 2 * HD), F32)],
        name="attention_backward",
    )
    gq, keep, send, got_a, got_b, out_got, in_la = stage(
        gq,
        keep,
        send,
        swap(far_a, "y"),
        swap(far_b, "x"),
        swap(out_send, "c"),
        lax.ppermute(in_la, ("za", "zl"), diagonal),
    )
    out_keep, out_send = split("x", out_keep, out_got, (1, 2, 8 * per, width))
    got, out_keep, out_send, outer_la = stage(swap(send, "c"), out_keep, out_send, outer_la)
    grads, parts, sums = call(
        partial_kernel,
        [
            ((16 * tok, 3 * HD), BF),
            ((8, 2, tok, width), BF),
            ((2, width), F32),
        ],
        blocks + [gq, keep, got, head_w],
        coords,
        raw=range(8),
        scratch=[pltpu.VMEM((16 * tok, width), BF), pltpu.SemaphoreType.DMA((16,))],
        name="partial",
    )
    grads, parts, sums, out_keep, out_got, outer_la = stage(
        grads,
        parts,
        sums,
        out_keep,
        swap(out_send, "x"),
        lax.ppermute(outer_la, ("za", "zl"), diagonal),
    )
    parts = lax.all_to_all(parts, cube, 0, 0, tiled=True)
    sums = jnp.concatenate([sums, sums_two], 0)
    sums = sums.reshape(4, 32, per).transpose(1, 0, 2).reshape(32, 4 * per)
    head_keep, head_send = call(
        head_grad_kernel,
        [((16, per + 16, 3 * HD), F32), ((16, per + 16, 3 * HD), BF)],
        [h1, grads, sums],
        coords,
        scratch=[pltpu.VMEM((width, 3 * HD), F32)],
        name="head_grad",
    )
    head_keep, head_send = stage(head_keep, head_send)
    out_keep, out_send = split(
        "y", out_keep, after(out_got, head_send), (4, 2, per, width)
    )
    inner_g = inner_g + after(in_l, head_send).astype(F32) + in_a.astype(F32) + in_la.astype(F32)
    inner_g = inner_g.astype(BF).reshape(4, 2, per, hidden_units)
    got_a = after(got_a, head_send)
    res_z = jnp.concatenate([res[1, :half] + got_a.astype(F32), res[1, half:]], 0).astype(BF)
    res_y = jnp.concatenate([res[2, :half], res[2, half:] + got_b.astype(F32)], 0).astype(BF)
    inner_own = pick(inner_g, lax.axis_index("c"), 1)
    inner_send = pick(inner_g, 1 - lax.axis_index("c"), 1)
    head_keep, head_got, out_keep, out_send, inner_own, inner_send, res_z, res_y = stage(
        head_keep, swap(head_send, "c"), out_keep, out_send, inner_own, inner_send, res_z, res_y
    )
    head_keep, head_send = split("za", head_keep, head_got, (2, 2, 4 * (per + 16), 3 * HD))
    head_keep, head_send, out_send = stage(head_keep, head_send, out_send)
    outer_g = (
        outer_g
        + after(outer_l, head_send).astype(F32)
        + outer_a.astype(F32)
        + outer_la.astype(F32)
    )
    head_keep, head_got, out_keep, out_got, inner_got, got_z, res_y, outer_g = stage(
        head_keep,
        swap(head_send, "za"),
        out_keep,
        swap(out_send, "y"),
        swap(inner_send, "c"),
        swap(res_z, "x"),
        res_y,
        outer_g,
    )
    inner_g = jnp.stack([inner_own, inner_got]).reshape(2, 2, 2, per, hidden_units)
    x = lax.axis_index("x")
    near_x, inner_send = pick(inner_g, x, 1), pick(inner_g, 1 - x, 1)
    (payload,) = call(
        payload_kernel,
        [((8, per + 16, 3 * HD), BF)],
        [head_keep, head_got],
        name="payload",
    )
    out_keep, out_send = split("za", out_keep, out_got, (1, 2, 2 * per, width))
    parts, payload, near_x, inner_send, out_keep, out_send = stage(
        parts, payload, near_x, inner_send, out_keep, out_send
    )
    payload = lax.all_to_all(payload, cube, 0, 0, tiled=True)
    total, send = call(
        total_kernel, [((tok, width), F32), ((tok, width), BF)], [parts], name="total"
    )
    total, send, near_x, inner_send, out_send, res_y = stage(
        total, send, near_x, inner_send, out_send, res_y
    )
    got, out_send, got_y, far_x, near_x = stage(
        swap(send, "za"),
        out_send,
        swap(res_y, "y"),
        swap(inner_send, "x"),
        near_x,
    )
    y = lax.axis_index("y")
    inner_send = jnp.stack([pick(near_x, 1 - y, 1), pick(far_x, 1 - y, 1)])
    near_x, far_x = pick(near_x, y, 1), pick(far_x, y, 1)
    (grad_tokens,) = call(
        input_kernel,
        [((seqs, tok, width), F32)],
        [total, got, tokens, grad_middle, gains],
        coords,
        name="input",
    )
    result = (
        middle + res[0] + after(got_z, got).astype(F32) + got_y.astype(F32)
    ).astype(BF)
    payload, out_got, grad_tokens, result, far_y, near_x, far_x = stage(
        payload,
        swap(out_send, "za"),
        grad_tokens,
        result,
        swap(inner_send, "y"),
        near_x,
        far_x,
    )
    out_keep, out_send = split("zl", out_keep, out_got, (1, 2, per, width))
    out_keep, out_send = stage(out_keep, out_send)
    query_g, key_g, value_g, *sums, inner_g = call(
        last_kernel,
        [((per, width), F32)] * 3
        + [((1, per), F32)] * 4
        + [((per, 8 * hidden_units), F32)],
        [payload, near_x, far_x, far_y],
        coords,
        name="last",
    )
    query_g, key_g, value_g, inner_g, out_got, result, *sums = stage(
        query_g, key_g, value_g, inner_g, swap(out_send, "zl"), result, *sums
    )
    sums = [v.reshape(per) for v in sums]
    return (
        result.reshape(seqs, tok, width),
        grad_tokens,
        sums[0],
        sums[1],
        query_g,
        key_g,
        value_g,
        out_keep[0] + out_got[0].astype(F32),
        sums[2],
        sums[3],
        inner_g,
        outer_g,
    )


def solution(mesh):
    blocks = mesh.shape["blk"]
    if blocks == 16:
        sizes = (2, 2, 1, 2, 2, 2)
        roles = (True, "za", ("x", "zl", "y"), ("c",), ("x", "za", "zl", "y"))
    else:
        sizes = (2, 8, blocks // 64, 2, 2, 2)
        roles = (False, "x", ("za",), ("zb", "zl", "y", "c"), ("x", "za"))
    fine = Mesh(mesh.devices.reshape(sizes), AXES)
    tok, row, vec = P(None, AXES, None), P(AXES, None), P(AXES)
    in_specs = (tok, tok, vec, vec, row, row, row, row, vec, vec, row, row)
    out_specs = (tok, tok, vec, vec, row, row, row, row, vec, vec, row, row)
    return jax.shard_map(
        fine_layer if blocks == 16 else functools.partial(on_device, roles),
        mesh=fine,
        in_specs=in_specs,
        out_specs=out_specs,
        check_vma=False,
    )
```

```python
import functools
import math

import jax
import jax.numpy as jnp
from jax import lax
from jax.experimental import pallas as pl
from jax.experimental.pallas import tpu as pltpu
from jax.sharding import Mesh
from jax.sharding import PartitionSpec as P

HD = 128
TILE = 256
SCALE = HD ** (-0.5)
MASKED = -1e30
eps_norm = 1e-05
gelu_coef = math.sqrt(2.0 / math.pi)
BF = jnp.bfloat16
F32 = jnp.float32
AXES = ("x", "za", "zb", "zl", "y", "c")
T_AXES = ("x", "za", "zb")
W_AXES = ("zl", "y", "c")


def mm(a, b):
    return jnp.dot(a, b, preferred_element_type=F32)


def mm_nt(a, b):
    return lax.dot_general(a, b, (((1,), (1,)), ((), ())), preferred_element_type=F32)


def mm_tn(a, b):
    return lax.dot_general(a, b, (((0,), (0,)), ((), ())), preferred_element_type=F32)


def norm_stats(values):
    centered = values - jnp.mean(values, -1, keepdims=True)
    inverse = lax.rsqrt(jnp.mean(centered * centered, -1, keepdims=True) + eps_norm)
    return centered * inverse, inverse


def norm_back(grad_normed, scaled, inverse, gain):
    g = grad_normed * gain
    return inverse * (
        g - jnp.mean(g, -1, keepdims=True) - scaled * jnp.mean(g * scaled, -1, keepdims=True)
    )


def swap(v, axis):
    return lax.ppermute(v, axis, [(0, 1), (1, 0)])


def pick(v, index, axis=0):
    return lax.dynamic_index_in_dim(v, index, axis, keepdims=False)


def pair_gather(v, axis):
    other = swap(v, axis)
    first = lax.axis_index(axis) == 0
    return jnp.stack([jnp.where(first, v, other), jnp.where(first, other, v)])


def pair_scatter(v, axis, dim):
    me = lax.axis_index(axis)
    return pick(v, me, dim) + swap(pick(v, 1 - me, dim).astype(BF), axis).astype(F32)


def after(v, *others):
    return lax.optimization_barrier((v,) + others)[0]


def t_gather(v):
    if lax.axis_size("za") * lax.axis_size("zb") != 2:
        return lax.all_gather(v, T_AXES, axis=0, tiled=False)
    x, z = lax.axis_index("x"), lax.axis_index("za")
    over_x, over_z = swap(v, "x"), swap(v, "za")
    out = jnp.zeros((4,) + v.shape, v.dtype)
    for part, at in (
        (v, 2 * x + z),
        (over_x, 2 * (1 - x) + z),
        (over_z, 2 * x + 1 - z),
        (swap(over_z, "x"), 2 * (1 - x) + 1 - z),
    ):
        out = lax.dynamic_update_index_in_dim(out, part, at, 0)
    return out


def t_scatter(v):
    if lax.axis_size("za") * lax.axis_size("zb") != 2:
        return lax.psum_scatter(v, T_AXES, scatter_dimension=0, tiled=False)
    v = pair_scatter(v.reshape((2, 2) + v.shape[1:]), "x", 0)
    return pair_scatter(v, "za", 0)


def plane_gather(v):
    half = v.shape[0] // 2
    a, b = v[:half], v[half:]
    a = jnp.stack([a, swap(a, "zl")])
    b = jnp.stack([b, swap(b, "y")])
    a = jnp.stack([a, swap(a, "y")])
    b = jnp.stack([b, swap(b, "zl")])
    both = jnp.stack([a, b])
    return jnp.stack([both, swap(both, "c")]).reshape(8 * v.shape[0], v.shape[1])


def plane_scatter(v):
    rows, width = v.shape
    v = v.reshape(2, 2, 2, 2, rows // 16, width)

    def fold(u, axis):
        return u[0] + swap(u[1].astype(BF), axis).astype(F32)

    v = fold(v, "c")
    a, b = v[0], v[1]
    a = fold(a, "y")
    b = fold(b, "zl")
    a = fold(a, "zl")
    b = fold(b, "y")
    return jnp.concatenate([a, b], 0)


def shares(count, body):
    if count <= 2:
        for k in range(count):
            body(k)
    else:
        lax.fori_loop(0, count, lambda k, c: (body(k), c)[1], 0)


def mask_of(count, q_tile, k_tile, q_share, k_share):
    rows = lax.broadcasted_iota(jnp.int32, (TILE, TILE), 0) + q_tile * TILE
    cols = lax.broadcasted_iota(jnp.int32, (TILE, TILE), 1) + k_tile * TILE
    q_pos = (lax.shift_right_logical(rows, 6) * count + q_share) * 64 + (rows & 63)
    k_pos = (lax.shift_right_logical(cols, 6) * count + k_share) * 64 + (cols & 63)
    return k_pos <= q_pos


def forward_kernel(count, meta, q_ref, k_ref, v_ref, o_ref, of_ref, lse_ref, qa, ka, va, s_ref):
    blocks = q_ref.shape[0]
    for j in range(blocks):
        slot = meta[j]
        rows = pl.ds(j * 64, 64)
        qa[rows, :] = q_ref[slot]

        def place(k, rows=rows, slot=slot):
            ka[k, rows, :] = k_ref[k, slot]
            va[k, rows, :] = v_ref[k, slot]

        shares(count, place)
    mine = meta[blocks]
    tiles = blocks * 64 // TILE
    for t in range(tiles):
        q = qa[pl.ds(t * TILE, TILE), :]
        top = jnp.full((TILE, 1), MASKED, F32)
        for u in range(t + 1):
            cols = pl.ds(u * TILE, TILE)

            def score(k, top, u=u, cols=cols):
                s = mm_nt(q, ka[k, cols, :]) * SCALE
                if u == t:
                    s = jnp.where(mask_of(count, t, u, mine, meta[blocks + 1 + k]), s, MASKED)
                s_ref[k * tiles + u] = s
                return jnp.maximum(top, jnp.max(s, -1, keepdims=True))

            if count <= 2:
                for k in range(count):
                    top = score(k, top)
            else:
                top = lax.fori_loop(0, count, score, top)
        total = jnp.zeros((TILE, 1), F32)
        for u in range(t + 1):

            def expo(k, total, u=u):
                p = jnp.exp(s_ref[k * tiles + u] - top)
                s_ref[k * tiles + u] = p
                return total + jnp.sum(p, -1, keepdims=True)

            if count <= 2:
                for k in range(count):
                    total = expo(k, total)
            else:
                total = lax.fori_loop(0, count, expo, total)
        inverse = 1.0 / total
        out = jnp.zeros((TILE, HD), F32)
        for u in range(t + 1):
            cols = pl.ds(u * TILE, TILE)

            def weigh(k, out, u=u, cols=cols):
                p = (s_ref[k * tiles + u] * inverse).astype(BF)
                return out + mm(p, va[k, cols, :])

            if count <= 2:
                for k in range(count):
                    out = weigh(k, out)
            else:
                out = lax.fori_loop(0, count, weigh, out)
        rows = pl.ds(t * TILE, TILE)
        of_ref[rows, :] = out
        o_ref[rows, :] = out.astype(BF)
        lse_ref[rows, :] = jnp.broadcast_to(top + jnp.log(total), (TILE, HD))


def attention_forward(count, meta, q, k, v):
    blocks = q.shape[0]
    rows = blocks * 64
    tiles = rows // TILE
    vm = pl.BlockSpec(memory_space=pltpu.VMEM)
    pairs = tiles * (tiles + 1) // 2 * count
    return pl.pallas_call(
        functools.partial(forward_kernel, count),
        in_specs=[pl.BlockSpec(memory_space=pltpu.SMEM), vm, vm, vm],
        out_specs=[vm] * 6,
        out_shape=[
            jax.ShapeDtypeStruct((rows, HD), BF),
            jax.ShapeDtypeStruct((rows, HD), F32),
            jax.ShapeDtypeStruct((rows, HD), F32),
            jax.ShapeDtypeStruct((rows, HD), BF),
            jax.ShapeDtypeStruct((count, rows, HD), BF),
            jax.ShapeDtypeStruct((count, rows, HD), BF),
        ],
        scratch_shapes=[pltpu.VMEM((count * tiles, TILE, TILE), F32)],
        cost_estimate=pl.CostEstimate(
            flops=pairs * TILE * TILE * HD * 4,
            bytes_accessed=rows * HD * 2 * (2 + 4 * count) + rows * HD * 8,
            transcendentals=pairs * TILE * TILE,
        ),
        compiler_params=pltpu.CompilerParams(vmem_limit_bytes=(16 if count <= 2 else 52) << 20),
        name="attention_forward",
    )(meta, q, k, v)


def backward_kernel(count, meta, q_ref, k_ref, v_ref, go_ref, of_ref, lse_ref, gq_ref, gk, gv):
    rows_all = q_ref.shape[0]
    blocks = rows_all // 64
    mine = meta[blocks]
    tiles = rows_all // TILE

    def zero(k):
        gk[k] = jnp.zeros((rows_all, HD), F32)
        gv[k] = jnp.zeros((rows_all, HD), F32)

    shares(count, zero)
    for t in range(tiles):
        rows = pl.ds(t * TILE, TILE)
        q = q_ref[rows, :]
        go = go_ref[rows, :]
        delta = jnp.sum(go.astype(F32) * of_ref[rows, :], -1, keepdims=True)
        lse = lse_ref[rows, :][:, :1]
        gq = jnp.zeros((TILE, HD), F32)
        for u in range(t + 1):
            cols = pl.ds(u * TILE, TILE)

            def one(k, gq, u=u, cols=cols):
                kk = k_ref[k, cols, :]
                p = jnp.exp(mm_nt(q, kk) * SCALE - lse)
                if u == t:
                    p = jnp.where(mask_of(count, t, u, mine, meta[blocks + 1 + k]), p, 0.0)
                gv[k, cols, :] += mm_tn(p.astype(BF), go)
                ds = (p * (mm_nt(go, v_ref[k, cols, :]) - delta)).astype(BF)
                gk[k, cols, :] += mm_tn(ds, q)
                return gq + mm(ds, kk)

            if count <= 2:
                for k in range(count):
                    gq = one(k, gq)
            else:
                gq = lax.fori_loop(0, count, one, gq)
        gq_ref[rows, :] = (gq * SCALE).astype(BF)

    def scale(k):
        gk[k] = gk[k] * SCALE

    shares(count, scale)


def attention_backward(count, meta, q, k, v, go, of, lse):
    rows = q.shape[0]
    tiles = rows // TILE
    vm = pl.BlockSpec(memory_space=pltpu.VMEM)
    pairs = tiles * (tiles + 1) // 2 * count
    return pl.pallas_call(
        functools.partial(backward_kernel, count),
        in_specs=[pl.BlockSpec(memory_space=pltpu.SMEM)] + [vm] * 6,
        out_specs=[vm] * 3,
        out_shape=[
            jax.ShapeDtypeStruct((rows, HD), BF),
            jax.ShapeDtypeStruct((count, rows, HD), F32),
            jax.ShapeDtypeStruct((count, rows, HD), F32),
        ],
        cost_estimate=pl.CostEstimate(
            flops=pairs * TILE * TILE * HD * 10,
            bytes_accessed=rows * HD * (16 + 12 * count),
            transcendentals=pairs * TILE * TILE,
        ),
        compiler_params=pltpu.CompilerParams(vmem_limit_bytes=(16 if count <= 2 else 52) << 20),
        name="attention_backward",
    )(meta, q, k, v, go, of, lse)


def reorder_kernel(meta, g_ref, out_ref):
    for j in range(g_ref.shape[0]):
        out_ref[meta[j]] = g_ref[j]


def reorder(meta, g):
    vm = pl.BlockSpec(memory_space=pltpu.VMEM)
    return pl.pallas_call(
        reorder_kernel,
        in_specs=[pl.BlockSpec(memory_space=pltpu.SMEM), vm],
        out_specs=vm,
        out_shape=jax.ShapeDtypeStruct(g.shape, g.dtype),
        cost_estimate=pl.CostEstimate(flops=0, bytes_accessed=4 * g.size, transcendentals=0),
        compiler_params=pltpu.CompilerParams(vmem_limit_bytes=8 << 20),
        name="reorder",
    )(meta, g)


def on_device(
    roles,
    tokens,
    cotangent,
    ln1_gain,
    ln1_bias,
    w_query,
    w_key,
    w_value,
    w_out,
    ln2_gain,
    ln2_bias,
    w_inner,
    w_outer,
):
    small, seq_axis, hd_axes, sh_axes, own_axes = roles
    planes = math.prod(lax.axis_size(a) for a in T_AXES)
    count = math.prod(lax.axis_size(a) for a in sh_axes)
    devices = 8 * planes
    seqs, tok, width = tokens.shape
    rows = seqs * tok
    per = w_query.shape[0]
    unit = w_outer.shape[0]
    seq = lax.axis_index(seq_axis)
    share = lax.axis_index(sh_axes)

    block = jnp.stack([pick(tokens, seq), swap(pick(tokens, 1 - seq), seq_axis)])
    if small:
        on_x, on_z, on_y = (swap(block, a) for a in hd_axes)
        on_xz, on_xy, on_zy = swap(on_x, "zl"), swap(on_y, "x"), swap(on_z, "y")
        on_xyz = swap(on_xz, "y")
        seen = jnp.stack([block, on_y, on_z, on_zy, on_x, on_xy, on_xz, on_xyz])
    else:
        seen = lax.all_gather(block, hd_axes, axis=0, tiled=False)
    at = jnp.arange(16, dtype=jnp.int32)
    if small:
        at_x, at_za, at_zl, at_y = at // 8, at // 4 % 2, at // 2 % 2, at % 2
        x, zl, y = (lax.axis_index(a) for a in hd_axes)
        slots = ((at_x ^ x) * 4 + (at_zl ^ zl) * 2 + (at_y ^ y)) * 2 + (at_za ^ seq)
    else:
        slots = at % 8 * 2 + (at // 8 ^ seq)

    gains = jnp.concatenate([ln1_gain, ln1_bias, ln2_gain, ln2_bias])
    gains = jnp.broadcast_to(jnp.pad(gains, (0, HD - gains.shape[0])), (8, 1, HD))
    head_w = jnp.stack([w_query, w_key, w_value]).reshape(3, per, 8, HD).transpose(2, 0, 1, 3)
    head_w = jnp.concatenate([head_w.reshape(8, 3 * per, HD), gains], 1)
    head_w = lax.all_to_all(head_w, hd_axes, 0, 0, tiled=True)
    head_w = pair_gather(head_w, seq_axis)
    for axis in reversed(sh_axes):
        if lax.axis_size(axis) == 2:
            head_w = pair_gather(head_w, axis)
        else:
            head_w = lax.all_gather(head_w, axis, axis=0, tiled=False)
    if small:
        head_w = head_w.reshape(2, 2, 2, 4, 3 * per + 1, HD).transpose(2, 1, 3, 0, 4, 5)
    else:
        head_w = head_w.reshape(count, 16, 3 * per + 1, HD).transpose(1, 0, 2, 3)
    head_w = head_w.reshape(devices, 3 * per + 1, HD)
    gains = head_w[:, -1, : 4 * per].reshape(devices, 4, per).transpose(1, 0, 2)
    gains = gains.reshape(4, width).astype(F32)
    gain_one, bias_one, gain_two, bias_two = gains[0], gains[1], gains[2], gains[3]
    head_w = head_w[:, :-1].reshape(devices, 3, per, HD).transpose(0, 2, 1, 3)
    head_w = head_w.reshape(width, 3 * HD)

    inner_w = w_inner.reshape(per, planes, 8, unit).transpose(2, 0, 1, 3)
    inner_w = lax.all_to_all(inner_w.reshape(8, per, planes * unit), W_AXES, 0, 0, tiled=True)
    inner_w = t_gather(after(inner_w, seen)).reshape(width, planes * unit)
    outer_w = t_gather(w_outer).reshape(planes * unit, width)
    grad_plane = plane_gather(after(cotangent, seen).reshape(rows, width))

    out_w = lax.all_gather(w_out, AXES, axis=0, tiled=True)
    qkv_w = jnp.concatenate([w_query, w_key, w_value], 1)
    qkv_w = lax.all_gather(after(qkv_w, seen), AXES, axis=0, tiled=True)

    normed, _ = norm_stats(seen.reshape(-1, width).astype(F32))
    h1 = (normed * gain_one + bias_one).astype(BF)
    qkv = mm(h1, head_w).astype(BF)
    query = qkv[:, :HD].reshape(16, tok, HD)
    kv = qkv[:, HD:]
    if count == 2:
        kv = jnp.stack([kv, swap(kv, "c")])
        order = jnp.stack([share, 1 - share])
    else:
        kv = lax.all_gather(kv, sh_axes, axis=0, tiled=False)
        order = jnp.arange(count)
    kv = kv.reshape(count, 16, tok, 2 * HD)
    meta = jnp.concatenate([slots, share.reshape(1), order]).astype(jnp.int32)
    out, out_f, lse, q_at, k_at, v_at = attention_forward(
        count, meta, query, kv[..., :HD], kv[..., HD:]
    )

    def to_tokens(v):
        v = lax.all_to_all(v, own_axes, 0, 0, tiled=True)
        n = v.shape[-1] // HD
        if small:
            v = v.reshape(2, 2, 4, tok, n, HD).transpose(1, 3, 4, 0, 2, 5)
        else:
            v = v.reshape(2, 8, tok, n, HD).transpose(0, 2, 3, 1, 4)
        return v.reshape(2, tok, n, 8 * HD)

    mixed = to_tokens(out.reshape(16, tok, HD)).reshape(rows, width)
    flat_in = tokens.reshape(rows, width).astype(F32)
    middle = flat_in + mm(mixed, out_w)
    scaled_two, inverse_two = norm_stats(middle)
    h2 = plane_gather((scaled_two * gain_two + bias_two).astype(BF))

    inner = mm(h2, inner_w)
    bent = jnp.tanh(gelu_coef * (inner + 0.044715 * inner * inner * inner))
    hidden = (0.5 * inner * (1.0 + bent)).astype(BF)
    slope = 0.5 * (1.0 + bent) + 0.5 * inner * (1.0 - bent * bent) * gelu_coef * (
        1.0 + 3.0 * 0.044715 * inner * inner
    )
    grad_inner = (mm_nt(grad_plane, outer_w) * slope).astype(BF)
    grad_h2 = plane_scatter(mm_nt(grad_inner, inner_w))
    grad_outer = mm_tn(hidden, grad_plane).reshape(planes, unit, width)
    grad_outer = t_scatter(grad_outer)
    grad_in = mm_tn(h2, grad_inner).reshape(planes, 8 * per, planes * unit)
    grad_in = t_scatter(grad_in).astype(BF).reshape(8, per, planes * unit)
    result = plane_scatter(mm(hidden, outer_w))

    grad_out = cotangent.reshape(rows, width).astype(F32)
    grad_middle = grad_out + norm_back(grad_h2, scaled_two, inverse_two, gain_two)
    branch = grad_middle.astype(BF)
    go = mm_nt(branch, out_w).astype(BF)
    if small:
        go = go.reshape(2, tok, 2, 4, HD).transpose(2, 0, 3, 1, 4)
    else:
        go = go.reshape(2, tok, 8, HD).transpose(0, 2, 1, 3)
    go = lax.all_to_all(go.reshape(16, tok, HD), own_axes, 0, 0, tiled=True)
    go = go.reshape(16 * tok, HD)

    gq, gk, gv = attention_backward(count, meta, q_at, k_at, v_at, go, out_f, lse)
    gkv = jnp.concatenate([gk, gv], -1)
    if count == 2:
        gkv = gkv[0] + swap(gkv[1].astype(BF), "c").astype(F32)
    else:
        gkv = lax.psum_scatter(gkv, sh_axes, scatter_dimension=0, tiled=False)
    grads = jnp.concatenate([gq, gkv.astype(BF)], -1).reshape(16, tok, 3 * HD)
    grads, result, grad_in, grad_outer = lax.optimization_barrier(
        (grads, result, grad_in, grad_outer)
    )
    back = to_tokens(grads).reshape(rows, 3 * width)
    result = (middle + result).astype(BF)
    grad_in = lax.all_to_all(after(grad_in, back), W_AXES, 0, 0, tiled=True)
    grad_in = grad_in.reshape(8, per, planes, unit).transpose(1, 2, 0, 3)
    grad_in = grad_in.reshape(per, devices * unit).astype(F32)

    head_g = mm_tn(h1, reorder(meta, grads).reshape(16 * tok, 3 * HD))
    head_g = head_g.reshape(tuple(lax.axis_size(a) for a in AXES) + (per, 3 * HD))
    dims = list(AXES)
    for axis in sh_axes[::-1] + (seq_axis,):
        dim = dims.index(axis)
        dims.remove(axis)
        if lax.axis_size(axis) == 2:
            head_g = pair_scatter(head_g, axis, dim)
        else:
            head_g = lax.psum_scatter(head_g, axis, scatter_dimension=dim, tiled=False)
    head_g = head_g.astype(BF).reshape(8, per, 3 * HD)
    head_g = lax.all_to_all(head_g, hd_axes, 0, 0, tiled=True)
    head_g = head_g.reshape(8, per, 3, HD).transpose(2, 1, 0, 3).reshape(3, per, width)
    head_g = head_g.astype(F32)

    grad_out_w = mm_tn(mixed, branch).reshape(planes, 2, 2, 2, per, width)
    grad_out_w = pair_scatter(grad_out_w, "c", 3)
    grad_out_w = pair_scatter(grad_out_w, "y", 2)
    grad_out_w = pair_scatter(grad_out_w, "zl", 1)
    grad_out_w = t_scatter(grad_out_w)

    scaled_one, inverse_one = norm_stats(flat_in)
    grad_h1 = mm_nt(back, qkv_w)
    grad_input = grad_middle + norm_back(grad_h1, scaled_one, inverse_one, gain_one)

    sums = jnp.stack(
        [
            jnp.sum(grad_h1 * scaled_one, 0),
            jnp.sum(grad_h1, 0),
            jnp.sum(grad_h2 * scaled_two, 0),
            jnp.sum(grad_h2, 0),
        ]
    )
    sums = sums.reshape(4, devices, per).transpose(1, 0, 2).reshape(devices, 4 * per)
    sums = lax.all_to_all(sums, AXES, 0, 0, tiled=True)
    sums = jnp.sum(sums, 0).reshape(4, per)
    return (
        result.reshape(seqs, tok, width),
        grad_input.reshape(seqs, tok, width),
        sums[0],
        sums[1],
        head_g[0],
        head_g[1],
        head_g[2],
        grad_out_w,
        sums[2],
        sums[3],
        grad_in,
        grad_outer,
    )


class Arriving:
    def __init__(self, ref, copy):
        self.ref, self.copy = ref, copy
        self.shape, self.dtype = ref.shape, ref.dtype

    def __getitem__(self, index):
        if self.copy is not None:
            self.copy.wait()
            self.copy = None
        return self.ref[index]


class Leaving:
    def __init__(self, ref, target, move):
        self.ref, self.target, self.move, self.pushed = ref, target, move, False
        self.shape, self.dtype = ref.shape, ref.dtype

    def __getitem__(self, index):
        return self.ref[index]

    def __setitem__(self, index, value):
        self.ref[index] = value

    def push(self, rows=None):
        self.pushed = True
        if rows is None:
            self.move(self.ref, self.target)
        else:
            self.move(self.ref.at[rows], self.target.at[rows])


def call(kernel, outs, ins, coords=None, raw=(), save=(), scratch=(), eager=False, name=None):
    hbm = pl.BlockSpec(memory_space=pltpu.HBM)
    outs = [tuple(o) + ("far",) * (3 - len(o)) for o in outs]
    far = [i for i in range(len(ins)) if i not in raw]
    lead = 0 if coords is None else 1
    late = [i for i, o in enumerate(outs) if o[2] == "far"]
    extra = [pltpu.VMEM(ins[i].shape, ins[i].dtype) for i in far]
    extra += [pltpu.VMEM(outs[i][0], outs[i][1]) for i in late]
    extra.append(pltpu.SemaphoreType.DMA((len(far) + 4 * len(late) + len(save),)))
    count_in, count_out = len(ins), len(outs) + len(save)

    def body(*refs):
        front, refs = refs[:lead], refs[lead:]
        got, put = list(refs[:count_in]), list(refs[count_in : count_in + count_out])
        work = refs[count_in + count_out :]
        own, work = work[: len(scratch)], work[len(scratch) :]
        started = []

        def move(source, target):
            copy = pltpu.make_async_copy(source, target, work[-1].at[len(started)])
            copy.start()
            started.append(copy)
            return copy

        for n, i in enumerate(far):
            got[i] = Arriving(work[n], move(got[i], work[n]))
        leaving = []
        for n, i in enumerate(save):
            got[i].copy.wait()
            got[i].copy = None
            leaving.append(move(got[i].ref, put[len(outs) + n]))
        if eager:
            for i in far:
                got[i].copy.wait()
                got[i].copy = None
        inside = put[: len(outs)]
        for n, i in enumerate(late):
            inside[i] = Leaving(
                work[len(far) + n], put[i], lambda a, b: leaving.append(move(a, b))
            )
        kernel(*front, *got, *inside, *own)
        for i in late:
            if not inside[i].pushed:
                inside[i].push()
        for i in far:
            if got[i].copy is not None:
                got[i].copy.wait()
        for copy in leaving:
            copy.wait()

    specs = [hbm] * len(ins)
    if coords is not None:
        specs = [pl.BlockSpec(memory_space=pltpu.SMEM)] + specs
    saved = [jax.ShapeDtypeStruct(ins[i].shape, ins[i].dtype) for i in save]
    return pl.pallas_call(
        body,
        in_specs=specs,
        out_specs=[hbm] * count_out,
        out_shape=[jax.ShapeDtypeStruct(o[0], o[1]) for o in outs] + saved,
        scratch_shapes=list(scratch) + extra,
        cost_estimate=pl.CostEstimate(flops=0, bytes_accessed=0, transcendentals=0),
        compiler_params=pltpu.CompilerParams(vmem_limit_bytes=58 << 20),
        name=name,
    )(*([] if coords is None else [coords]), *ins)


def aligned(index, size):
    if isinstance(index, int):
        return pl.ds(index * size, size)
    return pl.ds(pl.multiple_of(index * size, size), size)


def pack_kernel(wq, wk, wv, g1, b1, g2, b2, w_inner, head, inner):
    per = wq.shape[0]
    gains = jnp.concatenate([g1[...], b1[...], g2[...], b2[...]], 1)
    for d in range(16):
        cols = pl.ds(((d >> 3) * 4 + (d & 3)) * HD, HD)
        for n, w in enumerate((wq, wk, wv)):
            head[d, pl.ds(n * per, per), :] = w[:, cols]
        head[d, pl.ds(3 * per, 16), :] = jnp.broadcast_to(gains, (16, HD))
    for w in range(8):
        for t in range(4):
            p = (w >> 2) * 16 + t * 4 + (w & 3)
            inner[w, :, pl.ds(t * HD, HD)] = w_inner[:, pl.ds(p * HD, HD)]


def norm_of(values):
    centered = values - jnp.mean(values, -1, keepdims=True)
    inverse = lax.rsqrt(jnp.mean(centered * centered, -1, keepdims=True) + eps_norm)
    return centered * inverse, inverse


def qkv_kernel(at, *refs):
    blocks, pieces = refs[:8], refs[8:10]
    h1, query, kv, gains, weights = refs[10:]
    x, za, zl, y, c = (at[i] for i in range(5))
    width = h1.shape[1]
    per = width // 32
    got = jnp.concatenate([p[d, 3 * per : 3 * per + 1, :] for p in pieces for d in range(16)], 0)
    line = lax.broadcasted_iota(jnp.int32, (32, width), 0)
    lane = lax.broadcasted_iota(jnp.int32, (32, width), 1)
    owner = (line & 15) * 2 + (c ^ (line >> 4))
    mine = lax.shift_right_logical(lane, 5) == owner
    source = lax.broadcasted_iota(jnp.int32, (HD, width), 0)
    target = lax.broadcasted_iota(jnp.int32, (HD, width), 1)
    for k in range(4):
        spread = jnp.where(source == k * per + (target & (per - 1)), 1.0, 0.0).astype(BF)
        gains[k : k + 1, :] = jnp.sum(jnp.where(mine, mm(got, spread), 0.0), 0, keepdims=True)
    gain, bias = gains[0:1, :], gains[1:2, :]
    for n, block in enumerate(blocks):
        xx, zz, yy = x ^ (n >> 2), zl ^ (n >> 1 & 1), y ^ (n & 1)
        for s in range(2):
            j = xx * 8 + (za ^ s) * 4 + zz * 2 + yy
            normed, _ = norm_of(block[s].astype(F32))
            h1[aligned(j, 64), :] = (normed * gain + bias).astype(BF)
    h1.push()
    for n, piece in enumerate(pieces):
        for d in range(16):
            for i in range(3):
                weights[aligned(2 * d + (c ^ n), per), pl.ds(i * HD, HD)] = piece[
                    d, pl.ds(i * per, per), :
                ]
    weights.push()
    for t in range(h1.shape[0] // TILE):
        rows = pl.ds(t * TILE, TILE)
        out = mm(h1[rows, :], weights[...]).astype(BF)
        query[rows, :] = out[:, :HD]
        kv[rows, :] = out[:, HD:]
        query.push(rows)
        kv.push(rows)


def causal(q_share, k_share):
    rows = lax.broadcasted_iota(jnp.int32, (TILE, TILE), 0)
    cols = lax.broadcasted_iota(jnp.int32, (TILE, TILE), 1)
    q_pos = (lax.shift_right_logical(rows, 6) * 2 + q_share) * 64 + (rows & 63)
    k_pos = (lax.shift_right_logical(cols, 6) * 2 + k_share) * 64 + (cols & 63)
    return k_pos <= q_pos


def causal_t(q_share, k_share):
    rows = lax.broadcasted_iota(jnp.int32, (TILE, TILE), 0)
    cols = lax.broadcasted_iota(jnp.int32, (TILE, TILE), 1)
    k_pos = (lax.shift_right_logical(rows, 6) * 2 + k_share) * 64 + (rows & 63)
    q_pos = (lax.shift_right_logical(cols, 6) * 2 + q_share) * 64 + (cols & 63)
    return k_pos <= q_pos


def fine_forward_kernel(at, query, own, other, out, out_f, lse, s_ref):
    tiles = query.shape[0] // TILE
    c = at[4]
    both = (own, other)

    def tile(t, carry):
        rows = aligned(t, TILE)
        q = query[rows, :]

        def score(u, top, masked):
            for n in range(2):
                s = mm_nt(q, both[n][aligned(u, TILE), pl.ds(0, HD)]) * SCALE
                if masked:
                    s = jnp.where(causal(c, c if n == 0 else 1 - c), s, MASKED)
                s_ref[u * 2 + n] = s
                top = jnp.maximum(top, jnp.max(s, -1, keepdims=True))
            return top

        top = jnp.full((TILE, 1), MASKED, F32)
        for u in range(t + 1):
            top = score(u, top, u == t)

        total = jnp.zeros((TILE, 1), F32)
        acc = jnp.zeros((TILE, HD), F32)
        for u in range(t + 1):
            for n in range(2):
                p = jnp.exp(s_ref[u * 2 + n] - top)
                total = total + jnp.sum(p, -1, keepdims=True)
                acc = acc + mm(p.astype(BF), both[n][aligned(u, TILE), pl.ds(HD, HD)])
        acc = acc * (1.0 / total)
        out_f[rows, :] = acc
        out[pl.ds(t * (TILE // 64), TILE // 64)] = acc.astype(BF).reshape(TILE // 64, 64, HD)
        lse[rows, :] = jnp.broadcast_to(top + jnp.log(total), (TILE, HD))
        out.push(pl.ds(t * (TILE // 64), TILE // 64))
        out_f.push(rows)
        lse.push(rows)
        return carry

    for t in range(tiles):
        tile(t, 0)


def place_w_out(at, pieces, out_w, sems):
    x, za, zl, y, c = (at[i] for i in range(5))
    copies = []
    for n, piece in enumerate(pieces):
        side = (zl ^ (n & 1)) * 4 + (y ^ (n >> 1 & 1)) * 2 + (c ^ (n >> 2))
        for i in range(4):
            p = (x ^ (i >> 1)) * 16 + (za ^ (i & 1)) * 8 + side
            copies.append(
                pltpu.make_async_copy(
                    piece.at[i], out_w.at[aligned(p, piece.shape[1]), :], sems.at[len(copies)]
                )
            )
            copies[-1].start()
    return copies


def middle_kernel(at, got, tokens, gains, *refs):
    pieces, (mixed, middle, scaled, inverse, h2, out_w, sems) = refs[:8], refs[8:]
    copies = place_w_out(at, pieces, out_w, sems)
    rows, width = middle.shape
    tok = rows // 2
    for s in range(16):
        head = (s >> 3) * 4 + (s & 3)
        mixed[pl.ds((s >> 2 & 1) * tok, tok), pl.ds(head * HD, HD)] = got[s]
    for s in range(2):
        middle[pl.ds(s * tok, tok), :] = tokens[s].astype(F32)
    for copy in copies:
        copy.wait()
    mixed.push()
    middle[...] += mm(mixed[...], out_w[...])
    middle.push()
    normed, inv = norm_of(middle[...])
    scaled[...] = normed
    inverse[...] = jnp.broadcast_to(inv, (rows, HD))
    h2[...] = (normed * gains[2:3, :] + gains[3:4, :]).astype(BF)


def inner_kernel(at, *refs):
    h2_parts, cot_parts, in_parts, out_parts = refs[:10], refs[10:20], refs[20:24], refs[24:28]
    h2_out, cot_out, outer_out, hidden, grad_inner, keep, send = refs[28:35]
    h2, cot, w_in, w_outer, sems = refs[35:]
    za, zl = at[1], at[2]
    copies = []

    def move(source, target):
        copy = pltpu.make_async_copy(source, target, sems.at[len(copies)])
        copy.start()
        copies.append(copy)

    for n in range(4):
        t = (za ^ (n >> 1)) * 2 + (zl ^ (n & 1))
        for i in range(2):
            rows = in_parts[n].shape[1]
            move(in_parts[n].at[i], w_in.at[aligned(i * 4 + t, rows), :])
    for n in range(4):
        t = (za ^ (n >> 1)) * 2 + (zl ^ (n & 1))
        move(out_parts[n], w_outer.at[aligned(t, out_parts[n].shape[0]), :])
    row = 0
    for part in cot_parts:
        move(part, cot.at[pl.ds(row, part.shape[0]), :])
        row += part.shape[0]
    row = 0
    for part in h2_parts:
        h2[pl.ds(row, part.shape[0]), :] = part[...]
        row += part.shape[0]
    for copy in copies[:8]:
        copy.wait()
    first = mm(h2[pl.ds(0, TILE), :], w_in[...])
    for copy in copies[8:22]:
        copy.wait()
    arrived = 22
    move(h2, h2_out)
    move(cot, cot_out)
    move(w_outer, outer_out)
    half = h2.shape[0] // 2

    def tile(t, carry):
        rows = aligned(t, TILE)
        u = first if t == 0 else mm(h2[rows, :], w_in[...])
        squared = u * u
        bent = jnp.tanh(gelu_coef * (u + 0.044715 * squared * u))
        hidden[rows, :] = (0.5 * u * (1.0 + bent)).astype(BF)
        slope = 0.5 * (1.0 + bent) + 0.5 * u * (1.0 - bent * bent) * gelu_coef * (
            1.0 + 3.0 * 0.044715 * squared
        )
        grad = (mm_nt(cot[rows, :], w_outer[...]) * slope).astype(BF)
        grad_inner[rows, :] = grad
        hidden.push(rows)
        grad_inner.push(rows)
        return mm_nt(grad, w_in[...]), carry

    for out, first_tile in ((keep, 0), (send, half // TILE)):
        for t in range(2):
            rows = pl.ds(t * TILE, TILE)
            out[rows, :] = tile(first_tile + t, 0)[0].astype(BF)
            out.push(rows)
    for copy in copies[arrived:]:
        copy.wait()


def transposed_product(big, left, right, tile=TILE):
    left[0:8, :], right[0:8, :]

    def one(i, carry):
        cols = pl.ds(pl.multiple_of(i * tile, tile), tile)
        big[cols, :] = mm_tn(left[:, cols], right[...])
        return carry

    lax.fori_loop(0, left.shape[1] // tile, one, 0)


def others_of(at):
    za, zl = at[1], at[2]
    return za * 2 + zl, za * 2 + 1 - zl, 2 - 2 * za + zl, 3 - 2 * za - zl


def inner_grad_kernel(at, h2, grad_inner, own, to_l, to_a, to_la, big):
    transposed_product(big, h2, grad_inner)
    n = own.shape[0] // 2
    for t, out in zip(others_of(at), (own, to_l, to_a, to_la)):
        for i in range(2):
            out[pl.ds(i * n, n), :] = big[aligned(i * 4 + t, n), :].astype(out.dtype)


def outer_grad_kernel(at, hidden, cot, w_outer, own, to_l, to_a, to_la, keep, send, big):
    half = keep.shape[0]
    send[...] = mm(hidden[pl.ds(half, half), :], w_outer[...]).astype(BF)
    keep[...] = mm(hidden[pl.ds(0, half), :], w_outer[...])
    transposed_product(big, hidden, cot)
    n = own.shape[0]
    for t, out in zip(others_of(at), (own, to_l, to_a, to_la)):
        out[...] = big[aligned(t, n), :].astype(out.dtype)


def payload_kernel(head_keep, head_got, payload):
    m = head_keep.shape[1] // 4
    for d in range(8):
        rows = pl.ds((d & 3) * m, m)
        payload[d] = (head_keep[d >> 2, rows, :] + head_got[d >> 2, rows, :].astype(F32)).astype(BF)


def last_kernel(
    at, got, near_x, far_x, far_y, query, key, value, sum_a, sum_b, sum_c, sum_d, inner_g
):
    x, y, c = at[0], at[3], at[4]
    per = query.shape[0]
    for w in range(4):
        part = ((near_x, far_x)[w >> 1])[...] if w & 1 == 0 else far_y[w >> 1]
        for s in range(2):
            side = (x ^ (w >> 1)) * 16 + (y ^ (w & 1)) * 2 + (c ^ s)
            for t in range(part.shape[2] // HD):
                inner_g[:, aligned(t * 4 + side, HD)] = part[s, :, t * HD : (t + 1) * HD].astype(F32)
    inner_g.push()
    total = got[0, pl.ds(per, 16), pl.ds(0, HD)].astype(F32)
    for h in range(8):
        for n, out in enumerate((query, key, value)):
            out[:, pl.ds(h * HD, HD)] = got[h, pl.ds(0, per), pl.ds(n * HD, HD)].astype(F32)
        if h:
            total = total + got[h, pl.ds(per, 16), pl.ds(0, HD)].astype(F32)
    for n, out in enumerate((sum_a, sum_b, sum_c, sum_d)):
        out[...] = total[0:1, n * per : (n + 1) * per]


def branch_kernel(at, parts, scaled, inverse, gains, cot, *refs):
    pieces, (grad_middle, branch, go, sums, out_w, sems) = refs[:8], refs[8:]
    copies = place_w_out(at, pieces, out_w, sems)
    rows, width = scaled.shape
    tok = rows // 2
    grad = parts[0].astype(F32)
    for n in range(1, 4):
        grad = grad + parts[n].astype(F32)
    n2 = scaled[...]
    sums[0:1, :] = jnp.sum(grad * n2, 0, keepdims=True)
    sums[1:2, :] = jnp.sum(grad, 0, keepdims=True)
    a = grad * gains[2:3, :]
    grad = inverse[:, 0:1] * (
        a - jnp.mean(a, -1, keepdims=True) - n2 * jnp.mean(a * n2, -1, keepdims=True)
    )
    for s in range(2):
        part = pl.ds(s * tok, tok)
        grad_middle[part, :] = cot[s].astype(F32) + grad[s * tok : (s + 1) * tok]
    grad_middle.push()
    branch[...] = grad_middle[...].astype(BF)
    branch.push()
    for copy in copies:
        copy.wait()
    out = mm_nt(branch[...], out_w[...]).astype(BF)
    for s in range(16):
        head = (s >> 3) * 4 + (s & 3)
        seq = s >> 2 & 1
        go[s] = out[seq * tok : (seq + 1) * tok, head * HD : (head + 1) * HD]


def fine_backward_kernel(at, query, own, other, go_ref, out_f, lse_ref, gq_ref, keep, send, acc):
    rows_all = query.shape[0]
    tiles = rows_all // TILE
    c = at[4]
    both = (own, other)
    keep[...] = jnp.zeros(keep.shape, keep.dtype)
    acc[...] = jnp.zeros_like(acc)
    totals = (keep, acc)
    key_t = {}
    for t in range(tiles):
        rows = pl.ds(t * TILE, TILE)
        q = query[rows, :]
        go = go_ref[pl.ds(t * (TILE // 64), TILE // 64)].reshape(TILE, HD)
        lse = jnp.transpose(lse_ref[rows, :])[0:1, :]
        delta = jnp.sum(go.astype(F32) * out_f[rows, :], -1, keepdims=True)
        delta = jnp.transpose(jnp.broadcast_to(delta, (TILE, HD)))[0:1, :]
        gq = jnp.zeros((HD, TILE), F32)
        for u in range(t + 1):
            cols = pl.ds(u * TILE, TILE)
            for n in range(2):
                kk, vv = both[n][cols, pl.ds(0, HD)], both[n][cols, pl.ds(HD, HD)]
                if u == t:
                    key_t[u, n] = jnp.transpose(kk.astype(F32)).astype(BF)
                p = jnp.exp(mm_nt(kk, q) * SCALE - lse)
                if u == t:
                    p = jnp.where(causal_t(c, c if n == 0 else 1 - c), p, 0.0)
                totals[n][cols, pl.ds(HD, HD)] += mm(p.astype(BF), go)
                ds = (p * (mm_nt(vv, go) - delta)).astype(BF)
                totals[n][cols, pl.ds(0, HD)] += mm(ds, q)
                gq = gq + mm(key_t[u, n], ds)
        gq_ref[rows, :] = (jnp.transpose(gq) * SCALE).astype(BF)
        gq_ref.push(rows)
    send[:, :HD] = (acc[:, :HD] * SCALE).astype(BF)
    send[:, HD:] = acc[:, HD:].astype(BF)
    send.push()
    keep[:, :HD] = keep[:, :HD] * SCALE


def partial_kernel(at, *refs):
    blocks, (gq, keep, got, weights) = refs[:8], refs[8:12]
    grads, parts, sums, tokens, sems = refs[12:]
    x, za, zl, y = (at[i] for i in range(4))
    copies = []
    for n in range(8):
        for s in range(2):
            j = (x ^ (n >> 2)) * 8 + (za ^ s) * 4 + (zl ^ (n >> 1 & 1)) * 2 + (y ^ (n & 1))
            copies.append(
                pltpu.make_async_copy(
                    blocks[n].at[s], tokens.at[aligned(j, 64), :], sems.at[len(copies)]
                )
            )
            copies[-1].start()
    for copy in copies:
        copy.wait()
    tiles = gq.shape[0] // TILE
    for t in range(tiles):
        rows = pl.ds(t * TILE, TILE)
        grads[rows, pl.ds(0, HD)] = gq[rows, :]
        grads[rows, pl.ds(HD, 2 * HD)] = (keep[rows, :] + got[rows, :].astype(F32)).astype(BF)
        part = mm_nt(grads[rows, :], weights[...])
        normed, _ = norm_of(tokens[rows, :].astype(F32))
        one = jnp.sum(part * normed, 0, keepdims=True)
        two = jnp.sum(part, 0, keepdims=True)
        if t == 0:
            sums[0:1, :] = one
            sums[1:2, :] = two
        else:
            sums[0:1, :] += one
            sums[1:2, :] += two
        for i in range(4):
            parts[(t >> 1) * 4 + i, za ^ (t & 1)] = part[i * 64 : (i + 1) * 64].astype(BF)
        grads.push(rows)
        if t & 1:
            parts.push(pl.ds((t >> 1) * 4, 4))


def total_kernel(parts, keep, send):
    total = parts[0, 0].astype(F32)
    other = parts[0, 1].astype(F32)
    for n in range(1, 8):
        total = total + parts[n, 0].astype(F32)
        other = other + parts[n, 1].astype(F32)
    keep[...] = total
    send[...] = other.astype(BF)


def head_grad_kernel(at, left, right, sums, keep, send, big):
    c = at[4]
    per = left.shape[1] // 32
    transposed_product(big, left, right)
    spare = keep.shape[2] - sums.shape[1]

    def deal(q, carry):
        keep[q, pl.ds(0, per), :] = big[aligned(2 * q + c, per), :]
        send[q, pl.ds(0, per), :] = big[aligned(2 * q + 1 - c, per), :].astype(BF)
        return carry

    lax.fori_loop(0, 16, deal, 0)
    pad = jnp.zeros((16, spare), F32)
    for q in range(16):
        pair = jnp.concatenate([sums[2 * q : 2 * q + 2, :], pad[:2]], 1)
        mine = jnp.where(c == 0, pair[0:1], pair[1:2])
        other = jnp.where(c == 0, pair[1:2], pair[0:1])
        keep[q, pl.ds(per, 16), :] = jnp.broadcast_to(mine, (16, keep.shape[2]))
        send[q, pl.ds(per, 16), :] = jnp.broadcast_to(other, (16, keep.shape[2])).astype(BF)


def core_grad_kernel(at, left, right, keep, send, big):
    c = at[4]
    per = left.shape[1] // 32
    transposed_product(big, left, right)

    def deal(q, carry):
        rows = aligned(q, per)
        keep[rows, :] = big[aligned(2 * q + c, per), :]
        send[rows, :] = big[aligned(2 * q + 1 - c, per), :].astype(BF)
        return carry

    lax.fori_loop(0, 16, deal, 0)


def input_kernel(at, keep, got, tokens, grad_middle, gains, grad_tokens):
    za = at[1]
    tok = tokens.shape[1]
    for n in range(2):
        seq = za if n == 0 else 1 - za
        part = keep[...] if n == 0 else got[...].astype(F32)
        n1, inv = norm_of(tokens[seq].astype(F32))
        a = part * gains[0:1, :]
        grad_tokens[seq] = grad_middle[aligned(seq, tok), :] + inv * (
            a - jnp.mean(a, -1, keepdims=True) - n1 * jnp.mean(a * n1, -1, keepdims=True)
        )


def far_kernel(keep, got, own, on_z, on_y, far_a, far_b):
    n = own.shape[0]
    for i, out in enumerate((own, on_z, on_y)):
        rows = pl.ds(i * n, n)
        out[...] = keep[rows, :] + got[rows, :].astype(F32)
    for i, out in enumerate((far_a, far_b)):
        rows = pl.ds(3 * n + i * (n // 2), n // 2)
        out[...] = (keep[rows, :] + got[rows, :].astype(F32)).astype(BF)


def near_kernel(on_z, on_y, got_a, got_b, send_z, send_y):
    n = got_a.shape[0]
    first, second = pl.ds(0, n), pl.ds(n, n)
    send_z[first, :] = (on_z[first, :] + got_a[...].astype(F32)).astype(BF)
    send_z[second, :] = on_z[second, :].astype(BF)
    send_y[first, :] = on_y[first, :].astype(BF)
    send_y[second, :] = (on_y[second, :] + got_b[...].astype(F32)).astype(BF)


def result_sum_kernel(middle, own, got_z, got_y, out):
    out[...] = (
        middle[...] + own[...] + got_z[...].astype(F32) + got_y[...].astype(F32)
    ).astype(BF)


def fold_kernel(at, keep, got, parts):
    x, y = at[0], at[3]
    rows = parts.shape[1]
    for n in range(4):
        here = pl.ds(n * rows, rows)
        z = x ^ (1 if n in (1, 3) else 0)
        w = y ^ (1 if n in (2, 3) else 0)
        parts[z * 2 + w] = (keep[here, :].astype(F32) + got[here, :].astype(F32)).astype(BF)


def stage(*values):
    return lax.optimization_barrier(values)


def grow(v, axis):
    return jnp.concatenate([v, swap(v, axis)], 0)


def half_swap(v, axis):
    return swap(pick(v, 1 - lax.axis_index(axis)), axis)


def fine_layer(
    tokens,
    cotangent,
    ln1_gain,
    ln1_bias,
    w_query,
    w_key,
    w_value,
    w_out,
    ln2_gain,
    ln2_bias,
    w_inner,
    w_outer,
):
    seqs, tok, width = tokens.shape
    rows = seqs * tok
    half = rows // 2
    per = w_query.shape[0]
    unit = w_outer.shape[0]
    hidden_units = 4 * unit
    all_rows = 8 * rows
    coords = jnp.stack([lax.axis_index(a) for a in ("x", "za", "zl", "y", "c")]).astype(jnp.int32)
    x, za = lax.axis_index("x"), lax.axis_index("za")
    cube, owners = ("x", "zl", "y"), ("x", "za", "zl", "y")
    cot = cotangent.reshape(rows, width)

    def split(axis, keep, got, shape):
        keep, got = keep.reshape(shape), got.reshape(shape)
        i = lax.axis_index(axis)
        mine = pick(keep, i, 1) + pick(got, i, 1).astype(F32)
        return mine, (pick(keep, 1 - i, 1) + pick(got, 1 - i, 1).astype(F32)).astype(BF)

    head_w, inner_w = call(
        pack_kernel,
        [((16, 3 * per + 16, HD), BF), ((8, per, hidden_units), BF)],
        [w_query, w_key, w_value]
        + [g.reshape(1, per) for g in (ln1_gain, ln1_bias, ln2_gain, ln2_bias)]
        + [w_inner],
        name="pack",
    )
    moved, head_w, inner_w, w_out, w_outer = stage(
        swap(pick(tokens, 1 - za), "za"), head_w, inner_w, w_out, w_outer
    )
    block = jnp.stack([pick(tokens, za), moved])
    on_x, on_z, on_y, head_w = stage(
        swap(block, "x"), swap(block, "zl"), swap(block, "y"), head_w
    )
    on_xz, on_xy, on_zy, on_xyz, head_w, w_out_z = stage(
        swap(on_x, "zl"),
        swap(on_y, "x"),
        swap(on_z, "y"),
        lax.ppermute(block, cube, [(i, 7 - i) for i in range(8)]),
        lax.all_to_all(head_w, owners, 0, 0, tiled=True),
        swap(after(w_out, on_x), "za"),
    )
    head_c, w_outer, inner_w, w_out_z = stage(swap(head_w, "c"), w_outer, inner_w, w_out_z)
    blocks = [block, on_y, on_z, on_zy, on_x, on_xy, on_xz, on_xyz]
    out_w = jnp.stack([w_out, w_out_z])
    h1, query, kv, gains, head_w = call(
        qkv_kernel,
        [
            ((16 * tok, width), BF),
            ((16 * tok, HD), BF),
            ((16 * tok, 2 * HD), BF),
            ((8, width), F32),
            ((width, 3 * HD), BF),
        ],
        blocks + [head_w, head_c],
        coords,
        name="qkv",
    )
    kv, query, out_x, outer_a, outer_l, inner_w = stage(
        kv,
        query,
        swap(out_w, "x"),
        swap(w_outer, "za"),
        swap(w_outer, "zl"),
        lax.all_to_all(inner_w, ("x", "y", "c"), 0, 0, tiled=True),
    )
    out_w = jnp.concatenate([out_w, out_x], 0)
    kv_other, out_w, inner_w = stage(swap(kv, "c"), out_w, inner_w)
    out, out_f, lse, query, kv, kv_other = call(
        fine_forward_kernel,
        [((16, tok, HD), BF), ((16 * tok, HD), F32), ((16 * tok, HD), F32)],
        [query, kv, kv_other],
        coords,
        save=(0, 1, 2),
        scratch=[pltpu.VMEM((2 * 16 * tok // TILE, TILE, TILE), F32)],
        name="attention_forward",
    )
    out, out_z, out_y, inner_a, inner_l, cot = stage(
        out,
        swap(out_w, "zl"),
        swap(out_w, "y"),
        swap(inner_w, "za"),
        swap(inner_w, "zl"),
        cot,
    )
    mixed, cot_z, cot_y, cot_c, out_zy, outer_la, inner_la, *out_c = stage(
        lax.all_to_all(out, owners, 0, 0, tiled=True),
        swap(cot, "x"),
        swap(cot, "y"),
        swap(cot, "c"),
        swap(out_z, "y"),
        swap(outer_a, "zl"),
        swap(inner_a, "zl"),
        swap(out_w, "c"),
        swap(out_z, "c"),
        swap(out_y, "c"),
    )
    (out_zyc,) = stage(swap(out_zy, "c"))
    pieces = [out_w, out_z, out_y, out_zy] + out_c + [out_zyc]
    mixed, middle, scaled, inverse, h2 = call(
        middle_kernel,
        [
            ((rows, width), BF),
            ((rows, width), F32),
            ((rows, width), F32),
            ((rows, HD), F32),
            ((rows, width), BF),
        ],
        [mixed, tokens, gains] + pieces,
        coords,
        raw=range(3, 11),
        scratch=[pltpu.VMEM((width, width), BF), pltpu.SemaphoreType.DMA((32,))],
        name="middle",
    )
    cot_z, cot_y = after(cot_z, h2), after(cot_y, h2)
    h2_z, h2_y, h2_c, cot_a, cot_b, cot_zc, cot_yc = stage(
        swap(h2, "x"),
        swap(h2, "y"),
        swap(h2, "c"),
        swap(cot_z[:half], "y"),
        swap(cot_y[half:], "x"),
        swap(cot_z, "c"),
        swap(cot_y, "c"),
    )
    h2_a, h2_b, h2_zc, h2_yc, cot_ac, cot_bc = stage(
        swap(h2_z[:half], "y"),
        swap(h2_y[half:], "x"),
        swap(h2_z, "c"),
        swap(h2_y, "c"),
        swap(cot_a, "c"),
        swap(cot_b, "c"),
    )
    h2_ac, h2_bc = stage(swap(h2_a, "c"), swap(h2_b, "c"))
    h2_all, cot_all, outer_w, hidden, grad_inner, keep, send = call(
        inner_kernel,
        [
            ((all_rows, width), BF, "raw"),
            ((all_rows, width), BF, "raw"),
            ((hidden_units, width), BF, "raw"),
            ((all_rows, hidden_units), BF),
            ((all_rows, hidden_units), BF),
            ((all_rows // 2, width), BF),
            ((all_rows // 2, width), BF),
        ],
        [h2, h2_z, h2_y, h2_a, h2_b, h2_c, h2_zc, h2_yc, h2_ac, h2_bc]
        + [cot, cot_z, cot_y, cot_a, cot_b, cot_c, cot_zc, cot_yc, cot_ac, cot_bc]
        + [p.reshape(2, 4 * per, hidden_units) for p in (inner_w, inner_l, inner_a, inner_la)]
        + [w_outer, outer_l, outer_a, outer_la],
        coords,
        raw=range(10, 28),
        scratch=[
            pltpu.VMEM((all_rows, width), BF),
            pltpu.VMEM((all_rows, width), BF),
            pltpu.VMEM((width, hidden_units), BF),
            pltpu.VMEM((hidden_units, width), BF),
            pltpu.SemaphoreType.DMA((25,)),
        ],
        name="inner",
    )

    (got,) = stage(swap(send, "c"))
    (parts,) = call(
        fold_kernel, [((4, rows, width), BF)], [keep, got], coords, name="fold"
    )
    n_in, n_out = 8 * per, unit
    inner_g, in_l, in_a, in_la = call(
        inner_grad_kernel,
        [((n_in, hidden_units), F32)] + [((n_in, hidden_units), BF)] * 3,
        [h2_all, grad_inner],
        coords,
        scratch=[pltpu.VMEM((width, hidden_units), F32)],
        name="inner_grad",
    )
    parts, inner_g, in_l, in_a, in_la = stage(parts, inner_g, in_l, in_a, in_la)
    outer_g, outer_l, outer_a, outer_la, res_keep, res_send = call(
        outer_grad_kernel,
        [((n_out, width), F32)]
        + [((n_out, width), BF)] * 3
        + [((all_rows // 2, width), F32), ((all_rows // 2, width), BF)],
        [after(hidden, in_l), cot_all, outer_w],
        coords,
        scratch=[pltpu.VMEM((hidden_units, width), F32)],
        name="outer_grad",
    )
    parts, in_l, in_a, outer_g, outer_l, outer_a, outer_la, res_keep, res_send, in_la = stage(
        lax.all_to_all(parts, ("x", "y"), 0, 0, tiled=True),
        swap(in_l, "zl"),
        swap(in_a, "za"),
        outer_g,
        outer_l,
        outer_a,
        outer_la,
        res_keep,
        res_send,
        in_la,
    )
    grad_middle, branch, go, sums_two = call(
        branch_kernel,
        [
            ((rows, width), F32),
            ((rows, width), BF),
            ((16, tok, HD), BF),
            ((2, width), F32),
        ],
        [parts, scaled, inverse, gains, cotangent] + pieces,
        coords,
        raw=range(5, 13),
        scratch=[pltpu.VMEM((width, width), BF), pltpu.SemaphoreType.DMA((32,))],
        name="branch",
    )
    go, branch, res_got, outer_l, outer_a = stage(
        go, branch, swap(res_send, "c"), outer_l, outer_a
    )
    res = (res_keep + res_got.astype(F32)).reshape(4, rows, width)
    far_a, far_b = res[3, :half].astype(BF), res[3, half:].astype(BF)
    out_keep, out_send = call(
        core_grad_kernel,
        [((width // 2, width), F32), ((width // 2, width), BF)],
        [mixed, branch],
        coords,
        scratch=[pltpu.VMEM((width, width), F32)],
        name="out_grad",
    )
    diagonal = [(i, 3 - i) for i in range(4)]
    go, outer_l, outer_a, in_la, outer_la, out_keep, out_send, res, far_a, far_b = stage(
        lax.all_to_all(go, owners, 0, 0, tiled=True),
        swap(outer_l, "zl"),
        swap(outer_a, "za"),
        in_la,
        outer_la,
        out_keep,
        out_send,
        res,
        far_a,
        far_b,
    )
    gq, keep, send = call(
        fine_backward_kernel,
        [((16 * tok, HD), BF), ((16 * tok, 2 * HD), F32), ((16 * tok, 2 * HD), BF)],
        [query, kv, kv_other, go, out_f, lse],
        coords,
        scratch=[pltpu.VMEM((16 * tok, 2 * HD), F32)],
        name="attention_backward",
    )
    gq, keep, send, got_a, got_b, out_got, in_la = stage(
        gq,
        keep,
        send,
        swap(far_a, "y"),
        swap(far_b, "x"),
        swap(out_send, "c"),
        lax.ppermute(in_la, ("za", "zl"), diagonal),
    )
    out_keep, out_send = split("x", out_keep, out_got, (1, 2, 8 * per, width))
    got, out_keep, out_send, outer_la = stage(swap(send, "c"), out_keep, out_send, outer_la)
    grads, parts, sums = call(
        partial_kernel,
        [
            ((16 * tok, 3 * HD), BF),
            ((8, 2, tok, width), BF),
            ((2, width), F32),
        ],
        blocks + [gq, keep, got, head_w],
        coords,
        raw=range(8),
        scratch=[pltpu.VMEM((16 * tok, width), BF), pltpu.SemaphoreType.DMA((16,))],
        name="partial",
    )
    grads, parts, sums, out_keep, out_got, outer_la = stage(
        grads,
        parts,
        sums,
        out_keep,
        swap(out_send, "x"),
        lax.ppermute(outer_la, ("za", "zl"), diagonal),
    )
    parts = lax.all_to_all(parts, cube, 0, 0, tiled=True)
    sums = jnp.concatenate([sums, sums_two], 0)
    sums = sums.reshape(4, 32, per).transpose(1, 0, 2).reshape(32, 4 * per)
    head_keep, head_send = call(
        head_grad_kernel,
        [((16, per + 16, 3 * HD), F32), ((16, per + 16, 3 * HD), BF)],
        [h1, grads, sums],
        coords,
        scratch=[pltpu.VMEM((width, 3 * HD), F32)],
        name="head_grad",
    )
    head_keep, head_send = stage(head_keep, head_send)
    out_keep, out_send = split(
        "y", out_keep, after(out_got, head_send), (4, 2, per, width)
    )
    inner_g = inner_g + after(in_l, head_send).astype(F32) + in_a.astype(F32) + in_la.astype(F32)
    inner_g = inner_g.astype(BF).reshape(4, 2, per, hidden_units)
    got_a = after(got_a, head_send)
    res_z = jnp.concatenate([res[1, :half] + got_a.astype(F32), res[1, half:]], 0).astype(BF)
    res_y = jnp.concatenate([res[2, :half], res[2, half:] + got_b.astype(F32)], 0).astype(BF)
    inner_own = pick(inner_g, lax.axis_index("c"), 1)
    inner_send = pick(inner_g, 1 - lax.axis_index("c"), 1)
    head_keep, head_got, out_keep, out_send, inner_own, inner_send, res_z, res_y = stage(
        head_keep, swap(head_send, "c"), out_keep, out_send, inner_own, inner_send, res_z, res_y
    )
    head_keep, head_send = split("za", head_keep, head_got, (2, 2, 4 * (per + 16), 3 * HD))
    head_keep, head_send, out_send = stage(head_keep, head_send, out_send)
    outer_g = (
        outer_g
        + after(outer_l, head_send).astype(F32)
        + outer_a.astype(F32)
        + outer_la.astype(F32)
    )
    head_keep, head_got, out_keep, out_got, inner_got, got_z, res_y, outer_g = stage(
        head_keep,
        swap(head_send, "za"),
        out_keep,
        swap(out_send, "y"),
        swap(inner_send, "c"),
        swap(res_z, "x"),
        res_y,
        outer_g,
    )
    inner_g = jnp.stack([inner_own, inner_got]).reshape(2, 2, 2, per, hidden_units)
    x = lax.axis_index("x")
    near_x, inner_send = pick(inner_g, x, 1), pick(inner_g, 1 - x, 1)
    (payload,) = call(
        payload_kernel,
        [((8, per + 16, 3 * HD), BF)],
        [head_keep, head_got],
        name="payload",
    )
    out_keep, out_send = split("za", out_keep, out_got, (1, 2, 2 * per, width))
    parts, payload, near_x, inner_send, out_keep, out_send = stage(
        parts, payload, near_x, inner_send, out_keep, out_send
    )
    payload = lax.all_to_all(payload, cube, 0, 0, tiled=True)
    total, send = call(
        total_kernel, [((tok, width), F32), ((tok, width), BF)], [parts], name="total"
    )
    total, send, near_x, inner_send, out_send, res_y = stage(
        total, send, near_x, inner_send, out_send, res_y
    )
    got, out_send, got_y, far_x, near_x = stage(
        swap(send, "za"),
        out_send,
        swap(res_y, "y"),
        swap(inner_send, "x"),
        near_x,
    )
    y = lax.axis_index("y")
    inner_send = jnp.stack([pick(near_x, 1 - y, 1), pick(far_x, 1 - y, 1)])
    near_x, far_x = pick(near_x, y, 1), pick(far_x, y, 1)
    (grad_tokens,) = call(
        input_kernel,
        [((seqs, tok, width), F32)],
        [total, got, tokens, grad_middle, gains],
        coords,
        name="input",
    )
    result = (
        middle + res[0] + after(got_z, got).astype(F32) + got_y.astype(F32)
    ).astype(BF)
    payload, out_got, grad_tokens, result, far_y, near_x, far_x = stage(
        payload,
        swap(out_send, "za"),
        grad_tokens,
        result,
        swap(inner_send, "y"),
        near_x,
        far_x,
    )
    out_keep, out_send = split("zl", out_keep, out_got, (1, 2, per, width))
    out_keep, out_send = stage(out_keep, out_send)
    query_g, key_g, value_g, *sums, inner_g = call(
        last_kernel,
        [((per, width), F32)] * 3
        + [((1, per), F32)] * 4
        + [((per, 8 * hidden_units), F32)],
        [payload, near_x, far_x, far_y],
        coords,
        name="last",
    )
    query_g, key_g, value_g, inner_g, out_got, result, *sums = stage(
        query_g, key_g, value_g, inner_g, swap(out_send, "zl"), result, *sums
    )
    sums = [v.reshape(per) for v in sums]
    return (
        result.reshape(seqs, tok, width),
        grad_tokens,
        sums[0],
        sums[1],
        query_g,
        key_g,
        value_g,
        out_keep[0] + out_got[0].astype(F32),
        sums[2],
        sums[3],
        inner_g,
        outer_g,
    )


def solution(mesh):
    blocks = mesh.shape["blk"]
    if blocks == 16:
        sizes = (2, 2, 1, 2, 2, 2)
        roles = (True, "za", ("x", "zl", "y"), ("c",), ("x", "za", "zl", "y"))
    else:
        sizes = (2, 8, blocks // 64, 2, 2, 2)
        roles = (False, "x", ("za",), ("zb", "zl", "y", "c"), ("x", "za"))
    fine = Mesh(mesh.devices.reshape(sizes), AXES)
    tok, row, vec = P(None, AXES, None), P(AXES, None), P(AXES)
    in_specs = (tok, tok, vec, vec, row, row, row, row, vec, vec, row, row)
    out_specs = (tok, tok, vec, vec, row, row, row, row, vec, vec, row, row)
    return jax.shard_map(
        fine_layer if blocks == 16 else functools.partial(on_device, roles),
        mesh=fine,
        in_specs=in_specs,
        out_specs=out_specs,
        check_vma=False,
    )
```

```python
import functools
import math

import jax
import jax.numpy as jnp
from jax import lax
from jax.experimental import pallas as pl
from jax.experimental.pallas import tpu as pltpu
from jax.sharding import Mesh
from jax.sharding import PartitionSpec as P

HD = 128
TILE = 256
SCALE = HD ** (-0.5)
MASKED = -1e30
eps_norm = 1e-05
gelu_coef = math.sqrt(2.0 / math.pi)
BF = jnp.bfloat16
F32 = jnp.float32
AXES = ("x", "za", "zb", "zl", "y", "c")
T_AXES = ("x", "za", "zb")
W_AXES = ("zl", "y", "c")


def mm(a, b):
    return jnp.dot(a, b, preferred_element_type=F32)


def mm_nt(a, b):
    return lax.dot_general(a, b, (((1,), (1,)), ((), ())), preferred_element_type=F32)


def mm_tn(a, b):
    return lax.dot_general(a, b, (((0,), (0,)), ((), ())), preferred_element_type=F32)


def norm_stats(values):
    centered = values - jnp.mean(values, -1, keepdims=True)
    inverse = lax.rsqrt(jnp.mean(centered * centered, -1, keepdims=True) + eps_norm)
    return centered * inverse, inverse


def norm_back(grad_normed, scaled, inverse, gain):
    g = grad_normed * gain
    return inverse * (
        g - jnp.mean(g, -1, keepdims=True) - scaled * jnp.mean(g * scaled, -1, keepdims=True)
    )


def swap(v, axis):
    return lax.ppermute(v, axis, [(0, 1), (1, 0)])


def pick(v, index, axis=0):
    return lax.dynamic_index_in_dim(v, index, axis, keepdims=False)


def pair_gather(v, axis):
    other = swap(v, axis)
    first = lax.axis_index(axis) == 0
    return jnp.stack([jnp.where(first, v, other), jnp.where(first, other, v)])


def pair_scatter(v, axis, dim):
    me = lax.axis_index(axis)
    return pick(v, me, dim) + swap(pick(v, 1 - me, dim).astype(BF), axis).astype(F32)


def after(v, *others):
    return lax.optimization_barrier((v,) + others)[0]


def t_gather(v):
    if lax.axis_size("za") * lax.axis_size("zb") != 2:
        return lax.all_gather(v, T_AXES, axis=0, tiled=False)
    x, z = lax.axis_index("x"), lax.axis_index("za")
    over_x, over_z = swap(v, "x"), swap(v, "za")
    out = jnp.zeros((4,) + v.shape, v.dtype)
    for part, at in (
        (v, 2 * x + z),
        (over_x, 2 * (1 - x) + z),
        (over_z, 2 * x + 1 - z),
        (swap(over_z, "x"), 2 * (1 - x) + 1 - z),
    ):
        out = lax.dynamic_update_index_in_dim(out, part, at, 0)
    return out


def t_scatter(v):
    if lax.axis_size("za") * lax.axis_size("zb") != 2:
        return lax.psum_scatter(v, T_AXES, scatter_dimension=0, tiled=False)
    v = pair_scatter(v.reshape((2, 2) + v.shape[1:]), "x", 0)
    return pair_scatter(v, "za", 0)


def plane_gather(v):
    half = v.shape[0] // 2
    a, b = v[:half], v[half:]
    a = jnp.stack([a, swap(a, "zl")])
    b = jnp.stack([b, swap(b, "y")])
    a = jnp.stack([a, swap(a, "y")])
    b = jnp.stack([b, swap(b, "zl")])
    both = jnp.stack([a, b])
    return jnp.stack([both, swap(both, "c")]).reshape(8 * v.shape[0], v.shape[1])


def plane_scatter(v):
    rows, width = v.shape
    v = v.reshape(2, 2, 2, 2, rows // 16, width)

    def fold(u, axis):
        return u[0] + swap(u[1].astype(BF), axis).astype(F32)

    v = fold(v, "c")
    a, b = v[0], v[1]
    a = fold(a, "y")
    b = fold(b, "zl")
    a = fold(a, "zl")
    b = fold(b, "y")
    return jnp.concatenate([a, b], 0)


def shares(count, body):
    if count <= 2:
        for k in range(count):
            body(k)
    else:
        lax.fori_loop(0, count, lambda k, c: (body(k), c)[1], 0)


def mask_of(count, q_tile, k_tile, q_share, k_share):
    rows = lax.broadcasted_iota(jnp.int32, (TILE, TILE), 0) + q_tile * TILE
    cols = lax.broadcasted_iota(jnp.int32, (TILE, TILE), 1) + k_tile * TILE
    q_pos = (lax.shift_right_logical(rows, 6) * count + q_share) * 64 + (rows & 63)
    k_pos = (lax.shift_right_logical(cols, 6) * count + k_share) * 64 + (cols & 63)
    return k_pos <= q_pos


def forward_kernel(count, meta, q_ref, k_ref, v_ref, o_ref, of_ref, lse_ref, qa, ka, va, s_ref):
    blocks = q_ref.shape[0]
    for j in range(blocks):
        slot = meta[j]
        rows = pl.ds(j * 64, 64)
        qa[rows, :] = q_ref[slot]

        def place(k, rows=rows, slot=slot):
            ka[k, rows, :] = k_ref[k, slot]
            va[k, rows, :] = v_ref[k, slot]

        shares(count, place)
    mine = meta[blocks]
    tiles = blocks * 64 // TILE
    for t in range(tiles):
        q = qa[pl.ds(t * TILE, TILE), :]
        top = jnp.full((TILE, 1), MASKED, F32)
        for u in range(t + 1):
            cols = pl.ds(u * TILE, TILE)

            def score(k, top, u=u, cols=cols):
                s = mm_nt(q, ka[k, cols, :]) * SCALE
                if u == t:
                    s = jnp.where(mask_of(count, t, u, mine, meta[blocks + 1 + k]), s, MASKED)
                s_ref[k * tiles + u] = s
                return jnp.maximum(top, jnp.max(s, -1, keepdims=True))

            if count <= 2:
                for k in range(count):
                    top = score(k, top)
            else:
                top = lax.fori_loop(0, count, score, top)
        total = jnp.zeros((TILE, 1), F32)
        for u in range(t + 1):

            def expo(k, total, u=u):
                p = jnp.exp(s_ref[k * tiles + u] - top)
                s_ref[k * tiles + u] = p
                return total + jnp.sum(p, -1, keepdims=True)

            if count <= 2:
                for k in range(count):
                    total = expo(k, total)
            else:
                total = lax.fori_loop(0, count, expo, total)
        inverse = 1.0 / total
        out = jnp.zeros((TILE, HD), F32)
        for u in range(t + 1):
            cols = pl.ds(u * TILE, TILE)

            def weigh(k, out, u=u, cols=cols):
                p = (s_ref[k * tiles + u] * inverse).astype(BF)
                return out + mm(p, va[k, cols, :])

            if count <= 2:
                for k in range(count):
                    out = weigh(k, out)
            else:
                out = lax.fori_loop(0, count, weigh, out)
        rows = pl.ds(t * TILE, TILE)
        of_ref[rows, :] = out
        o_ref[rows, :] = out.astype(BF)
        lse_ref[rows, :] = jnp.broadcast_to(top + jnp.log(total), (TILE, HD))


def attention_forward(count, meta, q, k, v):
    blocks = q.shape[0]
    rows = blocks * 64
    tiles = rows // TILE
    vm = pl.BlockSpec(memory_space=pltpu.VMEM)
    pairs = tiles * (tiles + 1) // 2 * count
    return pl.pallas_call(
        functools.partial(forward_kernel, count),
        in_specs=[pl.BlockSpec(memory_space=pltpu.SMEM), vm, vm, vm],
        out_specs=[vm] * 6,
        out_shape=[
            jax.ShapeDtypeStruct((rows, HD), BF),
            jax.ShapeDtypeStruct((rows, HD), F32),
            jax.ShapeDtypeStruct((rows, HD), F32),
            jax.ShapeDtypeStruct((rows, HD), BF),
            jax.ShapeDtypeStruct((count, rows, HD), BF),
            jax.ShapeDtypeStruct((count, rows, HD), BF),
        ],
        scratch_shapes=[pltpu.VMEM((count * tiles, TILE, TILE), F32)],
        cost_estimate=pl.CostEstimate(
            flops=pairs * TILE * TILE * HD * 4,
            bytes_accessed=rows * HD * 2 * (2 + 4 * count) + rows * HD * 8,
            transcendentals=pairs * TILE * TILE,
        ),
        compiler_params=pltpu.CompilerParams(vmem_limit_bytes=(16 if count <= 2 else 52) << 20),
        name="attention_forward",
    )(meta, q, k, v)


def backward_kernel(count, meta, q_ref, k_ref, v_ref, go_ref, of_ref, lse_ref, gq_ref, gk, gv):
    rows_all = q_ref.shape[0]
    blocks = rows_all // 64
    mine = meta[blocks]
    tiles = rows_all // TILE

    def zero(k):
        gk[k] = jnp.zeros((rows_all, HD), F32)
        gv[k] = jnp.zeros((rows_all, HD), F32)

    shares(count, zero)
    for t in range(tiles):
        rows = pl.ds(t * TILE, TILE)
        q = q_ref[rows, :]
        go = go_ref[rows, :]
        delta = jnp.sum(go.astype(F32) * of_ref[rows, :], -1, keepdims=True)
        lse = lse_ref[rows, :][:, :1]
        gq = jnp.zeros((TILE, HD), F32)
        for u in range(t + 1):
            cols = pl.ds(u * TILE, TILE)

            def one(k, gq, u=u, cols=cols):
                kk = k_ref[k, cols, :]
                p = jnp.exp(mm_nt(q, kk) * SCALE - lse)
                if u == t:
                    p = jnp.where(mask_of(count, t, u, mine, meta[blocks + 1 + k]), p, 0.0)
                gv[k, cols, :] += mm_tn(p.astype(BF), go)
                ds = (p * (mm_nt(go, v_ref[k, cols, :]) - delta)).astype(BF)
                gk[k, cols, :] += mm_tn(ds, q)
                return gq + mm(ds, kk)

            if count <= 2:
                for k in range(count):
                    gq = one(k, gq)
            else:
                gq = lax.fori_loop(0, count, one, gq)
        gq_ref[rows, :] = (gq * SCALE).astype(BF)

    def scale(k):
        gk[k] = gk[k] * SCALE

    shares(count, scale)


def attention_backward(count, meta, q, k, v, go, of, lse):
    rows = q.shape[0]
    tiles = rows // TILE
    vm = pl.BlockSpec(memory_space=pltpu.VMEM)
    pairs = tiles * (tiles + 1) // 2 * count
    return pl.pallas_call(
        functools.partial(backward_kernel, count),
        in_specs=[pl.BlockSpec(memory_space=pltpu.SMEM)] + [vm] * 6,
        out_specs=[vm] * 3,
        out_shape=[
            jax.ShapeDtypeStruct((rows, HD), BF),
            jax.ShapeDtypeStruct((count, rows, HD), F32),
            jax.ShapeDtypeStruct((count, rows, HD), F32),
        ],
        cost_estimate=pl.CostEstimate(
            flops=pairs * TILE * TILE * HD * 10,
            bytes_accessed=rows * HD * (16 + 12 * count),
            transcendentals=pairs * TILE * TILE,
        ),
        compiler_params=pltpu.CompilerParams(vmem_limit_bytes=(16 if count <= 2 else 52) << 20),
        name="attention_backward",
    )(meta, q, k, v, go, of, lse)


def reorder_kernel(meta, g_ref, out_ref):
    for j in range(g_ref.shape[0]):
        out_ref[meta[j]] = g_ref[j]


def reorder(meta, g):
    vm = pl.BlockSpec(memory_space=pltpu.VMEM)
    return pl.pallas_call(
        reorder_kernel,
        in_specs=[pl.BlockSpec(memory_space=pltpu.SMEM), vm],
        out_specs=vm,
        out_shape=jax.ShapeDtypeStruct(g.shape, g.dtype),
        cost_estimate=pl.CostEstimate(flops=0, bytes_accessed=4 * g.size, transcendentals=0),
        compiler_params=pltpu.CompilerParams(vmem_limit_bytes=8 << 20),
        name="reorder",
    )(meta, g)


def on_device(
    roles,
    tokens,
    cotangent,
    ln1_gain,
    ln1_bias,
    w_query,
    w_key,
    w_value,
    w_out,
    ln2_gain,
    ln2_bias,
    w_inner,
    w_outer,
):
    small, seq_axis, hd_axes, sh_axes, own_axes = roles
    planes = math.prod(lax.axis_size(a) for a in T_AXES)
    count = math.prod(lax.axis_size(a) for a in sh_axes)
    devices = 8 * planes
    seqs, tok, width = tokens.shape
    rows = seqs * tok
    per = w_query.shape[0]
    unit = w_outer.shape[0]
    seq = lax.axis_index(seq_axis)
    share = lax.axis_index(sh_axes)

    block = jnp.stack([pick(tokens, seq), swap(pick(tokens, 1 - seq), seq_axis)])
    if small:
        on_x, on_z, on_y = (swap(block, a) for a in hd_axes)
        on_xz, on_xy, on_zy = swap(on_x, "zl"), swap(on_y, "x"), swap(on_z, "y")
        on_xyz = swap(on_xz, "y")
        seen = jnp.stack([block, on_y, on_z, on_zy, on_x, on_xy, on_xz, on_xyz])
    else:
        seen = lax.all_gather(block, hd_axes, axis=0, tiled=False)
    at = jnp.arange(16, dtype=jnp.int32)
    if small:
        at_x, at_za, at_zl, at_y = at // 8, at // 4 % 2, at // 2 % 2, at % 2
        x, zl, y = (lax.axis_index(a) for a in hd_axes)
        slots = ((at_x ^ x) * 4 + (at_zl ^ zl) * 2 + (at_y ^ y)) * 2 + (at_za ^ seq)
    else:
        slots = at % 8 * 2 + (at // 8 ^ seq)

    gains = jnp.concatenate([ln1_gain, ln1_bias, ln2_gain, ln2_bias])
    gains = jnp.broadcast_to(jnp.pad(gains, (0, HD - gains.shape[0])), (8, 1, HD))
    head_w = jnp.stack([w_query, w_key, w_value]).reshape(3, per, 8, HD).transpose(2, 0, 1, 3)
    head_w = jnp.concatenate([head_w.reshape(8, 3 * per, HD), gains], 1)
    head_w = lax.all_to_all(head_w, hd_axes, 0, 0, tiled=True)
    head_w = pair_gather(head_w, seq_axis)
    for axis in reversed(sh_axes):
        if lax.axis_size(axis) == 2:
            head_w = pair_gather(head_w, axis)
        else:
            head_w = lax.all_gather(head_w, axis, axis=0, tiled=False)
    if small:
        head_w = head_w.reshape(2, 2, 2, 4, 3 * per + 1, HD).transpose(2, 1, 3, 0, 4, 5)
    else:
        head_w = head_w.reshape(count, 16, 3 * per + 1, HD).transpose(1, 0, 2, 3)
    head_w = head_w.reshape(devices, 3 * per + 1, HD)
    gains = head_w[:, -1, : 4 * per].reshape(devices, 4, per).transpose(1, 0, 2)
    gains = gains.reshape(4, width).astype(F32)
    gain_one, bias_one, gain_two, bias_two = gains[0], gains[1], gains[2], gains[3]
    head_w = head_w[:, :-1].reshape(devices, 3, per, HD).transpose(0, 2, 1, 3)
    head_w = head_w.reshape(width, 3 * HD)

    inner_w = w_inner.reshape(per, planes, 8, unit).transpose(2, 0, 1, 3)
    inner_w = lax.all_to_all(inner_w.reshape(8, per, planes * unit), W_AXES, 0, 0, tiled=True)
    inner_w = t_gather(after(inner_w, seen)).reshape(width, planes * unit)
    outer_w = t_gather(w_outer).reshape(planes * unit, width)
    grad_plane = plane_gather(after(cotangent, seen).reshape(rows, width))

    out_w = lax.all_gather(w_out, AXES, axis=0, tiled=True)
    qkv_w = jnp.concatenate([w_query, w_key, w_value], 1)
    qkv_w = lax.all_gather(after(qkv_w, seen), AXES, axis=0, tiled=True)

    normed, _ = norm_stats(seen.reshape(-1, width).astype(F32))
    h1 = (normed * gain_one + bias_one).astype(BF)
    qkv = mm(h1, head_w).astype(BF)
    query = qkv[:, :HD].reshape(16, tok, HD)
    kv = qkv[:, HD:]
    if count == 2:
        kv = jnp.stack([kv, swap(kv, "c")])
        order = jnp.stack([share, 1 - share])
    else:
        kv = lax.all_gather(kv, sh_axes, axis=0, tiled=False)
        order = jnp.arange(count)
    kv = kv.reshape(count, 16, tok, 2 * HD)
    meta = jnp.concatenate([slots, share.reshape(1), order]).astype(jnp.int32)
    out, out_f, lse, q_at, k_at, v_at = attention_forward(
        count, meta, query, kv[..., :HD], kv[..., HD:]
    )

    def to_tokens(v):
        v = lax.all_to_all(v, own_axes, 0, 0, tiled=True)
        n = v.shape[-1] // HD
        if small:
            v = v.reshape(2, 2, 4, tok, n, HD).transpose(1, 3, 4, 0, 2, 5)
        else:
            v = v.reshape(2, 8, tok, n, HD).transpose(0, 2, 3, 1, 4)
        return v.reshape(2, tok, n, 8 * HD)

    mixed = to_tokens(out.reshape(16, tok, HD)).reshape(rows, width)
    flat_in = tokens.reshape(rows, width).astype(F32)
    middle = flat_in + mm(mixed, out_w)
    scaled_two, inverse_two = norm_stats(middle)
    h2 = plane_gather((scaled_two * gain_two + bias_two).astype(BF))

    inner = mm(h2, inner_w)
    bent = jnp.tanh(gelu_coef * (inner + 0.044715 * inner * inner * inner))
    hidden = (0.5 * inner * (1.0 + bent)).astype(BF)
    slope = 0.5 * (1.0 + bent) + 0.5 * inner * (1.0 - bent * bent) * gelu_coef * (
        1.0 + 3.0 * 0.044715 * inner * inner
    )
    grad_inner = (mm_nt(grad_plane, outer_w) * slope).astype(BF)
    grad_h2 = plane_scatter(mm_nt(grad_inner, inner_w))
    grad_outer = mm_tn(hidden, grad_plane).reshape(planes, unit, width)
    grad_outer = t_scatter(grad_outer)
    grad_in = mm_tn(h2, grad_inner).reshape(planes, 8 * per, planes * unit)
    grad_in = t_scatter(grad_in).astype(BF).reshape(8, per, planes * unit)
    result = plane_scatter(mm(hidden, outer_w))

    grad_out = cotangent.reshape(rows, width).astype(F32)
    grad_middle = grad_out + norm_back(grad_h2, scaled_two, inverse_two, gain_two)
    branch = grad_middle.astype(BF)
    go = mm_nt(branch, out_w).astype(BF)
    if small:
        go = go.reshape(2, tok, 2, 4, HD).transpose(2, 0, 3, 1, 4)
    else:
        go = go.reshape(2, tok, 8, HD).transpose(0, 2, 1, 3)
    go = lax.all_to_all(go.reshape(16, tok, HD), own_axes, 0, 0, tiled=True)
    go = go.reshape(16 * tok, HD)

    gq, gk, gv = attention_backward(count, meta, q_at, k_at, v_at, go, out_f, lse)
    gkv = jnp.concatenate([gk, gv], -1)
    if count == 2:
        gkv = gkv[0] + swap(gkv[1].astype(BF), "c").astype(F32)
    else:
        gkv = lax.psum_scatter(gkv, sh_axes, scatter_dimension=0, tiled=False)
    grads = jnp.concatenate([gq, gkv.astype(BF)], -1).reshape(16, tok, 3 * HD)
    grads, result, grad_in, grad_outer = lax.optimization_barrier(
        (grads, result, grad_in, grad_outer)
    )
    back = to_tokens(grads).reshape(rows, 3 * width)
    result = (middle + result).astype(BF)
    grad_in = lax.all_to_all(after(grad_in, back), W_AXES, 0, 0, tiled=True)
    grad_in = grad_in.reshape(8, per, planes, unit).transpose(1, 2, 0, 3)
    grad_in = grad_in.reshape(per, devices * unit).astype(F32)

    head_g = mm_tn(h1, reorder(meta, grads).reshape(16 * tok, 3 * HD))
    head_g = head_g.reshape(tuple(lax.axis_size(a) for a in AXES) + (per, 3 * HD))
    dims = list(AXES)
    for axis in sh_axes[::-1] + (seq_axis,):
        dim = dims.index(axis)
        dims.remove(axis)
        if lax.axis_size(axis) == 2:
            head_g = pair_scatter(head_g, axis, dim)
        else:
            head_g = lax.psum_scatter(head_g, axis, scatter_dimension=dim, tiled=False)
    head_g = head_g.astype(BF).reshape(8, per, 3 * HD)
    head_g = lax.all_to_all(head_g, hd_axes, 0, 0, tiled=True)
    head_g = head_g.reshape(8, per, 3, HD).transpose(2, 1, 0, 3).reshape(3, per, width)
    head_g = head_g.astype(F32)

    grad_out_w = mm_tn(mixed, branch).reshape(planes, 2, 2, 2, per, width)
    grad_out_w = pair_scatter(grad_out_w, "c", 3)
    grad_out_w = pair_scatter(grad_out_w, "y", 2)
    grad_out_w = pair_scatter(grad_out_w, "zl", 1)
    grad_out_w = t_scatter(grad_out_w)

    scaled_one, inverse_one = norm_stats(flat_in)
    grad_h1 = mm_nt(back, qkv_w)
    grad_input = grad_middle + norm_back(grad_h1, scaled_one, inverse_one, gain_one)

    sums = jnp.stack(
        [
            jnp.sum(grad_h1 * scaled_one, 0),
            jnp.sum(grad_h1, 0),
            jnp.sum(grad_h2 * scaled_two, 0),
            jnp.sum(grad_h2, 0),
        ]
    )
    sums = sums.reshape(4, devices, per).transpose(1, 0, 2).reshape(devices, 4 * per)
    sums = lax.all_to_all(sums, AXES, 0, 0, tiled=True)
    sums = jnp.sum(sums, 0).reshape(4, per)
    return (
        result.reshape(seqs, tok, width),
        grad_input.reshape(seqs, tok, width),
        sums[0],
        sums[1],
        head_g[0],
        head_g[1],
        head_g[2],
        grad_out_w,
        sums[2],
        sums[3],
        grad_in,
        grad_outer,
    )


class Arriving:
    def __init__(self, ref, copy):
        self.ref, self.copy = ref, copy
        self.shape, self.dtype = ref.shape, ref.dtype

    def __getitem__(self, index):
        if self.copy is not None:
            self.copy.wait()
            self.copy = None
        return self.ref[index]


class Leaving:
    def __init__(self, ref, target, move):
        self.ref, self.target, self.move, self.pushed = ref, target, move, False
        self.shape, self.dtype = ref.shape, ref.dtype

    def __getitem__(self, index):
        return self.ref[index]

    def __setitem__(self, index, value):
        self.ref[index] = value

    def push(self, rows=None):
        self.pushed = True
        if rows is None:
            self.move(self.ref, self.target)
        else:
            self.move(self.ref.at[rows], self.target.at[rows])


def call(kernel, outs, ins, coords=None, raw=(), save=(), scratch=(), eager=False, name=None):
    hbm = pl.BlockSpec(memory_space=pltpu.HBM)
    outs = [tuple(o) + ("far",) * (3 - len(o)) for o in outs]
    far = [i for i in range(len(ins)) if i not in raw]
    lead = 0 if coords is None else 1
    late = [i for i, o in enumerate(outs) if o[2] == "far"]
    extra = [pltpu.VMEM(ins[i].shape, ins[i].dtype) for i in far]
    extra += [pltpu.VMEM(outs[i][0], outs[i][1]) for i in late]
    extra.append(pltpu.SemaphoreType.DMA((len(far) + 4 * len(late) + len(save),)))
    count_in, count_out = len(ins), len(outs) + len(save)

    def body(*refs):
        front, refs = refs[:lead], refs[lead:]
        got, put = list(refs[:count_in]), list(refs[count_in : count_in + count_out])
        work = refs[count_in + count_out :]
        own, work = work[: len(scratch)], work[len(scratch) :]
        started = []

        def move(source, target):
            copy = pltpu.make_async_copy(source, target, work[-1].at[len(started)])
            copy.start()
            started.append(copy)
            return copy

        for n, i in enumerate(far):
            got[i] = Arriving(work[n], move(got[i], work[n]))
        leaving = []
        for n, i in enumerate(save):
            got[i].copy.wait()
            got[i].copy = None
            leaving.append(move(got[i].ref, put[len(outs) + n]))
        if eager:
            for i in far:
                got[i].copy.wait()
                got[i].copy = None
        inside = put[: len(outs)]
        for n, i in enumerate(late):
            inside[i] = Leaving(
                work[len(far) + n], put[i], lambda a, b: leaving.append(move(a, b))
            )
        kernel(*front, *got, *inside, *own)
        for i in late:
            if not inside[i].pushed:
                inside[i].push()
        for i in far:
            if got[i].copy is not None:
                got[i].copy.wait()
        for copy in leaving:
            copy.wait()

    specs = [hbm] * len(ins)
    if coords is not None:
        specs = [pl.BlockSpec(memory_space=pltpu.SMEM)] + specs
    saved = [jax.ShapeDtypeStruct(ins[i].shape, ins[i].dtype) for i in save]
    return pl.pallas_call(
        body,
        in_specs=specs,
        out_specs=[hbm] * count_out,
        out_shape=[jax.ShapeDtypeStruct(o[0], o[1]) for o in outs] + saved,
        scratch_shapes=list(scratch) + extra,
        cost_estimate=pl.CostEstimate(flops=0, bytes_accessed=0, transcendentals=0),
        compiler_params=pltpu.CompilerParams(vmem_limit_bytes=58 << 20),
        name=name,
    )(*([] if coords is None else [coords]), *ins)


def aligned(index, size):
    if isinstance(index, int):
        return pl.ds(index * size, size)
    return pl.ds(pl.multiple_of(index * size, size), size)


def pack_kernel(wq, wk, wv, g1, b1, g2, b2, w_inner, head, inner):
    per = wq.shape[0]
    gains = jnp.concatenate([g1[...], b1[...], g2[...], b2[...]], 1)
    for d in range(16):
        cols = pl.ds(((d >> 3) * 4 + (d & 3)) * HD, HD)
        for n, w in enumerate((wq, wk, wv)):
            head[d, pl.ds(n * per, per), :] = w[:, cols]
        head[d, pl.ds(3 * per, 16), :] = jnp.broadcast_to(gains, (16, HD))
    for w in range(8):
        for t in range(4):
            p = (w >> 2) * 16 + t * 4 + (w & 3)
            inner[w, :, pl.ds(t * HD, HD)] = w_inner[:, pl.ds(p * HD, HD)]


def norm_of(values):
    centered = values - jnp.mean(values, -1, keepdims=True)
    inverse = lax.rsqrt(jnp.mean(centered * centered, -1, keepdims=True) + eps_norm)
    return centered * inverse, inverse


def qkv_kernel(at, *refs):
    blocks, pieces = refs[:8], refs[8:10]
    h1, query, kv, gains, weights = refs[10:]
    x, za, zl, y, c = (at[i] for i in range(5))
    width = h1.shape[1]
    per = width // 32
    got = jnp.concatenate([p[d, 3 * per : 3 * per + 1, :] for p in pieces for d in range(16)], 0)
    line = lax.broadcasted_iota(jnp.int32, (32, width), 0)
    lane = lax.broadcasted_iota(jnp.int32, (32, width), 1)
    owner = (line & 15) * 2 + (c ^ (line >> 4))
    mine = lax.shift_right_logical(lane, 5) == owner
    source = lax.broadcasted_iota(jnp.int32, (HD, width), 0)
    target = lax.broadcasted_iota(jnp.int32, (HD, width), 1)
    for k in range(4):
        spread = jnp.where(source == k * per + (target & (per - 1)), 1.0, 0.0).astype(BF)
        gains[k : k + 1, :] = jnp.sum(jnp.where(mine, mm(got, spread), 0.0), 0, keepdims=True)
    gain, bias = gains[0:1, :], gains[1:2, :]
    for n, block in enumerate(blocks):
        xx, zz, yy = x ^ (n >> 2), zl ^ (n >> 1 & 1), y ^ (n & 1)
        for s in range(2):
            j = xx * 8 + (za ^ s) * 4 + zz * 2 + yy
            normed, _ = norm_of(block[s].astype(F32))
            h1[aligned(j, 64), :] = (normed * gain + bias).astype(BF)
    h1.push()
    for n, piece in enumerate(pieces):
        for d in range(16):
            for i in range(3):
                weights[aligned(2 * d + (c ^ n), per), pl.ds(i * HD, HD)] = piece[
                    d, pl.ds(i * per, per), :
                ]
    weights.push()
    for t in range(h1.shape[0] // TILE):
        rows = pl.ds(t * TILE, TILE)
        out = mm(h1[rows, :], weights[...]).astype(BF)
        query[rows, :] = out[:, :HD]
        kv[rows, :] = out[:, HD:]
        query.push(rows)
        kv.push(rows)


def causal(q_share, k_share):
    rows = lax.broadcasted_iota(jnp.int32, (TILE, TILE), 0)
    cols = lax.broadcasted_iota(jnp.int32, (TILE, TILE), 1)
    q_pos = (lax.shift_right_logical(rows, 6) * 2 + q_share) * 64 + (rows & 63)
    k_pos = (lax.shift_right_logical(cols, 6) * 2 + k_share) * 64 + (cols & 63)
    return k_pos <= q_pos


def fine_forward_kernel(at, query, own, other, out, out_f, lse, s_ref):
    tiles = query.shape[0] // TILE
    c = at[4]
    both = (own, other)

    def tile(t, carry):
        rows = aligned(t, TILE)
        q = query[rows, :]

        def score(u, top, masked):
            for n in range(2):
                s = mm_nt(q, both[n][aligned(u, TILE), pl.ds(0, HD)]) * SCALE
                if masked:
                    s = jnp.where(causal(c, c if n == 0 else 1 - c), s, MASKED)
                s_ref[u * 2 + n] = s
                top = jnp.maximum(top, jnp.max(s, -1, keepdims=True))
            return top

        top = jnp.full((TILE, 1), MASKED, F32)
        for u in range(t + 1):
            top = score(u, top, u == t)

        total = jnp.zeros((TILE, 1), F32)
        acc = jnp.zeros((TILE, HD), F32)
        for u in range(t + 1):
            for n in range(2):
                p = jnp.exp(s_ref[u * 2 + n] - top)
                total = total + jnp.sum(p, -1, keepdims=True)
                acc = acc + mm(p.astype(BF), both[n][aligned(u, TILE), pl.ds(HD, HD)])
        acc = acc * (1.0 / total)
        out_f[rows, :] = acc
        out[pl.ds(t * (TILE // 64), TILE // 64)] = acc.astype(BF).reshape(TILE // 64, 64, HD)
        lse[rows, :] = jnp.broadcast_to(top + jnp.log(total), (TILE, HD))
        out.push(pl.ds(t * (TILE // 64), TILE // 64))
        out_f.push(rows)
        lse.push(rows)
        return carry

    for t in range(tiles):
        tile(t, 0)


def place_w_out(at, pieces, out_w, sems):
    x, za, zl, y, c = (at[i] for i in range(5))
    copies = []
    for n, piece in enumerate(pieces):
        side = (zl ^ (n & 1)) * 4 + (y ^ (n >> 1 & 1)) * 2 + (c ^ (n >> 2))
        for i in range(4):
            p = (x ^ (i >> 1)) * 16 + (za ^ (i & 1)) * 8 + side
            copies.append(
                pltpu.make_async_copy(
                    piece.at[i], out_w.at[aligned(p, piece.shape[1]), :], sems.at[len(copies)]
                )
            )
            copies[-1].start()
    return copies


def middle_kernel(at, got, tokens, gains, *refs):
    pieces, (mixed, middle, scaled, inverse, h2, out_w, sems) = refs[:8], refs[8:]
    copies = place_w_out(at, pieces, out_w, sems)
    rows, width = middle.shape
    tok = rows // 2
    for s in range(16):
        head = (s >> 3) * 4 + (s & 3)
        mixed[pl.ds((s >> 2 & 1) * tok, tok), pl.ds(head * HD, HD)] = got[s]
    for s in range(2):
        middle[pl.ds(s * tok, tok), :] = tokens[s].astype(F32)
    for copy in copies:
        copy.wait()
    mixed.push()
    middle[...] += mm(mixed[...], out_w[...])
    middle.push()
    normed, inv = norm_of(middle[...])
    scaled[...] = normed
    inverse[...] = jnp.broadcast_to(inv, (rows, HD))
    h2[...] = (normed * gains[2:3, :] + gains[3:4, :]).astype(BF)


def inner_kernel(at, *refs):
    h2_parts, cot_parts, in_parts, out_parts = refs[:10], refs[10:20], refs[20:24], refs[24:28]
    h2_out, cot_out, outer_out, hidden, grad_inner, keep, send = refs[28:35]
    h2, cot, w_in, w_outer, sems = refs[35:]
    za, zl = at[1], at[2]
    copies = []

    def move(source, target):
        copy = pltpu.make_async_copy(source, target, sems.at[len(copies)])
        copy.start()
        copies.append(copy)

    for n in range(4):
        t = (za ^ (n >> 1)) * 2 + (zl ^ (n & 1))
        for i in range(2):
            rows = in_parts[n].shape[1]
            move(in_parts[n].at[i], w_in.at[aligned(i * 4 + t, rows), :])
    for n in range(4):
        t = (za ^ (n >> 1)) * 2 + (zl ^ (n & 1))
        move(out_parts[n], w_outer.at[aligned(t, out_parts[n].shape[0]), :])
    row = 0
    for part in cot_parts:
        move(part, cot.at[pl.ds(row, part.shape[0]), :])
        row += part.shape[0]
    row = 0
    for part in h2_parts:
        h2[pl.ds(row, part.shape[0]), :] = part[...]
        row += part.shape[0]
    for copy in copies[:8]:
        copy.wait()
    first = mm(h2[pl.ds(0, TILE), :], w_in[...])
    for copy in copies[8:22]:
        copy.wait()
    arrived = 22
    move(h2, h2_out)
    move(cot, cot_out)
    move(w_outer, outer_out)
    half = h2.shape[0] // 2

    def tile(t, carry):
        rows = aligned(t, TILE)
        u = first if t == 0 else mm(h2[rows, :], w_in[...])
        squared = u * u
        bent = jnp.tanh(gelu_coef * (u + 0.044715 * squared * u))
        hidden[rows, :] = (0.5 * u * (1.0 + bent)).astype(BF)
        slope = 0.5 * (1.0 + bent) + 0.5 * u * (1.0 - bent * bent) * gelu_coef * (
            1.0 + 3.0 * 0.044715 * squared
        )
        grad = (mm_nt(cot[rows, :], w_outer[...]) * slope).astype(BF)
        grad_inner[rows, :] = grad
        hidden.push(rows)
        grad_inner.push(rows)
        return mm_nt(grad, w_in[...]), carry

    for out, first_tile in ((keep, 0), (send, half // TILE)):
        for t in range(2):
            rows = pl.ds(t * TILE, TILE)
            out[rows, :] = tile(first_tile + t, 0)[0].astype(BF)
            out.push(rows)
    for copy in copies[arrived:]:
        copy.wait()


def transposed_product(big, left, right, tile=TILE):
    left[0:8, :], right[0:8, :]

    def one(i, carry):
        cols = pl.ds(pl.multiple_of(i * tile, tile), tile)
        big[cols, :] = mm_tn(left[:, cols], right[...])
        return carry

    lax.fori_loop(0, left.shape[1] // tile, one, 0)


def others_of(at):
    za, zl = at[1], at[2]
    return za * 2 + zl, za * 2 + 1 - zl, 2 - 2 * za + zl, 3 - 2 * za - zl


def inner_grad_kernel(at, h2, grad_inner, own, to_l, to_a, to_la, big):
    transposed_product(big, h2, grad_inner)
    n = own.shape[0] // 2
    for t, out in zip(others_of(at), (own, to_l, to_a, to_la)):
        for i in range(2):
            out[pl.ds(i * n, n), :] = big[aligned(i * 4 + t, n), :].astype(out.dtype)


def outer_grad_kernel(at, hidden, cot, w_outer, own, to_l, to_a, to_la, keep, send, big):
    half = keep.shape[0]
    send[...] = mm(hidden[pl.ds(half, half), :], w_outer[...]).astype(BF)
    keep[...] = mm(hidden[pl.ds(0, half), :], w_outer[...])
    transposed_product(big, hidden, cot)
    n = own.shape[0]
    for t, out in zip(others_of(at), (own, to_l, to_a, to_la)):
        out[...] = big[aligned(t, n), :].astype(out.dtype)


def payload_kernel(head_keep, head_got, payload):
    m = head_keep.shape[1] // 4
    for d in range(8):
        rows = pl.ds((d & 3) * m, m)
        payload[d] = (head_keep[d >> 2, rows, :] + head_got[d >> 2, rows, :].astype(F32)).astype(BF)


def last_kernel(
    at, got, near_x, far_x, far_y, query, key, value, sum_a, sum_b, sum_c, sum_d, inner_g
):
    x, y, c = at[0], at[3], at[4]
    per = query.shape[0]
    for w in range(4):
        part = ((near_x, far_x)[w >> 1])[...] if w & 1 == 0 else far_y[w >> 1]
        for s in range(2):
            side = (x ^ (w >> 1)) * 16 + (y ^ (w & 1)) * 2 + (c ^ s)
            for t in range(part.shape[2] // HD):
                inner_g[:, aligned(t * 4 + side, HD)] = part[s, :, t * HD : (t + 1) * HD].astype(F32)
    inner_g.push()
    total = got[0, pl.ds(per, 16), pl.ds(0, HD)].astype(F32)
    for h in range(8):
        for n, out in enumerate((query, key, value)):
            out[:, pl.ds(h * HD, HD)] = got[h, pl.ds(0, per), pl.ds(n * HD, HD)].astype(F32)
        if h:
            total = total + got[h, pl.ds(per, 16), pl.ds(0, HD)].astype(F32)
    for n, out in enumerate((sum_a, sum_b, sum_c, sum_d)):
        out[...] = total[0:1, n * per : (n + 1) * per]


def branch_kernel(at, parts, scaled, inverse, gains, cot, *refs):
    pieces, (grad_middle, branch, go, sums, out_w, sems) = refs[:8], refs[8:]
    copies = place_w_out(at, pieces, out_w, sems)
    rows, width = scaled.shape
    tok = rows // 2
    grad = parts[0].astype(F32)
    for n in range(1, 4):
        grad = grad + parts[n].astype(F32)
    n2 = scaled[...]
    sums[0:1, :] = jnp.sum(grad * n2, 0, keepdims=True)
    sums[1:2, :] = jnp.sum(grad, 0, keepdims=True)
    a = grad * gains[2:3, :]
    grad = inverse[:, 0:1] * (
        a - jnp.mean(a, -1, keepdims=True) - n2 * jnp.mean(a * n2, -1, keepdims=True)
    )
    for s in range(2):
        part = pl.ds(s * tok, tok)
        grad_middle[part, :] = cot[s].astype(F32) + grad[s * tok : (s + 1) * tok]
    grad_middle.push()
    branch[...] = grad_middle[...].astype(BF)
    branch.push()
    for copy in copies:
        copy.wait()
    out = mm_nt(branch[...], out_w[...]).astype(BF)
    for s in range(16):
        head = (s >> 3) * 4 + (s & 3)
        seq = s >> 2 & 1
        go[s] = out[seq * tok : (seq + 1) * tok, head * HD : (head + 1) * HD]


def fine_backward_kernel(at, query, own, other, go_ref, out_f, lse_ref, gq_ref, keep, send, acc):
    rows_all = query.shape[0]
    tiles = rows_all // TILE
    c = at[4]
    both = (own, other)
    keep[...] = jnp.zeros(keep.shape, keep.dtype)
    acc[...] = jnp.zeros_like(acc)
    totals = (keep, acc)

    def tile(t, carry):
        rows = aligned(t, TILE)
        q = query[rows, :]
        go = go_ref[pl.ds(t * (TILE // 64), TILE // 64)].reshape(TILE, HD)
        delta = jnp.sum(go.astype(F32) * out_f[rows, :], -1, keepdims=True)
        lse = lse_ref[rows, 0:1]

        def one(u, gq, masked):
            cols = aligned(u, TILE)
            for n in range(2):
                kk = both[n][cols, pl.ds(0, HD)]
                p = jnp.exp(mm_nt(q, kk) * SCALE - lse)
                if masked:
                    p = jnp.where(causal(c, c if n == 0 else 1 - c), p, 0.0)
                totals[n][cols, pl.ds(HD, HD)] += mm_tn(p.astype(BF), go)
                ds = (p * (mm_nt(go, both[n][cols, pl.ds(HD, HD)]) - delta)).astype(BF)
                totals[n][cols, pl.ds(0, HD)] += mm_tn(ds, q)
                gq = gq + mm(ds, kk)
            return gq

        gq = jnp.zeros((TILE, HD), F32)
        for u in range(t + 1):
            gq = one(u, gq, u == t)
        gq_ref[rows, :] = (gq * SCALE).astype(BF)
        gq_ref.push(rows)
        return carry

    for t in range(tiles):
        tile(t, 0)
    send[:, :HD] = (acc[:, :HD] * SCALE).astype(BF)
    send[:, HD:] = acc[:, HD:].astype(BF)
    send.push()
    keep[:, :HD] = keep[:, :HD] * SCALE


def partial_kernel(at, *refs):
    blocks, (gq, keep, got, weights) = refs[:8], refs[8:12]
    grads, parts, sums, tokens, sems = refs[12:]
    x, za, zl, y = (at[i] for i in range(4))
    copies = []
    for n in range(8):
        for s in range(2):
            j = (x ^ (n >> 2)) * 8 + (za ^ s) * 4 + (zl ^ (n >> 1 & 1)) * 2 + (y ^ (n & 1))
            copies.append(
                pltpu.make_async_copy(
                    blocks[n].at[s], tokens.at[aligned(j, 64), :], sems.at[len(copies)]
                )
            )
            copies[-1].start()
    for copy in copies:
        copy.wait()
    tiles = gq.shape[0] // TILE
    for t in range(tiles):
        rows = pl.ds(t * TILE, TILE)
        grads[rows, pl.ds(0, HD)] = gq[rows, :]
        grads[rows, pl.ds(HD, 2 * HD)] = (keep[rows, :] + got[rows, :].astype(F32)).astype(BF)
        part = mm_nt(grads[rows, :], weights[...])
        normed, _ = norm_of(tokens[rows, :].astype(F32))
        one = jnp.sum(part * normed, 0, keepdims=True)
        two = jnp.sum(part, 0, keepdims=True)
        if t == 0:
            sums[0:1, :] = one
            sums[1:2, :] = two
        else:
            sums[0:1, :] += one
            sums[1:2, :] += two
        for i in range(4):
            parts[(t >> 1) * 4 + i, za ^ (t & 1)] = part[i * 64 : (i + 1) * 64].astype(BF)
        grads.push(rows)
        if t & 1:
            parts.push(pl.ds((t >> 1) * 4, 4))


def total_kernel(parts, keep, send):
    total = parts[0, 0].astype(F32)
    other = parts[0, 1].astype(F32)
    for n in range(1, 8):
        total = total + parts[n, 0].astype(F32)
        other = other + parts[n, 1].astype(F32)
    keep[...] = total
    send[...] = other.astype(BF)


def head_grad_kernel(at, left, right, sums, keep, send, big):
    c = at[4]
    per = left.shape[1] // 32
    transposed_product(big, left, right)
    spare = keep.shape[2] - sums.shape[1]
    for q in range(16):
        keep[q, pl.ds(0, per), :] = big[aligned(2 * q + c, per), :]
        send[q, pl.ds(0, per), :] = big[aligned(2 * q + 1 - c, per), :].astype(BF)
    pad = jnp.zeros((16, spare), F32)
    for q in range(16):
        pair = jnp.concatenate([sums[2 * q : 2 * q + 2, :], pad[:2]], 1)
        mine = jnp.where(c == 0, pair[0:1], pair[1:2])
        other = jnp.where(c == 0, pair[1:2], pair[0:1])
        keep[q, pl.ds(per, 16), :] = jnp.broadcast_to(mine, (16, keep.shape[2]))
        send[q, pl.ds(per, 16), :] = jnp.broadcast_to(other, (16, keep.shape[2])).astype(BF)


def core_grad_kernel(at, left, right, keep, send, big):
    c = at[4]
    per = left.shape[1] // 32
    transposed_product(big, left, right)

    def deal(q, carry):
        rows = aligned(q, per)
        keep[rows, :] = big[aligned(2 * q + c, per), :]
        send[rows, :] = big[aligned(2 * q + 1 - c, per), :].astype(BF)
        return carry

    lax.fori_loop(0, 16, deal, 0)


def input_kernel(at, keep, got, tokens, grad_middle, gains, grad_tokens):
    za = at[1]
    tok = tokens.shape[1]
    for n in range(2):
        seq = za if n == 0 else 1 - za
        part = keep[...] if n == 0 else got[...].astype(F32)
        n1, inv = norm_of(tokens[seq].astype(F32))
        a = part * gains[0:1, :]
        grad_tokens[seq] = grad_middle[aligned(seq, tok), :] + inv * (
            a - jnp.mean(a, -1, keepdims=True) - n1 * jnp.mean(a * n1, -1, keepdims=True)
        )


def far_kernel(keep, got, own, on_z, on_y, far_a, far_b):
    n = own.shape[0]
    for i, out in enumerate((own, on_z, on_y)):
        rows = pl.ds(i * n, n)
        out[...] = keep[rows, :] + got[rows, :].astype(F32)
    for i, out in enumerate((far_a, far_b)):
        rows = pl.ds(3 * n + i * (n // 2), n // 2)
        out[...] = (keep[rows, :] + got[rows, :].astype(F32)).astype(BF)


def near_kernel(on_z, on_y, got_a, got_b, send_z, send_y):
    n = got_a.shape[0]
    first, second = pl.ds(0, n), pl.ds(n, n)
    send_z[first, :] = (on_z[first, :] + got_a[...].astype(F32)).astype(BF)
    send_z[second, :] = on_z[second, :].astype(BF)
    send_y[first, :] = on_y[first, :].astype(BF)
    send_y[second, :] = (on_y[second, :] + got_b[...].astype(F32)).astype(BF)


def result_sum_kernel(middle, own, got_z, got_y, out):
    out[...] = (
        middle[...] + own[...] + got_z[...].astype(F32) + got_y[...].astype(F32)
    ).astype(BF)


def fold_kernel(at, keep, got, parts):
    x, y = at[0], at[3]
    rows = parts.shape[1]
    for n in range(4):
        here = pl.ds(n * rows, rows)
        z = x ^ (1 if n in (1, 3) else 0)
        w = y ^ (1 if n in (2, 3) else 0)
        parts[z * 2 + w] = (keep[here, :].astype(F32) + got[here, :].astype(F32)).astype(BF)


def stage(*values):
    return lax.optimization_barrier(values)


def grow(v, axis):
    return jnp.concatenate([v, swap(v, axis)], 0)


def half_swap(v, axis):
    return swap(pick(v, 1 - lax.axis_index(axis)), axis)


def fine_layer(
    tokens,
    cotangent,
    ln1_gain,
    ln1_bias,
    w_query,
    w_key,
    w_value,
    w_out,
    ln2_gain,
    ln2_bias,
    w_inner,
    w_outer,
):
    seqs, tok, width = tokens.shape
    rows = seqs * tok
    half = rows // 2
    per = w_query.shape[0]
    unit = w_outer.shape[0]
    hidden_units = 4 * unit
    all_rows = 8 * rows
    coords = jnp.stack([lax.axis_index(a) for a in ("x", "za", "zl", "y", "c")]).astype(jnp.int32)
    x, za = lax.axis_index("x"), lax.axis_index("za")
    cube, owners = ("x", "zl", "y"), ("x", "za", "zl", "y")
    cot = cotangent.reshape(rows, width)

    def split(axis, keep, got, shape):
        keep, got = keep.reshape(shape), got.reshape(shape)
        i = lax.axis_index(axis)
        mine = pick(keep, i, 1) + pick(got, i, 1).astype(F32)
        return mine, (pick(keep, 1 - i, 1) + pick(got, 1 - i, 1).astype(F32)).astype(BF)

    head_w, inner_w = call(
        pack_kernel,
        [((16, 3 * per + 16, HD), BF), ((8, per, hidden_units), BF)],
        [w_query, w_key, w_value]
        + [g.reshape(1, per) for g in (ln1_gain, ln1_bias, ln2_gain, ln2_bias)]
        + [w_inner],
        name="pack",
    )
    moved, head_w, inner_w, w_out, w_outer = stage(
        swap(pick(tokens, 1 - za), "za"), head_w, inner_w, w_out, w_outer
    )
    block = jnp.stack([pick(tokens, za), moved])
    on_x, on_z, on_y, head_w = stage(
        swap(block, "x"), swap(block, "zl"), swap(block, "y"), head_w
    )
    on_xz, on_xy, on_zy, on_xyz, head_w, w_out_z = stage(
        swap(on_x, "zl"),
        swap(on_y, "x"),
        swap(on_z, "y"),
        lax.ppermute(block, cube, [(i, 7 - i) for i in range(8)]),
        lax.all_to_all(head_w, owners, 0, 0, tiled=True),
        swap(after(w_out, on_x), "za"),
    )
    head_c, w_outer, inner_w, w_out_z = stage(swap(head_w, "c"), w_outer, inner_w, w_out_z)
    blocks = [block, on_y, on_z, on_zy, on_x, on_xy, on_xz, on_xyz]
    out_w = jnp.stack([w_out, w_out_z])
    h1, query, kv, gains, head_w = call(
        qkv_kernel,
        [
            ((16 * tok, width), BF),
            ((16 * tok, HD), BF),
            ((16 * tok, 2 * HD), BF),
            ((8, width), F32),
            ((width, 3 * HD), BF),
        ],
        blocks + [head_w, head_c],
        coords,
        name="qkv",
    )
    kv, query, out_x, outer_a, outer_l, inner_w = stage(
        kv,
        query,
        swap(out_w, "x"),
        swap(w_outer, "za"),
        swap(w_outer, "zl"),
        lax.all_to_all(inner_w, ("x", "y", "c"), 0, 0, tiled=True),
    )
    out_w = jnp.concatenate([out_w, out_x], 0)
    kv_other, out_w, inner_w = stage(swap(kv, "c"), out_w, inner_w)
    out, out_f, lse, query, kv, kv_other = call(
        fine_forward_kernel,
        [((16, tok, HD), BF), ((16 * tok, HD), F32), ((16 * tok, HD), F32)],
        [query, kv, kv_other],
        coords,
        save=(0, 1, 2),
        scratch=[pltpu.VMEM((2 * 16 * tok // TILE, TILE, TILE), F32)],
        name="attention_forward",
    )
    out, out_z, out_y, inner_a, inner_l, cot = stage(
        out,
        swap(out_w, "zl"),
        swap(out_w, "y"),
        swap(inner_w, "za"),
        swap(inner_w, "zl"),
        cot,
    )
    mixed, cot_z, cot_y, cot_c, out_zy, outer_la, inner_la, *out_c = stage(
        lax.all_to_all(out, owners, 0, 0, tiled=True),
        swap(cot, "x"),
        swap(cot, "y"),
        swap(cot, "c"),
        swap(out_z, "y"),
        swap(outer_a, "zl"),
        swap(inner_a, "zl"),
        swap(out_w, "c"),
        swap(out_z, "c"),
        swap(out_y, "c"),
    )
    (out_zyc,) = stage(swap(out_zy, "c"))
    pieces = [out_w, out_z, out_y, out_zy] + out_c + [out_zyc]
    mixed, middle, scaled, inverse, h2 = call(
        middle_kernel,
        [
            ((rows, width), BF),
            ((rows, width), F32),
            ((rows, width), F32),
            ((rows, HD), F32),
            ((rows, width), BF),
        ],
        [mixed, tokens, gains] + pieces,
        coords,
        raw=range(3, 11),
        scratch=[pltpu.VMEM((width, width), BF), pltpu.SemaphoreType.DMA((32,))],
        name="middle",
    )
    cot_z, cot_y = after(cot_z, h2), after(cot_y, h2)
    h2_z, h2_y, h2_c, cot_a, cot_b, cot_zc, cot_yc = stage(
        swap(h2, "x"),
        swap(h2, "y"),
        swap(h2, "c"),
        swap(cot_z[:half], "y"),
        swap(cot_y[half:], "x"),
        swap(cot_z, "c"),
        swap(cot_y, "c"),
    )
    h2_a, h2_b, h2_zc, h2_yc, cot_ac, cot_bc = stage(
        swap(h2_z[:half], "y"),
        swap(h2_y[half:], "x"),
        swap(h2_z, "c"),
        swap(h2_y, "c"),
        swap(cot_a, "c"),
        swap(cot_b, "c"),
    )
    h2_ac, h2_bc = stage(swap(h2_a, "c"), swap(h2_b, "c"))
    h2_all, cot_all, outer_w, hidden, grad_inner, keep, send = call(
        inner_kernel,
        [
            ((all_rows, width), BF, "raw"),
            ((all_rows, width), BF, "raw"),
            ((hidden_units, width), BF, "raw"),
            ((all_rows, hidden_units), BF),
            ((all_rows, hidden_units), BF),
            ((all_rows // 2, width), BF),
            ((all_rows // 2, width), BF),
        ],
        [h2, h2_z, h2_y, h2_a, h2_b, h2_c, h2_zc, h2_yc, h2_ac, h2_bc]
        + [cot, cot_z, cot_y, cot_a, cot_b, cot_c, cot_zc, cot_yc, cot_ac, cot_bc]
        + [p.reshape(2, 4 * per, hidden_units) for p in (inner_w, inner_l, inner_a, inner_la)]
        + [w_outer, outer_l, outer_a, outer_la],
        coords,
        raw=range(10, 28),
        scratch=[
            pltpu.VMEM((all_rows, width), BF),
            pltpu.VMEM((all_rows, width), BF),
            pltpu.VMEM((width, hidden_units), BF),
            pltpu.VMEM((hidden_units, width), BF),
            pltpu.SemaphoreType.DMA((25,)),
        ],
        name="inner",
    )

    (got,) = stage(swap(send, "c"))
    (parts,) = call(
        fold_kernel, [((4, rows, width), BF)], [keep, got], coords, name="fold"
    )
    n_in, n_out = 8 * per, unit
    inner_g, in_l, in_a, in_la = call(
        inner_grad_kernel,
        [((n_in, hidden_units), F32)] + [((n_in, hidden_units), BF)] * 3,
        [h2_all, grad_inner],
        coords,
        scratch=[pltpu.VMEM((width, hidden_units), F32)],
        name="inner_grad",
    )
    parts, inner_g, in_l, in_a, in_la = stage(parts, inner_g, in_l, in_a, in_la)
    outer_g, outer_l, outer_a, outer_la, res_keep, res_send = call(
        outer_grad_kernel,
        [((n_out, width), F32)]
        + [((n_out, width), BF)] * 3
        + [((all_rows // 2, width), F32), ((all_rows // 2, width), BF)],
        [after(hidden, in_l), cot_all, outer_w],
        coords,
        scratch=[pltpu.VMEM((hidden_units, width), F32)],
        name="outer_grad",
    )
    parts, in_l, in_a, outer_g, outer_l, outer_a, outer_la, res_keep, res_send, in_la = stage(
        lax.all_to_all(parts, ("x", "y"), 0, 0, tiled=True),
        swap(in_l, "zl"),
        swap(in_a, "za"),
        outer_g,
        outer_l,
        outer_a,
        outer_la,
        res_keep,
        res_send,
        in_la,
    )
    grad_middle, branch, go, sums_two = call(
        branch_kernel,
        [
            ((rows, width), F32),
            ((rows, width), BF),
            ((16, tok, HD), BF),
            ((2, width), F32),
        ],
        [parts, scaled, inverse, gains, cotangent] + pieces,
        coords,
        raw=range(5, 13),
        scratch=[pltpu.VMEM((width, width), BF), pltpu.SemaphoreType.DMA((32,))],
        name="branch",
    )
    go, branch, res_got, outer_l, outer_a = stage(
        go, branch, swap(res_send, "c"), outer_l, outer_a
    )
    res = (res_keep + res_got.astype(F32)).reshape(4, rows, width)
    far_a, far_b = res[3, :half].astype(BF), res[3, half:].astype(BF)
    out_keep, out_send = call(
        core_grad_kernel,
        [((width // 2, width), F32), ((width // 2, width), BF)],
        [mixed, branch],
        coords,
        scratch=[pltpu.VMEM((width, width), F32)],
        name="out_grad",
    )
    diagonal = [(i, 3 - i) for i in range(4)]
    go, outer_l, outer_a, in_la, outer_la, out_keep, out_send, res, far_a, far_b = stage(
        lax.all_to_all(go, owners, 0, 0, tiled=True),
        swap(outer_l, "zl"),
        swap(outer_a, "za"),
        in_la,
        outer_la,
        out_keep,
        out_send,
        res,
        far_a,
        far_b,
    )
    gq, keep, send = call(
        fine_backward_kernel,
        [((16 * tok, HD), BF), ((16 * tok, 2 * HD), F32), ((16 * tok, 2 * HD), BF)],
        [query, kv, kv_other, go, out_f, lse],
        coords,
        scratch=[pltpu.VMEM((16 * tok, 2 * HD), F32)],
        name="attention_backward",
    )
    gq, keep, send, got_a, got_b, out_got, in_la = stage(
        gq,
        keep,
        send,
        swap(far_a, "y"),
        swap(far_b, "x"),
        swap(out_send, "c"),
        lax.ppermute(in_la, ("za", "zl"), diagonal),
    )
    out_keep, out_send = split("x", out_keep, out_got, (1, 2, 8 * per, width))
    got, out_keep, out_send, outer_la = stage(swap(send, "c"), out_keep, out_send, outer_la)
    grads, parts, sums = call(
        partial_kernel,
        [
            ((16 * tok, 3 * HD), BF),
            ((8, 2, tok, width), BF),
            ((2, width), F32),
        ],
        blocks + [gq, keep, got, head_w],
        coords,
        raw=range(8),
        scratch=[pltpu.VMEM((16 * tok, width), BF), pltpu.SemaphoreType.DMA((16,))],
        name="partial",
    )
    grads, parts, sums, out_keep, out_got, outer_la = stage(
        grads,
        parts,
        sums,
        out_keep,
        swap(out_send, "x"),
        lax.ppermute(outer_la, ("za", "zl"), diagonal),
    )
    parts = lax.all_to_all(parts, cube, 0, 0, tiled=True)
    sums = jnp.concatenate([sums, sums_two], 0)
    sums = sums.reshape(4, 32, per).transpose(1, 0, 2).reshape(32, 4 * per)
    head_keep, head_send = call(
        head_grad_kernel,
        [((16, per + 16, 3 * HD), F32), ((16, per + 16, 3 * HD), BF)],
        [h1, grads, sums],
        coords,
        scratch=[pltpu.VMEM((width, 3 * HD), F32)],
        name="head_grad",
    )
    head_keep, head_send = stage(head_keep, head_send)
    out_keep, out_send = split(
        "y", out_keep, after(out_got, head_send), (4, 2, per, width)
    )
    inner_g = inner_g + after(in_l, head_send).astype(F32) + in_a.astype(F32) + in_la.astype(F32)
    inner_g = inner_g.astype(BF).reshape(4, 2, per, hidden_units)
    got_a = after(got_a, head_send)
    res_z = jnp.concatenate([res[1, :half] + got_a.astype(F32), res[1, half:]], 0).astype(BF)
    res_y = jnp.concatenate([res[2, :half], res[2, half:] + got_b.astype(F32)], 0).astype(BF)
    inner_own = pick(inner_g, lax.axis_index("c"), 1)
    inner_send = pick(inner_g, 1 - lax.axis_index("c"), 1)
    head_keep, head_got, out_keep, out_send, inner_own, inner_send, res_z, res_y = stage(
        head_keep, swap(head_send, "c"), out_keep, out_send, inner_own, inner_send, res_z, res_y
    )
    head_keep, head_send = split("za", head_keep, head_got, (2, 2, 4 * (per + 16), 3 * HD))
    head_keep, head_send, out_send = stage(head_keep, head_send, out_send)
    outer_g = (
        outer_g
        + after(outer_l, head_send).astype(F32)
        + outer_a.astype(F32)
        + outer_la.astype(F32)
    )
    head_keep, head_got, out_keep, out_got, inner_got, got_z, res_y, outer_g = stage(
        head_keep,
        swap(head_send, "za"),
        out_keep,
        swap(out_send, "y"),
        swap(inner_send, "c"),
        swap(res_z, "x"),
        res_y,
        outer_g,
    )
    inner_g = jnp.stack([inner_own, inner_got]).reshape(2, 2, 2, per, hidden_units)
    x = lax.axis_index("x")
    near_x, inner_send = pick(inner_g, x, 1), pick(inner_g, 1 - x, 1)
    (payload,) = call(
        payload_kernel,
        [((8, per + 16, 3 * HD), BF)],
        [head_keep, head_got],
        name="payload",
    )
    out_keep, out_send = split("za", out_keep, out_got, (1, 2, 2 * per, width))
    parts, payload, near_x, inner_send, out_keep, out_send = stage(
        parts, payload, near_x, inner_send, out_keep, out_send
    )
    payload = lax.all_to_all(payload, cube, 0, 0, tiled=True)
    total, send = call(
        total_kernel, [((tok, width), F32), ((tok, width), BF)], [parts], name="total"
    )
    total, send, near_x, inner_send, out_send, res_y = stage(
        total, send, near_x, inner_send, out_send, res_y
    )
    got, out_send, got_y, far_x, near_x = stage(
        swap(send, "za"),
        out_send,
        swap(res_y, "y"),
        swap(inner_send, "x"),
        near_x,
    )
    y = lax.axis_index("y")
    inner_send = jnp.stack([pick(near_x, 1 - y, 1), pick(far_x, 1 - y, 1)])
    near_x, far_x = pick(near_x, y, 1), pick(far_x, y, 1)
    (grad_tokens,) = call(
        input_kernel,
        [((seqs, tok, width), F32)],
        [total, got, tokens, grad_middle, gains],
        coords,
        name="input",
    )
    result = (
        middle + res[0] + after(got_z, got).astype(F32) + got_y.astype(F32)
    ).astype(BF)
    payload, out_got, grad_tokens, result, far_y, near_x, far_x = stage(
        payload,
        swap(out_send, "za"),
        grad_tokens,
        result,
        swap(inner_send, "y"),
        near_x,
        far_x,
    )
    out_keep, out_send = split("zl", out_keep, out_got, (1, 2, per, width))
    out_keep, out_send = stage(out_keep, out_send)
    query_g, key_g, value_g, *sums, inner_g = call(
        last_kernel,
        [((per, width), F32)] * 3
        + [((1, per), F32)] * 4
        + [((per, 8 * hidden_units), F32)],
        [payload, near_x, far_x, far_y],
        coords,
        name="last",
    )
    query_g, key_g, value_g, inner_g, out_got, result, *sums = stage(
        query_g, key_g, value_g, inner_g, swap(out_send, "zl"), result, *sums
    )
    sums = [v.reshape(per) for v in sums]
    return (
        result.reshape(seqs, tok, width),
        grad_tokens,
        sums[0],
        sums[1],
        query_g,
        key_g,
        value_g,
        out_keep[0] + out_got[0].astype(F32),
        sums[2],
        sums[3],
        inner_g,
        outer_g,
    )


def solution(mesh):
    blocks = mesh.shape["blk"]
    if blocks == 16:
        sizes = (2, 2, 1, 2, 2, 2)
        roles = (True, "za", ("x", "zl", "y"), ("c",), ("x", "za", "zl", "y"))
    else:
        sizes = (2, 8, blocks // 64, 2, 2, 2)
        roles = (False, "x", ("za",), ("zb", "zl", "y", "c"), ("x", "za"))
    fine = Mesh(mesh.devices.reshape(sizes), AXES)
    tok, row, vec = P(None, AXES, None), P(AXES, None), P(AXES)
    in_specs = (tok, tok, vec, vec, row, row, row, row, vec, vec, row, row)
    out_specs = (tok, tok, vec, vec, row, row, row, row, vec, vec, row, row)
    return jax.shard_map(
        fine_layer if blocks == 16 else functools.partial(on_device, roles),
        mesh=fine,
        in_specs=in_specs,
        out_specs=out_specs,
        check_vma=False,
    )
```
